32 devices in a mesh: ctx: 8 (over y, x, core), fsdp: 4 (over z).
Axes of the slice: x: 2, y: 2, z: 4, core: 2. Of those that a mesh axis runs over, the one named last changes fastest.
Arguments:
- token_embed: bfloat16 [8, 2048, 768], P('fsdp', 'ctx'), may hold values from -6 to 6
- bigram_ids: int32 [8, 2048], P('fsdp', 'ctx'), may hold values from 0 to 409599, as said below
- trigram_ids: int32 [8, 2048], P('fsdp', 'ctx'), may hold values from 0 to 409599, as said below
- bigram_table: bfloat16 [409600, 192], P(('ctx', 'fsdp')), may hold values from -6 to 6
- trigram_table: bfloat16 [409600, 192], P(('ctx', 'fsdp')), may hold values from -6 to 6
- block_deal: int32 [16], replicated, may hold values from 0 to 15, each once
- lookup_weight: bfloat16 [192, 768], P('fsdp'), may hold values from -0.3125 to 0.3125
- attention_gain: bfloat16 [768], P('fsdp'), may hold values from 0.099609375 to 1.8984375
- joined_weight: bfloat16 [768, 2304], P('fsdp'), may hold values from -0.3125 to 0.3125
- output_weight: bfloat16 [768, 768], P('fsdp'), may hold values from -0.625 to 0.625
- feedforward_gain: bfloat16 [768], P('fsdp'), may hold values from 0.099609375 to 1.8984375
- expand_weight: bfloat16 [768, 4096], P('fsdp'), may hold values from -0.21875 to 0.21875
- contract_weight: bfloat16 [2048, 768], P('fsdp'), may hold values from -0.1875 to 0.1875
- cotangent: bfloat16 [8, 2048, 768], P('fsdp', 'ctx'), may hold values from -6 to 6
Outputs:
- layer_output: bfloat16 [8, 2048, 768], P('fsdp', 'ctx')
- token_grad: float32 [8, 2048, 768], P('fsdp', 'ctx')
- bigram_grad: float32 [409600, 192], P(('ctx', 'fsdp'))
- trigram_grad: float32 [409600, 192], P(('ctx', 'fsdp'))
- lookup_grad: float32 [192, 768], P('fsdp')
- attention_grad: float32 [768], P('fsdp')
- joined_grad: float32 [768, 2304], P('fsdp')
- output_grad: float32 [768, 768], P('fsdp')
- feedforward_grad: float32 [768], P('fsdp')
- expand_grad: float32 [768, 4096], P('fsdp')
- contract_grad: float32 [2048, 768], P('fsdp')
The draws below stay inside these ranges and needn't reach their ends.
Inputs may be any that keep to these rules, and one draw needn't show every extreme that they name: `bigram_ids`: row ids of the 2-gram table. Rows are owned in shards of 12800, shard id // 12800 by the device of that index along ctx+fsdp. The ids stored on one device name any one shard at most 32 times, and one shard exactly 32 times on every device. `trigram_ids`: row ids of the 3-gram table, with the same ownership and the same bound 32 on one device's ids in one shard, reached on every device.
All inputs are finite; a program needn't handle non-finite values.
Results may differ from the reference program's by a relative error of at most 0.017.
The reference program's roundings to bfloat16 on the way count: a program that leaves them out, or rounds other values in their place, can miss the bound.
Values may be sent and summed in bfloat16 or wider, within the bound.
No kernel may reach another device: no remote copies, remote signals or barrier semaphores. Data moves between devices by JAX's collectives and lax.ppermute only.
A program may use at most 384 MiB of HBM per device.

```python
import math
import jax
import jax.numpy as jnp
from jax import lax

D = 768
HEADS = 12
HD = 64
FF = 2048
E = 192
TROWS_DEV = 12800
LOC = 256
MB = 2
ABLK = 256
PIECE = 128
PIECES = 16
SEQ = 2048
SEQS = 8
CAP = 32
ROWS = 409600
N_CTX = 8
N_FSDP = 4


def owner_rows(key, salt):
    key = jax.random.fold_in(key, salt)
    devices = N_CTX * N_FSDP
    block_rows = MB * LOC
    pool_size = CAP * devices
    hot_key, block_key = jax.random.split(key)
    hottest = jax.random.randint(hot_key, (), 0, devices)
    pool_owner = jnp.arange(pool_size, dtype=jnp.int32) // CAP
    pool_rank = jnp.arange(pool_size, dtype=jnp.int32) % CAP

    def one_block(block_index, subkey):
        order_key, mix_key, offset_key = jax.random.split(subkey, 3)
        scores = jax.random.permutation(order_key, pool_size).astype(jnp.int32)
        scores = jnp.where(pool_owner == hottest, -1 - pool_rank, scores)
        first_entry = pool_rank == 0
        edge_low = (pool_owner == 0) & first_entry & (block_index == 0)
        edge_high = (pool_owner == devices - 1) & first_entry & (block_index == 0)
        scores = jnp.where(edge_low, -CAP - 2, scores)
        scores = jnp.where(edge_high, -CAP - 3, scores)
        chosen = jnp.argsort(scores, stable=True)[:block_rows]
        owners = pool_owner[chosen]
        offsets = jax.random.randint(offset_key, (block_rows,), 0, TROWS_DEV)
        position = jnp.arange(block_rows, dtype=jnp.int32)
        offsets = jnp.where((block_index == 0) & (position == 0), TROWS_DEV - 1, offsets)
        offsets = jnp.where((block_index == 0) & (position == 1), 0, offsets)
        identifiers = owners * TROWS_DEV + offsets
        return jax.random.permutation(mix_key, identifiers)
    block_keys = jax.random.split(block_key, devices)
    blocked = jax.vmap(one_block)(jnp.arange(devices, dtype=jnp.int32), block_keys)
    blocked = blocked.reshape(N_FSDP, N_CTX, MB, LOC).transpose(0, 2, 1, 3)
    return blocked.reshape(N_FSDP * MB, N_CTX * LOC).astype(jnp.int32)


def draw_bigram_ids(key, part):
    return owner_rows(key, 2)


def draw_trigram_ids(key, part):
    return owner_rows(key, 3)


def steps_of(rng, shape, pieces, low, top_value):
    level, own = 1.0, jax.random.fold_in(rng, 6)
    for dim, parts in pieces:
        heights = jnp.exp(jax.random.uniform(jax.random.fold_in(own, dim), (parts,), jnp.float32, low / len(pieces), top_value / len(pieces)))
        level = level * jnp.repeat(heights, shape[dim] // parts).reshape([-1 if axis == dim else 1 for axis in range(len(shape))])
    return level


def normal_values(key, shape, spread, reach, pieces=(), kind=jnp.bfloat16):
    array = spread * jax.random.normal(key, shape, jnp.float32)
    if pieces:
        array = array * steps_of(key, shape, pieces, -0.22, 0.18)
    return jnp.clip(array, -reach, reach).astype(kind)


def setup_inputs(seed: int = 0) -> dict:
    seeds = jax.random.split(jax.random.key(seed), 15)
    token_embed = normal_values(seeds[0], (SEQS, SEQ, D), 1.0, 6.0, ((0, 4), (1, 8)))
    bigram_ids = draw_bigram_ids(jax.random.fold_in(seeds[14], 71), 0)
    trigram_ids = draw_trigram_ids(jax.random.fold_in(seeds[14], 71), 0)
    bigram_table = normal_values(seeds[3], (ROWS, E), 1.0, 6.0, ((0, 32),))
    trigram_table = normal_values(seeds[4], (ROWS, E), 1.0, 6.0, ((0, 32),))
    block_deal = jax.random.permutation(seeds[5], PIECES).astype(jnp.int32)
    lookup_weight = normal_values(seeds[6], (E, D), (2 * E) ** -0.5, 0.3125, ((0, 4),))
    attention_gain = jnp.clip(1.0 + 0.18 * jax.random.normal(seeds[7], (D,), jnp.float32), 0.099609375, 1.8984375).astype(jnp.bfloat16)
    joined_weight = normal_values(seeds[8], (D, 3 * D), (D // 2) ** -0.5, 0.3125, ((0, 4),))
    output_weight = normal_values(seeds[9], (D, D), (D // 8) ** -0.5, 0.625, ((0, 4),))
    feedforward_gain = jnp.clip(1.0 + 0.18 * jax.random.normal(seeds[10], (D,), jnp.float32), 0.099609375, 1.8984375).astype(jnp.bfloat16)
    expand_weight = normal_values(seeds[11], (D, 2 * FF), D ** -0.5, 0.21875, ((0, 4),))
    contract_weight = normal_values(seeds[12], (FF, D), (FF // 2) ** -0.5, 0.1875, ((0, 4),))
    cotangent = normal_values(seeds[13], (SEQS, SEQ, D), 1.0, 6.0, ((0, 4), (1, 8)))
    return dict(token_embed=token_embed, bigram_ids=bigram_ids, trigram_ids=trigram_ids, bigram_table=bigram_table, trigram_table=trigram_table, block_deal=block_deal, lookup_weight=lookup_weight, attention_gain=attention_gain, joined_weight=joined_weight, output_weight=output_weight, feedforward_gain=feedforward_gain, expand_weight=expand_weight, contract_weight=contract_weight, cotangent=cotangent)


highest = lax.Precision.HIGHEST
epsilon = 1e-05
masked_score = -1e+30

@jax.custom_vjp
def low(v):
    return lax.optimization_barrier(v.astype(jnp.bfloat16)).astype(jnp.float32)

@jax.custom_vjp
def low_back(v):
    return v

def low_keep(v):
    return (low(v), None)

def low_pass(kept, grad):
    return (grad,)

def back_keep(v):
    return (v, None)

def back_low(kept, grad):
    return (low(grad),)
low.defvjp(low_keep, low_pass)
low_back.defvjp(back_keep, back_low)

def rotate(values, cosines, sines):
    half_size = values.shape[-1] // 2
    front_half = values[..., :half_size]
    back_half = values[..., half_size:]
    cosine_part = cosines[:, None, :]
    sine_part = sines[:, None, :]
    return jnp.concatenate([front_half * cosine_part - back_half * sine_part, back_half * cosine_part + front_half * sine_part], axis=-1)

def normalize(rows, gain):
    return rows * lax.rsqrt(lax.optimization_barrier(jnp.mean(rows * rows, axis=-1, keepdims=True)) + epsilon) * gain

def reference(token_embed, bigram_ids, trigram_ids, bigram_table, trigram_table, block_deal, lookup_weight, attention_gain, joined_weight, output_weight, feedforward_gain, expand_weight, contract_weight, cotangent):
    slot_index = jnp.arange(SEQ, dtype=jnp.int32)
    position = block_deal[slot_index // PIECE] * PIECE + slot_index % PIECE
    blocks = position // ABLK
    frequency = jnp.exp(-math.log(10000.0) * (2.0 * jnp.arange(HD // 2, dtype=jnp.float32) / HD))
    angles = position.astype(jnp.float32)[:, None] * frequency[None, :]
    cosines = jnp.cos(angles)
    sines = jnp.sin(angles)
    query_rows = math.gcd(SEQ, 512)
    score_scale = HD ** (-0.5)

    def forward(token_rows, gram_rows, params):
        lookup_matrix, first_gain, joined_matrix, output_matrix, second_gain, expand_matrix, contract_matrix = params
        embedded = low(gram_rows)
        start_rows = token_rows + low_back(jnp.dot(embedded, lookup_matrix, precision=highest))
        hidden_first = low(normalize(start_rows, first_gain))
        projected = low_back(jnp.dot(hidden_first, joined_matrix, precision=highest))
        queries = low(rotate(projected[:, :D].reshape(SEQ, HEADS, HD), cosines, sines))
        keys_all = low(rotate(projected[:, D:2 * D].reshape(SEQ, HEADS, HD), cosines, sines))
        values_all = low(projected[:, 2 * D:].reshape(SEQ, HEADS, HD))

        def attend(inputs):
            query_block, block_ids = inputs
            scores = low_back(jnp.einsum('qhd,khd->hqk', query_block, keys_all, precision=highest) * score_scale)
            visible = blocks[None, None, :] <= block_ids[None, :, None]
            scores = jnp.where(visible, scores, masked_score)
            shifted = jnp.exp(scores - lax.optimization_barrier(jnp.max(scores, axis=-1, keepdims=True)))
            attention_weights = low(shifted / lax.optimization_barrier(jnp.sum(shifted, axis=-1, keepdims=True)))
            return jnp.einsum('hqk,khd->qhd', attention_weights, values_all, precision=highest)
        attended = lax.map(jax.checkpoint(attend), (queries.reshape(SEQ // query_rows, query_rows, HEADS, HD), blocks.reshape(SEQ // query_rows, query_rows)))
        attended = low(low_back(attended.reshape(SEQ, D)))
        middle = start_rows + low_back(jnp.dot(attended, output_matrix, precision=highest))
        hidden_second = low(normalize(middle, second_gain))
        gate_up = low_back(jnp.dot(hidden_second, expand_matrix, precision=highest))
        gate_part = gate_up[:, :FF]
        activated = low(gate_part * jax.nn.sigmoid(gate_part) * gate_up[:, FF:])
        return middle + low_back(jnp.dot(activated, contract_matrix, precision=highest))
    params = tuple((weight.astype(jnp.float32) for weight in (lookup_weight, attention_gain, joined_weight, output_weight, feedforward_gain, expand_weight, contract_weight)))

    def one_sequence(totals, inputs):
        token_rows, bigram_rows, trigram_rows, upstream = inputs
        gram_rows = bigram_table[bigram_rows].astype(jnp.float32) + trigram_table[trigram_rows].astype(jnp.float32)
        result, pullback = jax.vjp(forward, token_rows.astype(jnp.float32), gram_rows, params)
        token_grad, gram_grad, param_grads = pullback(upstream.astype(jnp.float32))
        totals = tuple((earlier + later for earlier, later in zip(totals, param_grads)))
        return (totals, (result.astype(jnp.bfloat16), token_grad, gram_grad))
    zeros_init = tuple((jnp.zeros_like(weight) for weight in params))
    totals, (outputs, token_grads, gram_grads) = lax.scan(one_sequence, zeros_init, (token_embed, bigram_ids, trigram_ids, cotangent))
    flat_grads = gram_grads.reshape(-1, E)
    bigram_flat = bigram_ids.reshape(-1)
    trigram_flat = trigram_ids.reshape(-1)
    _, bigram_pull = jax.vjp(lambda source_table: source_table[bigram_flat], bigram_table.astype(jnp.float32))
    bigram_grad, = bigram_pull(flat_grads)
    _, trigram_pull = jax.vjp(lambda source_table: source_table[trigram_flat], trigram_table.astype(jnp.float32))
    trigram_grad, = trigram_pull(flat_grads)
    return (outputs, token_grads, bigram_grad, trigram_grad, totals[0], totals[1], totals[2], totals[3], totals[4], totals[5], totals[6])
```

```python
import functools
import math

import jax
import jax.numpy as jnp
from jax import lax
from jax.experimental import pallas as pl
from jax.experimental.pallas import tpu as pltpu
from jax.sharding import PartitionSpec as P

D = 768
HEADS = 12
HD = 64
FF = 2048
E = 192
ABLK = 256
BF = jnp.bfloat16
F32 = jnp.float32

epsilon = 1e-05
NT = (((1,), (1,)), ((), ()))
NN = (((1,), (0,)), ((), ()))
TN = (((0,), (0,)), ((), ()))


def mm(a, b, dims=NN):
    return lax.dot_general(a, b, dims, preferred_element_type=F32)


def eye(n):
    rows = lax.broadcasted_iota(jnp.int32, (n, n), 0)
    return jnp.where(rows == lax.broadcasted_iota(jnp.int32, (n, n), 1), 1.0, 0.0).astype(BF)


def vmem():
    return pl.BlockSpec(memory_space=pltpu.VMEM)


def smem():
    return pl.BlockSpec(memory_space=pltpu.SMEM)


def params(megabytes, **kw):
    return pltpu.CompilerParams(vmem_limit_bytes=megabytes << 20, **kw)


def placement_kernel(capacity, owner_row, owner_col, local_row, requests, target_row, target_col):
    tokens = owner_row.shape[1]
    devices = requests.shape[0]
    for table in range(2):
        own_r = owner_row[table : table + 1, :]
        own_c = owner_col[:, table : table + 1]
        t_row = lax.broadcasted_iota(jnp.int32, (tokens, tokens), 0)
        t_col = lax.broadcasted_iota(jnp.int32, (tokens, tokens), 1)
        same = own_c == own_r
        rank_r = jnp.sum(jnp.where(same & (t_row < t_col), 1.0, 0.0), axis=0, keepdims=True)
        rank_c = jnp.sum(jnp.where(same & (t_col < t_row), 1.0, 0.0), axis=1, keepdims=True)
        rank_r = rank_r.astype(jnp.int32)
        rank_c = rank_c.astype(jnp.int32)
        target_row[table : table + 1, :] = own_r * capacity + rank_r
        target_col[:, table : table + 1] = own_c * capacity + rank_c
        device = lax.broadcasted_iota(jnp.int32, (devices, tokens), 0)
        owned = device == own_r
        row = local_row[table : table + 1, :]
        high = jnp.where(owned, (row >> 7).astype(F32), 0.0).astype(BF)
        low = jnp.where(owned, (row & 127).astype(F32), 0.0).astype(BF)
        one = jnp.where(owned, 1.0, 0.0).astype(BF)
        slot = lax.broadcasted_iota(jnp.int32, (tokens, capacity), 1)
        ranked = jnp.where(slot == rank_c, 1.0, 0.0).astype(BF)
        code = 128.0 * mm(high, ranked) + mm(low, ranked) + mm(one, ranked)
        requests[:, table * capacity : (table + 1) * capacity] = code.astype(jnp.int32)


def placement(ids, table_rows, devices, capacity):
    tokens = ids.shape[1]
    owner = ids // table_rows
    local_row = ids - owner * table_rows
    return pl.pallas_call(
        functools.partial(placement_kernel, capacity),
        out_shape=(
            jax.ShapeDtypeStruct((devices, 2 * capacity), jnp.int32),
            jax.ShapeDtypeStruct((2, tokens), jnp.int32),
            jax.ShapeDtypeStruct((tokens, 2), jnp.int32),
        ),
        in_specs=[vmem()] * 3,
        out_specs=(vmem(),) * 3,
        compiler_params=params(32),
        name="placement",
    )(owner, owner.T, local_row)


def wide(ref, columns, table):
    ref[table] = jnp.broadcast_to(columns[:, table : table + 1].astype(F32), ref.shape[1:])


def onehot_block(ref, table, base, width):
    lane = lax.broadcasted_iota(jnp.int32, ref.shape[1:], 1).astype(F32)
    parts = []
    for j in range(width // 128):
        hit = ref[table] == lane + (base + 128 * j + 1).astype(F32)
        parts.append(jnp.where(hit, 1.0, 0.0).astype(BF))
    return jnp.concatenate(parts, axis=1)


def read_rows_kernel(codes, bigram, trigram, out, spread, total):
    step = pl.program_id(0)
    width = bigram.shape[1]

    @pl.when(step == 0)
    def _():
        for table in range(2):
            wide(spread, codes, table)
        total[...] = jnp.zeros_like(total)

    for table, source in enumerate((bigram, trigram)):
        hot = onehot_block(spread, table, step * width, width)
        total[table] += mm(hot, source[...], NT)

    @pl.when(step == pl.num_programs(0) - 1)
    def _():
        out[...] = jnp.concatenate([total[0], total[1]], axis=1).astype(BF)


def table_block(table_rows):
    for width in (1280, 640, 512, 256, 128):
        if table_rows % width == 0:
            return width
    return table_rows


def read_rows(codes, bigram_t, trigram_t):
    slots = codes.shape[0]
    rows = bigram_t.shape[1]
    width = table_block(rows)
    table = pl.BlockSpec((E, width), lambda i: (0, i))
    return pl.pallas_call(
        read_rows_kernel,
        grid=(rows // width,),
        out_shape=jax.ShapeDtypeStruct((slots, 2 * E), BF),
        in_specs=[pl.BlockSpec((slots, 2), lambda i: (0, 0)), table, table],
        out_specs=pl.BlockSpec((slots, 2 * E), lambda i: (0, 0)),
        scratch_shapes=[pltpu.VMEM((2, slots, 128), F32), pltpu.VMEM((2, slots, E), F32)],
        compiler_params=params(32),
        name="read_rows",
    )(codes, bigram_t, trigram_t)


def add_rows_kernel(codes, grads, bigram, trigram, spread, turned):
    step = pl.program_id(0)
    width = bigram.shape[1]

    @pl.when(step == 0)
    def _():
        for table in range(2):
            wide(spread, codes, table)
        turned[...] = mm(eye(2 * E), grads[...], NT).astype(BF)

    for table, out in enumerate((bigram, trigram)):
        hot = onehot_block(spread, table, step * width, width)
        out[...] = mm(turned[table * E : (table + 1) * E, :], hot)


def add_rows(codes, grads, rows):
    slots = codes.shape[0]
    width = table_block(rows)
    table = pl.BlockSpec((E, width), lambda i: (0, i))
    shape = jax.ShapeDtypeStruct((E, rows), F32)
    return pl.pallas_call(
        add_rows_kernel,
        grid=(rows // width,),
        out_shape=(shape, shape),
        in_specs=[
            pl.BlockSpec((slots, 2), lambda i: (0, 0)),
            pl.BlockSpec((slots, 2 * E), lambda i: (0, 0)),
        ],
        out_specs=(table, table),
        scratch_shapes=[pltpu.VMEM((2, slots, 128), F32), pltpu.VMEM((2 * E, slots), BF)],
        compiler_params=params(32),
        name="add_rows",
    )(codes, grads)


def attend_kernel(pairs, piece, order, rows, out, attended_t, logsum, q_s, k_s, vt_s, s_s):
    length = rows.shape[0]
    blocks = length // ABLK
    per_block = ABLK // piece
    width = pairs * HD
    identity = eye(HD)

    def sort(j, _):
        block = rows[pl.ds(pl.multiple_of(order[j] * piece, piece), piece), :]
        to = pl.ds(pl.multiple_of(j * piece, piece), piece)
        for p in range(pairs):
            q = block[:, p * HD : (p + 1) * HD]
            q_s[p, to, :] = (q.astype(F32) * HD ** (-0.5)).astype(BF)
            k_s[p, to, :] = block[:, width + p * HD : width + (p + 1) * HD]
            v = block[:, 2 * width + p * HD : 2 * width + (p + 1) * HD]
            vt_s[p, :, to] = mm(identity, v, NT).astype(BF)
        return 0

    lax.fori_loop(0, length // piece, sort, 0)

    for p in range(pairs):

        def one(i, _):
            at = pl.ds(pl.multiple_of(i * ABLK, ABLK), ABLK)
            queries = q_s[p, at, :]

            def score(j, peak):
                to = pl.ds(pl.multiple_of(j * ABLK, ABLK), ABLK)
                s = mm(k_s[p, to, :], queries, NT)
                s_s[to, :] = s
                return jnp.maximum(peak, jnp.max(s, axis=0, keepdims=True))

            peak = lax.fori_loop(0, i + 1, score, jnp.full((1, ABLK), -jnp.inf, F32))

            def raise_(j, total):
                to = pl.ds(pl.multiple_of(j * ABLK, ABLK), ABLK)
                e = jnp.exp(s_s[to, :] - peak)
                s_s[to, :] = e
                return total + jnp.sum(e, axis=0, keepdims=True)

            total = lax.fori_loop(0, i + 1, raise_, jnp.zeros((1, ABLK), F32))
            scale = 1.0 / total

            def weigh(j, o):
                to = pl.ds(pl.multiple_of(j * ABLK, ABLK), ABLK)
                probs = (s_s[to, :] * scale).astype(BF)
                return o + mm(vt_s[p, :, to], probs)

            o = lax.fori_loop(0, i + 1, weigh, jnp.zeros((HD, ABLK), F32))
            attended_t[p, :, at] = o
            logsum[p, :, at] = peak + jnp.log(total)
            o = o.T.astype(BF)
            for h in range(per_block):
                to = pl.ds(pl.multiple_of(order[per_block * i + h] * piece, piece), piece)
                out[to, p * HD : (p + 1) * HD] = o[h * piece : (h + 1) * piece, :]
            return 0

        lax.fori_loop(0, blocks, one, 0)


def attend(order, rows, pairs, piece):
    length = rows.shape[0]
    return pl.pallas_call(
        functools.partial(attend_kernel, pairs, piece),
        out_shape=(
            jax.ShapeDtypeStruct((length, pairs * HD), BF),
            jax.ShapeDtypeStruct((pairs, HD, length), F32),
            jax.ShapeDtypeStruct((pairs, 1, length), F32),
        ),
        in_specs=[smem(), vmem()],
        out_specs=(vmem(),) * 3,
        scratch_shapes=[
            pltpu.VMEM((pairs, length, HD), BF),
            pltpu.VMEM((pairs, length, HD), BF),
            pltpu.VMEM((pairs, HD, length), BF),
            pltpu.VMEM((length, ABLK), F32),
        ],
        compiler_params=params(48),
        name="attend",
    )(order, rows)


def attend_grad_kernel(
    pairs,
    piece,
    order,
    rows,
    grads,
    attended_t,
    logsum,
    cos,
    sin,
    cos_t,
    sin_t,
    out,
    q_s,
    k_s,
    v_s,
    g_s,
    kt_s,
    dq_s,
    dk_s,
    dv_s,
    dk_o,
    dv_o,
):
    length = rows.shape[0]
    blocks = length // ABLK
    width = pairs * HD
    half = HD // 2
    scale = HD ** (-0.5)
    identity = eye(HD)

    for p in range(pairs):

        def sort(j, _):
            take = pl.ds(pl.multiple_of(order[j] * piece, piece), piece)
            block = rows[take, :]
            to = pl.ds(pl.multiple_of(j * piece, piece), piece)
            q_s[to, :] = (block[:, p * HD : (p + 1) * HD].astype(F32) * scale).astype(BF)
            k = block[:, width + p * HD : width + (p + 1) * HD]
            k_s[to, :] = k
            kt_s[:, to] = mm(identity, k, NT).astype(BF)
            v_s[to, :] = block[:, 2 * width + p * HD : 2 * width + (p + 1) * HD]
            g_s[to, :] = grads[take, :][:, p * HD : (p + 1) * HD]
            return 0

        lax.fori_loop(0, length // piece, sort, 0)
        dk_s[...] = jnp.zeros_like(dk_s)
        dv_s[...] = jnp.zeros_like(dv_s)

        def one(i, _):
            at = pl.ds(pl.multiple_of(i * ABLK, ABLK), ABLK)
            queries = q_s[at, :]
            grad = g_s[at, :]
            delta = jnp.sum(
                mm(identity, grad, NT) * attended_t[p, :, at], axis=0, keepdims=True
            )
            level = logsum[p, :, at]

            def tile(j, dq):
                to = pl.ds(pl.multiple_of(j * ABLK, ABLK), ABLK)
                probs = jnp.exp(mm(k_s[to, :], queries, NT) - level)
                ds = (probs * (mm(v_s[to, :], grad, NT) - delta)).astype(BF)
                dv_s[to, :] += mm(probs.astype(BF), grad)
                dk_s[to, :] += mm(ds, queries)
                return dq + mm(kt_s[:, to], ds)

            dq = lax.fori_loop(0, i + 1, tile, jnp.zeros((HD, ABLK), F32)) * scale
            c, s = cos_t[:, at], sin_t[:, at]
            a, b = dq[:half, :], dq[half:, :]
            dq = jnp.concatenate([a * c + b * s, b * c - a * s], axis=0)
            dq_s[p, at, :] = dq.T.astype(BF)
            return 0

        lax.fori_loop(0, blocks, one, 0)

        def turn(j, _):
            to = pl.ds(pl.multiple_of(j * ABLK, ABLK), ABLK)
            dk = dk_s[to, :]
            a, b = dk[:, :half], dk[:, half:]
            c, s = cos[to, :], sin[to, :]
            dk_o[p, to, :] = jnp.concatenate([a * c + b * s, b * c - a * s], axis=1).astype(BF)
            dv_o[p, to, :] = dv_s[to, :].astype(BF)
            return 0

        lax.fori_loop(0, blocks, turn, 0)

    def unsort(j, _):
        take = pl.ds(pl.multiple_of(j * piece, piece), piece)
        to = pl.ds(pl.multiple_of(order[j] * piece, piece), piece)
        parts = [ref[p, take, :] for ref in (dq_s, dk_o, dv_o) for p in range(pairs)]
        out[to, :] = jnp.concatenate(parts, axis=1)
        return 0

    lax.fori_loop(0, length // piece, unsort, 0)


def attend_grad(order, rows, grads, attended_t, logsum, cos, sin, pairs, piece):
    length = rows.shape[0]
    low = pltpu.VMEM((length, HD), BF)
    full = pltpu.VMEM((length, HD), F32)
    each = pltpu.VMEM((pairs, length, HD), BF)
    return pl.pallas_call(
        functools.partial(attend_grad_kernel, pairs, piece),
        out_shape=jax.ShapeDtypeStruct((length, 3 * pairs * HD), BF),
        in_specs=[smem()] + [vmem()] * 8,
        out_specs=vmem(),
        scratch_shapes=[low] * 4 + [pltpu.VMEM((HD, length), BF), each, full, full, each, each],
        compiler_params=params(56),
        name="attend_grad",
    )(order, rows, grads, attended_t, logsum, cos, sin, cos.T, sin.T)


def over_ctx(value, mask):
    size = lax.axis_size("ctx")
    return lax.ppermute(value, "ctx", [(i, i ^ mask) for i in range(size)])


def along_fsdp(value, shift):
    size = lax.axis_size("fsdp")
    return lax.ppermute(value, "fsdp", [(i, (i + shift) % size) for i in range(size)])


def by_index(blocks, index):
    if len(blocks) == 1:
        return blocks
    half = len(blocks) // 2
    flip = (index // half) % 2 == 1
    lower = [jnp.where(flip, b, a) for a, b in zip(blocks[:half], blocks[half:])]
    upper = [jnp.where(flip, a, b) for a, b in zip(blocks[:half], blocks[half:])]
    return by_index(lower, index) + by_index(upper, index)


def place():
    ctx = lax.axis_index("ctx")
    return ctx % 2, ctx // 2, lax.axis_index("fsdp")


def gather_weight(shard):
    core, chip, z = place()
    chips = lax.axis_size("ctx") // 2
    shards = lax.axis_size("fsdp")
    rows, columns = shard.shape
    r, half = rows // chips, columns // 2
    mine = lax.dynamic_slice(shard, (chip * r, core * half), (r, half))
    along = [mine] + [along_fsdp(mine, k) for k in range(1, shards)]
    turned = jnp.stack([along[(shards - m) % shards] for m in range(shards)])
    column = lax.dynamic_slice_in_dim(
        jnp.concatenate([turned, turned]), (shards - z) % shards, shards
    )
    blocks = [column] + [over_ctx(column, 2 * k) for k in range(1, chips)]
    own = jnp.stack(by_index(blocks, chip), axis=1).reshape(shards * rows, half)
    other = over_ctx(own, 1)
    return jnp.where(
        core == 0, jnp.concatenate([own, other], axis=1), jnp.concatenate([other, own], axis=1)
    )


def gather_gains(gains):
    _, _, z = place()
    shards = lax.axis_size("fsdp")
    along = [gains] + [along_fsdp(gains, k) for k in range(1, shards)]
    turned = jnp.stack([along[(shards - m) % shards] for m in range(shards)])
    every = lax.dynamic_slice_in_dim(
        jnp.concatenate([turned, turned]), (shards - z) % shards, shards
    )
    return jnp.moveaxis(every, 0, 1).reshape(gains.shape[0], -1)


def reduce_grad(grad):
    core, chip, z = place()
    chips = lax.axis_size("ctx") // 2
    shards = lax.axis_size("fsdp")
    rows, columns = grad.shape[0] // shards, grad.shape[1]
    r, half = rows // chips, columns // 2
    view = grad.reshape(shards, chips, r, columns)

    def columns_of(which):
        return lax.dynamic_slice_in_dim(view, which * half, half, axis=3)

    total = columns_of(core).astype(F32) + over_ctx(columns_of(1 - core), 1).astype(F32)
    low = total.astype(BF)
    sent = [
        over_ctx(lax.dynamic_index_in_dim(low, chip ^ k, 1, keepdims=False), 2 * k)
        for k in range(1, chips)
    ]
    total = lax.dynamic_index_in_dim(low, chip, 1, keepdims=False).astype(F32)
    total = sum((s.astype(F32) for s in sent), total)
    low = total.astype(BF)
    sent = [
        along_fsdp(lax.dynamic_index_in_dim(low, (z + k) % shards, 0, keepdims=False), k)
        for k in range(1, shards)
    ]
    total = lax.dynamic_index_in_dim(low, z, 0, keepdims=False).astype(F32)
    total = sum((s.astype(F32) for s in sent), total)
    piece = total.astype(BF)
    blocks = [piece] + [over_ctx(piece, 2 * k) for k in range(1, chips)]
    own = jnp.stack(by_index(blocks, chip)).reshape(rows, half)
    other = over_ctx(own, 1)
    return jnp.where(
        core == 0, jnp.concatenate([own, other], axis=1), jnp.concatenate([other, own], axis=1)
    ).astype(F32)


def by_head(values, devices, pairs):
    batches, tokens, kinds, _ = values.shape
    groups = HEADS // pairs
    values = values.reshape(batches, tokens, kinds, groups, pairs * HD)
    values = values.transpose(0, 3, 1, 2, 4).reshape(batches * groups, tokens, kinds * pairs * HD)
    spare = devices - batches * groups
    return jnp.pad(values, ((0, spare), (0, 0), (0, 0)))


def by_token(values, batches, kinds, pairs):
    groups = HEADS // pairs
    tokens = values.shape[1]
    values = values[: batches * groups].reshape(batches, groups, tokens, kinds, pairs * HD)
    return values.transpose(0, 2, 3, 1, 4).reshape(batches, tokens, kinds, HEADS * HD)


def exchange(values, axes):
    return lax.all_to_all(values, axes, split_axis=0, concat_axis=0, tiled=True)


def rotate(values, cosines, sines):
    half = values.shape[-1] // 2
    a, b = values[..., :half], values[..., half:]
    c, s = cosines[:, None, :], sines[:, None, :]
    return jnp.concatenate([a * c - b * s, b * c + a * s], axis=-1)


def normalize(rows):
    inverse = lax.rsqrt(jnp.mean(rows * rows, axis=-1, keepdims=True) + epsilon)
    return rows * inverse, inverse


def norm_backward(hidden_grad, normed, inverse, gain):
    weighted = hidden_grad * gain
    return inverse * (weighted - normed * jnp.mean(weighted * normed, axis=-1, keepdims=True))


def local(
    token_embed,
    bigram_ids,
    trigram_ids,
    bigram_table,
    trigram_table,
    block_deal,
    lookup_weight,
    attention_gain,
    joined_weight,
    output_weight,
    feedforward_gain,
    expand_weight,
    contract_weight,
    cotangent,
):
    contexts = lax.axis_size("ctx")
    shards = lax.axis_size("fsdp")
    devices = contexts * shards
    batches, local_rows = token_embed.shape[:2]
    tokens = batches * local_rows
    length = local_rows * contexts
    capacity = max(2, 2 * tokens // devices)
    table_rows = bigram_table.shape[0]
    piece = local_rows // 2
    pieces = length // piece
    pairs = -(-batches * HEADS // contexts)
    while HEADS % pairs:
        pairs += 1
    both = ("ctx", "fsdp")

    ids = jnp.stack([bigram_ids.reshape(-1), trigram_ids.reshape(-1)])
    requests, target_row, target_col = placement(ids, table_rows, devices, capacity)
    asked = exchange(requests, both)
    codes = jnp.stack([asked[:, :capacity].reshape(-1), asked[:, capacity:].reshape(-1)], axis=1)
    got = exchange(
        read_rows(codes, bigram_table.T, trigram_table.T).reshape(devices, capacity, 2 * E), both
    ).reshape(devices * capacity, 2 * E)

    lookup = gather_weight(lookup_weight)
    joined = gather_weight(joined_weight)
    output = gather_weight(output_weight)
    gains = gather_gains(jnp.stack([attention_gain, feedforward_gain])).astype(F32)
    first_gain, second_gain = gains[0], gains[1]
    expand = gather_weight(expand_weight)
    contract = gather_weight(contract_weight)

    order = jnp.argmin(
        jnp.abs(block_deal[None, :] - jnp.arange(pieces, dtype=jnp.int32)[:, None]), axis=1
    ).astype(jnp.int32)
    frequency = jnp.exp(-math.log(10000.0) * (2.0 * jnp.arange(HD // 2, dtype=F32) / HD))
    slot = lax.axis_index("ctx") * local_rows + jnp.arange(local_rows, dtype=jnp.int32)
    position = block_deal[slot // piece] * piece + slot % piece
    angles = position.astype(F32)[:, None] * frequency[None, :]
    cosines, sines = jnp.cos(angles), jnp.sin(angles)
    all_angles = jnp.arange(length, dtype=F32)[:, None] * frequency[None, :]
    all_cosines, all_sines = jnp.cos(all_angles), jnp.sin(all_angles)

    slots = jnp.arange(devices * capacity, dtype=jnp.int32)
    hot_b = (target_col[:, 0:1] == slots[None, :]).astype(BF)
    hot_t = (target_col[:, 1:2] == slots[None, :]).astype(BF)
    embedded = (mm(hot_b, got[:, :E]) + mm(hot_t, got[:, E:])).astype(BF)
    start = token_embed.reshape(tokens, D).astype(F32) + mm(embedded, lookup)
    normed_first, inverse_first = normalize(start)
    hidden_first = (normed_first * first_gain).astype(BF)
    projected = mm(hidden_first, joined).reshape(batches, local_rows, 3, HEADS, HD)
    cos_b, sin_b = cosines[None, :, None, :], sines[None, :, None, :]
    turn = lambda x: jnp.concatenate(
        [
            x[..., : HD // 2] * cos_b - x[..., HD // 2 :] * sin_b,
            x[..., HD // 2 :] * cos_b + x[..., : HD // 2] * sin_b,
        ],
        axis=-1,
    )
    qkv = jnp.stack(
        [turn(projected[:, :, 0]), turn(projected[:, :, 1]), projected[:, :, 2]], axis=2
    ).astype(BF)
    qkv = qkv.reshape(batches, local_rows, 3, D)
    rows = exchange(by_head(qkv, contexts, pairs), "ctx").reshape(length, 3 * pairs * HD)
    attended_rows, attended_t, logsum = attend(order, rows, pairs, piece)
    attended = by_token(
        exchange(attended_rows.reshape(contexts, local_rows, pairs * HD), "ctx"), batches, 1, pairs
    ).reshape(tokens, D)
    middle = start + mm(attended, output)
    normed_second, inverse_second = normalize(middle)
    hidden_second = (normed_second * second_gain).astype(BF)
    gate_up = mm(hidden_second, expand)
    gate, up = gate_up[:, :FF], gate_up[:, FF:]
    sigmoid = jax.nn.sigmoid(gate)
    swish = gate * sigmoid
    activated = (swish * up).astype(BF)
    result = (middle + mm(activated, contract)).astype(BF)

    upstream = cotangent.reshape(tokens, D)
    activated_grad = mm(upstream, contract, NT)
    gate_up_grad = jnp.concatenate(
        [
            activated_grad * up * sigmoid * (1.0 + gate * (1.0 - sigmoid)),
            activated_grad * swish,
        ],
        axis=-1,
    ).astype(BF)
    hidden_second_grad = mm(gate_up_grad, expand, NT)
    second_gain_term = jnp.sum(hidden_second_grad * normed_second, axis=0)
    middle_grad = upstream.astype(F32) + norm_backward(
        hidden_second_grad, normed_second, inverse_second, second_gain
    )
    middle_low = middle_grad.astype(BF)
    attended_grad = mm(middle_low, output, NT).astype(BF)
    grad_rows = exchange(
        by_head(attended_grad.reshape(batches, local_rows, 1, D), contexts, pairs), "ctx"
    ).reshape(length, pairs * HD)
    contract_term = mm(activated, upstream, TN).astype(BF)
    expand_term = mm(hidden_second, gate_up_grad, TN).astype(BF)
    output_term = mm(attended, middle_low, TN).astype(BF)
    contract_grad = reduce_grad(contract_term)
    expand_grad = reduce_grad(expand_term)
    output_grad = reduce_grad(output_term)

    grad_rows = attend_grad(
        order, rows, grad_rows, attended_t, logsum, all_cosines, all_sines, pairs, piece
    )
    joined_local = by_token(
        exchange(grad_rows.reshape(contexts, local_rows, 3 * pairs * HD), "ctx"), batches, 3, pairs
    ).reshape(tokens, 3 * D)
    joined_grad = reduce_grad(mm(hidden_first, joined_local, TN).astype(BF))
    hidden_first_grad = mm(joined_local, joined, NT)
    first_gain_term = jnp.sum(hidden_first_grad * normed_first, axis=0)
    start_grad = middle_grad + norm_backward(
        hidden_first_grad, normed_first, inverse_first, first_gain
    )
    start_low = start_grad.astype(BF)
    lookup_grad = reduce_grad(mm(embedded, start_low, TN).astype(BF))
    embed_grad = mm(start_low, lookup, NT).astype(BF)
    give_b = (target_row[0:1, :] == slots[:, None]).astype(BF)
    give_t = (target_row[1:2, :] == slots[:, None]).astype(BF)
    send = jnp.concatenate([mm(give_b, embed_grad), mm(give_t, embed_grad)], axis=1).astype(BF)
    arrived = exchange(send.reshape(devices, capacity, 2 * E), both)
    bigram_grad, trigram_grad = add_rows(
        codes, arrived.reshape(devices * capacity, 2 * E), table_rows
    )
    gain_terms = lax.psum(jnp.stack([first_gain_term, second_gain_term]), both)
    gain_share = lax.dynamic_slice_in_dim(
        gain_terms, lax.axis_index("fsdp") * (D // shards), D // shards, axis=1
    )
    return (
        result.reshape(batches, local_rows, D),
        start_grad.reshape(batches, local_rows, D),
        bigram_grad.T,
        trigram_grad.T,
        lookup_grad,
        gain_share[0],
        joined_grad,
        output_grad,
        gain_share[1],
        expand_grad,
        contract_grad,
    )


def solution(mesh):
    return jax.shard_map(
        local,
        mesh=mesh,
        in_specs=(
            P("fsdp", "ctx", None),
            P("fsdp", "ctx"),
            P("fsdp", "ctx"),
            P(("ctx", "fsdp"), None),
            P(("ctx", "fsdp"), None),
            P(),
            P("fsdp", None),
            P("fsdp"),
            P("fsdp", None),
            P("fsdp", None),
            P("fsdp"),
            P("fsdp", None),
            P("fsdp", None),
            P("fsdp", "ctx", None),
        ),
        out_specs=(
            P("fsdp", "ctx", None),
            P("fsdp", "ctx", None),
            P(("ctx", "fsdp"), None),
            P(("ctx", "fsdp"), None),
            P("fsdp", None),
            P("fsdp"),
            P("fsdp", None),
            P("fsdp", None),
            P("fsdp"),
            P("fsdp", None),
            P("fsdp", None),
        ),
        check_vma=False,
    )
```

```python
import functools
import math

import jax
import jax.numpy as jnp
from jax import lax
from jax.experimental import pallas as pl
from jax.experimental.pallas import tpu as pltpu
from jax.sharding import PartitionSpec as P

D = 768
HEADS = 12
HD = 64
FF = 2048
E = 192
ABLK = 256
BF = jnp.bfloat16
F32 = jnp.float32

epsilon = 1e-05
NT = (((1,), (1,)), ((), ()))
NN = (((1,), (0,)), ((), ()))
TN = (((0,), (0,)), ((), ()))


def mm(a, b, dims=NN):
    return lax.dot_general(a, b, dims, preferred_element_type=F32)


def eye(n):
    rows = lax.broadcasted_iota(jnp.int32, (n, n), 0)
    return jnp.where(rows == lax.broadcasted_iota(jnp.int32, (n, n), 1), 1.0, 0.0).astype(BF)


def vmem():
    return pl.BlockSpec(memory_space=pltpu.VMEM)


def smem():
    return pl.BlockSpec(memory_space=pltpu.SMEM)


def params(megabytes, **kw):
    return pltpu.CompilerParams(vmem_limit_bytes=megabytes << 20, **kw)


def cost(microseconds):
    return pl.CostEstimate(
        flops=int(microseconds * 6e8), bytes_accessed=int(microseconds * 2.5e6), transcendentals=0
    )


def in_hbm(value):
    return pltpu.with_memory_space_constraint(value, pltpu.HBM)


def after(value, *others):
    return lax.optimization_barrier((value, others))[0]


def placement_kernel(capacity, owner_row, owner_col, local_row, requests, target_row, target_col):
    tokens = owner_row.shape[1]
    devices = requests.shape[0]
    for table in range(2):
        own_r = owner_row[table : table + 1, :]
        own_c = owner_col[:, table : table + 1]
        t_row = lax.broadcasted_iota(jnp.int32, (tokens, tokens), 0)
        t_col = lax.broadcasted_iota(jnp.int32, (tokens, tokens), 1)
        same = own_c == own_r
        rank_r = jnp.sum(jnp.where(same & (t_row < t_col), 1.0, 0.0), axis=0, keepdims=True)
        rank_c = jnp.sum(jnp.where(same & (t_col < t_row), 1.0, 0.0), axis=1, keepdims=True)
        rank_r = rank_r.astype(jnp.int32)
        rank_c = rank_c.astype(jnp.int32)
        target_row[table : table + 1, :] = own_r * capacity + rank_r
        target_col[:, table : table + 1] = own_c * capacity + rank_c
        device = lax.broadcasted_iota(jnp.int32, (devices, tokens), 0)
        owned = device == own_r
        row = local_row[table : table + 1, :]
        high = jnp.where(owned, (row >> 7).astype(F32), 0.0).astype(BF)
        low = jnp.where(owned, (row & 127).astype(F32), 0.0).astype(BF)
        one = jnp.where(owned, 1.0, 0.0).astype(BF)
        slot = lax.broadcasted_iota(jnp.int32, (tokens, capacity), 1)
        ranked = jnp.where(slot == rank_c, 1.0, 0.0).astype(BF)
        code = 128.0 * mm(high, ranked) + mm(low, ranked) + mm(one, ranked)
        requests[:, table * capacity : (table + 1) * capacity] = code.astype(jnp.int32)


def placement(ids, table_rows, devices, capacity):
    tokens = ids.shape[1]
    owner = ids // table_rows
    local_row = ids - owner * table_rows
    return pl.pallas_call(
        functools.partial(placement_kernel, capacity),
        out_shape=(
            jax.ShapeDtypeStruct((devices, 2 * capacity), jnp.int32),
            jax.ShapeDtypeStruct((2, tokens), jnp.int32),
            jax.ShapeDtypeStruct((tokens, 2), jnp.int32),
        ),
        in_specs=[vmem()] * 3,
        out_specs=(vmem(),) * 3,
        compiler_params=params(32),
        cost_estimate=cost(2),
        name="placement",
    )(owner, owner.T, local_row)


def wide(ref, columns, table):
    ref[table] = jnp.broadcast_to(columns[:, table : table + 1].astype(F32), ref.shape[1:])


def onehot_block(ref, table, base, width):
    lane = lax.broadcasted_iota(jnp.int32, ref.shape[1:], 1).astype(F32)
    parts = []
    for j in range(width // 128):
        hit = ref[table] == lane + (base + 128 * j + 1).astype(F32)
        parts.append(jnp.where(hit, 1.0, 0.0).astype(BF))
    return jnp.concatenate(parts, axis=1)


def read_rows_kernel(codes, bigram, trigram, out, spread, total):
    step = pl.program_id(0)
    width = bigram.shape[1]

    @pl.when(step == 0)
    def _():
        for table in range(2):
            wide(spread, codes, table)
        total[...] = jnp.zeros_like(total)

    for table, source in enumerate((bigram, trigram)):
        hot = onehot_block(spread, table, step * width, width)
        total[table] += mm(hot, source[...], NT)

    @pl.when(step == pl.num_programs(0) - 1)
    def _():
        out[...] = jnp.concatenate([total[0], total[1]], axis=1).astype(BF)


def table_block(table_rows):
    for width in (1280, 640, 512, 256, 128):
        if table_rows % width == 0:
            return width
    return table_rows


def read_rows(codes, bigram_t, trigram_t):
    slots = codes.shape[0]
    rows = bigram_t.shape[1]
    width = table_block(rows)
    table = pl.BlockSpec((E, width), lambda i: (0, i))
    return pl.pallas_call(
        read_rows_kernel,
        grid=(rows // width,),
        out_shape=jax.ShapeDtypeStruct((slots, 2 * E), BF),
        in_specs=[pl.BlockSpec((slots, 2), lambda i: (0, 0)), table, table],
        out_specs=pl.BlockSpec((slots, 2 * E), lambda i: (0, 0)),
        scratch_shapes=[pltpu.VMEM((2, slots, 128), F32), pltpu.VMEM((2, slots, E), F32)],
        compiler_params=params(32),
        cost_estimate=cost(17),
        name="read_rows",
    )(codes, bigram_t, trigram_t)


def add_rows_kernel(codes, grads, bigram, trigram, spread, turned):
    step = pl.program_id(0)
    width = bigram.shape[1]

    @pl.when(step == 0)
    def _():
        for table in range(2):
            wide(spread, codes, table)
        turned[...] = mm(eye(2 * E), grads[...], NT).astype(BF)

    for table, out in enumerate((bigram, trigram)):
        hot = onehot_block(spread, table, step * width, width)
        out[...] = mm(turned[table * E : (table + 1) * E, :], hot)


def add_rows(codes, grads, rows):
    slots = codes.shape[0]
    width = table_block(rows)
    table = pl.BlockSpec((E, width), lambda i: (0, i))
    shape = jax.ShapeDtypeStruct((E, rows), F32)
    return pl.pallas_call(
        add_rows_kernel,
        grid=(rows // width,),
        out_shape=(shape, shape),
        in_specs=[
            pl.BlockSpec((slots, 2), lambda i: (0, 0)),
            pl.BlockSpec((slots, 2 * E), lambda i: (0, 0)),
        ],
        out_specs=(table, table),
        scratch_shapes=[pltpu.VMEM((2, slots, 128), F32), pltpu.VMEM((2 * E, slots), BF)],
        compiler_params=params(32),
        cost_estimate=cost(14),
        name="add_rows",
    )(codes, grads)


def attend_kernel(pairs, piece, order, rows, out, attended_t, logsum, q_s, k_s, vt_s, s_s):
    length = rows.shape[0]
    blocks = length // ABLK
    per_block = ABLK // piece
    width = pairs * HD
    identity = eye(HD)

    def sort(j, _):
        block = rows[pl.ds(pl.multiple_of(order[j] * piece, piece), piece), :]
        to = pl.ds(pl.multiple_of(j * piece, piece), piece)
        for p in range(pairs):
            q = block[:, p * HD : (p + 1) * HD]
            q_s[p, to, :] = (q.astype(F32) * HD ** (-0.5)).astype(BF)
            k_s[p, to, :] = block[:, width + p * HD : width + (p + 1) * HD]
            v = block[:, 2 * width + p * HD : 2 * width + (p + 1) * HD]
            vt_s[p, :, to] = mm(identity, v, NT).astype(BF)
        return 0

    lax.fori_loop(0, length // piece, sort, 0)

    for p in range(pairs):

        def one(i, _):
            at = pl.ds(pl.multiple_of(i * ABLK, ABLK), ABLK)
            queries = q_s[p, at, :]

            def score(j, peak):
                to = pl.ds(pl.multiple_of(j * ABLK, ABLK), ABLK)
                s = mm(k_s[p, to, :], queries, NT)
                s_s[to, :] = s
                return jnp.maximum(peak, jnp.max(s, axis=0, keepdims=True))

            peak = lax.fori_loop(0, i + 1, score, jnp.full((1, ABLK), -jnp.inf, F32))

            def raise_(j, total):
                to = pl.ds(pl.multiple_of(j * ABLK, ABLK), ABLK)
                e = jnp.exp(s_s[to, :] - peak)
                s_s[to, :] = e
                return total + jnp.sum(e, axis=0, keepdims=True)

            total = lax.fori_loop(0, i + 1, raise_, jnp.zeros((1, ABLK), F32))
            scale = 1.0 / total

            def weigh(j, o):
                to = pl.ds(pl.multiple_of(j * ABLK, ABLK), ABLK)
                probs = (s_s[to, :] * scale).astype(BF)
                return o + mm(vt_s[p, :, to], probs)

            o = lax.fori_loop(0, i + 1, weigh, jnp.zeros((HD, ABLK), F32))
            attended_t[p, :, at] = o
            logsum[p, :, at] = peak + jnp.log(total)
            o = o.T.astype(BF)
            for h in range(per_block):
                to = pl.ds(pl.multiple_of(order[per_block * i + h] * piece, piece), piece)
                out[to, p * HD : (p + 1) * HD] = o[h * piece : (h + 1) * piece, :]
            return 0

        lax.fori_loop(0, blocks, one, 0)


def attend(order, rows, pairs, piece):
    length = rows.shape[0]
    return pl.pallas_call(
        functools.partial(attend_kernel, pairs, piece),
        out_shape=(
            jax.ShapeDtypeStruct((length, pairs * HD), BF),
            jax.ShapeDtypeStruct((pairs, HD, length), F32),
            jax.ShapeDtypeStruct((pairs, 1, length), F32),
        ),
        in_specs=[smem(), vmem()],
        out_specs=(vmem(),) * 3,
        scratch_shapes=[
            pltpu.VMEM((pairs, length, HD), BF),
            pltpu.VMEM((pairs, length, HD), BF),
            pltpu.VMEM((pairs, HD, length), BF),
            pltpu.VMEM((length, ABLK), F32),
        ],
        compiler_params=params(48),
        cost_estimate=cost(50),
        name="attend",
    )(order, rows)


def attend_grad_kernel(
    pairs,
    piece,
    order,
    rows,
    grads,
    attended_t,
    logsum,
    cos,
    sin,
    cos_t,
    sin_t,
    out,
    q_s,
    k_s,
    v_s,
    g_s,
    kt_s,
    dq_s,
    dk_s,
    dv_s,
    dk_o,
    dv_o,
):
    length = rows.shape[0]
    blocks = length // ABLK
    width = pairs * HD
    half = HD // 2
    scale = HD ** (-0.5)
    identity = eye(HD)

    for p in range(pairs):

        def sort(j, _):
            take = pl.ds(pl.multiple_of(order[j] * piece, piece), piece)
            block = rows[take, :]
            to = pl.ds(pl.multiple_of(j * piece, piece), piece)
            q_s[to, :] = (block[:, p * HD : (p + 1) * HD].astype(F32) * scale).astype(BF)
            k = block[:, width + p * HD : width + (p + 1) * HD]
            k_s[to, :] = k
            kt_s[:, to] = mm(identity, k, NT).astype(BF)
            v_s[to, :] = block[:, 2 * width + p * HD : 2 * width + (p + 1) * HD]
            g_s[to, :] = grads[take, :][:, p * HD : (p + 1) * HD]
            return 0

        lax.fori_loop(0, length // piece, sort, 0)
        dk_s[...] = jnp.zeros_like(dk_s)
        dv_s[...] = jnp.zeros_like(dv_s)

        def one(i, _):
            at = pl.ds(pl.multiple_of(i * ABLK, ABLK), ABLK)
            queries = q_s[at, :]
            grad = g_s[at, :]
            delta = jnp.sum(
                mm(identity, grad, NT) * attended_t[p, :, at], axis=0, keepdims=True
            )
            level = logsum[p, :, at]

            def tile(j, dq):
                to = pl.ds(pl.multiple_of(j * ABLK, ABLK), ABLK)
                probs = jnp.exp(mm(k_s[to, :], queries, NT) - level)
                ds = (probs * (mm(v_s[to, :], grad, NT) - delta)).astype(BF)
                dv_s[to, :] += mm(probs.astype(BF), grad)
                dk_s[to, :] += mm(ds, queries)
                return dq + mm(kt_s[:, to], ds)

            dq = lax.fori_loop(0, i + 1, tile, jnp.zeros((HD, ABLK), F32)) * scale
            c, s = cos_t[:, at], sin_t[:, at]
            a, b = dq[:half, :], dq[half:, :]
            dq = jnp.concatenate([a * c + b * s, b * c - a * s], axis=0)
            dq_s[p, at, :] = dq.T.astype(BF)
            return 0

        lax.fori_loop(0, blocks, one, 0)

        def turn(j, _):
            to = pl.ds(pl.multiple_of(j * ABLK, ABLK), ABLK)
            dk = dk_s[to, :]
            a, b = dk[:, :half], dk[:, half:]
            c, s = cos[to, :], sin[to, :]
            dk_o[p, to, :] = jnp.concatenate([a * c + b * s, b * c - a * s], axis=1).astype(BF)
            dv_o[p, to, :] = dv_s[to, :].astype(BF)
            return 0

        lax.fori_loop(0, blocks, turn, 0)

    def unsort(j, _):
        take = pl.ds(pl.multiple_of(j * piece, piece), piece)
        to = pl.ds(pl.multiple_of(order[j] * piece, piece), piece)
        parts = [ref[p, take, :] for ref in (dq_s, dk_o, dv_o) for p in range(pairs)]
        out[to, :] = jnp.concatenate(parts, axis=1)
        return 0

    lax.fori_loop(0, length // piece, unsort, 0)


def attend_grad(order, rows, grads, attended_t, logsum, cos, sin, cos_t, sin_t, pairs, piece):
    length = rows.shape[0]
    low = pltpu.VMEM((length, HD), BF)
    full = pltpu.VMEM((length, HD), F32)
    each = pltpu.VMEM((pairs, length, HD), BF)
    return pl.pallas_call(
        functools.partial(attend_grad_kernel, pairs, piece),
        out_shape=jax.ShapeDtypeStruct((length, 3 * pairs * HD), BF),
        in_specs=[smem()] + [vmem()] * 8,
        out_specs=vmem(),
        scratch_shapes=[low] * 4 + [pltpu.VMEM((HD, length), BF), each, full, full, each, each],
        compiler_params=params(56),
        cost_estimate=cost(68),
        name="attend_grad",
    )(order, rows, grads, attended_t, logsum, cos, sin, cos_t, sin_t)


def fold_max(peak, tile):
    return jnp.maximum(peak, jnp.max(tile.reshape(-1, 8, tile.shape[1]), axis=0))


def fold_sum(total, tile):
    return total + jnp.sum(tile.reshape(-1, 8, tile.shape[1]), axis=0)


def attend_short_kernel(pairs, piece, order, rows, out, attended_t, logsum, q_s, k_s, vt_s, s_s, o_s):
    length = rows.shape[0]
    blocks = length // ABLK
    width = pairs * HD
    identity = eye(HD)

    def sort(j, _):
        block = rows[pl.ds(pl.multiple_of(order[j] * piece, piece), piece), :]
        to = pl.ds(pl.multiple_of(j * piece, piece), piece)
        for p in range(pairs):
            q = block[:, p * HD : (p + 1) * HD]
            q_s[p, to, :] = (q.astype(F32) * HD ** (-0.5)).astype(BF)
            k_s[p, to, :] = block[:, width + p * HD : width + (p + 1) * HD]
            v = block[:, 2 * width + p * HD : 2 * width + (p + 1) * HD]
            vt_s[p, :, to] = mm(identity, v, NT).astype(BF)
        return 0

    lax.fori_loop(0, length // piece, sort, 0)

    def pair(p, _):
        for i in range(blocks):
            at = slice(i * ABLK, (i + 1) * ABLK)
            queries = q_s[p, at, :]
            peak = jnp.full((8, ABLK), -jnp.inf, F32)
            for j in range(i + 1):
                s = mm(k_s[p, j * ABLK : (j + 1) * ABLK, :], queries, NT)
                s_s[i % 2, j * ABLK : (j + 1) * ABLK, :] = s
                peak = fold_max(peak, s)
            peak = jnp.max(peak, axis=0, keepdims=True)
            total = jnp.zeros((8, ABLK), F32)
            o = jnp.zeros((HD, ABLK), F32)
            for j in range(i + 1):
                e = jnp.exp(s_s[i % 2, j * ABLK : (j + 1) * ABLK, :] - peak)
                total = fold_sum(total, e)
                o += mm(vt_s[p, :, j * ABLK : (j + 1) * ABLK], e.astype(BF))
            total = jnp.sum(total, axis=0, keepdims=True)
            o = o * (1.0 / total)
            attended_t[p, :, at] = o
            logsum[p, :, at] = peak + jnp.log(total)
            o_s[p, at, :] = o.T.astype(BF)
        return 0

    lax.fori_loop(0, pairs, pair, 0)

    def unsort(j, _):
        take = pl.ds(pl.multiple_of(j * piece, piece), piece)
        to = pl.ds(pl.multiple_of(order[j] * piece, piece), piece)
        out[to, :] = jnp.concatenate([o_s[p, take, :] for p in range(pairs)], axis=1)
        return 0

    lax.fori_loop(0, length // piece, unsort, 0)


def attend_short(order, rows, pairs, piece):
    length = rows.shape[0]
    return pl.pallas_call(
        functools.partial(attend_short_kernel, pairs, piece),
        out_shape=(
            jax.ShapeDtypeStruct((length, pairs * HD), BF),
            jax.ShapeDtypeStruct((pairs, HD, length), F32),
            jax.ShapeDtypeStruct((pairs, 1, length), F32),
        ),
        in_specs=[smem(), vmem()],
        out_specs=(vmem(),) * 3,
        scratch_shapes=[
            pltpu.VMEM((pairs, length, HD), BF),
            pltpu.VMEM((pairs, length, HD), BF),
            pltpu.VMEM((pairs, HD, length), BF),
            pltpu.VMEM((2, length, ABLK), F32),
            pltpu.VMEM((pairs, length, HD), BF),
        ],
        compiler_params=params(48),
        cost_estimate=cost(25),
        name="attend",
    )(order, rows)


def attend_grad_short_kernel(
    pairs,
    begin,
    count,
    piece,
    order,
    rows,
    grads,
    attended_t,
    logsum,
    cos,
    sin,
    cos_t,
    sin_t,
    out,
    q_s,
    k_s,
    v_s,
    g_s,
    kt_s,
    dq_s,
    dk_s,
    dv_s,
    dk_o,
    dv_o,
):
    length = rows.shape[0]
    blocks = length // ABLK
    width = pairs * HD
    half = HD // 2
    scale = HD ** (-0.5)
    identity = eye(HD)

    def sort(j, _):
        take = pl.ds(pl.multiple_of(order[j] * piece, piece), piece)
        block = rows[take, :]
        grad = grads[take, :]
        to = pl.ds(pl.multiple_of(j * piece, piece), piece)
        for p in range(count):
            lane = (begin + p) * HD
            q_s[p, to, :] = (block[:, lane : lane + HD].astype(F32) * scale).astype(BF)
            k = block[:, width + lane : width + lane + HD]
            k_s[p, to, :] = k
            kt_s[p, :, to] = mm(identity, k, NT).astype(BF)
            v_s[p, to, :] = block[:, 2 * width + lane : 2 * width + lane + HD]
            g_s[p, to, :] = grad[:, lane : lane + HD]
        return 0

    lax.fori_loop(0, length // piece, sort, 0)

    def pair(p, _):
        for i in range(blocks):
            at = slice(i * ABLK, (i + 1) * ABLK)
            queries = q_s[p, at, :]
            grad = g_s[p, at, :]
            delta = jnp.sum(mm(identity, grad, NT) * attended_t[begin + p, :, at], axis=0, keepdims=True)
            level = logsum[begin + p, :, at]
            dq = jnp.zeros((HD, ABLK), F32)
            for j in range(i, -1, -1):
                to = slice(j * ABLK, (j + 1) * ABLK)
                probs = jnp.exp(mm(k_s[p, to, :], queries, NT) - level)
                ds = (probs * (mm(v_s[p, to, :], grad, NT) - delta)).astype(BF)
                dv = mm(probs.astype(BF), grad)
                dk = mm(ds, queries)
                if i == j:
                    dv_s[to, :] = dv
                    dk_s[to, :] = dk
                else:
                    dv_s[to, :] += dv
                    dk_s[to, :] += dk
                dq += mm(kt_s[p, :, to], ds)
            dq = dq * scale
            c, s = cos_t[:, at], sin_t[:, at]
            a, b = dq[:half, :], dq[half:, :]
            dq = jnp.concatenate([a * c + b * s, b * c - a * s], axis=0)
            dq_s[p, at, :] = dq.T.astype(BF)

        def turn(j, _):
            to = pl.ds(pl.multiple_of(j * ABLK, ABLK), ABLK)
            dk = dk_s[to, :]
            a, b = dk[:, :half], dk[:, half:]
            c, s = cos[to, :], sin[to, :]
            dk_o[p, to, :] = jnp.concatenate([a * c + b * s, b * c - a * s], axis=1).astype(BF)
            dv_o[p, to, :] = dv_s[to, :].astype(BF)
            return 0

        lax.fori_loop(0, blocks, turn, 0)
        return 0

    lax.fori_loop(0, count, pair, 0)

    def unsort(j, _):
        take = pl.ds(pl.multiple_of(j * piece, piece), piece)
        to = pl.ds(pl.multiple_of(order[j] * piece, piece), piece)
        parts = [ref[p, take, :] for ref in (dq_s, dk_o, dv_o) for p in range(count)]
        out[to, :] = jnp.concatenate(parts, axis=1)
        return 0

    lax.fori_loop(0, length // piece, unsort, 0)


def attend_grad_short(
    order, rows, grads, attended_t, logsum, cos, sin, cos_t, sin_t, pairs, piece, begin, count
):
    length = rows.shape[0]
    full = pltpu.VMEM((length, HD), F32)
    each = pltpu.VMEM((count, length, HD), BF)
    return pl.pallas_call(
        functools.partial(attend_grad_short_kernel, pairs, begin, count, piece),
        out_shape=jax.ShapeDtypeStruct((length, 3 * count * HD), BF),
        in_specs=[smem()] + [vmem()] * 8,
        out_specs=vmem(),
        scratch_shapes=[each] * 4
        + [pltpu.VMEM((count, HD, length), BF), each, full, full, each, each],
        compiler_params=params(48),
        cost_estimate=cost(14 * count),
        name=f"attend_grad_{begin}",
    )(order, rows, grads, attended_t, logsum, cos, sin, cos_t, sin_t)


def over_ctx(value, mask):
    size = lax.axis_size("ctx")
    return lax.ppermute(value, "ctx", [(i, i ^ mask) for i in range(size)])


def along_fsdp(value, shift):
    size = lax.axis_size("fsdp")
    return lax.ppermute(value, "fsdp", [(i, (i + shift) % size) for i in range(size)])


def by_index(blocks, index):
    if len(blocks) == 1:
        return blocks
    half = len(blocks) // 2
    flip = (index // half) % 2 == 1
    lower = [jnp.where(flip, b, a) for a, b in zip(blocks[:half], blocks[half:])]
    upper = [jnp.where(flip, a, b) for a, b in zip(blocks[:half], blocks[half:])]
    return by_index(lower, index) + by_index(upper, index)


def place():
    ctx = lax.axis_index("ctx")
    return ctx % 2, ctx // 2, lax.axis_index("fsdp")


def gather_weight(shard):
    core, chip, z = place()
    chips = lax.axis_size("ctx") // 2
    shards = lax.axis_size("fsdp")
    rows, columns = shard.shape
    r, half = rows // chips, columns // 2
    mine = lax.dynamic_slice(shard, (chip * r, core * half), (r, half))
    along = [mine] + [along_fsdp(mine, k) for k in range(1, shards)]
    turned = jnp.stack([along[(shards - m) % shards] for m in range(shards)])
    column = lax.dynamic_slice_in_dim(
        jnp.concatenate([turned, turned]), (shards - z) % shards, shards
    )
    blocks = [column] + [over_ctx(column, 2 * k) for k in range(1, chips)]
    own = jnp.stack(by_index(blocks, chip), axis=1).reshape(shards * rows, half)
    other = over_ctx(own, 1)
    return jnp.where(
        core == 0, jnp.concatenate([own, other], axis=1), jnp.concatenate([other, own], axis=1)
    )


def gather_gains(gains):
    _, _, z = place()
    shards = lax.axis_size("fsdp")
    along = [gains] + [along_fsdp(gains, k) for k in range(1, shards)]
    turned = jnp.stack([along[(shards - m) % shards] for m in range(shards)])
    every = lax.dynamic_slice_in_dim(
        jnp.concatenate([turned, turned]), (shards - z) % shards, shards
    )
    return jnp.moveaxis(every, 0, 1).reshape(gains.shape[0], -1)


def reduce_grad(grad):
    core, chip, z = place()
    chips = lax.axis_size("ctx") // 2
    shards = lax.axis_size("fsdp")
    rows, columns = grad.shape[0] // shards, grad.shape[1]
    r, half = rows // chips, columns // 2
    view = grad.reshape(shards, chips, r, columns)

    def columns_of(which):
        return lax.dynamic_slice_in_dim(view, which * half, half, axis=3)

    total = columns_of(core).astype(F32) + over_ctx(columns_of(1 - core), 1).astype(F32)
    low = total.astype(BF)
    sent = [
        over_ctx(lax.dynamic_index_in_dim(low, chip ^ k, 1, keepdims=False), 2 * k)
        for k in range(1, chips)
    ]
    total = lax.dynamic_index_in_dim(low, chip, 1, keepdims=False).astype(F32)
    total = sum((s.astype(F32) for s in sent), total)
    low = total.astype(BF)
    sent = [
        along_fsdp(lax.dynamic_index_in_dim(low, (z + k) % shards, 0, keepdims=False), k)
        for k in range(1, shards)
    ]
    total = lax.dynamic_index_in_dim(low, z, 0, keepdims=False).astype(F32)
    total = sum((s.astype(F32) for s in sent), total)
    piece = total.astype(BF)
    blocks = [piece] + [over_ctx(piece, 2 * k) for k in range(1, chips)]
    own = jnp.stack(by_index(blocks, chip)).reshape(rows, half)
    other = over_ctx(own, 1)
    return jnp.where(
        core == 0, jnp.concatenate([own, other], axis=1), jnp.concatenate([other, own], axis=1)
    ).astype(F32)


def by_head(values, devices, pairs):
    batches, tokens, kinds, _ = values.shape
    groups = HEADS // pairs
    values = values.reshape(batches, tokens, kinds, groups, pairs * HD)
    values = values.transpose(0, 3, 1, 2, 4).reshape(batches * groups, tokens, kinds * pairs * HD)
    spare = devices - batches * groups
    return jnp.pad(values, ((0, spare), (0, 0), (0, 0)))


def by_token(values, batches, kinds, pairs):
    groups = HEADS // pairs
    tokens = values.shape[1]
    values = values[: batches * groups].reshape(batches, groups, tokens, kinds, pairs * HD)
    return values.transpose(0, 2, 3, 1, 4).reshape(batches, tokens, kinds, HEADS * HD)


def exchange(values, axes):
    return lax.all_to_all(values, axes, split_axis=0, concat_axis=0, tiled=True)


def aligned(value, by=16):
    return pl.multiple_of(value, by)


def pack_weights_kernel(where, joined, output, lookup, gains, expand, contract, first, second):
    core, chip = where[0], where[1]
    rows = pl.ds(aligned(chip * 48), 48)
    for t in range(3):
        first[t * 48 : (t + 1) * 48, :] = joined[rows, pl.ds(aligned(t * D + core * 384, 128), 384)]
    columns = pl.ds(aligned(core * 384, 128), 384)
    first[144:192, :] = lookup[:, columns]
    first[192:208, :] = gains[...]
    for j in range(16):
        second[j * 48 : (j + 1) * 48, :] = expand[
            rows, pl.ds(aligned(core * FF + j * 128, 128), 128)
        ]
    for j in range(3):
        second[768 + j * 128 : 896 + j * 128, :] = contract[
            pl.ds(aligned(chip * 128), 128), pl.ds(aligned(core * 384 + j * 128, 128), 128)
        ]
        second[1152 + j * 48 : 1200 + j * 48, :] = output[
            rows, pl.ds(aligned(core * 384 + j * 128, 128), 128)
        ]


def pack_weights(where, *weights):
    return pl.pallas_call(
        pack_weights_kernel,
        out_shape=(
            jax.ShapeDtypeStruct((208, 384), BF),
            jax.ShapeDtypeStruct((1296, 128), BF),
        ),
        in_specs=[smem()] + [vmem()] * 6,
        out_specs=(vmem(),) * 2,
        compiler_params=params(16),
        cost_estimate=cost(2),
        name="pack_weights",
    )(where, *weights)


def assemble_first_kernel(where, own, other, own_tail, other_tail, joined, lookup, gains):
    core, chip, z = where[0], where[1], where[2]
    for source, tail, half in ((own, own_tail, core), (other, other_tail, 1 - core)):
        columns = pl.ds(aligned(half * 384, 128), 384)
        for m in range(4):
            zz = lax.rem(z + m, 4)
            for k in range(4):
                rows = pl.ds(aligned(zz * 192 + (chip ^ k) * 48), 48)
                for t in range(3):
                    joined[rows, pl.ds(aligned(t * D + half * 384, 128), 384)] = source[
                        k, m, t * 48 : (t + 1) * 48, :
                    ]
            lookup[pl.ds(aligned(zz * 48), 48), columns] = tail[m, 0:48, :]
    for m in range(4):
        gains[lax.rem(z + m, 4)] = own_tail[m, 48:64, :]


def assemble_first(where, *blocks):
    return pl.pallas_call(
        assemble_first_kernel,
        out_shape=(
            jax.ShapeDtypeStruct((D, 3 * D), BF),
            jax.ShapeDtypeStruct((E, D), BF),
            jax.ShapeDtypeStruct((4, 16, 384), BF),
        ),
        in_specs=[smem()] + [vmem()] * 4,
        out_specs=(vmem(),) * 3,
        compiler_params=params(24),
        cost_estimate=cost(3),
        name="assemble_first",
    )(where, *blocks)


def assemble_second_kernel(where, own, other, expand, contract, output):
    core, chip, z = where[0], where[1], where[2]
    for source, half in ((own, core), (other, 1 - core)):

        def block(i, _):
            k, m = i // 4, lax.rem(i, 4)
            zz, yx = lax.rem(z + m, 4), chip ^ k
            rows = pl.ds(aligned(zz * 192 + yx * 48), 48)
            for j in range(16):
                expand[rows, pl.ds(aligned(half * FF + j * 128, 128), 128)] = source[
                    k, m, j * 48 : (j + 1) * 48, :
                ]
            tall = pl.ds(aligned(zz * 512 + yx * 128), 128)
            for j in range(3):
                to = pl.ds(aligned(half * 384 + j * 128, 128), 128)
                contract[tall, to] = source[k, m, 768 + j * 128 : 896 + j * 128, :]
                output[rows, to] = source[k, m, 1152 + j * 48 : 1200 + j * 48, :]
            return 0

        lax.fori_loop(0, 16, block, 0)


def assemble_second(where, *blocks):
    return pl.pallas_call(
        assemble_second_kernel,
        out_shape=(
            jax.ShapeDtypeStruct((D, 2 * FF), BF),
            jax.ShapeDtypeStruct((FF, D), BF),
            jax.ShapeDtypeStruct((D, D), BF),
        ),
        in_specs=[smem()] + [vmem()] * 2,
        out_specs=(vmem(),) * 3,
        compiler_params=params(32),
        cost_estimate=cost(7),
        name="assemble_second",
    )(where, *blocks)


def spread_fsdp(piece):
    along = [piece] + [along_fsdp(piece, k) for k in range(1, 4)]
    return [along[(4 - m) % 4] for m in range(4)]


def add_cores(own, came):
    return [(own[k].astype(F32) + came[k].astype(F32)).astype(BF) for k in range(4)]


def add_blocks(own, came):
    total = own.astype(F32)
    for block in came:
        total = total + block.astype(F32)
    return total.astype(BF)


def to_chips(blocks):
    return [over_ctx(blocks[k], 2 * k) for k in range(1, 4)]


def to_fsdp(total):
    return [along_fsdp(total[m], m) for m in range(1, 4)]


def unpack_second_kernel(where, own, other, expand, contract, output):
    core, chip = where[0], where[1]
    for k in range(4):
        yx = chip ^ k
        rows = pl.ds(aligned(yx * 48), 48)
        for half in range(2):

            def taken(begin, count):
                part = slice(begin, begin + count)
                return jnp.where(core == half, own[k, part, :].astype(F32), other[k, part, :].astype(F32))

            for j in range(16):
                expand[rows, half * FF + j * 128 : half * FF + (j + 1) * 128] = taken(j * 48, 48)
            for j in range(3):
                to = slice(half * 384 + j * 128, half * 384 + (j + 1) * 128)
                contract[pl.ds(aligned(yx * 128), 128), to] = taken(768 + j * 128, 128)
                output[rows, to] = taken(1152 + j * 48, 48)


def unpack_second(where, own, other):
    return pl.pallas_call(
        unpack_second_kernel,
        out_shape=(
            jax.ShapeDtypeStruct((192, 2 * FF), F32),
            jax.ShapeDtypeStruct((512, D), F32),
            jax.ShapeDtypeStruct((192, D), F32),
        ),
        in_specs=[smem()] + [vmem()] * 2,
        out_specs=(vmem(),) * 3,
        compiler_params=params(24),
        cost_estimate=cost(4),
        name="unpack_second",
    )(where, own, other)


def unpack_first_kernel(where, own, other, joined, lookup, gains):
    core, chip = where[0], where[1]
    for k in range(4):
        yx = chip ^ k
        rows = pl.ds(aligned(yx * 48), 48)
        for half in range(2):

            def taken(begin, count):
                part = slice(begin, begin + count)
                return jnp.where(core == half, own[k, part, :].astype(F32), other[k, part, :].astype(F32))

            for t in range(3):
                for j in range(3):
                    to = t * D + half * 384 + j * 128
                    joined[rows, to : to + 128] = taken((t * 3 + j) * 48, 48)

            @pl.when(yx < 3)
            def _():
                at = pl.ds(aligned(half * 384 + yx * 128, 128), 128)
                lookup[:, at] = taken(432, 48)

            @pl.when(yx == 3)
            def _():
                gains[half] = taken(432, 48)


def unpack_first(where, own, other):
    return pl.pallas_call(
        unpack_first_kernel,
        out_shape=(
            jax.ShapeDtypeStruct((192, 3 * D), F32),
            jax.ShapeDtypeStruct((48, D), F32),
            jax.ShapeDtypeStruct((2, 48, 128), F32),
        ),
        in_specs=[smem()] + [vmem()] * 2,
        out_specs=(vmem(),) * 3,
        compiler_params=params(24),
        cost_estimate=cost(2),
        name="unpack_first",
    )(where, own, other)


def unit_rows(x):
    inverse = lax.rsqrt(jnp.mean(x * x, axis=-1, keepdims=True) + epsilon)
    return x * inverse, inverse


def front_kernel(
    pairs, starts, got, target, token, lookup, gain, joined, cos, sin, start, embed, hidden, send
):
    tokens = token.shape[0]
    piece = 128
    per_batch = tokens // 2 // piece
    groups = HEADS // pairs
    wide_ = pairs * HD
    slots = got.shape[0]
    lane = lax.broadcasted_iota(jnp.int32, (piece, 128), 1)
    first_half = lax.rem(lane, HD) < HD // 2

    def block(i, _):
        at = pl.ds(aligned(i * piece, piece), piece)
        goal = target[at, :]
        slot = lax.broadcasted_iota(jnp.int32, (piece, slots), 1)
        parts = []
        for table in range(2):
            hot = jnp.where(goal[:, table : table + 1] == slot, 1.0, 0.0).astype(BF)
            parts.append(mm(hot, got[:, table * E : (table + 1) * E]))
        rows = (parts[0] + parts[1]).astype(BF)
        embed[at, :] = rows
        x = token[at, :].astype(F32) + mm(rows, lookup[...])
        start[at, :] = x
        normed, _ = unit_rows(x)
        low = (normed * gain[...]).astype(BF)
        hidden[at, :] = low
        projected = mm(low, joined[...])
        begin = pl.ds(aligned(starts[lax.rem(i, per_batch)] * piece, piece), piece)
        c = cos[begin, :]
        s = sin[begin, :]
        c = jnp.concatenate([c, c, c, c], axis=1)
        s = jnp.concatenate([-s, s, -s, s], axis=1)
        turned = []
        for j in range(12):
            v = projected[:, j * 128 : (j + 1) * 128]
            swapped = jnp.where(first_half, pltpu.roll(v, 96, 1), pltpu.roll(v, 32, 1))
            turned.append((v * c + swapped * s).astype(BF))
        q = jnp.concatenate(turned[:6], axis=1)
        k = jnp.concatenate(turned[6:], axis=1)
        v = projected[:, 2 * D :].astype(BF)
        batch = i // per_batch
        to = pl.ds(aligned(lax.rem(i, per_batch) * piece, piece), piece)
        for g in range(groups):
            take = slice(g * wide_, (g + 1) * wide_)
            send[batch * groups + g, to, :] = jnp.concatenate(
                [q[:, take], k[:, take], v[:, take]], axis=1
            )
        return 0

    lax.fori_loop(0, tokens // piece, block, 0)


def front(pairs, devices, starts, got, target, token, lookup, gain, joined, cos, sin):
    tokens = token.shape[0]
    return pl.pallas_call(
        functools.partial(front_kernel, pairs),
        out_shape=(
            jax.ShapeDtypeStruct((tokens, D), F32),
            jax.ShapeDtypeStruct((tokens, E), BF),
            jax.ShapeDtypeStruct((tokens, D), BF),
            jax.ShapeDtypeStruct((devices, tokens // 2, 3 * pairs * HD), BF),
        ),
        in_specs=[smem()] + [vmem()] * 8,
        out_specs=(vmem(),) * 4,
        compiler_params=params(40),
        cost_estimate=cost(9),
        name="front",
    )(starts, got, target, token, lookup, gain, joined, cos, sin)


def mlp_kernel(
    pairs,
    came,
    start,
    output,
    gain,
    upstream,
    w_gate,
    w_up,
    w_down,
    result,
    hidden_out,
    attended_out,
    act_out,
    gate_out,
    up_out,
    gain_grad,
    middle_grad,
    send,
    hidden,
    total,
    back,
):
    step = pl.program_id(0)
    groups = HEADS // pairs
    wide_ = pairs * HD
    half = came.shape[1]

    @pl.when(step == 0)
    def _():
        for batch in range(2):
            at = slice(batch * half, (batch + 1) * half)
            rows = jnp.concatenate([came[batch * groups + g] for g in range(groups)], axis=1)
            attended_out[at, :] = rows
            x = start[at, :] + mm(rows, output[...])
            total[at, :] = x
            middle_grad[at, :] = x
            normed, _ = unit_rows(x)
            low = (normed * gain[...]).astype(BF)
            hidden[at, :] = low
            hidden_out[at, :] = low
        back[...] = jnp.zeros_like(back)

    for batch in range(2):
        at = slice(batch * half, (batch + 1) * half)
        gate = mm(hidden[at, :], w_gate[...])
        up = mm(hidden[at, :], w_up[...])
        sigmoid = jax.nn.sigmoid(gate)
        swish = gate * sigmoid
        act = (swish * up).astype(BF)
        act_out[at, :] = act
        total[at, :] += mm(act, w_down[...])
        grad = mm(upstream[at, :], w_down[...], NT)
        gate_grad = (grad * up * sigmoid * (1.0 + gate * (1.0 - sigmoid))).astype(BF)
        up_grad = (grad * swish).astype(BF)
        gate_out[at, :] = gate_grad
        up_out[at, :] = up_grad
        back[at, :] += mm(gate_grad, w_gate[...], NT) + mm(up_grad, w_up[...], NT)

    @pl.when(step == pl.num_programs(0) - 1)
    def _():
        gains = jnp.zeros((1, D), F32)
        for batch in range(2):
            at = slice(batch * half, (batch + 1) * half)
            result[at, :] = total[at, :].astype(BF)
            normed, inverse = unit_rows(middle_grad[at, :])
            grad = back[at, :]
            gains += jnp.sum(grad * normed, axis=0, keepdims=True)
            weighted = grad * gain[...]
            grad = upstream[at, :].astype(F32) + inverse * (
                weighted - normed * jnp.mean(weighted * normed, axis=-1, keepdims=True)
            )
            middle_grad[at, :] = grad
            heads = mm(grad.astype(BF), output[...], NT).astype(BF)
            for g in range(groups):
                send[batch * groups + g] = heads[:, g * wide_ : (g + 1) * wide_]
        gain_grad[...] = gains


def mlp(pairs, came, start, output, gain, upstream, expand, contract):
    tokens = start.shape[0]
    width = 256
    steps = FF // width
    whole = lambda *shape: pl.BlockSpec(shape, lambda i: (0,) * len(shape))
    column = pl.BlockSpec((tokens, width), lambda i: (0, i))
    return pl.pallas_call(
        functools.partial(mlp_kernel, pairs),
        grid=(steps,),
        out_shape=(
            jax.ShapeDtypeStruct((tokens, D), BF),
            jax.ShapeDtypeStruct((tokens, D), BF),
            jax.ShapeDtypeStruct((tokens, D), BF),
            jax.ShapeDtypeStruct((tokens, FF), BF),
            jax.ShapeDtypeStruct((tokens, FF), BF),
            jax.ShapeDtypeStruct((tokens, FF), BF),
            jax.ShapeDtypeStruct((1, D), F32),
            jax.ShapeDtypeStruct((tokens, D), F32),
            jax.ShapeDtypeStruct(came.shape, BF),
        ),
        in_specs=[
            whole(*came.shape),
            whole(tokens, D),
            whole(D, D),
            whole(1, D),
            whole(tokens, D),
            pl.BlockSpec((D, width), lambda i: (0, i)),
            pl.BlockSpec((D, width), lambda i: (0, steps + i)),
            pl.BlockSpec((width, D), lambda i: (i, 0)),
        ],
        out_specs=(
            whole(tokens, D),
            whole(tokens, D),
            whole(tokens, D),
            column,
            column,
            column,
            whole(1, D),
            whole(tokens, D),
            whole(*came.shape),
        ),
        scratch_shapes=[
            pltpu.VMEM((tokens, D), BF),
            pltpu.VMEM((tokens, D), F32),
            pltpu.VMEM((tokens, D), F32),
        ],
        compiler_params=params(48),
        cost_estimate=cost(23),
        name="mlp",
    )(came, start, output, gain, upstream, expand, expand, contract)


def weight_grads_kernel(
    where, hidden, gate, up, act, upstream, attended, middle, own, other, wide_s, tall_s, out_s
):
    core, chip, z = where[0], where[1], where[2]

    def chunk(c, _):
        at = pl.ds(aligned(c * 256, 256), 256)
        wide_s[0] = mm(hidden[...], gate[:, at], TN).astype(BF)
        wide_s[1] = mm(hidden[...], up[:, at], TN).astype(BF)
        tall = mm(act[:, at], upstream[...], TN).astype(BF)
        tall_s[0] = tall[:, :384]
        tall_s[1] = tall[:, 384:]
        for out, half in ((own, core), (other, 1 - core)):
            for m in range(4):
                zz = lax.rem(z + m, 4)
                for k in range(4):
                    block = wide_s[half, pl.ds(aligned(zz * 192 + (chip ^ k) * 48), 48), :]
                    for j in range(2):
                        to = pl.ds(aligned((2 * c + j) * 48), 48)
                        out[k, m, to, :] = block[:, j * 128 : (j + 1) * 128]
            m = lax.rem(c // 2 - z + 4, 4)
            for b in range(2):
                k = (lax.rem(c, 2) * 2 + b) ^ chip
                block = tall_s[half, b * 128 : (b + 1) * 128, :]
                for j in range(3):
                    out[k, m, 768 + j * 128 : 896 + j * 128, :] = block[:, j * 128 : (j + 1) * 128]
        return 0

    lax.fori_loop(0, FF // 256, chunk, 0)
    square = mm(attended[...], middle[...].astype(BF), TN).astype(BF)
    out_s[0] = square[:, :384]
    out_s[1] = square[:, 384:]
    for out, half in ((own, core), (other, 1 - core)):
        for m in range(4):
            zz = lax.rem(z + m, 4)
            for k in range(4):
                block = out_s[half, pl.ds(aligned(zz * 192 + (chip ^ k) * 48), 48), :]
                for j in range(3):
                    out[k, m, 1152 + j * 48 : 1200 + j * 48, :] = block[:, j * 128 : (j + 1) * 128]


def weight_grads(where, *operands):
    shape = jax.ShapeDtypeStruct((4, 4, 1296, 128), BF)
    return pl.pallas_call(
        weight_grads_kernel,
        out_shape=(shape, shape),
        in_specs=[smem()] + [vmem()] * 7,
        out_specs=(vmem(),) * 2,
        scratch_shapes=[
            pltpu.VMEM((2, D, 256), BF),
            pltpu.VMEM((2, 256, 384), BF),
            pltpu.VMEM((2, D, 384), BF),
        ],
        compiler_params=params(48),
        cost_estimate=cost(15),
        name="weight_grads",
    )(where, *operands)


def back_kernel(
    where,
    came_a,
    came_b,
    hidden,
    start,
    middle,
    joined,
    lookup,
    gain,
    second_gain,
    embed,
    target,
    token_grad,
    send,
    own,
    other,
    df_s,
    half_s,
    look_s,
    gain_s,
):
    core, chip, z = where[0], where[1], where[2]
    widths = [(ref, ref.shape[2] // 3) for ref in (came_a, came_b)]
    groups = D // sum(w for _, w in widths)
    rows = came_a.shape[1]
    tokens = 2 * rows
    for batch in range(2):
        for t in range(3):
            parts = [
                ref[batch * groups + g, :, t * w : (t + 1) * w]
                for g in range(groups)
                for ref, w in widths
            ]
            df_s[batch * rows : (batch + 1) * rows, t * D : (t + 1) * D] = jnp.concatenate(
                parts, axis=1
            )

    def kind(t, _):
        grad = mm(hidden[...], df_s[:, pl.ds(aligned(t * D, 128), D)], TN).astype(BF)
        half_s[0] = grad[:, :384]
        half_s[1] = grad[:, 384:]
        for out, half in ((own, core), (other, 1 - core)):
            for m in range(4):
                zz = lax.rem(z + m, 4)
                for k in range(4):
                    block = half_s[half, pl.ds(aligned(zz * 192 + (chip ^ k) * 48), 48), :]
                    for j in range(3):
                        to = pl.ds(aligned((t * 3 + j) * 48), 48)
                        out[k, m, to, :] = block[:, j * 128 : (j + 1) * 128]
        return 0

    lax.fori_loop(0, 3, kind, 0)

    gains = jnp.zeros((1, D), F32)
    lows = []
    for batch in range(2):
        at = slice(batch * rows, (batch + 1) * rows)
        grad = mm(df_s[at, :], joined[...], NT)
        normed, inverse = unit_rows(start[at, :])
        gains += jnp.sum(grad * normed, axis=0, keepdims=True)
        weighted = grad * gain[...]
        grad = middle[at, :] + inverse * (
            weighted - normed * jnp.mean(weighted * normed, axis=-1, keepdims=True)
        )
        token_grad[at, :] = grad
        lows.append(grad.astype(BF))
    low = jnp.concatenate(lows, axis=0)
    look = mm(embed[...], low, TN).astype(BF)
    for half in range(2):
        for j in range(3):
            begin = half * 384 + j * 128
            look_s[half, j] = look[:, begin : begin + 128]
    for half, row in enumerate((gains, second_gain[...])):
        parts = [row[:, j * 128 : (j + 1) * 128] for j in range(6)]
        gain_s[half] = jnp.concatenate(parts + [jnp.zeros((42, 128), F32)], axis=0).astype(BF)
    for out, half in ((own, core), (other, 1 - core)):
        for m in range(4):
            zz = lax.rem(z + m, 4)
            for k in range(4):
                yx = chip ^ k

                @pl.when(yx < 3)
                def _():
                    out[k, m, 432:480, :] = look_s[
                        half, lax.rem(yx, 3), pl.ds(aligned(zz * 48), 48), :
                    ]

                @pl.when(yx == 3)
                def _():
                    out[k, m, 432:480, :] = gain_s[half]

    de = mm(low, lookup[...], NT).astype(BF)
    slots = send.shape[0]
    slot = lax.broadcasted_iota(jnp.int32, (slots, tokens), 0)
    parts = []
    for table in range(2):
        hot = jnp.where(slot == target[table : table + 1, :], 1.0, 0.0).astype(BF)
        parts.append(mm(hot, de))
    send[...] = jnp.concatenate(parts, axis=1).astype(BF)


def back_pass(slots, where, *operands):
    tokens = operands[2].shape[0]
    shape = jax.ShapeDtypeStruct((4, 4, 480, 128), BF)
    return pl.pallas_call(
        back_kernel,
        out_shape=(
            jax.ShapeDtypeStruct((tokens, D), F32),
            jax.ShapeDtypeStruct((slots, 2 * E), BF),
            shape,
            shape,
        ),
        in_specs=[smem()] + [vmem()] * 11,
        out_specs=(vmem(),) * 4,
        scratch_shapes=[
            pltpu.VMEM((tokens, 3 * D), BF),
            pltpu.VMEM((2, D, 384), BF),
            pltpu.VMEM((2, 3, E, 128), BF),
            pltpu.VMEM((2, 48, 128), BF),
        ],
        compiler_params=params(48),
        cost_estimate=cost(13),
        name="back",
    )(where, *operands)


def rotate(values, cosines, sines):
    half = values.shape[-1] // 2
    a, b = values[..., :half], values[..., half:]
    c, s = cosines[:, None, :], sines[:, None, :]
    return jnp.concatenate([a * c - b * s, b * c + a * s], axis=-1)


def normalize(rows):
    inverse = lax.rsqrt(jnp.mean(rows * rows, axis=-1, keepdims=True) + epsilon)
    return rows * inverse, inverse


def norm_backward(hidden_grad, normed, inverse, gain):
    weighted = hidden_grad * gain
    return inverse * (weighted - normed * jnp.mean(weighted * normed, axis=-1, keepdims=True))


def local(
    token_embed,
    bigram_ids,
    trigram_ids,
    bigram_table,
    trigram_table,
    block_deal,
    lookup_weight,
    attention_gain,
    joined_weight,
    output_weight,
    feedforward_gain,
    expand_weight,
    contract_weight,
    cotangent,
):
    contexts = lax.axis_size("ctx")
    shards = lax.axis_size("fsdp")
    devices = contexts * shards
    batches, local_rows = token_embed.shape[:2]
    tokens = batches * local_rows
    length = local_rows * contexts
    capacity = max(2, 2 * tokens // devices)
    table_rows = bigram_table.shape[0]
    piece = local_rows // 2
    pieces = length // piece
    pairs = -(-batches * HEADS // contexts)
    while HEADS % pairs:
        pairs += 1
    both = ("ctx", "fsdp")

    ids = jnp.stack([bigram_ids.reshape(-1), trigram_ids.reshape(-1)])
    requests, target_row, target_col = placement(ids, table_rows, devices, capacity)
    asked = exchange(requests, both)
    codes = jnp.stack([asked[:, :capacity].reshape(-1), asked[:, capacity:].reshape(-1)], axis=1)
    got = exchange(
        read_rows(codes, bigram_table.T, trigram_table.T).reshape(devices, capacity, 2 * E), both
    ).reshape(devices * capacity, 2 * E)

    lookup = gather_weight(lookup_weight)
    joined = gather_weight(joined_weight)
    output = gather_weight(output_weight)
    gains = gather_gains(jnp.stack([attention_gain, feedforward_gain])).astype(F32)
    first_gain, second_gain = gains[0], gains[1]
    expand = gather_weight(expand_weight)
    contract = gather_weight(contract_weight)

    order = jnp.argmin(
        jnp.abs(block_deal[None, :] - jnp.arange(pieces, dtype=jnp.int32)[:, None]), axis=1
    ).astype(jnp.int32)
    frequency = jnp.exp(-math.log(10000.0) * (2.0 * jnp.arange(HD // 2, dtype=F32) / HD))
    slot = lax.axis_index("ctx") * local_rows + jnp.arange(local_rows, dtype=jnp.int32)
    position = block_deal[slot // piece] * piece + slot % piece
    angles = position.astype(F32)[:, None] * frequency[None, :]
    cosines, sines = jnp.cos(angles), jnp.sin(angles)
    all_angles = jnp.arange(length, dtype=F32)[:, None] * frequency[None, :]
    all_cosines, all_sines = jnp.cos(all_angles), jnp.sin(all_angles)

    slots = jnp.arange(devices * capacity, dtype=jnp.int32)
    hot_b = (target_col[:, 0:1] == slots[None, :]).astype(BF)
    hot_t = (target_col[:, 1:2] == slots[None, :]).astype(BF)
    embedded = (mm(hot_b, got[:, :E]) + mm(hot_t, got[:, E:])).astype(BF)
    start = token_embed.reshape(tokens, D).astype(F32) + mm(embedded, lookup)
    normed_first, inverse_first = normalize(start)
    hidden_first = (normed_first * first_gain).astype(BF)
    projected = mm(hidden_first, joined).reshape(batches, local_rows, 3, HEADS, HD)
    cos_b, sin_b = cosines[None, :, None, :], sines[None, :, None, :]
    turn = lambda x: jnp.concatenate(
        [
            x[..., : HD // 2] * cos_b - x[..., HD // 2 :] * sin_b,
            x[..., HD // 2 :] * cos_b + x[..., : HD // 2] * sin_b,
        ],
        axis=-1,
    )
    qkv = jnp.stack(
        [turn(projected[:, :, 0]), turn(projected[:, :, 1]), projected[:, :, 2]], axis=2
    ).astype(BF)
    qkv = qkv.reshape(batches, local_rows, 3, D)
    rows = exchange(by_head(qkv, contexts, pairs), "ctx").reshape(length, 3 * pairs * HD)
    attended_rows, attended_t, logsum = attend(order, rows, pairs, piece)
    attended = by_token(
        exchange(attended_rows.reshape(contexts, local_rows, pairs * HD), "ctx"), batches, 1, pairs
    ).reshape(tokens, D)
    middle = start + mm(attended, output)
    normed_second, inverse_second = normalize(middle)
    hidden_second = (normed_second * second_gain).astype(BF)
    gate_up = mm(hidden_second, expand)
    gate, up = gate_up[:, :FF], gate_up[:, FF:]
    sigmoid = jax.nn.sigmoid(gate)
    swish = gate * sigmoid
    activated = (swish * up).astype(BF)
    result = (middle + mm(activated, contract)).astype(BF)

    upstream = cotangent.reshape(tokens, D)
    activated_grad = mm(upstream, contract, NT)
    gate_up_grad = jnp.concatenate(
        [
            activated_grad * up * sigmoid * (1.0 + gate * (1.0 - sigmoid)),
            activated_grad * swish,
        ],
        axis=-1,
    ).astype(BF)
    hidden_second_grad = mm(gate_up_grad, expand, NT)
    second_gain_term = jnp.sum(hidden_second_grad * normed_second, axis=0)
    middle_grad = upstream.astype(F32) + norm_backward(
        hidden_second_grad, normed_second, inverse_second, second_gain
    )
    middle_low = middle_grad.astype(BF)
    attended_grad = mm(middle_low, output, NT).astype(BF)
    grad_rows = exchange(
        by_head(attended_grad.reshape(batches, local_rows, 1, D), contexts, pairs), "ctx"
    ).reshape(length, pairs * HD)
    contract_term = mm(activated, upstream, TN).astype(BF)
    expand_term = mm(hidden_second, gate_up_grad, TN).astype(BF)
    output_term = mm(attended, middle_low, TN).astype(BF)
    contract_grad = reduce_grad(contract_term)
    expand_grad = reduce_grad(expand_term)
    output_grad = reduce_grad(output_term)

    grad_rows = attend_grad(
        order,
        rows,
        grad_rows,
        attended_t,
        logsum,
        all_cosines,
        all_sines,
        all_cosines.T,
        all_sines.T,
        pairs,
        piece,
    )
    joined_local = by_token(
        exchange(grad_rows.reshape(contexts, local_rows, 3 * pairs * HD), "ctx"), batches, 3, pairs
    ).reshape(tokens, 3 * D)
    joined_grad = reduce_grad(mm(hidden_first, joined_local, TN).astype(BF))
    hidden_first_grad = mm(joined_local, joined, NT)
    first_gain_term = jnp.sum(hidden_first_grad * normed_first, axis=0)
    start_grad = middle_grad + norm_backward(
        hidden_first_grad, normed_first, inverse_first, first_gain
    )
    start_low = start_grad.astype(BF)
    lookup_grad = reduce_grad(mm(embedded, start_low, TN).astype(BF))
    embed_grad = mm(start_low, lookup, NT).astype(BF)
    give_b = (target_row[0:1, :] == slots[:, None]).astype(BF)
    give_t = (target_row[1:2, :] == slots[:, None]).astype(BF)
    send = jnp.concatenate([mm(give_b, embed_grad), mm(give_t, embed_grad)], axis=1).astype(BF)
    arrived = exchange(send.reshape(devices, capacity, 2 * E), both)
    bigram_grad, trigram_grad = add_rows(
        codes, arrived.reshape(devices * capacity, 2 * E), table_rows
    )
    gain_terms = lax.psum(jnp.stack([first_gain_term, second_gain_term]), both)
    gain_share = lax.dynamic_slice_in_dim(
        gain_terms, lax.axis_index("fsdp") * (D // shards), D // shards, axis=1
    )
    return (
        result.reshape(batches, local_rows, D),
        start_grad.reshape(batches, local_rows, D),
        bigram_grad.T,
        trigram_grad.T,
        lookup_grad,
        gain_share[0],
        joined_grad,
        output_grad,
        gain_share[1],
        expand_grad,
        contract_grad,
    )


def local_packed(
    token_embed,
    bigram_ids,
    trigram_ids,
    bigram_table,
    trigram_table,
    block_deal,
    lookup_weight,
    attention_gain,
    joined_weight,
    output_weight,
    feedforward_gain,
    expand_weight,
    contract_weight,
    cotangent,
):
    contexts = lax.axis_size("ctx")
    shards = lax.axis_size("fsdp")
    devices = contexts * shards
    batches, local_rows = token_embed.shape[:2]
    tokens = batches * local_rows
    length = local_rows * contexts
    capacity = max(2, 2 * tokens // devices)
    table_rows = bigram_table.shape[0]
    piece = local_rows // 2
    pieces = length // piece
    pairs = -(-batches * HEADS // contexts)
    while HEADS % pairs:
        pairs += 1
    both = ("ctx", "fsdp")


    core, chip, z = place()
    where = jnp.stack([core, chip, z]).astype(jnp.int32)
    ids = jnp.stack([bigram_ids.reshape(-1), trigram_ids.reshape(-1)])
    requests, target_row, target_col = placement(ids, table_rows, devices, capacity)
    asked = exchange(requests, both)
    gain_rows = jnp.pad(jnp.stack([attention_gain, feedforward_gain]), ((0, 14), (0, 192)))
    first, second = pack_weights(
        after(where, requests),
        joined_weight,
        output_weight,
        lookup_weight,
        gain_rows,
        expand_weight,
        contract_weight,
    )
    along = spread_fsdp(first)
    column = jnp.stack([p[:144] for p in along])
    tail = jnp.stack([p[144:] for p in along])
    blocks = [over_ctx(column, 2 * k) for k in range(1, 4)]
    codes = jnp.stack([asked[:, :capacity].reshape(-1), asked[:, capacity:].reshape(-1)], axis=1)
    answer = read_rows(
        after(codes, column, tail), in_hbm(bigram_table.T), in_hbm(trigram_table.T)
    )
    got = exchange(answer.reshape(devices, capacity, 2 * E), both)
    own = jnp.stack([after(block, answer) for block in [column] + blocks])
    joined, lookup, gains = assemble_first(
        where, own, over_ctx(own, 1), tail, over_ctx(tail, 1)
    )
    second_column = jnp.stack(spread_fsdp(after(second, own)))
    gains = gains[:, :2, :192].astype(F32).transpose(1, 0, 2).reshape(2, D)
    first_gain, second_gain = gains[0:1], gains[1:2]
    got = got.reshape(devices * capacity, 2 * E)

    order = jnp.sum(
        jnp.where(
            block_deal[None, :] == jnp.arange(pieces, dtype=jnp.int32)[:, None],
            jnp.arange(pieces, dtype=jnp.int32)[None, :],
            0,
        ),
        axis=1,
    )
    starts = lax.dynamic_slice_in_dim(block_deal, lax.axis_index("ctx") * 2, 2)
    frequency = jnp.exp(-math.log(10000.0) * (2.0 * jnp.arange(HD // 2, dtype=F32) / HD))
    angles = frequency[:, None] * jnp.arange(length, dtype=F32)[None, :]
    cos_t, sin_t = lax.optimization_barrier((jnp.cos(angles), jnp.sin(angles)))
    cos, sin = cos_t.T, sin_t.T

    start, embedded, hidden_first, sent = front(
        pairs,
        contexts,
        starts,
        got,
        target_col,
        token_embed.reshape(tokens, D),
        lookup,
        first_gain,
        joined,
        cos,
        sin,
    )
    rows = exchange(sent, "ctx").reshape(length, 3 * pairs * HD)
    second_column = after(second_column, rows)
    blocks = [over_ctx(second_column, 2 * k) for k in range(1, 4)]
    attended_rows, attended_t, logsum = attend_short(order, rows, pairs, piece)
    came = exchange(attended_rows.reshape(contexts, local_rows, pairs * HD), "ctx")
    own = jnp.stack([after(block, attended_rows) for block in [second_column] + blocks])
    expand, contract, output = assemble_second(where, own, over_ctx(own, 1))
    upstream = cotangent.reshape(tokens, D)
    (
        result,
        hidden_second,
        attended,
        activated,
        gate_grad,
        up_grad,
        second_gain_term,
        middle_grad,
        sent,
    ) = mlp(pairs, came, start, output, second_gain, upstream, expand, contract)

    grad_rows = exchange(sent, "ctx").reshape(length, pairs * HD)
    own_m, other_m = weight_grads(
        where, hidden_second, gate_grad, up_grad, activated, upstream, attended, middle_grad
    )
    from_core = over_ctx(after(other_m, grad_rows), 1)
    part = functools.partial(attend_grad_short, order)
    shared = (attended_t, logsum, cos, sin, cos_t, sin_t, pairs, piece)
    grad_a = part(rows, grad_rows, *shared, 0, 1)
    came_a = exchange(grad_a.reshape(contexts, local_rows, 3 * HD), "ctx")
    half_m = add_cores(own_m, after(from_core, grad_a))
    from_chips = [over_ctx(half_m[k], 2 * k) for k in (1, 2)]
    grad_b = part(after(rows, half_m), grad_rows, *shared, 1, pairs - 1)
    grad_b = after(grad_b, from_chips)
    from_chips.append(over_ctx(after(half_m[3], grad_b), 6))
    came_b = exchange(grad_b.reshape(contexts, local_rows, 3 * (pairs - 1) * HD), "ctx")
    start_grad, send, own_j, other_j = back_pass(
        devices * capacity,
        where,
        came_a,
        came_b,
        hidden_first,
        start,
        middle_grad,
        joined,
        lookup,
        first_gain,
        second_gain_term,
        embedded,
        target_row,
    )
    from_core = over_ctx(other_j, 1)
    arrived = exchange(send.reshape(devices, capacity, 2 * E), both)
    total_m = add_blocks(half_m[0], [after(block, own_j) for block in from_chips])
    from_fsdp_m = to_fsdp(total_m)
    half_j = add_cores(own_j, after(from_core, total_m))
    total_j = add_blocks(half_j[0], to_chips(half_j))
    from_fsdp_j = to_fsdp(total_j)
    piece_m = add_blocks(total_m[0], [after(block, total_j) for block in from_fsdp_m])
    every_m = to_chips([piece_m] * 4)
    bigram_grad, trigram_grad = add_rows(
        after(codes, total_j, piece_m), arrived.reshape(devices * capacity, 2 * E), table_rows
    )
    piece_j = add_blocks(total_j[0], [after(block, bigram_grad) for block in from_fsdp_j])
    every_j = to_chips([piece_j] * 4)
    blocks_m = jnp.stack([piece_m] + [after(block, piece_j) for block in every_m])
    other_m = over_ctx(blocks_m, 1)
    blocks_j = jnp.stack([piece_j] + [after(block, blocks_m) for block in every_j])
    other_j = over_ctx(blocks_j, 1)
    expand_grad, contract_grad, output_grad = unpack_second(
        where, blocks_m, after(other_m, blocks_j)
    )
    joined_grad, lookup_grad, gain_grads = unpack_first(where, blocks_j, other_j)
    gain_share = lax.dynamic_slice_in_dim(
        gain_grads[:, :6].reshape(2, D), z * (D // shards), D // shards, axis=1
    )
    return (
        result.reshape(batches, local_rows, D),
        start_grad.reshape(batches, local_rows, D),
        bigram_grad.T,
        trigram_grad.T,
        lookup_grad,
        gain_share[0],
        joined_grad,
        output_grad,
        gain_share[1],
        expand_grad,
        contract_grad,
    )


def solution(mesh):
    fits = mesh.shape["ctx"] == 8 and mesh.shape["fsdp"] == 4
    return jax.shard_map(
        local_packed if fits else local,
        mesh=mesh,
        in_specs=(
            P("fsdp", "ctx", None),
            P("fsdp", "ctx"),
            P("fsdp", "ctx"),
            P(("ctx", "fsdp"), None),
            P(("ctx", "fsdp"), None),
            P(),
            P("fsdp", None),
            P("fsdp"),
            P("fsdp", None),
            P("fsdp", None),
            P("fsdp"),
            P("fsdp", None),
            P("fsdp", None),
            P("fsdp", "ctx", None),
        ),
        out_specs=(
            P("fsdp", "ctx", None),
            P("fsdp", "ctx", None),
            P(("ctx", "fsdp"), None),
            P(("ctx", "fsdp"), None),
            P("fsdp", None),
            P("fsdp"),
            P("fsdp", None),
            P("fsdp", None),
            P("fsdp"),
            P("fsdp", None),
            P("fsdp", None),
        ),
        check_vma=False,
    )
```

```python
import functools
import math

import jax
import jax.numpy as jnp
from jax import lax
from jax.experimental import pallas as pl
from jax.experimental.pallas import tpu as pltpu
from jax.sharding import PartitionSpec as P

D = 768
HEADS = 12
HD = 64
FF = 2048
E = 192
ABLK = 256
BF = jnp.bfloat16
F32 = jnp.float32

epsilon = 1e-05
NT = (((1,), (1,)), ((), ()))
NN = (((1,), (0,)), ((), ()))
TN = (((0,), (0,)), ((), ()))


def mm(a, b, dims=NN):
    return lax.dot_general(a, b, dims, preferred_element_type=F32)


def eye(n):
    rows = lax.broadcasted_iota(jnp.int32, (n, n), 0)
    return jnp.where(rows == lax.broadcasted_iota(jnp.int32, (n, n), 1), 1.0, 0.0).astype(BF)


def vmem():
    return pl.BlockSpec(memory_space=pltpu.VMEM)


def smem():
    return pl.BlockSpec(memory_space=pltpu.SMEM)


def params(megabytes, **kw):
    return pltpu.CompilerParams(vmem_limit_bytes=megabytes << 20, **kw)


def cost(microseconds):
    return pl.CostEstimate(
        flops=int(microseconds * 6e8), bytes_accessed=int(microseconds * 2.5e6), transcendentals=0
    )


def in_hbm(value):
    return pltpu.with_memory_space_constraint(value, pltpu.HBM)


def after(value, *others):
    return lax.optimization_barrier((value, others))[0]


def placement_kernel(capacity, owner_row, owner_col, local_row, requests, target_row, target_col):
    tokens = owner_row.shape[1]
    devices = requests.shape[0]
    for table in range(2):
        own_r = owner_row[table : table + 1, :]
        own_c = owner_col[:, table : table + 1]
        t_row = lax.broadcasted_iota(jnp.int32, (tokens, tokens), 0)
        t_col = lax.broadcasted_iota(jnp.int32, (tokens, tokens), 1)
        same = own_c == own_r
        rank_r = jnp.sum(jnp.where(same & (t_row < t_col), 1.0, 0.0), axis=0, keepdims=True)
        rank_c = jnp.sum(jnp.where(same & (t_col < t_row), 1.0, 0.0), axis=1, keepdims=True)
        rank_r = rank_r.astype(jnp.int32)
        rank_c = rank_c.astype(jnp.int32)
        target_row[table : table + 1, :] = own_r * capacity + rank_r
        target_col[:, table : table + 1] = own_c * capacity + rank_c
        device = lax.broadcasted_iota(jnp.int32, (devices, tokens), 0)
        owned = device == own_r
        row = local_row[table : table + 1, :]
        high = jnp.where(owned, (row >> 7).astype(F32), 0.0).astype(BF)
        low = jnp.where(owned, (row & 127).astype(F32), 0.0).astype(BF)
        one = jnp.where(owned, 1.0, 0.0).astype(BF)
        slot = lax.broadcasted_iota(jnp.int32, (tokens, capacity), 1)
        ranked = jnp.where(slot == rank_c, 1.0, 0.0).astype(BF)
        code = 128.0 * mm(high, ranked) + mm(low, ranked) + mm(one, ranked)
        requests[:, table * capacity : (table + 1) * capacity] = code.astype(jnp.int32)


def placement(ids, table_rows, devices, capacity):
    tokens = ids.shape[1]
    owner = ids // table_rows
    local_row = ids - owner * table_rows
    return pl.pallas_call(
        functools.partial(placement_kernel, capacity),
        out_shape=(
            jax.ShapeDtypeStruct((devices, 2 * capacity), jnp.int32),
            jax.ShapeDtypeStruct((2, tokens), jnp.int32),
            jax.ShapeDtypeStruct((tokens, 2), jnp.int32),
        ),
        in_specs=[vmem()] * 3,
        out_specs=(vmem(),) * 3,
        compiler_params=params(32),
        cost_estimate=cost(2),
        name="placement",
    )(owner, owner.T, local_row)


def wide(ref, columns, table):
    ref[table] = jnp.broadcast_to(columns[:, table : table + 1].astype(F32), ref.shape[1:])


def onehot_block(ref, table, base, width):
    lane = lax.broadcasted_iota(jnp.int32, ref.shape[1:], 1).astype(F32)
    parts = []
    for j in range(width // 128):
        hit = ref[table] == lane + (base + 128 * j + 1).astype(F32)
        parts.append(jnp.where(hit, 1.0, 0.0).astype(BF))
    return jnp.concatenate(parts, axis=1)


def read_rows_kernel(codes, bigram, trigram, out, spread, total):
    step = pl.program_id(0)
    width = bigram.shape[1]

    @pl.when(step == 0)
    def _():
        for table in range(2):
            wide(spread, codes, table)
        total[...] = jnp.zeros_like(total)

    for table, source in enumerate((bigram, trigram)):
        hot = onehot_block(spread, table, step * width, width)
        total[table] += mm(hot, source[...], NT)

    @pl.when(step == pl.num_programs(0) - 1)
    def _():
        out[...] = jnp.concatenate([total[0], total[1]], axis=1).astype(BF)


def table_block(table_rows):
    for width in (1280, 640, 512, 256, 128):
        if table_rows % width == 0:
            return width
    return table_rows


def read_rows(codes, bigram_t, trigram_t):
    slots = codes.shape[0]
    rows = bigram_t.shape[1]
    width = table_block(rows)
    table = pl.BlockSpec((E, width), lambda i: (0, i))
    return pl.pallas_call(
        read_rows_kernel,
        grid=(rows // width,),
        out_shape=jax.ShapeDtypeStruct((slots, 2 * E), BF),
        in_specs=[pl.BlockSpec((slots, 2), lambda i: (0, 0)), table, table],
        out_specs=pl.BlockSpec((slots, 2 * E), lambda i: (0, 0)),
        scratch_shapes=[pltpu.VMEM((2, slots, 128), F32), pltpu.VMEM((2, slots, E), F32)],
        compiler_params=params(32),
        cost_estimate=cost(17),
        name="read_rows",
    )(codes, bigram_t, trigram_t)


def add_rows_kernel(codes, grads, bigram, trigram, spread, turned):
    step = pl.program_id(0)
    width = bigram.shape[1]

    @pl.when(step == 0)
    def _():
        for table in range(2):
            wide(spread, codes, table)
        turned[...] = mm(eye(2 * E), grads[...], NT).astype(BF)

    for table, out in enumerate((bigram, trigram)):
        hot = onehot_block(spread, table, step * width, width)
        out[...] = mm(turned[table * E : (table + 1) * E, :], hot)


def add_rows(codes, grads, rows):
    slots = codes.shape[0]
    width = table_block(rows)
    table = pl.BlockSpec((E, width), lambda i: (0, i))
    shape = jax.ShapeDtypeStruct((E, rows), F32)
    return pl.pallas_call(
        add_rows_kernel,
        grid=(rows // width,),
        out_shape=(shape, shape),
        in_specs=[
            pl.BlockSpec((slots, 2), lambda i: (0, 0)),
            pl.BlockSpec((slots, 2 * E), lambda i: (0, 0)),
        ],
        out_specs=(table, table),
        scratch_shapes=[pltpu.VMEM((2, slots, 128), F32), pltpu.VMEM((2 * E, slots), BF)],
        compiler_params=params(32),
        cost_estimate=cost(14),
        name="add_rows",
    )(codes, grads)


def attend_kernel(pairs, piece, order, rows, out, attended_t, logsum, q_s, k_s, vt_s, s_s):
    length = rows.shape[0]
    blocks = length // ABLK
    per_block = ABLK // piece
    width = pairs * HD
    identity = eye(HD)

    def sort(j, _):
        block = rows[pl.ds(pl.multiple_of(order[j] * piece, piece), piece), :]
        to = pl.ds(pl.multiple_of(j * piece, piece), piece)
        for p in range(pairs):
            q = block[:, p * HD : (p + 1) * HD]
            q_s[p, to, :] = (q.astype(F32) * HD ** (-0.5)).astype(BF)
            k_s[p, to, :] = block[:, width + p * HD : width + (p + 1) * HD]
            v = block[:, 2 * width + p * HD : 2 * width + (p + 1) * HD]
            vt_s[p, :, to] = mm(identity, v, NT).astype(BF)
        return 0

    lax.fori_loop(0, length // piece, sort, 0)

    for p in range(pairs):

        def one(i, _):
            at = pl.ds(pl.multiple_of(i * ABLK, ABLK), ABLK)
            queries = q_s[p, at, :]

            def score(j, peak):
                to = pl.ds(pl.multiple_of(j * ABLK, ABLK), ABLK)
                s = mm(k_s[p, to, :], queries, NT)
                s_s[to, :] = s
                return jnp.maximum(peak, jnp.max(s, axis=0, keepdims=True))

            peak = lax.fori_loop(0, i + 1, score, jnp.full((1, ABLK), -jnp.inf, F32))

            def raise_(j, total):
                to = pl.ds(pl.multiple_of(j * ABLK, ABLK), ABLK)
                e = jnp.exp(s_s[to, :] - peak)
                s_s[to, :] = e
                return total + jnp.sum(e, axis=0, keepdims=True)

            total = lax.fori_loop(0, i + 1, raise_, jnp.zeros((1, ABLK), F32))
            scale = 1.0 / total

            def weigh(j, o):
                to = pl.ds(pl.multiple_of(j * ABLK, ABLK), ABLK)
                probs = (s_s[to, :] * scale).astype(BF)
                return o + mm(vt_s[p, :, to], probs)

            o = lax.fori_loop(0, i + 1, weigh, jnp.zeros((HD, ABLK), F32))
            attended_t[p, :, at] = o
            logsum[p, :, at] = peak + jnp.log(total)
            o = o.T.astype(BF)
            for h in range(per_block):
                to = pl.ds(pl.multiple_of(order[per_block * i + h] * piece, piece), piece)
                out[to, p * HD : (p + 1) * HD] = o[h * piece : (h + 1) * piece, :]
            return 0

        lax.fori_loop(0, blocks, one, 0)


def attend(order, rows, pairs, piece):
    length = rows.shape[0]
    return pl.pallas_call(
        functools.partial(attend_kernel, pairs, piece),
        out_shape=(
            jax.ShapeDtypeStruct((length, pairs * HD), BF),
            jax.ShapeDtypeStruct((pairs, HD, length), F32),
            jax.ShapeDtypeStruct((pairs, 1, length), F32),
        ),
        in_specs=[smem(), vmem()],
        out_specs=(vmem(),) * 3,
        scratch_shapes=[
            pltpu.VMEM((pairs, length, HD), BF),
            pltpu.VMEM((pairs, length, HD), BF),
            pltpu.VMEM((pairs, HD, length), BF),
            pltpu.VMEM((length, ABLK), F32),
        ],
        compiler_params=params(48),
        cost_estimate=cost(50),
        name="attend",
    )(order, rows)


def attend_grad_kernel(
    pairs,
    piece,
    order,
    rows,
    grads,
    attended_t,
    logsum,
    cos,
    sin,
    cos_t,
    sin_t,
    out,
    q_s,
    k_s,
    v_s,
    g_s,
    kt_s,
    dq_s,
    dk_s,
    dv_s,
    dk_o,
    dv_o,
):
    length = rows.shape[0]
    blocks = length // ABLK
    width = pairs * HD
    half = HD // 2
    scale = HD ** (-0.5)
    identity = eye(HD)

    for p in range(pairs):

        def sort(j, _):
            take = pl.ds(pl.multiple_of(order[j] * piece, piece), piece)
            block = rows[take, :]
            to = pl.ds(pl.multiple_of(j * piece, piece), piece)
            q_s[to, :] = (block[:, p * HD : (p + 1) * HD].astype(F32) * scale).astype(BF)
            k = block[:, width + p * HD : width + (p + 1) * HD]
            k_s[to, :] = k
            kt_s[:, to] = mm(identity, k, NT).astype(BF)
            v_s[to, :] = block[:, 2 * width + p * HD : 2 * width + (p + 1) * HD]
            g_s[to, :] = grads[take, :][:, p * HD : (p + 1) * HD]
            return 0

        lax.fori_loop(0, length // piece, sort, 0)
        dk_s[...] = jnp.zeros_like(dk_s)
        dv_s[...] = jnp.zeros_like(dv_s)

        def one(i, _):
            at = pl.ds(pl.multiple_of(i * ABLK, ABLK), ABLK)
            queries = q_s[at, :]
            grad = g_s[at, :]
            delta = jnp.sum(
                mm(identity, grad, NT) * attended_t[p, :, at], axis=0, keepdims=True
            )
            level = logsum[p, :, at]

            def tile(j, dq):
                to = pl.ds(pl.multiple_of(j * ABLK, ABLK), ABLK)
                probs = jnp.exp(mm(k_s[to, :], queries, NT) - level)
                ds = (probs * (mm(v_s[to, :], grad, NT) - delta)).astype(BF)
                dv_s[to, :] += mm(probs.astype(BF), grad)
                dk_s[to, :] += mm(ds, queries)
                return dq + mm(kt_s[:, to], ds)

            dq = lax.fori_loop(0, i + 1, tile, jnp.zeros((HD, ABLK), F32)) * scale
            c, s = cos_t[:, at], sin_t[:, at]
            a, b = dq[:half, :], dq[half:, :]
            dq = jnp.concatenate([a * c + b * s, b * c - a * s], axis=0)
            dq_s[p, at, :] = dq.T.astype(BF)
            return 0

        lax.fori_loop(0, blocks, one, 0)

        def turn(j, _):
            to = pl.ds(pl.multiple_of(j * ABLK, ABLK), ABLK)
            dk = dk_s[to, :]
            a, b = dk[:, :half], dk[:, half:]
            c, s = cos[to, :], sin[to, :]
            dk_o[p, to, :] = jnp.concatenate([a * c + b * s, b * c - a * s], axis=1).astype(BF)
            dv_o[p, to, :] = dv_s[to, :].astype(BF)
            return 0

        lax.fori_loop(0, blocks, turn, 0)

    def unsort(j, _):
        take = pl.ds(pl.multiple_of(j * piece, piece), piece)
        to = pl.ds(pl.multiple_of(order[j] * piece, piece), piece)
        parts = [ref[p, take, :] for ref in (dq_s, dk_o, dv_o) for p in range(pairs)]
        out[to, :] = jnp.concatenate(parts, axis=1)
        return 0

    lax.fori_loop(0, length // piece, unsort, 0)


def attend_grad(order, rows, grads, attended_t, logsum, cos, sin, cos_t, sin_t, pairs, piece):
    length = rows.shape[0]
    low = pltpu.VMEM((length, HD), BF)
    full = pltpu.VMEM((length, HD), F32)
    each = pltpu.VMEM((pairs, length, HD), BF)
    return pl.pallas_call(
        functools.partial(attend_grad_kernel, pairs, piece),
        out_shape=jax.ShapeDtypeStruct((length, 3 * pairs * HD), BF),
        in_specs=[smem()] + [vmem()] * 8,
        out_specs=vmem(),
        scratch_shapes=[low] * 4 + [pltpu.VMEM((HD, length), BF), each, full, full, each, each],
        compiler_params=params(56),
        cost_estimate=cost(68),
        name="attend_grad",
    )(order, rows, grads, attended_t, logsum, cos, sin, cos_t, sin_t)


def fold_max(peak, tile):
    return jnp.maximum(peak, jnp.max(tile.reshape(-1, 8, tile.shape[1]), axis=0))


def fold_sum(total, tile):
    return total + jnp.sum(tile.reshape(-1, 8, tile.shape[1]), axis=0)


def swap(value):
    return mm(eye(value.shape[1]), value, NT).astype(BF)


def piece_of(order, j, piece):
    at = order[j]
    return at // 2, pl.ds(pl.multiple_of(lax.rem(at, 2) * piece, piece), piece)


def attend_short_kernel(pairs, piece, order, rows, out, attended_t, logsum, q_s, k_s, v_s, s_s):
    length = rows.shape[0] * rows.shape[2]
    blocks = length // ABLK
    width = pairs * HD

    def sort(j, _):
        device, lanes = piece_of(order, j, piece)
        block = rows[device, :, lanes]
        to = pl.ds(pl.multiple_of(j * piece, piece), piece)
        for p in range(pairs):
            q = block[p * HD : (p + 1) * HD, :]
            q_s[p, :, to] = (q.astype(F32) * HD ** (-0.5)).astype(BF)
            k_s[p, to, :] = swap(block[width + p * HD : width + (p + 1) * HD, :])
            v_s[p, :, to] = block[2 * width + p * HD : 2 * width + (p + 1) * HD, :]
        return 0

    lax.fori_loop(0, length // piece, sort, 0)

    def pair(p, _):
        features = pl.ds(pl.multiple_of(p * HD, HD), HD)
        for i in range(blocks):
            at = slice(i * ABLK, (i + 1) * ABLK)
            queries = q_s[p, :, at]
            peak = jnp.full((8, ABLK), -jnp.inf, F32)
            for j in range(i + 1):
                s = mm(k_s[p, j * ABLK : (j + 1) * ABLK, :], queries)
                s_s[i % 2, j * ABLK : (j + 1) * ABLK, :] = s
                peak = fold_max(peak, s)
            peak = jnp.max(peak, axis=0, keepdims=True)
            total = jnp.zeros((8, ABLK), F32)
            o = jnp.zeros((HD, ABLK), F32)
            for j in range(i + 1):
                e = jnp.exp(s_s[i % 2, j * ABLK : (j + 1) * ABLK, :] - peak)
                total = fold_sum(total, e)
                o += mm(v_s[p, :, j * ABLK : (j + 1) * ABLK], e.astype(BF))
            total = jnp.sum(total, axis=0, keepdims=True)
            o = o * (1.0 / total)
            attended_t[p, :, at] = o
            logsum[p, :, at] = peak + jnp.log(total)
            o = o.astype(BF)
            for h in range(ABLK // piece):
                device, lanes = piece_of(order, ABLK // piece * i + h, piece)
                out[device, features, lanes] = o[:, h * piece : (h + 1) * piece]
        return 0

    lax.fori_loop(0, pairs, pair, 0)


def attend_short(order, rows, pairs, piece):
    contexts, _, tokens = rows.shape
    length = contexts * tokens
    return pl.pallas_call(
        functools.partial(attend_short_kernel, pairs, piece),
        out_shape=(
            jax.ShapeDtypeStruct((contexts, pairs * HD, tokens), BF),
            jax.ShapeDtypeStruct((pairs, HD, length), F32),
            jax.ShapeDtypeStruct((pairs, 1, length), F32),
        ),
        in_specs=[smem(), vmem()],
        out_specs=(vmem(),) * 3,
        scratch_shapes=[
            pltpu.VMEM((pairs, HD, length), BF),
            pltpu.VMEM((pairs, length, HD), BF),
            pltpu.VMEM((pairs, HD, length), BF),
            pltpu.VMEM((2, length, ABLK), F32),
        ],
        compiler_params=params(48),
        cost_estimate=cost(25),
        name="attend",
    )(order, rows)


def attend_grad_short_kernel(
    pairs,
    begin,
    count,
    piece,
    order,
    rows,
    grads,
    attended_t,
    logsum,
    cos_t,
    sin_t,
    out,
    q_s,
    g_s,
    kt_s,
    k_s,
    v_s,
    dk_s,
    dv_s,
):
    length = rows.shape[0] * rows.shape[2]
    blocks = length // ABLK
    width = pairs * HD
    half = HD // 2
    scale = HD ** (-0.5)

    def sort(j, _):
        device, lanes = piece_of(order, j, piece)
        block = rows[device, :, lanes]
        grad = grads[device, :, lanes]
        to = pl.ds(pl.multiple_of(j * piece, piece), piece)
        for p in range(count):
            row = (begin + p) * HD
            q_s[p, :, to] = (block[row : row + HD, :].astype(F32) * scale).astype(BF)
            k = block[width + row : width + row + HD, :]
            kt_s[p, :, to] = k
            k_s[p, to, :] = swap(k)
            v_s[p, to, :] = swap(block[2 * width + row : 2 * width + row + HD, :])
            g_s[p, :, to] = grad[row : row + HD, :]
        return 0

    lax.fori_loop(0, length // piece, sort, 0)

    def turn(x, at):
        c, s = cos_t[:, at], sin_t[:, at]
        a, b = x[:half, :], x[half:, :]
        return jnp.concatenate([a * c + b * s, b * c - a * s], axis=0)

    def pair(p, _):
        def put(kind, i, value):
            features = pl.ds(pl.multiple_of((kind * count + p) * HD, HD), HD)
            value = value.astype(BF)
            for h in range(ABLK // piece):
                device, lanes = piece_of(order, ABLK // piece * i + h, piece)
                out[device, features, lanes] = value[:, h * piece : (h + 1) * piece]

        for i in range(blocks):
            at = slice(i * ABLK, (i + 1) * ABLK)
            queries = q_s[p, :, at]
            grad = g_s[p, :, at]
            delta = jnp.sum(
                grad.astype(F32) * attended_t[begin + p, :, at], axis=0, keepdims=True
            )
            level = logsum[begin + p, :, at]
            dq = jnp.zeros((HD, ABLK), F32)
            for j in range(i, -1, -1):
                to = slice(j * ABLK, (j + 1) * ABLK)
                probs = jnp.exp(mm(k_s[p, to, :], queries) - level)
                ds = (probs * (mm(v_s[p, to, :], grad) - delta)).astype(BF)
                dv = mm(grad, probs.astype(BF), NT)
                dk = mm(queries, ds, NT)
                if i == j:
                    dv_s[:, to] = dv
                    dk_s[:, to] = dk
                else:
                    dv_s[:, to] += dv
                    dk_s[:, to] += dk
                dq += mm(kt_s[p, :, to], ds)
            put(0, i, turn(dq * scale, at))
        for i in range(blocks):
            at = slice(i * ABLK, (i + 1) * ABLK)
            put(1, i, turn(dk_s[:, at], at))
            put(2, i, dv_s[:, at])
        return 0

    lax.fori_loop(0, count, pair, 0)


def attend_grad_short(
    order, rows, grads, attended_t, logsum, cos_t, sin_t, pairs, piece, begin, count
):
    contexts, _, tokens = rows.shape
    length = contexts * tokens
    wide_ = pltpu.VMEM((count, HD, length), BF)
    tall = pltpu.VMEM((count, length, HD), BF)
    full = pltpu.VMEM((HD, length), F32)
    return pl.pallas_call(
        functools.partial(attend_grad_short_kernel, pairs, begin, count, piece),
        out_shape=jax.ShapeDtypeStruct((contexts, 3 * count * HD, tokens), BF),
        in_specs=[smem()] + [vmem()] * 6,
        out_specs=vmem(),
        scratch_shapes=[wide_] * 3 + [tall] * 2 + [full] * 2,
        compiler_params=params(48),
        cost_estimate=cost(14 * count),
        name=f"attend_grad_{begin}",
    )(order, rows, grads, attended_t, logsum, cos_t, sin_t)


def over_ctx(value, mask):
    size = lax.axis_size("ctx")
    return lax.ppermute(value, "ctx", [(i, i ^ mask) for i in range(size)])


def along_fsdp(value, shift):
    size = lax.axis_size("fsdp")
    return lax.ppermute(value, "fsdp", [(i, (i + shift) % size) for i in range(size)])


def by_index(blocks, index):
    if len(blocks) == 1:
        return blocks
    half = len(blocks) // 2
    flip = (index // half) % 2 == 1
    lower = [jnp.where(flip, b, a) for a, b in zip(blocks[:half], blocks[half:])]
    upper = [jnp.where(flip, a, b) for a, b in zip(blocks[:half], blocks[half:])]
    return by_index(lower, index) + by_index(upper, index)


def place():
    ctx = lax.axis_index("ctx")
    return ctx % 2, ctx // 2, lax.axis_index("fsdp")


def gather_weight(shard):
    core, chip, z = place()
    chips = lax.axis_size("ctx") // 2
    shards = lax.axis_size("fsdp")
    rows, columns = shard.shape
    r, half = rows // chips, columns // 2
    mine = lax.dynamic_slice(shard, (chip * r, core * half), (r, half))
    along = [mine] + [along_fsdp(mine, k) for k in range(1, shards)]
    turned = jnp.stack([along[(shards - m) % shards] for m in range(shards)])
    column = lax.dynamic_slice_in_dim(
        jnp.concatenate([turned, turned]), (shards - z) % shards, shards
    )
    blocks = [column] + [over_ctx(column, 2 * k) for k in range(1, chips)]
    own = jnp.stack(by_index(blocks, chip), axis=1).reshape(shards * rows, half)
    other = over_ctx(own, 1)
    return jnp.where(
        core == 0, jnp.concatenate([own, other], axis=1), jnp.concatenate([other, own], axis=1)
    )


def gather_gains(gains):
    _, _, z = place()
    shards = lax.axis_size("fsdp")
    along = [gains] + [along_fsdp(gains, k) for k in range(1, shards)]
    turned = jnp.stack([along[(shards - m) % shards] for m in range(shards)])
    every = lax.dynamic_slice_in_dim(
        jnp.concatenate([turned, turned]), (shards - z) % shards, shards
    )
    return jnp.moveaxis(every, 0, 1).reshape(gains.shape[0], -1)


def reduce_grad(grad):
    core, chip, z = place()
    chips = lax.axis_size("ctx") // 2
    shards = lax.axis_size("fsdp")
    rows, columns = grad.shape[0] // shards, grad.shape[1]
    r, half = rows // chips, columns // 2
    view = grad.reshape(shards, chips, r, columns)

    def columns_of(which):
        return lax.dynamic_slice_in_dim(view, which * half, half, axis=3)

    total = columns_of(core).astype(F32) + over_ctx(columns_of(1 - core), 1).astype(F32)
    low = total.astype(BF)
    sent = [
        over_ctx(lax.dynamic_index_in_dim(low, chip ^ k, 1, keepdims=False), 2 * k)
        for k in range(1, chips)
    ]
    total = lax.dynamic_index_in_dim(low, chip, 1, keepdims=False).astype(F32)
    total = sum((s.astype(F32) for s in sent), total)
    low = total.astype(BF)
    sent = [
        along_fsdp(lax.dynamic_index_in_dim(low, (z + k) % shards, 0, keepdims=False), k)
        for k in range(1, shards)
    ]
    total = lax.dynamic_index_in_dim(low, z, 0, keepdims=False).astype(F32)
    total = sum((s.astype(F32) for s in sent), total)
    piece = total.astype(BF)
    blocks = [piece] + [over_ctx(piece, 2 * k) for k in range(1, chips)]
    own = jnp.stack(by_index(blocks, chip)).reshape(rows, half)
    other = over_ctx(own, 1)
    return jnp.where(
        core == 0, jnp.concatenate([own, other], axis=1), jnp.concatenate([other, own], axis=1)
    ).astype(F32)


def by_head(values, devices, pairs):
    batches, tokens, kinds, _ = values.shape
    groups = HEADS // pairs
    values = values.reshape(batches, tokens, kinds, groups, pairs * HD)
    values = values.transpose(0, 3, 1, 2, 4).reshape(batches * groups, tokens, kinds * pairs * HD)
    spare = devices - batches * groups
    return jnp.pad(values, ((0, spare), (0, 0), (0, 0)))


def by_token(values, batches, kinds, pairs):
    groups = HEADS // pairs
    tokens = values.shape[1]
    values = values[: batches * groups].reshape(batches, groups, tokens, kinds, pairs * HD)
    return values.transpose(0, 2, 3, 1, 4).reshape(batches, tokens, kinds, HEADS * HD)


def exchange(values, axes):
    return lax.all_to_all(values, axes, split_axis=0, concat_axis=0, tiled=True)


def aligned(value, by=16):
    return pl.multiple_of(value, by)


def pack_weights_kernel(where, joined, output, lookup, gains, expand, contract, first, second):
    core, chip = where[0], where[1]
    rows = pl.ds(aligned(chip * 48), 48)
    for t in range(3):
        first[t * 48 : (t + 1) * 48, :] = joined[rows, pl.ds(aligned(t * D + core * 384, 128), 384)]
    columns = pl.ds(aligned(core * 384, 128), 384)
    first[144:192, :] = lookup[:, columns]
    first[192:208, :] = gains[...]
    for j in range(16):
        second[j * 48 : (j + 1) * 48, :] = expand[
            rows, pl.ds(aligned(core * FF + j * 128, 128), 128)
        ]
    for j in range(3):
        second[768 + j * 128 : 896 + j * 128, :] = contract[
            pl.ds(aligned(chip * 128), 128), pl.ds(aligned(core * 384 + j * 128, 128), 128)
        ]
        second[1152 + j * 48 : 1200 + j * 48, :] = output[
            rows, pl.ds(aligned(core * 384 + j * 128, 128), 128)
        ]


def pack_weights(where, *weights):
    return pl.pallas_call(
        pack_weights_kernel,
        out_shape=(
            jax.ShapeDtypeStruct((208, 384), BF),
            jax.ShapeDtypeStruct((1296, 128), BF),
        ),
        in_specs=[smem()] + [vmem()] * 6,
        out_specs=(vmem(),) * 2,
        compiler_params=params(16),
        cost_estimate=cost(2),
        name="pack_weights",
    )(where, *weights)


CUT = 14 * 48


def by_chip(near_x, near_y, far_y, far_x):
    return (
        [near_x.at[0], near_x.at[1], far_y.at[0], far_y.at[1]],
        [near_y.at[0], far_x.at[0], near_y.at[1], far_x.at[1]],
    )


def spread_fsdp(piece):
    along = [piece] + [along_fsdp(piece, k) for k in range(1, 4)]
    return [along[(4 - m) % 4] for m in range(4)]


def add_cores(own, came):
    return [(own[k].astype(F32) + came[k].astype(F32)).astype(BF) for k in range(4)]


def add_blocks(own, came):
    total = own.astype(F32)
    for block in came:
        total = total + block.astype(F32)
    return total.astype(BF)


def to_chips(blocks):
    return [over_ctx(blocks[k], 2 * k) for k in range(1, 4)]


def add_all(*blocks):
    return sum((b.astype(F32) for b in blocks[1:]), blocks[0].astype(F32))


def over_fsdp(value, mask):
    return lax.ppermute(value, "fsdp", [(i, i ^ mask) for i in range(4)])


def unpack_second_kernel(where, own, other, expand, contract, output):
    core, chip = where[0], where[1]
    for k in range(4):
        yx = chip ^ k
        rows = pl.ds(aligned(yx * 48), 48)
        for half in range(2):

            def taken(begin, count):
                part = slice(begin, begin + count)
                return jnp.where(core == half, own[k, part, :].astype(F32), other[k, part, :].astype(F32))

            for j in range(16):
                expand[rows, half * FF + j * 128 : half * FF + (j + 1) * 128] = taken(j * 48, 48)
            for j in range(3):
                to = slice(half * 384 + j * 128, half * 384 + (j + 1) * 128)
                contract[pl.ds(aligned(yx * 128), 128), to] = taken(768 + j * 128, 128)
                output[rows, to] = taken(1152 + j * 48, 48)


def unpack_second(where, own, other):
    return pl.pallas_call(
        unpack_second_kernel,
        out_shape=(
            jax.ShapeDtypeStruct((192, 2 * FF), F32),
            jax.ShapeDtypeStruct((512, D), F32),
            jax.ShapeDtypeStruct((192, D), F32),
        ),
        in_specs=[smem()] + [vmem()] * 2,
        out_specs=(vmem(),) * 3,
        compiler_params=params(24),
        cost_estimate=cost(4),
        name="unpack_second",
    )(where, own, other)


def unpack_first_kernel(where, own, other, joined, lookup, gains):
    core, chip = where[0], where[1]
    for k in range(4):
        yx = chip ^ k
        rows = pl.ds(aligned(yx * 48), 48)
        for half in range(2):

            def taken(begin, count):
                part = slice(begin, begin + count)
                return jnp.where(core == half, own[k, part, :].astype(F32), other[k, part, :].astype(F32))

            for t in range(3):
                for j in range(3):
                    to = t * D + half * 384 + j * 128
                    joined[rows, to : to + 128] = taken((t * 3 + j) * 48, 48)

            @pl.when(yx < 3)
            def _():
                at = pl.ds(aligned(half * 384 + yx * 128, 128), 128)
                lookup[:, at] = taken(432, 48)

            @pl.when(yx == 3)
            def _():
                gains[half] = taken(432, 48)


def unpack_first(where, own, other):
    return pl.pallas_call(
        unpack_first_kernel,
        out_shape=(
            jax.ShapeDtypeStruct((192, 3 * D), F32),
            jax.ShapeDtypeStruct((48, D), F32),
            jax.ShapeDtypeStruct((2, 48, 128), F32),
        ),
        in_specs=[smem()] + [vmem()] * 2,
        out_specs=(vmem(),) * 3,
        compiler_params=params(24),
        cost_estimate=cost(2),
        name="unpack_first",
    )(where, own, other)


def unit_rows(x):
    inverse = lax.rsqrt(jnp.mean(x * x, axis=-1, keepdims=True) + epsilon)
    return x * inverse, inverse


def front_kernel(
    pairs,
    where,
    starts,
    got,
    target,
    token,
    cos_t,
    sin_t,
    *refs,
):
    own_tail, other_tail = refs[8:10]
    start, embed, hidden, send, joined, lookup, gains, t_s, g_s = refs[10:]
    core, chip, z = where[0], where[1], where[2]
    for blocks, tail, half in ((refs[:4], own_tail, core), (refs[4:8], other_tail, 1 - core)):
        upper, lower = by_chip(*blocks)
        for m in range(4):
            zz = lax.rem(z + m, 4)
            for k in range(4):
                begin = zz * 192 + (chip ^ k) * 48
                for t, source, first, last, at in (
                    (0, upper, 0, 48, 0),
                    (1, upper, 48, 80, 0),
                    (1, lower, 0, 16, 32),
                    (2, lower, 16, 64, 0),
                ):
                    joined[
                        pl.ds(aligned(begin + at), last - first),
                        pl.ds(aligned(t * D + half * 384, 128), 384),
                    ] = source[k][m, first:last, :]
            lookup[pl.ds(aligned(zz * 48), 48), pl.ds(aligned(half * 384, 128), 384)] = tail[
                m, 0:48, :
            ]
    for m in range(4):
        g_s[lax.rem(z + m, 4)] = own_tail[m, 48:64, :].astype(F32)
    for row in range(2):
        gains[row : row + 1, :] = jnp.concatenate(
            [g_s[zz, row : row + 1, :192] for zz in range(4)], axis=1
        )
    gain = gains[0:1, :]
    tokens = token.shape[0]
    piece = 128
    per_batch = tokens // 2 // piece
    groups = HEADS // pairs
    wide_ = pairs * HD
    slots = got.shape[0]
    lane = lax.broadcasted_iota(jnp.int32, (piece, 128), 1)
    first_half = lax.rem(lane, HD) < HD // 2

    def block(i, _):
        at = pl.ds(aligned(i * piece, piece), piece)
        goal = target[at, :]
        slot = lax.broadcasted_iota(jnp.int32, (piece, slots), 1)
        parts = []
        for table in range(2):
            hot = jnp.where(goal[:, table : table + 1] == slot, 1.0, 0.0).astype(BF)
            parts.append(mm(hot, got[:, table * E : (table + 1) * E]))
        rows = (parts[0] + parts[1]).astype(BF)
        embed[at, :] = rows
        x = token[at, :].astype(F32) + mm(rows, lookup[...])
        start[at, :] = x
        normed, _ = unit_rows(x)
        low = (normed * gain).astype(BF)
        hidden[at, :] = low
        projected = mm(low, joined[...])
        begin = pl.ds(aligned(starts[lax.rem(i, per_batch)] * piece, piece), piece)
        c = cos_t[:, begin].T
        s = sin_t[:, begin].T
        c = jnp.concatenate([c, c, c, c], axis=1)
        s = jnp.concatenate([-s, s, -s, s], axis=1)
        turned = []
        for j in range(12):
            v = projected[:, j * 128 : (j + 1) * 128]
            swapped = jnp.where(first_half, pltpu.roll(v, 96, 1), pltpu.roll(v, 32, 1))
            turned.append((v * c + swapped * s).astype(BF))
        for j in range(12, 18):
            turned.append(projected[:, j * 128 : (j + 1) * 128].astype(BF))
        for j, v in enumerate(turned):
            t_s[j * 128 : (j + 1) * 128, :] = swap(v)
        batch = i // per_batch
        to = pl.ds(aligned(lax.rem(i, per_batch) * piece, piece), piece)
        for g in range(groups):
            for t in range(3):
                begin = t * D + g * wide_
                send[batch * groups + g, t * wide_ : (t + 1) * wide_, to] = t_s[
                    begin : begin + wide_, :
                ]
        return 0

    lax.fori_loop(0, tokens // piece, block, 0)


def front(pairs, devices, where, starts, got, target, token, cos_t, sin_t, *blocks):
    tokens = token.shape[0]
    return pl.pallas_call(
        functools.partial(front_kernel, pairs),
        out_shape=(
            jax.ShapeDtypeStruct((tokens, D), F32),
            jax.ShapeDtypeStruct((tokens, E), BF),
            jax.ShapeDtypeStruct((tokens, D), BF),
            jax.ShapeDtypeStruct((devices, 3 * pairs * HD, tokens // 2), BF),
            jax.ShapeDtypeStruct((D, 3 * D), BF),
            jax.ShapeDtypeStruct((E, D), BF),
            jax.ShapeDtypeStruct((2, D), F32),
        ),
        in_specs=[smem()] * 2 + [vmem()] * 15,
        out_specs=(vmem(),) * 7,
        scratch_shapes=[pltpu.VMEM((3 * D, 128), BF), pltpu.VMEM((4, 16, 384), F32)],
        compiler_params=params(60),
        cost_estimate=cost(9),
        name="front",
    )(where, starts, got, target, token, cos_t, sin_t, *blocks)


def mlp_kernel(
    pairs,
    where,
    came,
    start,
    gains,
    upstream,
    *refs,
):
    blocks_own, blocks_other = refs[:4], refs[4:8]
    (
        result,
        hidden_out,
        attended_out,
        act_out,
        gate_out,
        up_out,
        gain_grad,
        middle_grad,
        send,
        hidden,
        total,
        back,
        output,
        pair_s,
        w_down,
    ) = refs[8:]
    step = pl.program_id(0)
    core, chip, z = where[0], where[1], where[2]
    gain = gains[1:2, :]
    sides = [
        by_chip(*blocks) + (half,)
        for blocks, half in ((blocks_own, core), (blocks_other, 1 - core))
    ]

    def fill(which, begin):
        for side in sides:
            for m in range(4):
                for k in range(4):
                    rows = pl.ds(aligned(lax.rem(z + m, 4) * 192 + (chip ^ k) * 48), 48)
                    for j in range(2):
                        take = pl.ds(aligned((2 * step + j) * 48 - begin), 48)
                        pair_s[side[2], rows, j * 128 : (j + 1) * 128] = side[which][k][m, take, :]

    @pl.when(step < 7)
    def _():
        fill(0, 0)

    @pl.when(step == 7)
    def _():
        fill(1, CUT)

    m = lax.rem(step // 2 - z + 4, 4)
    for k in range(4):
        yx = chip ^ k

        @pl.when(yx // 2 == lax.rem(step, 2))
        def _():
            rows = pl.ds(aligned(lax.rem(yx, 2) * 128), 128)
            for _, lower, half in sides:
                for j in range(3):
                    begin = 768 + j * 128 - CUT
                    w_down[rows, pl.ds(aligned(half * 384 + j * 128, 128), 128)] = lower[k][
                        m, begin : begin + 128, :
                    ]

    groups = HEADS // pairs
    wide_ = pairs * HD
    half = came.shape[2]

    @pl.when(step == 0)
    def _():
        for _, lower, side in sides:
            for m in range(4):
                for k in range(4):
                    rows = pl.ds(aligned(lax.rem(z + m, 4) * 192 + (chip ^ k) * 48), 48)
                    for j in range(3):
                        begin = 1152 + j * 48 - CUT
                        output[rows, pl.ds(aligned(side * 384 + j * 128, 128), 128)] = lower[k][
                            m, begin : begin + 48, :
                        ]
        for batch in range(2):
            at = slice(batch * half, (batch + 1) * half)
            parts = []
            for h in range(half // 128):
                lanes = slice(h * 128, (h + 1) * 128)
                parts.append(
                    jnp.concatenate(
                        [swap(came[batch * groups + g, :, lanes]) for g in range(groups)], axis=1
                    )
                )
            rows = jnp.concatenate(parts, axis=0)
            attended_out[at, :] = rows
            x = start[at, :] + mm(rows, output[...])
            total[at, :] = x
            middle_grad[at, :] = x
            normed, _ = unit_rows(x)
            low = (normed * gain).astype(BF)
            hidden[at, :] = low
            hidden_out[at, :] = low
        back[...] = jnp.zeros_like(back)

    for batch in range(2):
        at = slice(batch * half, (batch + 1) * half)
        gate = mm(hidden[at, :], pair_s[0])
        up = mm(hidden[at, :], pair_s[1])
        sigmoid = jax.nn.sigmoid(gate)
        swish = gate * sigmoid
        act = (swish * up).astype(BF)
        act_out[at, :] = act
        total[at, :] += mm(act, w_down[...])
        grad = mm(upstream[at, :], w_down[...], NT)
        gate_grad = (grad * up * sigmoid * (1.0 + gate * (1.0 - sigmoid))).astype(BF)
        up_grad = (grad * swish).astype(BF)
        gate_out[at, :] = gate_grad
        up_out[at, :] = up_grad
        back[at, :] += mm(gate_grad, pair_s[0], NT) + mm(up_grad, pair_s[1], NT)

    @pl.when(step == pl.num_programs(0) - 1)
    def _():
        gains = jnp.zeros((1, D), F32)
        for batch in range(2):
            at = slice(batch * half, (batch + 1) * half)
            result[at, :] = total[at, :].astype(BF)
            normed, inverse = unit_rows(middle_grad[at, :])
            grad = back[at, :]
            gains += jnp.sum(grad * normed, axis=0, keepdims=True)
            weighted = grad * gain
            grad = upstream[at, :].astype(F32) + inverse * (
                weighted - normed * jnp.mean(weighted * normed, axis=-1, keepdims=True)
            )
            middle_grad[at, :] = grad
            heads = mm(output[...], grad.astype(BF), NT).astype(BF)
            for g in range(groups):
                send[batch * groups + g] = heads[g * wide_ : (g + 1) * wide_, :]
        gain_grad[...] = gains


def mlp(pairs, where, came, start, gains, upstream, *blocks):
    tokens = start.shape[0]
    width = 256
    steps = FF // width
    whole = lambda shape: pl.BlockSpec(
        shape, lambda i: (0,) * len(shape), pipeline_mode=pl.Buffered(1)
    )
    column = pl.BlockSpec((tokens, width), lambda i: (0, i))
    return pl.pallas_call(
        functools.partial(mlp_kernel, pairs),
        grid=(steps,),
        out_shape=(
            jax.ShapeDtypeStruct((tokens, D), BF),
            jax.ShapeDtypeStruct((tokens, D), BF),
            jax.ShapeDtypeStruct((tokens, D), BF),
            jax.ShapeDtypeStruct((tokens, FF), BF),
            jax.ShapeDtypeStruct((tokens, FF), BF),
            jax.ShapeDtypeStruct((tokens, FF), BF),
            jax.ShapeDtypeStruct((1, D), F32),
            jax.ShapeDtypeStruct((tokens, D), F32),
            jax.ShapeDtypeStruct(came.shape, BF),
        ),
        in_specs=[smem()] + [whole(x.shape) for x in (came, start, gains, upstream, *blocks)],
        out_specs=(
            whole((tokens, D)),
            whole((tokens, D)),
            whole((tokens, D)),
            column,
            column,
            column,
            whole((1, D)),
            whole((tokens, D)),
            whole(came.shape),
        ),
        scratch_shapes=[
            pltpu.VMEM((tokens, D), BF),
            pltpu.VMEM((tokens, D), F32),
            pltpu.VMEM((tokens, D), F32),
            pltpu.VMEM((D, D), BF),
            pltpu.VMEM((2, D, width), BF),
            pltpu.VMEM((width, D), BF),
        ],
        compiler_params=params(40),
        cost_estimate=cost(23),
        name="mlp",
    )(where, came, start, gains, upstream, *blocks)


UPPER, LOWER, ALONG = (1, 3, 2, 0), (2, 3, 1, 0), (1, 3, 2, 0)


def placed(order, value):
    at = jnp.int32(3)
    for place_, here in enumerate(order[:3]):
        at = jnp.where(value == here, place_, at)
    return at


def weight_grads_kernel(
    where,
    hidden,
    gate,
    up,
    act,
    upstream,
    attended,
    middle,
    own_u,
    own_l,
    other_u,
    other_l,
    wide_s,
    tall_s,
    out_s,
):
    core, chip, z = where[0], where[1], where[2]
    sides = ((own_u, own_l, core), (other_u, other_l, 1 - core))

    def rows_of(k, m):
        return pl.ds(aligned((z ^ m) * 192 + (chip ^ k) * 48), 48)

    def chunk(c, _):
        at = pl.ds(aligned(c * 256, 256), 256)
        wide_s[0] = mm(hidden[...], gate[:, at], TN).astype(BF)
        wide_s[1] = mm(hidden[...], up[:, at], TN).astype(BF)
        tall = mm(act[:, at], upstream[...], TN).astype(BF)
        tall_s[0] = tall[:, :384]
        tall_s[1] = tall[:, 384:]

        def put(which, ks, begin):
            for side in sides:
                for i, m in enumerate(ALONG):
                    for n, k in enumerate(ks):
                        block = wide_s[side[2], rows_of(k, m), :]
                        for j in range(2):
                            to = pl.ds(aligned((2 * c + j) * 48 - begin), 48)
                            side[which][n, i, to, :] = block[:, j * 128 : (j + 1) * 128]

        @pl.when(c < 7)
        def _():
            put(0, UPPER, 0)

        @pl.when(c == 7)
        def _():
            put(1, LOWER, CUT)

        i = placed(ALONG, (c // 2) ^ z)
        for _, lower, half in sides:
            for b in range(2):
                n = placed(LOWER, (lax.rem(c, 2) * 2 + b) ^ chip)
                block = tall_s[half, b * 128 : (b + 1) * 128, :]
                for j in range(3):
                    begin = 768 + j * 128 - CUT
                    lower[n, i, begin : begin + 128, :] = block[:, j * 128 : (j + 1) * 128]
        return 0

    lax.fori_loop(0, FF // 256, chunk, 0)
    square = mm(attended[...], middle[...].astype(BF), TN).astype(BF)
    out_s[0] = square[:, :384]
    out_s[1] = square[:, 384:]
    for _, lower, half in sides:
        for i, m in enumerate(ALONG):
            for n, k in enumerate(LOWER):
                block = out_s[half, rows_of(k, m), :]
                for j in range(3):
                    begin = 1152 + j * 48 - CUT
                    lower[n, i, begin : begin + 48, :] = block[:, j * 128 : (j + 1) * 128]


def weight_grads(where, *operands):
    upper = jax.ShapeDtypeStruct((4, 4, CUT, 128), BF)
    lower = jax.ShapeDtypeStruct((4, 4, 1296 - CUT, 128), BF)
    return pl.pallas_call(
        weight_grads_kernel,
        out_shape=(upper, lower) * 2,
        in_specs=[smem()] + [vmem()] * 7,
        out_specs=(vmem(),) * 4,
        scratch_shapes=[
            pltpu.VMEM((2, D, 256), BF),
            pltpu.VMEM((2, 256, 384), BF),
            pltpu.VMEM((2, D, 384), BF),
        ],
        compiler_params=params(60),
        cost_estimate=cost(15),
        name="weight_grads",
    )(where, *operands)


def back_kernel(
    where,
    came_a,
    came_b,
    hidden,
    start,
    middle,
    joined,
    lookup,
    gain,
    second_gain,
    embed,
    target,
    token_grad,
    send,
    own,
    other,
    df_s,
    half_s,
    look_s,
    gain_s,
):
    core, chip, z = where[0], where[1], where[2]
    widths = [ref.shape[1] // 3 for ref in (came_a, came_b)]
    groups = D // sum(widths)
    rows = came_a.shape[2]
    tokens = 2 * rows
    for i in range(tokens // 128):
        batch, lanes = divmod(i * 128, rows)
        lanes = slice(lanes, lanes + 128)
        parts = [
            (swap(ref[batch * groups + g, :, lanes]), w)
            for g in range(groups)
            for ref, w in zip((came_a, came_b), widths)
        ]
        for t in range(3):
            df_s[i * 128 : (i + 1) * 128, t * D : (t + 1) * D] = jnp.concatenate(
                [part[:, t * w : (t + 1) * w] for part, w in parts], axis=1
            )

    def kind(t, _):
        grad = mm(hidden[...], df_s[:, pl.ds(aligned(t * D, 128), D)], TN).astype(BF)
        half_s[0] = grad[:, :384]
        half_s[1] = grad[:, 384:]
        for out, half in ((own, core), (other, 1 - core)):
            for m in range(4):
                zz = z ^ m
                for k in range(4):
                    block = half_s[half, pl.ds(aligned(zz * 192 + (chip ^ k) * 48), 48), :]
                    for j in range(3):
                        to = pl.ds(aligned((t * 3 + j) * 48), 48)
                        out[k, m, to, :] = block[:, j * 128 : (j + 1) * 128]
        return 0

    lax.fori_loop(0, 3, kind, 0)

    gains = jnp.zeros((1, D), F32)
    lows = []
    for batch in range(2):
        at = slice(batch * rows, (batch + 1) * rows)
        grad = mm(df_s[at, :], joined[...], NT)
        normed, inverse = unit_rows(start[at, :])
        gains += jnp.sum(grad * normed, axis=0, keepdims=True)
        weighted = grad * gain[0:1, :]
        grad = middle[at, :] + inverse * (
            weighted - normed * jnp.mean(weighted * normed, axis=-1, keepdims=True)
        )
        token_grad[at, :] = grad
        lows.append(grad.astype(BF))
    low = jnp.concatenate(lows, axis=0)
    look = mm(embed[...], low, TN).astype(BF)
    for half in range(2):
        for j in range(3):
            begin = half * 384 + j * 128
            look_s[half, j] = look[:, begin : begin + 128]
    for half, row in enumerate((gains, second_gain[...])):
        parts = [row[:, j * 128 : (j + 1) * 128] for j in range(6)]
        gain_s[half] = jnp.concatenate(parts + [jnp.zeros((42, 128), F32)], axis=0).astype(BF)
    for out, half in ((own, core), (other, 1 - core)):
        for m in range(4):
            zz = z ^ m
            for k in range(4):
                yx = chip ^ k

                @pl.when(yx < 3)
                def _():
                    out[k, m, 432:480, :] = look_s[
                        half, lax.rem(yx, 3), pl.ds(aligned(zz * 48), 48), :
                    ]

                @pl.when(yx == 3)
                def _():
                    out[k, m, 432:480, :] = gain_s[half]

    de = mm(low, lookup[...], NT).astype(BF)
    slots = send.shape[0]
    slot = lax.broadcasted_iota(jnp.int32, (slots, tokens), 0)
    parts = []
    for table in range(2):
        hot = jnp.where(slot == target[table : table + 1, :], 1.0, 0.0).astype(BF)
        parts.append(mm(hot, de))
    send[...] = jnp.concatenate(parts, axis=1).astype(BF)


def back_pass(slots, where, *operands):
    tokens = operands[2].shape[0]
    shape = jax.ShapeDtypeStruct((4, 4, 480, 128), BF)
    return pl.pallas_call(
        back_kernel,
        out_shape=(
            jax.ShapeDtypeStruct((tokens, D), F32),
            jax.ShapeDtypeStruct((slots, 2 * E), BF),
            shape,
            shape,
        ),
        in_specs=[smem()] + [vmem()] * 11,
        out_specs=(vmem(),) * 4,
        scratch_shapes=[
            pltpu.VMEM((tokens, 3 * D), BF),
            pltpu.VMEM((2, D, 384), BF),
            pltpu.VMEM((2, 3, E, 128), BF),
            pltpu.VMEM((2, 48, 128), BF),
        ],
        compiler_params=params(48),
        cost_estimate=cost(13),
        name="back",
    )(where, *operands)


def rotate(values, cosines, sines):
    half = values.shape[-1] // 2
    a, b = values[..., :half], values[..., half:]
    c, s = cosines[:, None, :], sines[:, None, :]
    return jnp.concatenate([a * c - b * s, b * c + a * s], axis=-1)


def normalize(rows):
    inverse = lax.rsqrt(jnp.mean(rows * rows, axis=-1, keepdims=True) + epsilon)
    return rows * inverse, inverse


def norm_backward(hidden_grad, normed, inverse, gain):
    weighted = hidden_grad * gain
    return inverse * (weighted - normed * jnp.mean(weighted * normed, axis=-1, keepdims=True))


def local(
    token_embed,
    bigram_ids,
    trigram_ids,
    bigram_table,
    trigram_table,
    block_deal,
    lookup_weight,
    attention_gain,
    joined_weight,
    output_weight,
    feedforward_gain,
    expand_weight,
    contract_weight,
    cotangent,
):
    contexts = lax.axis_size("ctx")
    shards = lax.axis_size("fsdp")
    devices = contexts * shards
    batches, local_rows = token_embed.shape[:2]
    tokens = batches * local_rows
    length = local_rows * contexts
    capacity = max(2, 2 * tokens // devices)
    table_rows = bigram_table.shape[0]
    piece = local_rows // 2
    pieces = length // piece
    pairs = -(-batches * HEADS // contexts)
    while HEADS % pairs:
        pairs += 1
    both = ("ctx", "fsdp")

    ids = jnp.stack([bigram_ids.reshape(-1), trigram_ids.reshape(-1)])
    requests, target_row, target_col = placement(ids, table_rows, devices, capacity)
    asked = exchange(requests, both)
    codes = jnp.stack([asked[:, :capacity].reshape(-1), asked[:, capacity:].reshape(-1)], axis=1)
    got = exchange(
        read_rows(codes, bigram_table.T, trigram_table.T).reshape(devices, capacity, 2 * E), both
    ).reshape(devices * capacity, 2 * E)

    lookup = gather_weight(lookup_weight)
    joined = gather_weight(joined_weight)
    output = gather_weight(output_weight)
    gains = gather_gains(jnp.stack([attention_gain, feedforward_gain])).astype(F32)
    first_gain, second_gain = gains[0], gains[1]
    expand = gather_weight(expand_weight)
    contract = gather_weight(contract_weight)

    order = jnp.argmin(
        jnp.abs(block_deal[None, :] - jnp.arange(pieces, dtype=jnp.int32)[:, None]), axis=1
    ).astype(jnp.int32)
    frequency = jnp.exp(-math.log(10000.0) * (2.0 * jnp.arange(HD // 2, dtype=F32) / HD))
    slot = lax.axis_index("ctx") * local_rows + jnp.arange(local_rows, dtype=jnp.int32)
    position = block_deal[slot // piece] * piece + slot % piece
    angles = position.astype(F32)[:, None] * frequency[None, :]
    cosines, sines = jnp.cos(angles), jnp.sin(angles)
    all_angles = jnp.arange(length, dtype=F32)[:, None] * frequency[None, :]
    all_cosines, all_sines = jnp.cos(all_angles), jnp.sin(all_angles)

    slots = jnp.arange(devices * capacity, dtype=jnp.int32)
    hot_b = (target_col[:, 0:1] == slots[None, :]).astype(BF)
    hot_t = (target_col[:, 1:2] == slots[None, :]).astype(BF)
    embedded = (mm(hot_b, got[:, :E]) + mm(hot_t, got[:, E:])).astype(BF)
    start = token_embed.reshape(tokens, D).astype(F32) + mm(embedded, lookup)
    normed_first, inverse_first = normalize(start)
    hidden_first = (normed_first * first_gain).astype(BF)
    projected = mm(hidden_first, joined).reshape(batches, local_rows, 3, HEADS, HD)
    cos_b, sin_b = cosines[None, :, None, :], sines[None, :, None, :]
    turn = lambda x: jnp.concatenate(
        [
            x[..., : HD // 2] * cos_b - x[..., HD // 2 :] * sin_b,
            x[..., HD // 2 :] * cos_b + x[..., : HD // 2] * sin_b,
        ],
        axis=-1,
    )
    qkv = jnp.stack(
        [turn(projected[:, :, 0]), turn(projected[:, :, 1]), projected[:, :, 2]], axis=2
    ).astype(BF)
    qkv = qkv.reshape(batches, local_rows, 3, D)
    rows = exchange(by_head(qkv, contexts, pairs), "ctx").reshape(length, 3 * pairs * HD)
    attended_rows, attended_t, logsum = attend(order, rows, pairs, piece)
    attended = by_token(
        exchange(attended_rows.reshape(contexts, local_rows, pairs * HD), "ctx"), batches, 1, pairs
    ).reshape(tokens, D)
    middle = start + mm(attended, output)
    normed_second, inverse_second = normalize(middle)
    hidden_second = (normed_second * second_gain).astype(BF)
    gate_up = mm(hidden_second, expand)
    gate, up = gate_up[:, :FF], gate_up[:, FF:]
    sigmoid = jax.nn.sigmoid(gate)
    swish = gate * sigmoid
    activated = (swish * up).astype(BF)
    result = (middle + mm(activated, contract)).astype(BF)

    upstream = cotangent.reshape(tokens, D)
    activated_grad = mm(upstream, contract, NT)
    gate_up_grad = jnp.concatenate(
        [
            activated_grad * up * sigmoid * (1.0 + gate * (1.0 - sigmoid)),
            activated_grad * swish,
        ],
        axis=-1,
    ).astype(BF)
    hidden_second_grad = mm(gate_up_grad, expand, NT)
    second_gain_term = jnp.sum(hidden_second_grad * normed_second, axis=0)
    middle_grad = upstream.astype(F32) + norm_backward(
        hidden_second_grad, normed_second, inverse_second, second_gain
    )
    middle_low = middle_grad.astype(BF)
    attended_grad = mm(middle_low, output, NT).astype(BF)
    grad_rows = exchange(
        by_head(attended_grad.reshape(batches, local_rows, 1, D), contexts, pairs), "ctx"
    ).reshape(length, pairs * HD)
    contract_term = mm(activated, upstream, TN).astype(BF)
    expand_term = mm(hidden_second, gate_up_grad, TN).astype(BF)
    output_term = mm(attended, middle_low, TN).astype(BF)
    contract_grad = reduce_grad(contract_term)
    expand_grad = reduce_grad(expand_term)
    output_grad = reduce_grad(output_term)

    grad_rows = attend_grad(
        order,
        rows,
        grad_rows,
        attended_t,
        logsum,
        all_cosines,
        all_sines,
        all_cosines.T,
        all_sines.T,
        pairs,
        piece,
    )
    joined_local = by_token(
        exchange(grad_rows.reshape(contexts, local_rows, 3 * pairs * HD), "ctx"), batches, 3, pairs
    ).reshape(tokens, 3 * D)
    joined_grad = reduce_grad(mm(hidden_first, joined_local, TN).astype(BF))
    hidden_first_grad = mm(joined_local, joined, NT)
    first_gain_term = jnp.sum(hidden_first_grad * normed_first, axis=0)
    start_grad = middle_grad + norm_backward(
        hidden_first_grad, normed_first, inverse_first, first_gain
    )
    start_low = start_grad.astype(BF)
    lookup_grad = reduce_grad(mm(embedded, start_low, TN).astype(BF))
    embed_grad = mm(start_low, lookup, NT).astype(BF)
    give_b = (target_row[0:1, :] == slots[:, None]).astype(BF)
    give_t = (target_row[1:2, :] == slots[:, None]).astype(BF)
    send = jnp.concatenate([mm(give_b, embed_grad), mm(give_t, embed_grad)], axis=1).astype(BF)
    arrived = exchange(send.reshape(devices, capacity, 2 * E), both)
    bigram_grad, trigram_grad = add_rows(
        codes, arrived.reshape(devices * capacity, 2 * E), table_rows
    )
    gain_terms = lax.psum(jnp.stack([first_gain_term, second_gain_term]), both)
    gain_share = lax.dynamic_slice_in_dim(
        gain_terms, lax.axis_index("fsdp") * (D // shards), D // shards, axis=1
    )
    return (
        result.reshape(batches, local_rows, D),
        start_grad.reshape(batches, local_rows, D),
        bigram_grad.T,
        trigram_grad.T,
        lookup_grad,
        gain_share[0],
        joined_grad,
        output_grad,
        gain_share[1],
        expand_grad,
        contract_grad,
    )


def local_packed(
    token_embed,
    bigram_ids,
    trigram_ids,
    bigram_table,
    trigram_table,
    block_deal,
    lookup_weight,
    attention_gain,
    joined_weight,
    output_weight,
    feedforward_gain,
    expand_weight,
    contract_weight,
    cotangent,
):
    contexts = lax.axis_size("ctx")
    shards = lax.axis_size("fsdp")
    devices = contexts * shards
    batches, local_rows = token_embed.shape[:2]
    tokens = batches * local_rows
    length = local_rows * contexts
    capacity = max(2, 2 * tokens // devices)
    table_rows = bigram_table.shape[0]
    piece = local_rows // 2
    pieces = length // piece
    pairs = -(-batches * HEADS // contexts)
    while HEADS % pairs:
        pairs += 1
    both = ("ctx", "fsdp")


    core, chip, z = place()
    where = jnp.stack([core, chip, z]).astype(jnp.int32)
    ids = jnp.stack([bigram_ids.reshape(-1), trigram_ids.reshape(-1)])
    requests, target_row, target_col = placement(ids, table_rows, devices, capacity)
    asked = exchange(requests, both)
    gain_rows = jnp.pad(jnp.stack([attention_gain, feedforward_gain]), ((0, 14), (0, 192)))
    first, second = pack_weights(
        after(where, requests),
        joined_weight,
        output_weight,
        lookup_weight,
        gain_rows,
        expand_weight,
        contract_weight,
    )
    along = spread_fsdp(first)
    column = jnp.stack([p[:144] for p in along])
    tail = jnp.stack([p[144:] for p in along])
    upper, lower = column[:, :80], column[:, 80:]
    near = [over_ctx(upper, 2), over_ctx(lower, 4)]
    codes = jnp.stack([asked[:, :capacity].reshape(-1), asked[:, capacity:].reshape(-1)], axis=1)
    answer = read_rows(
        after(codes, column, tail), in_hbm(bigram_table.T), in_hbm(trigram_table.T)
    )
    ready = after(second, column)
    along = [along_fsdp(ready, k) for k in (1, 2, 3)]
    answer, near, along = lax.optimization_barrier((answer, near, along))
    got = exchange(answer.reshape(devices, capacity, 2 * E), both)
    first_near = [jnp.stack([upper, near[0]]), jnp.stack([lower, near[1]])]
    first_far = [over_ctx(first_near[0], 4), over_ctx(first_near[1], 2)]
    first_own = first_near + first_far
    first_other = [over_ctx(block, 1) for block in first_own]
    first_blocks = (*first_own, *first_other, tail, over_ctx(tail, 1))
    along = [second] + [after(along[k], first_far) for k in (2, 1, 0)]
    upper = jnp.stack([block[:CUT] for block in along])
    lower = jnp.stack([block[CUT:] for block in along])
    near = [over_ctx(upper, 2), over_ctx(lower, 4)]
    got = got.reshape(devices * capacity, 2 * E)

    order = jnp.sum(
        jnp.where(
            block_deal[None, :] == jnp.arange(pieces, dtype=jnp.int32)[:, None],
            jnp.arange(pieces, dtype=jnp.int32)[None, :],
            0,
        ),
        axis=1,
    )
    starts = lax.dynamic_slice_in_dim(block_deal, lax.axis_index("ctx") * 2, 2)
    frequency = jnp.exp(-math.log(10000.0) * (2.0 * jnp.arange(HD // 2, dtype=F32) / HD))
    angles = frequency[:, None] * jnp.arange(length, dtype=F32)[None, :]
    cos_t, sin_t = lax.optimization_barrier((jnp.cos(angles), jnp.sin(angles)))

    start, embedded, hidden_first, sent, joined, lookup, gains = front(
        pairs,
        contexts,
        where,
        starts,
        got,
        target_col,
        token_embed.reshape(tokens, D),
        cos_t,
        sin_t,
        *first_blocks,
    )
    sent, near = lax.optimization_barrier((sent, near))
    rows = exchange(sent, "ctx")
    near_x, near_y = jnp.stack([upper, near[0]]), jnp.stack([lower, near[1]])
    rows, near_x, near_y = lax.optimization_barrier((rows, near_x, near_y))
    far_y, far_x = over_ctx(near_x, 4), over_ctx(near_y, 2)
    others = [over_ctx(near_x, 1), over_ctx(near_y, 1)]
    attended_rows, attended_t, logsum = attend_short(order, rows, pairs, piece)
    came = exchange(attended_rows, "ctx")
    far_y, far_x = after((far_y, far_x), attended_rows)
    others += [over_ctx(far_y, 1), over_ctx(far_x, 1)]
    upstream = cotangent.reshape(tokens, D)
    (
        result,
        hidden_second,
        attended,
        activated,
        gate_grad,
        up_grad,
        second_gain_term,
        middle_grad,
        sent,
    ) = mlp(pairs, where, came, start, gains, upstream, near_x, near_y, far_y, far_x, *others)

    grad_rows = exchange(sent, "ctx")
    own_u, own_l, other_u, other_l = weight_grads(
        where, hidden_second, gate_grad, up_grad, activated, upstream, attended, middle_grad
    )
    other_u, other_l = after((other_u, other_l), grad_rows)
    core_u, core_l = over_ctx(other_u, 1), over_ctx(other_l, 1)
    part = functools.partial(attend_grad_short, order)
    shared = (attended_t, logsum, cos_t, sin_t, pairs, piece)
    grad_a = part(rows, grad_rows, *shared, 0, 1)
    came_a = exchange(grad_a, "ctx")
    core_u, core_l = after((core_u, core_l), grad_a)
    near_u = add_all(own_u[:2], core_u[:2]).astype(BF)
    near_l = add_all(own_l[:2], core_l[:2]).astype(BF)
    from_x, from_y = over_ctx(near_u, 2), over_ctx(near_l, 4)
    grad_b = part(after(rows, near_u, near_l), grad_rows, *shared, 1, pairs - 1)
    grad_b, came_a, from_x, from_y = lax.optimization_barrier((grad_b, came_a, from_x, from_y))
    far_u = add_all(own_u[2], core_u[2], from_x[1]).astype(BF)
    far_l = add_all(own_l[2], core_l[2], from_y[1]).astype(BF)
    from_far = [over_ctx(far_u, 4), over_ctx(far_l, 2)]
    came_b = exchange(grad_b, "ctx")
    came_b, from_far = lax.optimization_barrier((came_b, from_far))
    sums_u = add_all(own_u[3], core_u[3], from_x[0], from_far[0]).astype(BF)
    sums_l = add_all(own_l[3], core_l[3], from_y[0], from_far[1]).astype(BF)
    from_z = over_fsdp(jnp.concatenate([sums_u[:2], sums_l[:2]], axis=1), 1)
    total_m = jnp.concatenate([sums_u[2:], sums_l[2:]], axis=1)
    start_grad, send, own_j, other_j = back_pass(
        devices * capacity,
        where,
        came_a,
        came_b,
        hidden_first,
        start,
        middle_grad,
        joined,
        lookup,
        gains,
        second_gain_term,
        embedded,
        target_row,
    )
    from_core = over_ctx(other_j, 1)
    arrived = exchange(send.reshape(devices, capacity, 2 * E), both)
    half_j = add_cores(own_j, from_core)
    from_chips = to_chips(half_j)
    from_z, kept = lax.optimization_barrier((from_z, half_j[0]))
    near_m, far_m = add_blocks(total_m[1], [from_z[0]]), add_blocks(total_m[0], [from_z[1]])
    from_z = over_fsdp(far_m, 2)
    total_j = add_blocks(kept, from_chips)
    from_fsdp = [over_fsdp(total_j[m], m) for m in (1, 2, 3)]
    from_z, kept = lax.optimization_barrier((from_z, total_j[0]))
    piece_m = add_blocks(near_m, [from_z])
    every_m = [over_ctx(piece_m, 2 * k) for k in (1, 2)]
    late_codes, kept, piece_m = lax.optimization_barrier((codes, kept, piece_m))
    bigram_grad, trigram_grad = add_rows(
        late_codes, arrived.reshape(devices * capacity, 2 * E), table_rows
    )
    bigram_grad, from_fsdp = lax.optimization_barrier((bigram_grad, from_fsdp))
    piece_j = add_blocks(kept, from_fsdp)
    every_j = to_chips([piece_j] * 4)
    piece_j, piece_m = lax.optimization_barrier((piece_j, piece_m))
    every_m.append(over_ctx(piece_m, 6))
    every_m, every_j = lax.optimization_barrier((every_m, every_j))
    blocks_m = jnp.stack([piece_m] + every_m)
    other_m = over_ctx(blocks_m, 1)
    blocks_j = jnp.stack([piece_j] + every_j)
    other_j = over_ctx(blocks_j, 1)
    expand_grad, contract_grad, output_grad = unpack_second(where, blocks_m, other_m)
    joined_grad, lookup_grad, gain_grads = unpack_first(where, blocks_j, other_j)
    gain_share = lax.dynamic_slice_in_dim(
        gain_grads[:, :6].reshape(2, D), z * (D // shards), D // shards, axis=1
    )
    return (
        result.reshape(batches, local_rows, D),
        start_grad.reshape(batches, local_rows, D),
        bigram_grad.T,
        trigram_grad.T,
        lookup_grad,
        gain_share[0],
        joined_grad,
        output_grad,
        gain_share[1],
        expand_grad,
        contract_grad,
    )


def solution(mesh):
    fits = mesh.shape["ctx"] == 8 and mesh.shape["fsdp"] == 4
    return jax.shard_map(
        local_packed if fits else local,
        mesh=mesh,
        in_specs=(
            P("fsdp", "ctx", None),
            P("fsdp", "ctx"),
            P("fsdp", "ctx"),
            P(("ctx", "fsdp"), None),
            P(("ctx", "fsdp"), None),
            P(),
            P("fsdp", None),
            P("fsdp"),
            P("fsdp", None),
            P("fsdp", None),
            P("fsdp"),
            P("fsdp", None),
            P("fsdp", None),
            P("fsdp", "ctx", None),
        ),
        out_specs=(
            P("fsdp", "ctx", None),
            P("fsdp", "ctx", None),
            P(("ctx", "fsdp"), None),
            P(("ctx", "fsdp"), None),
            P("fsdp", None),
            P("fsdp"),
            P("fsdp", None),
            P("fsdp", None),
            P("fsdp"),
            P("fsdp", None),
            P("fsdp", None),
        ),
        check_vma=False,
    )
```

```python
import functools
import math

import jax
import jax.numpy as jnp
from jax import lax
from jax.experimental import pallas as pl
from jax.experimental.pallas import tpu as pltpu
from jax.sharding import PartitionSpec as P

D = 768
HEADS = 12
HD = 64
FF = 2048
E = 192
ABLK = 256
BF = jnp.bfloat16
F32 = jnp.float32

epsilon = 1e-05
NT = (((1,), (1,)), ((), ()))
NN = (((1,), (0,)), ((), ()))
TN = (((0,), (0,)), ((), ()))


def mm(a, b, dims=NN):
    return lax.dot_general(a, b, dims, preferred_element_type=F32)


def eye(n):
    rows = lax.broadcasted_iota(jnp.int32, (n, n), 0)
    return jnp.where(rows == lax.broadcasted_iota(jnp.int32, (n, n), 1), 1.0, 0.0).astype(BF)


def vmem():
    return pl.BlockSpec(memory_space=pltpu.VMEM)


def smem():
    return pl.BlockSpec(memory_space=pltpu.SMEM)


def params(megabytes, **kw):
    return pltpu.CompilerParams(vmem_limit_bytes=megabytes << 20, **kw)


def cost(microseconds):
    return pl.CostEstimate(
        flops=int(microseconds * 6e8), bytes_accessed=int(microseconds * 2.5e6), transcendentals=0
    )


def in_hbm(value):
    return pltpu.with_memory_space_constraint(value, pltpu.HBM)


def after(value, *others):
    return lax.optimization_barrier((value, others))[0]


def placement_kernel(capacity, owner_row, owner_col, local_row, requests, target_row, target_col):
    tokens = owner_row.shape[1]
    devices = requests.shape[0]
    for table in range(2):
        own_r = owner_row[table : table + 1, :]
        own_c = owner_col[:, table : table + 1]
        t_row = lax.broadcasted_iota(jnp.int32, (tokens, tokens), 0)
        t_col = lax.broadcasted_iota(jnp.int32, (tokens, tokens), 1)
        same = own_c == own_r
        rank_r = jnp.sum(jnp.where(same & (t_row < t_col), 1.0, 0.0), axis=0, keepdims=True)
        rank_c = jnp.sum(jnp.where(same & (t_col < t_row), 1.0, 0.0), axis=1, keepdims=True)
        rank_r = rank_r.astype(jnp.int32)
        rank_c = rank_c.astype(jnp.int32)
        target_row[table : table + 1, :] = own_r * capacity + rank_r
        target_col[:, table : table + 1] = own_c * capacity + rank_c
        device = lax.broadcasted_iota(jnp.int32, (devices, tokens), 0)
        owned = device == own_r
        row = local_row[table : table + 1, :]
        high = jnp.where(owned, (row >> 7).astype(F32), 0.0).astype(BF)
        low = jnp.where(owned, (row & 127).astype(F32), 0.0).astype(BF)
        one = jnp.where(owned, 1.0, 0.0).astype(BF)
        slot = lax.broadcasted_iota(jnp.int32, (tokens, capacity), 1)
        ranked = jnp.where(slot == rank_c, 1.0, 0.0).astype(BF)
        code = 128.0 * mm(high, ranked) + mm(low, ranked) + mm(one, ranked)
        requests[:, table * capacity : (table + 1) * capacity] = code.astype(jnp.int32)


def placement(ids, table_rows, devices, capacity):
    tokens = ids.shape[1]
    owner = ids // table_rows
    local_row = ids - owner * table_rows
    return pl.pallas_call(
        functools.partial(placement_kernel, capacity),
        out_shape=(
            jax.ShapeDtypeStruct((devices, 2 * capacity), jnp.int32),
            jax.ShapeDtypeStruct((2, tokens), jnp.int32),
            jax.ShapeDtypeStruct((tokens, 2), jnp.int32),
        ),
        in_specs=[vmem()] * 3,
        out_specs=(vmem(),) * 3,
        compiler_params=params(32),
        cost_estimate=cost(2),
        name="placement",
    )(owner, owner.T, local_row)


def wide(ref, columns, table):
    ref[table] = jnp.broadcast_to(columns[:, table : table + 1].astype(F32), ref.shape[1:])


def onehot_block(ref, table, base, width):
    lane = lax.broadcasted_iota(jnp.int32, ref.shape[1:], 1).astype(F32)
    parts = []
    for j in range(width // 128):
        hit = ref[table] == lane + (base + 128 * j + 1).astype(F32)
        parts.append(jnp.where(hit, 1.0, 0.0).astype(BF))
    return jnp.concatenate(parts, axis=1)


def swap(value):
    return mm(eye(value.shape[1]), value, NT).astype(BF)


def read_rows_kernel(codes, bigram, trigram, out, total):
    step = pl.program_id(0)
    width = bigram.shape[1]
    slots = codes.shape[1]

    @pl.when(step == 0)
    def _():
        total[...] = jnp.zeros_like(total)

    row = lax.broadcasted_iota(jnp.int32, (width, slots), 0) + (step * width + 1)
    for table, source in enumerate((bigram, trigram)):
        hot = jnp.where(row == codes[table : table + 1, :], 1.0, 0.0).astype(BF)
        total[table * E : (table + 1) * E, :] += mm(source[...], hot)

    @pl.when(step == pl.num_programs(0) - 1)
    def _():
        for begin in range(0, slots, 128):
            out[begin : begin + 128, :] = swap(total[:, begin : begin + 128].astype(BF))


def table_block(table_rows):
    for width in (2560, 1280, 640, 512, 256, 128):
        if table_rows % width == 0:
            return width
    return table_rows


def read_rows(codes, bigram_t, trigram_t):
    slots = codes.shape[1]
    rows = bigram_t.shape[1]
    width = table_block(rows)
    table = pl.BlockSpec((E, width), lambda i: (0, i))
    return pl.pallas_call(
        read_rows_kernel,
        grid=(rows // width,),
        out_shape=jax.ShapeDtypeStruct((slots, 2 * E), BF),
        in_specs=[pl.BlockSpec((2, slots), lambda i: (0, 0)), table, table],
        out_specs=pl.BlockSpec((slots, 2 * E), lambda i: (0, 0)),
        scratch_shapes=[pltpu.VMEM((2 * E, slots), F32)],
        compiler_params=params(40),
        cost_estimate=cost(17),
        name="read_rows",
    )(codes, bigram_t, trigram_t)


def add_rows_kernel(codes, grads, bigram, trigram, spread, turned):
    step = pl.program_id(0)
    width = bigram.shape[1]

    @pl.when(step == 0)
    def _():
        for table in range(2):
            wide(spread, codes, table)
        turned[...] = mm(eye(2 * E), grads[...], NT).astype(BF)

    for table, out in enumerate((bigram, trigram)):
        hot = onehot_block(spread, table, step * width, width)
        out[...] = mm(turned[table * E : (table + 1) * E, :], hot)


def add_rows(codes, grads, rows):
    slots = codes.shape[0]
    width = table_block(rows)
    table = pl.BlockSpec((E, width), lambda i: (0, i))
    shape = jax.ShapeDtypeStruct((E, rows), F32)
    return pl.pallas_call(
        add_rows_kernel,
        grid=(rows // width,),
        out_shape=(shape, shape),
        in_specs=[
            pl.BlockSpec((slots, 2), lambda i: (0, 0)),
            pl.BlockSpec((slots, 2 * E), lambda i: (0, 0)),
        ],
        out_specs=(table, table),
        scratch_shapes=[pltpu.VMEM((2, slots, 128), F32), pltpu.VMEM((2 * E, slots), BF)],
        compiler_params=params(32),
        cost_estimate=cost(14),
        name="add_rows",
    )(codes, grads)


def attend_kernel(pairs, piece, order, rows, out, attended_t, logsum, q_s, k_s, vt_s, s_s):
    length = rows.shape[0]
    blocks = length // ABLK
    per_block = ABLK // piece
    width = pairs * HD
    identity = eye(HD)

    def sort(j, _):
        block = rows[pl.ds(pl.multiple_of(order[j] * piece, piece), piece), :]
        to = pl.ds(pl.multiple_of(j * piece, piece), piece)
        for p in range(pairs):
            q = block[:, p * HD : (p + 1) * HD]
            q_s[p, to, :] = (q.astype(F32) * HD ** (-0.5)).astype(BF)
            k_s[p, to, :] = block[:, width + p * HD : width + (p + 1) * HD]
            v = block[:, 2 * width + p * HD : 2 * width + (p + 1) * HD]
            vt_s[p, :, to] = mm(identity, v, NT).astype(BF)
        return 0

    lax.fori_loop(0, length // piece, sort, 0)

    for p in range(pairs):

        def one(i, _):
            at = pl.ds(pl.multiple_of(i * ABLK, ABLK), ABLK)
            queries = q_s[p, at, :]

            def score(j, peak):
                to = pl.ds(pl.multiple_of(j * ABLK, ABLK), ABLK)
                s = mm(k_s[p, to, :], queries, NT)
                s_s[to, :] = s
                return jnp.maximum(peak, jnp.max(s, axis=0, keepdims=True))

            peak = lax.fori_loop(0, i + 1, score, jnp.full((1, ABLK), -jnp.inf, F32))

            def raise_(j, total):
                to = pl.ds(pl.multiple_of(j * ABLK, ABLK), ABLK)
                e = jnp.exp(s_s[to, :] - peak)
                s_s[to, :] = e
                return total + jnp.sum(e, axis=0, keepdims=True)

            total = lax.fori_loop(0, i + 1, raise_, jnp.zeros((1, ABLK), F32))
            scale = 1.0 / total

            def weigh(j, o):
                to = pl.ds(pl.multiple_of(j * ABLK, ABLK), ABLK)
                probs = (s_s[to, :] * scale).astype(BF)
                return o + mm(vt_s[p, :, to], probs)

            o = lax.fori_loop(0, i + 1, weigh, jnp.zeros((HD, ABLK), F32))
            attended_t[p, :, at] = o
            logsum[p, :, at] = peak + jnp.log(total)
            o = o.T.astype(BF)
            for h in range(per_block):
                to = pl.ds(pl.multiple_of(order[per_block * i + h] * piece, piece), piece)
                out[to, p * HD : (p + 1) * HD] = o[h * piece : (h + 1) * piece, :]
            return 0

        lax.fori_loop(0, blocks, one, 0)


def attend(order, rows, pairs, piece):
    length = rows.shape[0]
    return pl.pallas_call(
        functools.partial(attend_kernel, pairs, piece),
        out_shape=(
            jax.ShapeDtypeStruct((length, pairs * HD), BF),
            jax.ShapeDtypeStruct((pairs, HD, length), F32),
            jax.ShapeDtypeStruct((pairs, 1, length), F32),
        ),
        in_specs=[smem(), vmem()],
        out_specs=(vmem(),) * 3,
        scratch_shapes=[
            pltpu.VMEM((pairs, length, HD), BF),
            pltpu.VMEM((pairs, length, HD), BF),
            pltpu.VMEM((pairs, HD, length), BF),
            pltpu.VMEM((length, ABLK), F32),
        ],
        compiler_params=params(48),
        cost_estimate=cost(50),
        name="attend",
    )(order, rows)


def attend_grad_kernel(
    pairs,
    piece,
    order,
    rows,
    grads,
    attended_t,
    logsum,
    cos,
    sin,
    cos_t,
    sin_t,
    out,
    q_s,
    k_s,
    v_s,
    g_s,
    kt_s,
    dq_s,
    dk_s,
    dv_s,
    dk_o,
    dv_o,
):
    length = rows.shape[0]
    blocks = length // ABLK
    width = pairs * HD
    half = HD // 2
    scale = HD ** (-0.5)
    identity = eye(HD)

    for p in range(pairs):

        def sort(j, _):
            take = pl.ds(pl.multiple_of(order[j] * piece, piece), piece)
            block = rows[take, :]
            to = pl.ds(pl.multiple_of(j * piece, piece), piece)
            q_s[to, :] = (block[:, p * HD : (p + 1) * HD].astype(F32) * scale).astype(BF)
            k = block[:, width + p * HD : width + (p + 1) * HD]
            k_s[to, :] = k
            kt_s[:, to] = mm(identity, k, NT).astype(BF)
            v_s[to, :] = block[:, 2 * width + p * HD : 2 * width + (p + 1) * HD]
            g_s[to, :] = grads[take, :][:, p * HD : (p + 1) * HD]
            return 0

        lax.fori_loop(0, length // piece, sort, 0)
        dk_s[...] = jnp.zeros_like(dk_s)
        dv_s[...] = jnp.zeros_like(dv_s)

        def one(i, _):
            at = pl.ds(pl.multiple_of(i * ABLK, ABLK), ABLK)
            queries = q_s[at, :]
            grad = g_s[at, :]
            delta = jnp.sum(
                mm(identity, grad, NT) * attended_t[p, :, at], axis=0, keepdims=True
            )
            level = logsum[p, :, at]

            def tile(j, dq):
                to = pl.ds(pl.multiple_of(j * ABLK, ABLK), ABLK)
                probs = jnp.exp(mm(k_s[to, :], queries, NT) - level)
                ds = (probs * (mm(v_s[to, :], grad, NT) - delta)).astype(BF)
                dv_s[to, :] += mm(probs.astype(BF), grad)
                dk_s[to, :] += mm(ds, queries)
                return dq + mm(kt_s[:, to], ds)

            dq = lax.fori_loop(0, i + 1, tile, jnp.zeros((HD, ABLK), F32)) * scale
            c, s = cos_t[:, at], sin_t[:, at]
            a, b = dq[:half, :], dq[half:, :]
            dq = jnp.concatenate([a * c + b * s, b * c - a * s], axis=0)
            dq_s[p, at, :] = dq.T.astype(BF)
            return 0

        lax.fori_loop(0, blocks, one, 0)

        def turn(j, _):
            to = pl.ds(pl.multiple_of(j * ABLK, ABLK), ABLK)
            dk = dk_s[to, :]
            a, b = dk[:, :half], dk[:, half:]
            c, s = cos[to, :], sin[to, :]
            dk_o[p, to, :] = jnp.concatenate([a * c + b * s, b * c - a * s], axis=1).astype(BF)
            dv_o[p, to, :] = dv_s[to, :].astype(BF)
            return 0

        lax.fori_loop(0, blocks, turn, 0)

    def unsort(j, _):
        take = pl.ds(pl.multiple_of(j * piece, piece), piece)
        to = pl.ds(pl.multiple_of(order[j] * piece, piece), piece)
        parts = [ref[p, take, :] for ref in (dq_s, dk_o, dv_o) for p in range(pairs)]
        out[to, :] = jnp.concatenate(parts, axis=1)
        return 0

    lax.fori_loop(0, length // piece, unsort, 0)


def attend_grad(order, rows, grads, attended_t, logsum, cos, sin, cos_t, sin_t, pairs, piece):
    length = rows.shape[0]
    low = pltpu.VMEM((length, HD), BF)
    full = pltpu.VMEM((length, HD), F32)
    each = pltpu.VMEM((pairs, length, HD), BF)
    return pl.pallas_call(
        functools.partial(attend_grad_kernel, pairs, piece),
        out_shape=jax.ShapeDtypeStruct((length, 3 * pairs * HD), BF),
        in_specs=[smem()] + [vmem()] * 8,
        out_specs=vmem(),
        scratch_shapes=[low] * 4 + [pltpu.VMEM((HD, length), BF), each, full, full, each, each],
        compiler_params=params(56),
        cost_estimate=cost(68),
        name="attend_grad",
    )(order, rows, grads, attended_t, logsum, cos, sin, cos_t, sin_t)


def fold_max(peak, tile):
    return jnp.maximum(peak, jnp.max(tile.reshape(-1, 8, tile.shape[1]), axis=0))


def fold_sum(total, tile):
    return total + jnp.sum(tile.reshape(-1, 8, tile.shape[1]), axis=0)


def piece_of(order, j, piece):
    at = order[j]
    return at // 2, pl.ds(pl.multiple_of(lax.rem(at, 2) * piece, piece), piece)


def attend_short_kernel(pairs, piece, order, rows, out, attended_t, logsum, q_s, k_s, v_s, s_s):
    length = rows.shape[0] * rows.shape[2]
    blocks = length // ABLK
    width = pairs * HD

    def sort(j, _):
        device, lanes = piece_of(order, j, piece)
        block = rows[device, :, lanes]
        to = pl.ds(pl.multiple_of(j * piece, piece), piece)
        for p in range(pairs):
            q = block[p * HD : (p + 1) * HD, :]
            q_s[p, :, to] = (q.astype(F32) * HD ** (-0.5)).astype(BF)
            k_s[p, to, :] = swap(block[width + p * HD : width + (p + 1) * HD, :])
            v_s[p, :, to] = block[2 * width + p * HD : 2 * width + (p + 1) * HD, :]
        return 0

    lax.fori_loop(0, length // piece, sort, 0)

    def pair(p, _):
        features = pl.ds(pl.multiple_of(p * HD, HD), HD)
        for i in range(blocks):
            at = slice(i * ABLK, (i + 1) * ABLK)
            queries = q_s[p, :, at]
            peak = jnp.full((8, ABLK), -jnp.inf, F32)
            for j in range(i + 1):
                s = mm(k_s[p, j * ABLK : (j + 1) * ABLK, :], queries)
                s_s[i % 2, j * ABLK : (j + 1) * ABLK, :] = s
                peak = fold_max(peak, s)
            peak = jnp.max(peak, axis=0, keepdims=True)
            total = jnp.zeros((8, ABLK), F32)
            o = jnp.zeros((HD, ABLK), F32)
            for j in range(i + 1):
                e = jnp.exp(s_s[i % 2, j * ABLK : (j + 1) * ABLK, :] - peak)
                total = fold_sum(total, e)
                o += mm(v_s[p, :, j * ABLK : (j + 1) * ABLK], e.astype(BF))
            total = jnp.sum(total, axis=0, keepdims=True)
            o = o * (1.0 / total)
            attended_t[p, :, at] = o
            logsum[p, :, at] = peak + jnp.log(total)
            o = o.astype(BF)
            for h in range(ABLK // piece):
                device, lanes = piece_of(order, ABLK // piece * i + h, piece)
                out[device, features, lanes] = o[:, h * piece : (h + 1) * piece]
        return 0

    lax.fori_loop(0, pairs, pair, 0)


def attend_short(order, rows, pairs, piece):
    contexts, _, tokens = rows.shape
    length = contexts * tokens
    return pl.pallas_call(
        functools.partial(attend_short_kernel, pairs, piece),
        out_shape=(
            jax.ShapeDtypeStruct((contexts, pairs * HD, tokens), BF),
            jax.ShapeDtypeStruct((pairs, HD, length), F32),
            jax.ShapeDtypeStruct((pairs, 1, length), F32),
        ),
        in_specs=[smem(), vmem()],
        out_specs=(vmem(),) * 3,
        scratch_shapes=[
            pltpu.VMEM((pairs, HD, length), BF),
            pltpu.VMEM((pairs, length, HD), BF),
            pltpu.VMEM((pairs, HD, length), BF),
            pltpu.VMEM((2, length, ABLK), F32),
        ],
        compiler_params=params(48),
        cost_estimate=cost(25),
        name="attend",
    )(order, rows)


def attend_grad_short_kernel(
    pairs,
    begin,
    count,
    piece,
    order,
    rows,
    grads,
    attended_t,
    logsum,
    cos_t,
    sin_t,
    out,
    q_s,
    g_s,
    kt_s,
    k_s,
    v_s,
    dk_s,
    dv_s,
):
    length = rows.shape[0] * rows.shape[2]
    blocks = length // ABLK
    width = pairs * HD
    half = HD // 2
    scale = HD ** (-0.5)

    def sort(j, _):
        device, lanes = piece_of(order, j, piece)
        block = rows[device, :, lanes]
        grad = grads[device, :, lanes]
        to = pl.ds(pl.multiple_of(j * piece, piece), piece)
        for p in range(count):
            row = (begin + p) * HD
            q_s[p, :, to] = (block[row : row + HD, :].astype(F32) * scale).astype(BF)
            k = block[width + row : width + row + HD, :]
            kt_s[p, :, to] = k
            k_s[p, to, :] = swap(k)
            v_s[p, to, :] = swap(block[2 * width + row : 2 * width + row + HD, :])
            g_s[p, :, to] = grad[row : row + HD, :]
        return 0

    lax.fori_loop(0, length // piece, sort, 0)

    def turn(x, at):
        c, s = cos_t[:, at], sin_t[:, at]
        a, b = x[:half, :], x[half:, :]
        return jnp.concatenate([a * c + b * s, b * c - a * s], axis=0)

    def pair(p, _):
        def put(kind, i, value):
            features = pl.ds(pl.multiple_of((kind * count + p) * HD, HD), HD)
            value = value.astype(BF)
            for h in range(ABLK // piece):
                device, lanes = piece_of(order, ABLK // piece * i + h, piece)
                out[device, features, lanes] = value[:, h * piece : (h + 1) * piece]

        for i in range(blocks):
            at = slice(i * ABLK, (i + 1) * ABLK)
            queries = q_s[p, :, at]
            grad = g_s[p, :, at]
            delta = jnp.sum(
                grad.astype(F32) * attended_t[begin + p, :, at], axis=0, keepdims=True
            )
            level = logsum[begin + p, :, at]
            dq = jnp.zeros((HD, ABLK), F32)
            for j in range(i, -1, -1):
                to = slice(j * ABLK, (j + 1) * ABLK)
                probs = jnp.exp(mm(k_s[p, to, :], queries) - level)
                ds = (probs * (mm(v_s[p, to, :], grad) - delta)).astype(BF)
                dv = mm(grad, probs.astype(BF), NT)
                dk = mm(queries, ds, NT)
                if i == j:
                    dv_s[:, to] = dv
                    dk_s[:, to] = dk
                else:
                    dv_s[:, to] += dv
                    dk_s[:, to] += dk
                dq += mm(kt_s[p, :, to], ds)
            put(0, i, turn(dq * scale, at))
        for i in range(blocks):
            at = slice(i * ABLK, (i + 1) * ABLK)
            put(1, i, turn(dk_s[:, at], at))
            put(2, i, dv_s[:, at])
        return 0

    lax.fori_loop(0, count, pair, 0)


def attend_grad_short(
    order, rows, grads, attended_t, logsum, cos_t, sin_t, pairs, piece, begin, count
):
    contexts, _, tokens = rows.shape
    length = contexts * tokens
    wide_ = pltpu.VMEM((count, HD, length), BF)
    tall = pltpu.VMEM((count, length, HD), BF)
    full = pltpu.VMEM((HD, length), F32)
    return pl.pallas_call(
        functools.partial(attend_grad_short_kernel, pairs, begin, count, piece),
        out_shape=jax.ShapeDtypeStruct((contexts, 3 * count * HD, tokens), BF),
        in_specs=[smem()] + [vmem()] * 6,
        out_specs=vmem(),
        scratch_shapes=[wide_] * 3 + [tall] * 2 + [full] * 2,
        compiler_params=params(48),
        cost_estimate=cost(14 * count),
        name=f"attend_grad_{begin}",
    )(order, rows, grads, attended_t, logsum, cos_t, sin_t)


def over_ctx(value, mask):
    size = lax.axis_size("ctx")
    return lax.ppermute(value, "ctx", [(i, i ^ mask) for i in range(size)])


def along_fsdp(value, shift):
    size = lax.axis_size("fsdp")
    return lax.ppermute(value, "fsdp", [(i, (i + shift) % size) for i in range(size)])


def by_index(blocks, index):
    if len(blocks) == 1:
        return blocks
    half = len(blocks) // 2
    flip = (index // half) % 2 == 1
    lower = [jnp.where(flip, b, a) for a, b in zip(blocks[:half], blocks[half:])]
    upper = [jnp.where(flip, a, b) for a, b in zip(blocks[:half], blocks[half:])]
    return by_index(lower, index) + by_index(upper, index)


def place():
    ctx = lax.axis_index("ctx")
    return ctx % 2, ctx // 2, lax.axis_index("fsdp")


def gather_weight(shard):
    core, chip, z = place()
    chips = lax.axis_size("ctx") // 2
    shards = lax.axis_size("fsdp")
    rows, columns = shard.shape
    r, half = rows // chips, columns // 2
    mine = lax.dynamic_slice(shard, (chip * r, core * half), (r, half))
    along = [mine] + [along_fsdp(mine, k) for k in range(1, shards)]
    turned = jnp.stack([along[(shards - m) % shards] for m in range(shards)])
    column = lax.dynamic_slice_in_dim(
        jnp.concatenate([turned, turned]), (shards - z) % shards, shards
    )
    blocks = [column] + [over_ctx(column, 2 * k) for k in range(1, chips)]
    own = jnp.stack(by_index(blocks, chip), axis=1).reshape(shards * rows, half)
    other = over_ctx(own, 1)
    return jnp.where(
        core == 0, jnp.concatenate([own, other], axis=1), jnp.concatenate([other, own], axis=1)
    )


def gather_gains(gains):
    _, _, z = place()
    shards = lax.axis_size("fsdp")
    along = [gains] + [along_fsdp(gains, k) for k in range(1, shards)]
    turned = jnp.stack([along[(shards - m) % shards] for m in range(shards)])
    every = lax.dynamic_slice_in_dim(
        jnp.concatenate([turned, turned]), (shards - z) % shards, shards
    )
    return jnp.moveaxis(every, 0, 1).reshape(gains.shape[0], -1)


def reduce_grad(grad):
    core, chip, z = place()
    chips = lax.axis_size("ctx") // 2
    shards = lax.axis_size("fsdp")
    rows, columns = grad.shape[0] // shards, grad.shape[1]
    r, half = rows // chips, columns // 2
    view = grad.reshape(shards, chips, r, columns)

    def columns_of(which):
        return lax.dynamic_slice_in_dim(view, which * half, half, axis=3)

    total = columns_of(core).astype(F32) + over_ctx(columns_of(1 - core), 1).astype(F32)
    low = total.astype(BF)
    sent = [
        over_ctx(lax.dynamic_index_in_dim(low, chip ^ k, 1, keepdims=False), 2 * k)
        for k in range(1, chips)
    ]
    total = lax.dynamic_index_in_dim(low, chip, 1, keepdims=False).astype(F32)
    total = sum((s.astype(F32) for s in sent), total)
    low = total.astype(BF)
    sent = [
        along_fsdp(lax.dynamic_index_in_dim(low, (z + k) % shards, 0, keepdims=False), k)
        for k in range(1, shards)
    ]
    total = lax.dynamic_index_in_dim(low, z, 0, keepdims=False).astype(F32)
    total = sum((s.astype(F32) for s in sent), total)
    piece = total.astype(BF)
    blocks = [piece] + [over_ctx(piece, 2 * k) for k in range(1, chips)]
    own = jnp.stack(by_index(blocks, chip)).reshape(rows, half)
    other = over_ctx(own, 1)
    return jnp.where(
        core == 0, jnp.concatenate([own, other], axis=1), jnp.concatenate([other, own], axis=1)
    ).astype(F32)


def by_head(values, devices, pairs):
    batches, tokens, kinds, _ = values.shape
    groups = HEADS // pairs
    values = values.reshape(batches, tokens, kinds, groups, pairs * HD)
    values = values.transpose(0, 3, 1, 2, 4).reshape(batches * groups, tokens, kinds * pairs * HD)
    spare = devices - batches * groups
    return jnp.pad(values, ((0, spare), (0, 0), (0, 0)))


def by_token(values, batches, kinds, pairs):
    groups = HEADS // pairs
    tokens = values.shape[1]
    values = values[: batches * groups].reshape(batches, groups, tokens, kinds, pairs * HD)
    return values.transpose(0, 2, 3, 1, 4).reshape(batches, tokens, kinds, HEADS * HD)


def exchange(values, axes):
    return lax.all_to_all(values, axes, split_axis=0, concat_axis=0, tiled=True)


def aligned(value, by=16):
    return pl.multiple_of(value, by)


def pack_weights_kernel(where, joined, output, lookup, gains, expand, contract, first, second):
    core, chip = where[0], where[1]
    rows = pl.ds(aligned(chip * 48), 48)
    for t in range(3):
        first[t * 48 : (t + 1) * 48, :] = joined[rows, pl.ds(aligned(t * D + core * 384, 128), 384)]
    columns = pl.ds(aligned(core * 384, 128), 384)
    first[144:192, :] = lookup[:, columns]
    first[192:208, :] = gains[...]
    for j in range(16):
        second[j * 48 : (j + 1) * 48, :] = expand[
            rows, pl.ds(aligned(core * FF + j * 128, 128), 128)
        ]
    for j in range(3):
        second[768 + j * 128 : 896 + j * 128, :] = contract[
            pl.ds(aligned(chip * 128), 128), pl.ds(aligned(core * 384 + j * 128, 128), 128)
        ]
        second[1152 + j * 48 : 1200 + j * 48, :] = output[
            rows, pl.ds(aligned(core * 384 + j * 128, 128), 128)
        ]


def pack_weights(where, *weights):
    return pl.pallas_call(
        pack_weights_kernel,
        out_shape=(
            jax.ShapeDtypeStruct((208, 384), BF),
            jax.ShapeDtypeStruct((1296, 128), BF),
        ),
        in_specs=[smem()] + [vmem()] * 6,
        out_specs=(vmem(),) * 2,
        compiler_params=params(16),
        cost_estimate=cost(2),
        name="pack_weights",
    )(where, *weights)


CUT = 14 * 48


def by_chip(near_x, near_y, far_y, far_x):
    return (
        [near_x.at[0], near_x.at[1], far_y.at[0], far_y.at[1]],
        [near_y.at[0], far_x.at[0], near_y.at[1], far_x.at[1]],
    )


def spread_fsdp(piece):
    along = [piece] + [along_fsdp(piece, k) for k in range(1, 4)]
    return [along[(4 - m) % 4] for m in range(4)]


def add_cores(own, came):
    return [(own[k].astype(F32) + came[k].astype(F32)).astype(BF) for k in range(4)]


def add_blocks(own, came):
    total = own.astype(F32)
    for block in came:
        total = total + block.astype(F32)
    return total.astype(BF)


def to_chips(blocks):
    return [over_ctx(blocks[k], 2 * k) for k in range(1, 4)]


def add_all(*blocks):
    return sum((b.astype(F32) for b in blocks[1:]), blocks[0].astype(F32))


def over_fsdp(value, mask):
    return lax.ppermute(value, "fsdp", [(i, i ^ mask) for i in range(4)])


def unpack_second_kernel(where, own, other, expand, contract, output):
    core, chip = where[0], where[1]
    for k in range(4):
        yx = chip ^ k
        rows = pl.ds(aligned(yx * 48), 48)
        for half in range(2):

            def taken(begin, count):
                part = slice(begin, begin + count)
                return jnp.where(core == half, own[k, part, :].astype(F32), other[k, part, :].astype(F32))

            for j in range(16):
                expand[rows, half * FF + j * 128 : half * FF + (j + 1) * 128] = taken(j * 48, 48)
            for j in range(3):
                to = slice(half * 384 + j * 128, half * 384 + (j + 1) * 128)
                contract[pl.ds(aligned(yx * 128), 128), to] = taken(768 + j * 128, 128)
                output[rows, to] = taken(1152 + j * 48, 48)


def unpack_second(where, own, other):
    return pl.pallas_call(
        unpack_second_kernel,
        out_shape=(
            jax.ShapeDtypeStruct((192, 2 * FF), F32),
            jax.ShapeDtypeStruct((512, D), F32),
            jax.ShapeDtypeStruct((192, D), F32),
        ),
        in_specs=[smem()] + [vmem()] * 2,
        out_specs=(vmem(),) * 3,
        compiler_params=params(24),
        cost_estimate=cost(4),
        name="unpack_second",
    )(where, own, other)


def unpack_first_kernel(where, own, other, joined, lookup, gains):
    core, chip = where[0], where[1]
    for k in range(4):
        yx = chip ^ k
        rows = pl.ds(aligned(yx * 48), 48)
        for half in range(2):

            def taken(begin, count):
                part = slice(begin, begin + count)
                return jnp.where(core == half, own[k, part, :].astype(F32), other[k, part, :].astype(F32))

            for t in range(3):
                for j in range(3):
                    to = t * D + half * 384 + j * 128
                    joined[rows, to : to + 128] = taken((t * 3 + j) * 48, 48)

            @pl.when(yx < 3)
            def _():
                at = pl.ds(aligned(half * 384 + yx * 128, 128), 128)
                lookup[:, at] = taken(432, 48)

            @pl.when(yx == 3)
            def _():
                gains[half] = taken(432, 48)


def unpack_first(where, own, other):
    return pl.pallas_call(
        unpack_first_kernel,
        out_shape=(
            jax.ShapeDtypeStruct((192, 3 * D), F32),
            jax.ShapeDtypeStruct((48, D), F32),
            jax.ShapeDtypeStruct((2, 48, 128), F32),
        ),
        in_specs=[smem()] + [vmem()] * 2,
        out_specs=(vmem(),) * 3,
        compiler_params=params(24),
        cost_estimate=cost(2),
        name="unpack_first",
    )(where, own, other)


def unit_rows(x):
    inverse = lax.rsqrt(jnp.mean(x * x, axis=-1, keepdims=True) + epsilon)
    return x * inverse, inverse


def front_kernel(
    pairs,
    where,
    starts,
    got,
    target,
    token,
    cos_t,
    sin_t,
    *refs,
):
    own_tail, other_tail = refs[8:10]
    start, embed, hidden, send, joined, lookup, gains, t_s, g_s = refs[10:]
    core, chip, z = where[0], where[1], where[2]
    for blocks, tail, half in ((refs[:4], own_tail, core), (refs[4:8], other_tail, 1 - core)):
        for m in range(4):
            zz = lax.rem(z + m, 4)
            for k in range(4):
                rows = pl.ds(aligned(zz * 192 + (chip ^ k) * 48), 48)
                for t in range(3):
                    joined[rows, pl.ds(aligned(t * D + half * 384, 128), 384)] = blocks[k][
                        m, t * 48 : (t + 1) * 48, :
                    ]
            lookup[pl.ds(aligned(zz * 48), 48), pl.ds(aligned(half * 384, 128), 384)] = tail[
                m, 0:48, :
            ]
    for m in range(4):
        g_s[lax.rem(z + m, 4)] = own_tail[m, 48:64, :].astype(F32)
    for row in range(2):
        gains[row : row + 1, :] = jnp.concatenate(
            [g_s[zz, row : row + 1, :192] for zz in range(4)], axis=1
        )
    gain = gains[0:1, :]
    tokens = token.shape[0]
    piece = 128
    per_batch = tokens // 2 // piece
    groups = HEADS // pairs
    wide_ = pairs * HD
    slots = got.shape[0]
    lane = lax.broadcasted_iota(jnp.int32, (piece, 128), 1)
    first_half = lax.rem(lane, HD) < HD // 2

    def block(i, _):
        at = pl.ds(aligned(i * piece, piece), piece)
        goal = target[at, :]
        slot = lax.broadcasted_iota(jnp.int32, (piece, slots), 1)
        parts = []
        for table in range(2):
            hot = jnp.where(goal[:, table : table + 1] == slot, 1.0, 0.0).astype(BF)
            parts.append(mm(hot, got[:, table * E : (table + 1) * E]))
        rows = (parts[0] + parts[1]).astype(BF)
        embed[at, :] = rows
        x = token[at, :].astype(F32) + mm(rows, lookup[...])
        start[at, :] = x
        normed, _ = unit_rows(x)
        low = (normed * gain).astype(BF)
        hidden[at, :] = low
        projected = mm(low, joined[...])
        begin = pl.ds(aligned(starts[lax.rem(i, per_batch)] * piece, piece), piece)
        c = cos_t[:, begin].T
        s = sin_t[:, begin].T
        c = jnp.concatenate([c, c, c, c], axis=1)
        s = jnp.concatenate([-s, s, -s, s], axis=1)
        turned = []
        for j in range(12):
            v = projected[:, j * 128 : (j + 1) * 128]
            swapped = jnp.where(first_half, pltpu.roll(v, 96, 1), pltpu.roll(v, 32, 1))
            turned.append((v * c + swapped * s).astype(BF))
        for j in range(12, 18):
            turned.append(projected[:, j * 128 : (j + 1) * 128].astype(BF))
        for j, v in enumerate(turned):
            t_s[j * 128 : (j + 1) * 128, :] = swap(v)
        batch = i // per_batch
        to = pl.ds(aligned(lax.rem(i, per_batch) * piece, piece), piece)
        for g in range(groups):
            for t in range(3):
                begin = t * D + g * wide_
                send[batch * groups + g, t * wide_ : (t + 1) * wide_, to] = t_s[
                    begin : begin + wide_, :
                ]
        return 0

    lax.fori_loop(0, tokens // piece, block, 0)


def front(pairs, devices, where, starts, got, target, token, cos_t, sin_t, *blocks):
    tokens = token.shape[0]
    return pl.pallas_call(
        functools.partial(front_kernel, pairs),
        out_shape=(
            jax.ShapeDtypeStruct((tokens, D), F32),
            jax.ShapeDtypeStruct((tokens, E), BF),
            jax.ShapeDtypeStruct((tokens, D), BF),
            jax.ShapeDtypeStruct((devices, 3 * pairs * HD, tokens // 2), BF),
            jax.ShapeDtypeStruct((D, 3 * D), BF),
            jax.ShapeDtypeStruct((E, D), BF),
            jax.ShapeDtypeStruct((2, D), F32),
        ),
        in_specs=[smem()] * 2 + [vmem()] * 15,
        out_specs=(vmem(),) * 7,
        scratch_shapes=[pltpu.VMEM((3 * D, 128), BF), pltpu.VMEM((4, 16, 384), F32)],
        compiler_params=params(60),
        cost_estimate=cost(9),
        name="front",
    )(where, starts, got, target, token, cos_t, sin_t, *blocks)


def mlp_kernel(
    pairs,
    where,
    came,
    start,
    gains,
    upstream,
    *refs,
):
    blocks_own, blocks_other = refs[:4], refs[4:8]
    (
        result,
        hidden_out,
        attended_out,
        act_out,
        gate_out,
        up_out,
        gain_grad,
        middle_grad,
        send,
        hidden,
        total,
        back,
        output,
        pair_s,
        w_down,
    ) = refs[8:]
    step = pl.program_id(0)
    core, chip, z = where[0], where[1], where[2]
    gain = gains[1:2, :]
    sides = [
        by_chip(*blocks) + (half,)
        for blocks, half in ((blocks_own, core), (blocks_other, 1 - core))
    ]

    def fill(which, j, take):
        for side in sides:
            for m in range(4):
                for k in range(4):
                    rows = pl.ds(aligned(lax.rem(z + m, 4) * 192 + (chip ^ k) * 48), 48)
                    pair_s[side[2], rows, j * 128 : (j + 1) * 128] = side[which][k][
                        m, take, :
                    ]

    for j in range(4):
        tile = pl.ds(aligned((4 * step + j) * 48), 48)
        if j < 2:
            fill(0, j, tile)
            continue

        @pl.when(step < 3)
        def _():
            fill(0, j, tile)

        @pl.when(step == 3)
        def _():
            fill(1, j, slice((j - 2) * 48, (j - 1) * 48))

    m = lax.rem(step - z + 4, 4)
    for k in range(4):
        rows = pl.ds(aligned((chip ^ k) * 128), 128)
        for _, lower, side in sides:
            for j in range(3):
                begin = 768 + j * 128 - CUT
                w_down[rows, pl.ds(aligned(side * 384 + j * 128, 128), 128)] = lower[k][
                    m, begin : begin + 128, :
                ]

    groups = HEADS // pairs
    wide_ = pairs * HD
    half = came.shape[2]

    @pl.when(step == 0)
    def _():
        for _, lower, side in sides:
            for m in range(4):
                for k in range(4):
                    rows = pl.ds(aligned(lax.rem(z + m, 4) * 192 + (chip ^ k) * 48), 48)
                    for j in range(3):
                        begin = 1152 + j * 48 - CUT
                        output[rows, pl.ds(aligned(side * 384 + j * 128, 128), 128)] = lower[k][
                            m, begin : begin + 48, :
                        ]
        for batch in range(2):
            at = slice(batch * half, (batch + 1) * half)
            parts = []
            for h in range(half // 128):
                lanes = slice(h * 128, (h + 1) * 128)
                parts.append(
                    jnp.concatenate(
                        [swap(came[batch * groups + g, :, lanes]) for g in range(groups)], axis=1
                    )
                )
            rows = jnp.concatenate(parts, axis=0)
            attended_out[at, :] = rows
            x = start[at, :] + mm(rows, output[...])
            total[at, :] = x
            middle_grad[at, :] = x
            normed, _ = unit_rows(x)
            low = (normed * gain).astype(BF)
            hidden[at, :] = low
            hidden_out[at, :] = low
        back[...] = jnp.zeros_like(back)

    for batch in range(2):
        at = slice(batch * half, (batch + 1) * half)
        gate = mm(hidden[at, :], pair_s[0])
        up = mm(hidden[at, :], pair_s[1])
        sigmoid = jax.nn.sigmoid(gate)
        swish = gate * sigmoid
        act = (swish * up).astype(BF)
        act_out[at, :] = act
        total[at, :] += mm(act, w_down[...])
        grad = mm(upstream[at, :], w_down[...], NT)
        gate_grad = (grad * up * sigmoid * (1.0 + gate * (1.0 - sigmoid))).astype(BF)
        up_grad = (grad * swish).astype(BF)
        gate_out[at, :] = gate_grad
        up_out[at, :] = up_grad
        back[at, :] += mm(gate_grad, pair_s[0], NT) + mm(up_grad, pair_s[1], NT)

    @pl.when(step == pl.num_programs(0) - 1)
    def _():
        gains = jnp.zeros((1, D), F32)
        for batch in range(2):
            at = slice(batch * half, (batch + 1) * half)
            result[at, :] = total[at, :].astype(BF)
            normed, inverse = unit_rows(middle_grad[at, :])
            grad = back[at, :]
            gains += jnp.sum(grad * normed, axis=0, keepdims=True)
            weighted = grad * gain
            grad = upstream[at, :].astype(F32) + inverse * (
                weighted - normed * jnp.mean(weighted * normed, axis=-1, keepdims=True)
            )
            middle_grad[at, :] = grad
            heads = mm(output[...], grad.astype(BF), NT).astype(BF)
            for g in range(groups):
                send[batch * groups + g] = heads[g * wide_ : (g + 1) * wide_, :]
        gain_grad[...] = gains


def mlp(pairs, where, came, start, gains, upstream, *blocks):
    tokens = start.shape[0]
    width = 512
    steps = FF // width
    whole = lambda shape: pl.BlockSpec(
        shape, lambda i: (0,) * len(shape), pipeline_mode=pl.Buffered(1)
    )
    column = pl.BlockSpec((tokens, width), lambda i: (0, i))
    return pl.pallas_call(
        functools.partial(mlp_kernel, pairs),
        grid=(steps,),
        out_shape=(
            jax.ShapeDtypeStruct((tokens, D), BF),
            jax.ShapeDtypeStruct((tokens, D), BF),
            jax.ShapeDtypeStruct((tokens, D), BF),
            jax.ShapeDtypeStruct((tokens, FF), BF),
            jax.ShapeDtypeStruct((tokens, FF), BF),
            jax.ShapeDtypeStruct((tokens, FF), BF),
            jax.ShapeDtypeStruct((1, D), F32),
            jax.ShapeDtypeStruct((tokens, D), F32),
            jax.ShapeDtypeStruct(came.shape, BF),
        ),
        in_specs=[smem()] + [whole(x.shape) for x in (came, start, gains, upstream, *blocks)],
        out_specs=(
            whole((tokens, D)),
            whole((tokens, D)),
            whole((tokens, D)),
            column,
            column,
            column,
            whole((1, D)),
            whole((tokens, D)),
            whole(came.shape),
        ),
        scratch_shapes=[
            pltpu.VMEM((tokens, D), BF),
            pltpu.VMEM((tokens, D), F32),
            pltpu.VMEM((tokens, D), F32),
            pltpu.VMEM((D, D), BF),
            pltpu.VMEM((2, D, width), BF),
            pltpu.VMEM((width, D), BF),
        ],
        compiler_params=params(44),
        cost_estimate=cost(23),
        name="mlp",
    )(where, came, start, gains, upstream, *blocks)


UPPER, LOWER, ALONG = (1, 3, 2, 0), (2, 3, 1, 0), (1, 3, 2, 0)


def placed(order, value):
    at = jnp.int32(3)
    for place_, here in enumerate(order[:3]):
        at = jnp.where(value == here, place_, at)
    return at


def weight_grads_kernel(
    where,
    hidden,
    gate,
    up,
    act,
    upstream,
    attended,
    middle,
    own_u,
    own_l,
    other_u,
    other_l,
    wide_s,
    tall_s,
    out_s,
):
    core, chip, z = where[0], where[1], where[2]
    sides = ((own_u, own_l, core), (other_u, other_l, 1 - core))

    def rows_of(k, m):
        return pl.ds(aligned((z ^ m) * 192 + (chip ^ k) * 48), 48)

    def chunk(c, _):
        at = pl.ds(aligned(c * 256, 256), 256)
        wide_s[0] = mm(hidden[...], gate[:, at], TN).astype(BF)
        wide_s[1] = mm(hidden[...], up[:, at], TN).astype(BF)
        tall = mm(act[:, at], upstream[...], TN).astype(BF)
        tall_s[0] = tall[:, :384]
        tall_s[1] = tall[:, 384:]

        def put(which, ks, begin):
            for side in sides:
                for i, m in enumerate(ALONG):
                    for n, k in enumerate(ks):
                        block = wide_s[side[2], rows_of(k, m), :]
                        for j in range(2):
                            to = pl.ds(aligned((2 * c + j) * 48 - begin), 48)
                            side[which][n, i, to, :] = block[:, j * 128 : (j + 1) * 128]

        @pl.when(c < 7)
        def _():
            put(0, UPPER, 0)

        @pl.when(c == 7)
        def _():
            put(1, LOWER, CUT)

        i = placed(ALONG, (c // 2) ^ z)
        for _, lower, half in sides:
            for b in range(2):
                n = placed(LOWER, (lax.rem(c, 2) * 2 + b) ^ chip)
                block = tall_s[half, b * 128 : (b + 1) * 128, :]
                for j in range(3):
                    begin = 768 + j * 128 - CUT
                    lower[n, i, begin : begin + 128, :] = block[:, j * 128 : (j + 1) * 128]
        return 0

    lax.fori_loop(0, FF // 256, chunk, 0)
    square = mm(attended[...], middle[...].astype(BF), TN).astype(BF)
    out_s[0] = square[:, :384]
    out_s[1] = square[:, 384:]
    for _, lower, half in sides:
        for i, m in enumerate(ALONG):
            for n, k in enumerate(LOWER):
                block = out_s[half, rows_of(k, m), :]
                for j in range(3):
                    begin = 1152 + j * 48 - CUT
                    lower[n, i, begin : begin + 48, :] = block[:, j * 128 : (j + 1) * 128]


def weight_grads(where, *operands):
    upper = jax.ShapeDtypeStruct((4, 4, CUT, 128), BF)
    lower = jax.ShapeDtypeStruct((4, 4, 1296 - CUT, 128), BF)
    return pl.pallas_call(
        weight_grads_kernel,
        out_shape=(upper, lower) * 2,
        in_specs=[smem()] + [vmem()] * 7,
        out_specs=(vmem(),) * 4,
        scratch_shapes=[
            pltpu.VMEM((2, D, 256), BF),
            pltpu.VMEM((2, 256, 384), BF),
            pltpu.VMEM((2, D, 384), BF),
        ],
        compiler_params=params(60),
        cost_estimate=cost(15),
        name="weight_grads",
    )(where, *operands)


def back_kernel(
    where,
    came_a,
    came_b,
    hidden,
    start,
    middle,
    joined,
    lookup,
    gain,
    second_gain,
    embed,
    target,
    token_grad,
    send,
    own,
    other,
    df_s,
    half_s,
    look_s,
    gain_s,
):
    core, chip, z = where[0], where[1], where[2]
    widths = [ref.shape[1] // 3 for ref in (came_a, came_b)]
    groups = D // sum(widths)
    rows = came_a.shape[2]
    tokens = 2 * rows
    for i in range(tokens // 128):
        batch, lanes = divmod(i * 128, rows)
        lanes = slice(lanes, lanes + 128)
        parts = [
            (swap(ref[batch * groups + g, :, lanes]), w)
            for g in range(groups)
            for ref, w in zip((came_a, came_b), widths)
        ]
        for t in range(3):
            df_s[i * 128 : (i + 1) * 128, t * D : (t + 1) * D] = jnp.concatenate(
                [part[:, t * w : (t + 1) * w] for part, w in parts], axis=1
            )

    def kind(t, _):
        grad = mm(hidden[...], df_s[:, pl.ds(aligned(t * D, 128), D)], TN).astype(BF)
        half_s[0] = grad[:, :384]
        half_s[1] = grad[:, 384:]
        for out, half in ((own, core), (other, 1 - core)):
            for m in range(4):
                zz = z ^ m
                for k in range(4):
                    block = half_s[half, pl.ds(aligned(zz * 192 + (chip ^ k) * 48), 48), :]
                    for j in range(3):
                        to = pl.ds(aligned((t * 3 + j) * 48), 48)
                        out[k, m, to, :] = block[:, j * 128 : (j + 1) * 128]
        return 0

    lax.fori_loop(0, 3, kind, 0)

    gains = jnp.zeros((1, D), F32)
    lows = []
    for batch in range(2):
        at = slice(batch * rows, (batch + 1) * rows)
        grad = mm(df_s[at, :], joined[...], NT)
        normed, inverse = unit_rows(start[at, :])
        gains += jnp.sum(grad * normed, axis=0, keepdims=True)
        weighted = grad * gain[0:1, :]
        grad = middle[at, :] + inverse * (
            weighted - normed * jnp.mean(weighted * normed, axis=-1, keepdims=True)
        )
        token_grad[at, :] = grad
        lows.append(grad.astype(BF))
    low = jnp.concatenate(lows, axis=0)
    look = mm(embed[...], low, TN).astype(BF)
    for half in range(2):
        for j in range(3):
            begin = half * 384 + j * 128
            look_s[half, j] = look[:, begin : begin + 128]
    for half, row in enumerate((gains, second_gain[...])):
        parts = [row[:, j * 128 : (j + 1) * 128] for j in range(6)]
        gain_s[half] = jnp.concatenate(parts + [jnp.zeros((42, 128), F32)], axis=0).astype(BF)
    for out, half in ((own, core), (other, 1 - core)):
        for m in range(4):
            zz = z ^ m
            for k in range(4):
                yx = chip ^ k

                @pl.when(yx < 3)
                def _():
                    out[k, m, 432:480, :] = look_s[
                        half, lax.rem(yx, 3), pl.ds(aligned(zz * 48), 48), :
                    ]

                @pl.when(yx == 3)
                def _():
                    out[k, m, 432:480, :] = gain_s[half]

    de = mm(low, lookup[...], NT).astype(BF)
    slots = send.shape[0]
    slot = lax.broadcasted_iota(jnp.int32, (slots, tokens), 0)
    parts = []
    for table in range(2):
        hot = jnp.where(slot == target[table : table + 1, :], 1.0, 0.0).astype(BF)
        parts.append(mm(hot, de))
    send[...] = jnp.concatenate(parts, axis=1).astype(BF)


def back_pass(slots, where, *operands):
    tokens = operands[2].shape[0]
    shape = jax.ShapeDtypeStruct((4, 4, 480, 128), BF)
    return pl.pallas_call(
        back_kernel,
        out_shape=(
            jax.ShapeDtypeStruct((tokens, D), F32),
            jax.ShapeDtypeStruct((slots, 2 * E), BF),
            shape,
            shape,
        ),
        in_specs=[smem()] + [vmem()] * 11,
        out_specs=(vmem(),) * 4,
        scratch_shapes=[
            pltpu.VMEM((tokens, 3 * D), BF),
            pltpu.VMEM((2, D, 384), BF),
            pltpu.VMEM((2, 3, E, 128), BF),
            pltpu.VMEM((2, 48, 128), BF),
        ],
        compiler_params=params(60),
        cost_estimate=cost(13),
        name="back",
    )(where, *operands)


def rotate(values, cosines, sines):
    half = values.shape[-1] // 2
    a, b = values[..., :half], values[..., half:]
    c, s = cosines[:, None, :], sines[:, None, :]
    return jnp.concatenate([a * c - b * s, b * c + a * s], axis=-1)


def normalize(rows):
    inverse = lax.rsqrt(jnp.mean(rows * rows, axis=-1, keepdims=True) + epsilon)
    return rows * inverse, inverse


def norm_backward(hidden_grad, normed, inverse, gain):
    weighted = hidden_grad * gain
    return inverse * (weighted - normed * jnp.mean(weighted * normed, axis=-1, keepdims=True))


def local(
    token_embed,
    bigram_ids,
    trigram_ids,
    bigram_table,
    trigram_table,
    block_deal,
    lookup_weight,
    attention_gain,
    joined_weight,
    output_weight,
    feedforward_gain,
    expand_weight,
    contract_weight,
    cotangent,
):
    contexts = lax.axis_size("ctx")
    shards = lax.axis_size("fsdp")
    devices = contexts * shards
    batches, local_rows = token_embed.shape[:2]
    tokens = batches * local_rows
    length = local_rows * contexts
    capacity = max(2, 2 * tokens // devices)
    table_rows = bigram_table.shape[0]
    piece = local_rows // 2
    pieces = length // piece
    pairs = -(-batches * HEADS // contexts)
    while HEADS % pairs:
        pairs += 1
    both = ("ctx", "fsdp")

    ids = jnp.stack([bigram_ids.reshape(-1), trigram_ids.reshape(-1)])
    requests, target_row, target_col = placement(ids, table_rows, devices, capacity)
    asked = exchange(requests, both)
    codes = jnp.stack([asked[:, :capacity].reshape(-1), asked[:, capacity:].reshape(-1)], axis=1)
    got = exchange(
        read_rows(codes.T, bigram_table.T, trigram_table.T).reshape(devices, capacity, 2 * E), both
    ).reshape(devices * capacity, 2 * E)

    lookup = gather_weight(lookup_weight)
    joined = gather_weight(joined_weight)
    output = gather_weight(output_weight)
    gains = gather_gains(jnp.stack([attention_gain, feedforward_gain])).astype(F32)
    first_gain, second_gain = gains[0], gains[1]
    expand = gather_weight(expand_weight)
    contract = gather_weight(contract_weight)

    order = jnp.argmin(
        jnp.abs(block_deal[None, :] - jnp.arange(pieces, dtype=jnp.int32)[:, None]), axis=1
    ).astype(jnp.int32)
    frequency = jnp.exp(-math.log(10000.0) * (2.0 * jnp.arange(HD // 2, dtype=F32) / HD))
    slot = lax.axis_index("ctx") * local_rows + jnp.arange(local_rows, dtype=jnp.int32)
    position = block_deal[slot // piece] * piece + slot % piece
    angles = position.astype(F32)[:, None] * frequency[None, :]
    cosines, sines = jnp.cos(angles), jnp.sin(angles)
    all_angles = jnp.arange(length, dtype=F32)[:, None] * frequency[None, :]
    all_cosines, all_sines = jnp.cos(all_angles), jnp.sin(all_angles)

    slots = jnp.arange(devices * capacity, dtype=jnp.int32)
    hot_b = (target_col[:, 0:1] == slots[None, :]).astype(BF)
    hot_t = (target_col[:, 1:2] == slots[None, :]).astype(BF)
    embedded = (mm(hot_b, got[:, :E]) + mm(hot_t, got[:, E:])).astype(BF)
    start = token_embed.reshape(tokens, D).astype(F32) + mm(embedded, lookup)
    normed_first, inverse_first = normalize(start)
    hidden_first = (normed_first * first_gain).astype(BF)
    projected = mm(hidden_first, joined).reshape(batches, local_rows, 3, HEADS, HD)
    cos_b, sin_b = cosines[None, :, None, :], sines[None, :, None, :]
    turn = lambda x: jnp.concatenate(
        [
            x[..., : HD // 2] * cos_b - x[..., HD // 2 :] * sin_b,
            x[..., HD // 2 :] * cos_b + x[..., : HD // 2] * sin_b,
        ],
        axis=-1,
    )
    qkv = jnp.stack(
        [turn(projected[:, :, 0]), turn(projected[:, :, 1]), projected[:, :, 2]], axis=2
    ).astype(BF)
    qkv = qkv.reshape(batches, local_rows, 3, D)
    rows = exchange(by_head(qkv, contexts, pairs), "ctx").reshape(length, 3 * pairs * HD)
    attended_rows, attended_t, logsum = attend(order, rows, pairs, piece)
    attended = by_token(
        exchange(attended_rows.reshape(contexts, local_rows, pairs * HD), "ctx"), batches, 1, pairs
    ).reshape(tokens, D)
    middle = start + mm(attended, output)
    normed_second, inverse_second = normalize(middle)
    hidden_second = (normed_second * second_gain).astype(BF)
    gate_up = mm(hidden_second, expand)
    gate, up = gate_up[:, :FF], gate_up[:, FF:]
    sigmoid = jax.nn.sigmoid(gate)
    swish = gate * sigmoid
    activated = (swish * up).astype(BF)
    result = (middle + mm(activated, contract)).astype(BF)

    upstream = cotangent.reshape(tokens, D)
    activated_grad = mm(upstream, contract, NT)
    gate_up_grad = jnp.concatenate(
        [
            activated_grad * up * sigmoid * (1.0 + gate * (1.0 - sigmoid)),
            activated_grad * swish,
        ],
        axis=-1,
    ).astype(BF)
    hidden_second_grad = mm(gate_up_grad, expand, NT)
    second_gain_term = jnp.sum(hidden_second_grad * normed_second, axis=0)
    middle_grad = upstream.astype(F32) + norm_backward(
        hidden_second_grad, normed_second, inverse_second, second_gain
    )
    middle_low = middle_grad.astype(BF)
    attended_grad = mm(middle_low, output, NT).astype(BF)
    grad_rows = exchange(
        by_head(attended_grad.reshape(batches, local_rows, 1, D), contexts, pairs), "ctx"
    ).reshape(length, pairs * HD)
    contract_term = mm(activated, upstream, TN).astype(BF)
    expand_term = mm(hidden_second, gate_up_grad, TN).astype(BF)
    output_term = mm(attended, middle_low, TN).astype(BF)
    contract_grad = reduce_grad(contract_term)
    expand_grad = reduce_grad(expand_term)
    output_grad = reduce_grad(output_term)

    grad_rows = attend_grad(
        order,
        rows,
        grad_rows,
        attended_t,
        logsum,
        all_cosines,
        all_sines,
        all_cosines.T,
        all_sines.T,
        pairs,
        piece,
    )
    joined_local = by_token(
        exchange(grad_rows.reshape(contexts, local_rows, 3 * pairs * HD), "ctx"), batches, 3, pairs
    ).reshape(tokens, 3 * D)
    joined_grad = reduce_grad(mm(hidden_first, joined_local, TN).astype(BF))
    hidden_first_grad = mm(joined_local, joined, NT)
    first_gain_term = jnp.sum(hidden_first_grad * normed_first, axis=0)
    start_grad = middle_grad + norm_backward(
        hidden_first_grad, normed_first, inverse_first, first_gain
    )
    start_low = start_grad.astype(BF)
    lookup_grad = reduce_grad(mm(embedded, start_low, TN).astype(BF))
    embed_grad = mm(start_low, lookup, NT).astype(BF)
    give_b = (target_row[0:1, :] == slots[:, None]).astype(BF)
    give_t = (target_row[1:2, :] == slots[:, None]).astype(BF)
    send = jnp.concatenate([mm(give_b, embed_grad), mm(give_t, embed_grad)], axis=1).astype(BF)
    arrived = exchange(send.reshape(devices, capacity, 2 * E), both)
    bigram_grad, trigram_grad = add_rows(
        codes, arrived.reshape(devices * capacity, 2 * E), table_rows
    )
    gain_terms = lax.psum(jnp.stack([first_gain_term, second_gain_term]), both)
    gain_share = lax.dynamic_slice_in_dim(
        gain_terms, lax.axis_index("fsdp") * (D // shards), D // shards, axis=1
    )
    return (
        result.reshape(batches, local_rows, D),
        start_grad.reshape(batches, local_rows, D),
        bigram_grad.T,
        trigram_grad.T,
        lookup_grad,
        gain_share[0],
        joined_grad,
        output_grad,
        gain_share[1],
        expand_grad,
        contract_grad,
    )


def local_packed(
    token_embed,
    bigram_ids,
    trigram_ids,
    bigram_table,
    trigram_table,
    block_deal,
    lookup_weight,
    attention_gain,
    joined_weight,
    output_weight,
    feedforward_gain,
    expand_weight,
    contract_weight,
    cotangent,
):
    contexts = lax.axis_size("ctx")
    shards = lax.axis_size("fsdp")
    devices = contexts * shards
    batches, local_rows = token_embed.shape[:2]
    tokens = batches * local_rows
    length = local_rows * contexts
    capacity = max(2, 2 * tokens // devices)
    table_rows = bigram_table.shape[0]
    piece = local_rows // 2
    pieces = length // piece
    pairs = -(-batches * HEADS // contexts)
    while HEADS % pairs:
        pairs += 1
    both = ("ctx", "fsdp")


    core, chip, z = place()
    where = jnp.stack([core, chip, z]).astype(jnp.int32)
    ids = jnp.stack([bigram_ids.reshape(-1), trigram_ids.reshape(-1)])
    requests, target_row, target_col = placement(ids, table_rows, devices, capacity)
    asked = exchange(requests, both)
    gain_rows = jnp.pad(jnp.stack([attention_gain, feedforward_gain]), ((0, 14), (0, 192)))
    first, second = pack_weights(
        after(where, requests),
        joined_weight,
        output_weight,
        lookup_weight,
        gain_rows,
        expand_weight,
        contract_weight,
    )
    along = spread_fsdp(first)
    column = jnp.stack([p[:144] for p in along])
    pieces_z = along
    near = [over_ctx(column, 2), over_ctx(column, 4)]
    codes = jnp.stack([asked[:, :capacity].reshape(-1), asked[:, capacity:].reshape(-1)])
    answer = read_rows(
        after(codes, column), in_hbm(bigram_table.T), in_hbm(trigram_table.T)
    )
    ready = after(second, column)
    early = [along_fsdp(ready, k) for k in (1, 3)]
    answer, near, early = lax.optimization_barrier((answer, near, early))
    got = exchange(answer.reshape(devices, capacity, 2 * E), both)
    answer, column = lax.optimization_barrier((answer, column))
    last = over_ctx(column, 6)
    last, near, pieces_z, early = lax.optimization_barrier((last, near, pieces_z, early))
    tail = jnp.stack([p[144:] for p in pieces_z])
    first_own = [column, *near, last]
    first_other = [over_ctx(block, 1) for block in first_own]
    first_blocks = (*first_own, *first_other, tail, over_ctx(tail, 1))
    three = [second, early[1], early[0]]
    near = [
        over_ctx(jnp.stack([block[:CUT] for block in three]), 2),
        over_ctx(jnp.stack([block[CUT:] for block in three]), 4),
    ]
    got, ready = lax.optimization_barrier((got, ready))
    late = along_fsdp(ready, 2)
    got = got.reshape(devices * capacity, 2 * E)

    order = jnp.sum(
        jnp.where(
            block_deal[None, :] == jnp.arange(pieces, dtype=jnp.int32)[:, None],
            jnp.arange(pieces, dtype=jnp.int32)[None, :],
            0,
        ),
        axis=1,
    )
    starts = lax.dynamic_slice_in_dim(block_deal, lax.axis_index("ctx") * 2, 2)
    frequency = jnp.exp(-math.log(10000.0) * (2.0 * jnp.arange(HD // 2, dtype=F32) / HD))
    angles = frequency[:, None] * jnp.arange(length, dtype=F32)[None, :]
    cos_t, sin_t = lax.optimization_barrier((jnp.cos(angles), jnp.sin(angles)))

    start, embedded, hidden_first, sent, joined, lookup, gains = front(
        pairs,
        contexts,
        where,
        starts,
        got,
        target_col,
        token_embed.reshape(tokens, D),
        cos_t,
        sin_t,
        *first_blocks,
    )
    sent, near, late = lax.optimization_barrier((sent, near, late))
    near_late = [over_ctx(late[:CUT], 2), over_ctx(late[CUT:], 4)]
    rows = exchange(sent, "ctx")
    own_blocks = [three[0], three[1], late, three[2]]
    near_x, near_y = (
        jnp.stack([*[block[cut] for block in own_blocks], part[0], part[1], last, part[2]]).reshape(
            2, 4, -1, 128
        )
        for cut, part, last in zip((slice(CUT), slice(CUT, None)), near, near_late)
    )
    rows, near_x, near_y = lax.optimization_barrier((rows, near_x, near_y))
    far_y, far_x = over_ctx(near_x, 4), over_ctx(near_y, 2)
    others = [over_ctx(near_x, 1), over_ctx(near_y, 1)]
    attended_rows, attended_t, logsum = attend_short(order, rows, pairs, piece)
    came = exchange(attended_rows, "ctx")
    far_y, far_x = after((far_y, far_x), attended_rows)
    others += [over_ctx(far_y, 1), over_ctx(far_x, 1)]
    upstream = cotangent.reshape(tokens, D)
    (
        result,
        hidden_second,
        attended,
        activated,
        gate_grad,
        up_grad,
        second_gain_term,
        middle_grad,
        sent,
    ) = mlp(pairs, where, came, start, gains, upstream, near_x, near_y, far_y, far_x, *others)

    grad_rows = exchange(sent, "ctx")
    own_u, own_l, other_u, other_l = weight_grads(
        where, hidden_second, gate_grad, up_grad, activated, upstream, attended, middle_grad
    )
    other_u, other_l = after((other_u, other_l), grad_rows)
    core_u, core_l = over_ctx(other_u, 1), over_ctx(other_l, 1)
    part = functools.partial(attend_grad_short, order)
    shared = (attended_t, logsum, cos_t, sin_t, pairs, piece)
    grad_a = part(rows, grad_rows, *shared, 0, 1)
    came_a = exchange(grad_a, "ctx")
    core_u, core_l = after((core_u, core_l), grad_a)
    near_u = add_all(own_u[:2], core_u[:2]).astype(BF)
    near_l = add_all(own_l[:2], core_l[:2]).astype(BF)
    from_x, from_y = over_ctx(near_u, 2), over_ctx(near_l, 4)
    grad_b = part(after(rows, near_u, near_l), grad_rows, *shared, 1, pairs - 1)
    grad_b, came_a, from_x, from_y = lax.optimization_barrier((grad_b, came_a, from_x, from_y))
    far_u = add_all(own_u[2], core_u[2], from_x[1]).astype(BF)
    far_l = add_all(own_l[2], core_l[2], from_y[1]).astype(BF)
    came_b = exchange(grad_b, "ctx")
    came_b, far_u, far_l = lax.optimization_barrier((came_b, far_u, far_l))
    from_far = [over_ctx(far_u, 4), over_ctx(far_l, 2)]
    start_grad, send, own_j, other_j = back_pass(
        devices * capacity,
        where,
        came_a,
        came_b,
        hidden_first,
        start,
        middle_grad,
        joined,
        lookup,
        gains,
        second_gain_term,
        embedded,
        target_row,
    )
    from_core = over_ctx(other_j, 1)
    send, from_far = lax.optimization_barrier((send, from_far))
    sums_u = add_all(own_u[3], core_u[3], from_x[0], from_far[0]).astype(BF)
    sums_l = add_all(own_l[3], core_l[3], from_y[0], from_far[1]).astype(BF)
    from_z = over_fsdp(jnp.concatenate([sums_u[:2], sums_l[:2]], axis=1), 1)
    total_m = jnp.concatenate([sums_u[2:], sums_l[2:]], axis=1)
    arrived = exchange(send.reshape(devices, capacity, 2 * E), both)
    half_j = add_cores(own_j, from_core)
    from_chips = to_chips(half_j)
    from_z, kept = lax.optimization_barrier((from_z, half_j[0]))
    near_m, far_m = add_blocks(total_m[1], [from_z[0]]), add_blocks(total_m[0], [from_z[1]])
    from_z = over_fsdp(far_m, 2)
    total_j = add_blocks(kept, from_chips)
    from_fsdp = [over_fsdp(total_j[m], m) for m in (1, 2, 3)]
    from_z, kept = lax.optimization_barrier((from_z, total_j[0]))
    piece_m = add_blocks(near_m, [from_z])
    every_m = [over_ctx(piece_m, 2 * k) for k in (1, 2)]
    late_codes, kept, piece_m = lax.optimization_barrier((codes.T, kept, piece_m))
    bigram_grad, trigram_grad = add_rows(
        late_codes, arrived.reshape(devices * capacity, 2 * E), table_rows
    )
    bigram_grad, from_fsdp, every_m = lax.optimization_barrier((bigram_grad, from_fsdp, every_m))
    piece_j = add_blocks(kept, from_fsdp)
    every_j = to_chips([piece_j] * 4)
    piece_j, piece_m = lax.optimization_barrier((piece_j, piece_m))
    every_m.append(over_ctx(piece_m, 6))
    every_m, every_j = lax.optimization_barrier((every_m, every_j))
    blocks_m = jnp.stack([piece_m] + every_m)
    other_m = over_ctx(blocks_m, 1)
    blocks_j = jnp.stack([piece_j] + every_j)
    other_j = over_ctx(blocks_j, 1)
    expand_grad, contract_grad, output_grad = unpack_second(where, blocks_m, other_m)
    joined_grad, lookup_grad, gain_grads = unpack_first(where, blocks_j, other_j)
    gain_share = lax.dynamic_slice_in_dim(
        gain_grads[:, :6].reshape(2, D), z * (D // shards), D // shards, axis=1
    )
    return (
        result.reshape(batches, local_rows, D),
        start_grad.reshape(batches, local_rows, D),
        bigram_grad.T,
        trigram_grad.T,
        lookup_grad,
        gain_share[0],
        joined_grad,
        output_grad,
        gain_share[1],
        expand_grad,
        contract_grad,
    )


def solution(mesh):
    fits = mesh.shape["ctx"] == 8 and mesh.shape["fsdp"] == 4
    return jax.shard_map(
        local_packed if fits else local,
        mesh=mesh,
        in_specs=(
            P("fsdp", "ctx", None),
            P("fsdp", "ctx"),
            P("fsdp", "ctx"),
            P(("ctx", "fsdp"), None),
            P(("ctx", "fsdp"), None),
            P(),
            P("fsdp", None),
            P("fsdp"),
            P("fsdp", None),
            P("fsdp", None),
            P("fsdp"),
            P("fsdp", None),
            P("fsdp", None),
            P("fsdp", "ctx", None),
        ),
        out_specs=(
            P("fsdp", "ctx", None),
            P("fsdp", "ctx", None),
            P(("ctx", "fsdp"), None),
            P(("ctx", "fsdp"), None),
            P("fsdp", None),
            P("fsdp"),
            P("fsdp", None),
            P("fsdp", None),
            P("fsdp"),
            P("fsdp", None),
            P("fsdp", None),
        ),
        check_vma=False,
    )
```

```python
import functools
import math

import jax
import jax.numpy as jnp
from jax import lax
from jax.experimental import pallas as pl
from jax.experimental.pallas import tpu as pltpu
from jax.sharding import PartitionSpec as P

D = 768
HEADS = 12
HD = 64
FF = 2048
E = 192
ABLK = 256
BF = jnp.bfloat16
F32 = jnp.float32

epsilon = 1e-05
NT = (((1,), (1,)), ((), ()))
NN = (((1,), (0,)), ((), ()))
TN = (((0,), (0,)), ((), ()))


def mm(a, b, dims=NN):
    return lax.dot_general(a, b, dims, preferred_element_type=F32)


def eye(n):
    rows = lax.broadcasted_iota(jnp.int32, (n, n), 0)
    return jnp.where(rows == lax.broadcasted_iota(jnp.int32, (n, n), 1), 1.0, 0.0).astype(BF)


def vmem():
    return pl.BlockSpec(memory_space=pltpu.VMEM)


def smem():
    return pl.BlockSpec(memory_space=pltpu.SMEM)


def params(megabytes, **kw):
    return pltpu.CompilerParams(vmem_limit_bytes=megabytes << 20, **kw)


def cost(microseconds):
    return pl.CostEstimate(
        flops=int(microseconds * 6e8), bytes_accessed=int(microseconds * 2.5e6), transcendentals=0
    )


def in_hbm(value):
    return pltpu.with_memory_space_constraint(value, pltpu.HBM)


def after(value, *others):
    return lax.optimization_barrier((value, others))[0]


def placement_kernel(capacity, owner_row, owner_col, local_row, requests, target_row, target_col):
    tokens = owner_row.shape[1]
    devices = requests.shape[0]
    for table in range(2):
        own_r = owner_row[table : table + 1, :]
        own_c = owner_col[:, table : table + 1]
        t_row = lax.broadcasted_iota(jnp.int32, (tokens, tokens), 0)
        t_col = lax.broadcasted_iota(jnp.int32, (tokens, tokens), 1)
        same = own_c == own_r
        rank_r = jnp.sum(jnp.where(same & (t_row < t_col), 1.0, 0.0), axis=0, keepdims=True)
        rank_c = jnp.sum(jnp.where(same & (t_col < t_row), 1.0, 0.0), axis=1, keepdims=True)
        rank_r = rank_r.astype(jnp.int32)
        rank_c = rank_c.astype(jnp.int32)
        target_row[table : table + 1, :] = own_r * capacity + rank_r
        target_col[:, table : table + 1] = own_c * capacity + rank_c
        device = lax.broadcasted_iota(jnp.int32, (devices, tokens), 0)
        owned = device == own_r
        row = local_row[table : table + 1, :]
        high = jnp.where(owned, (row >> 7).astype(F32), 0.0).astype(BF)
        low = jnp.where(owned, (row & 127).astype(F32), 0.0).astype(BF)
        one = jnp.where(owned, 1.0, 0.0).astype(BF)
        slot = lax.broadcasted_iota(jnp.int32, (tokens, capacity), 1)
        ranked = jnp.where(slot == rank_c, 1.0, 0.0).astype(BF)
        code = 128.0 * mm(high, ranked) + mm(low, ranked) + mm(one, ranked)
        requests[:, table * capacity : (table + 1) * capacity] = code.astype(jnp.int32)


def placement(ids, table_rows, devices, capacity):
    tokens = ids.shape[1]
    owner = ids // table_rows
    local_row = ids - owner * table_rows
    return pl.pallas_call(
        functools.partial(placement_kernel, capacity),
        out_shape=(
            jax.ShapeDtypeStruct((devices, 2 * capacity), jnp.int32),
            jax.ShapeDtypeStruct((2, tokens), jnp.int32),
            jax.ShapeDtypeStruct((tokens, 2), jnp.int32),
        ),
        in_specs=[vmem()] * 3,
        out_specs=(vmem(),) * 3,
        compiler_params=params(32),
        cost_estimate=cost(2),
        name="placement",
    )(owner, owner.T, local_row)


def wide(ref, columns, table):
    ref[table] = jnp.broadcast_to(columns[:, table : table + 1].astype(F32), ref.shape[1:])


def onehot_block(ref, table, base, width):
    lane = lax.broadcasted_iota(jnp.int32, ref.shape[1:], 1).astype(F32)
    parts = []
    for j in range(width // 128):
        hit = ref[table] == lane + (base + 128 * j + 1).astype(F32)
        parts.append(jnp.where(hit, 1.0, 0.0).astype(BF))
    return jnp.concatenate(parts, axis=1)


def swap(value):
    return mm(eye(value.shape[1]), value, NT).astype(BF)


def read_rows_kernel(codes, bigram, trigram, out, total):
    step = pl.program_id(0)
    width = bigram.shape[1]
    slots = codes.shape[1]

    @pl.when(step == 0)
    def _():
        total[...] = jnp.zeros_like(total)

    row = lax.broadcasted_iota(jnp.int32, (width, slots), 0) + (step * width + 1)
    for table, source in enumerate((bigram, trigram)):
        hot = jnp.where(row == codes[table : table + 1, :], 1.0, 0.0).astype(BF)
        total[table * E : (table + 1) * E, :] += mm(source[...], hot)

    @pl.when(step == pl.num_programs(0) - 1)
    def _():
        for begin in range(0, slots, 128):
            out[begin : begin + 128, :] = swap(total[:, begin : begin + 128].astype(BF))


def table_block(table_rows):
    for width in (2560, 1280, 640, 512, 256, 128):
        if table_rows % width == 0:
            return width
    return table_rows


def read_rows(codes, bigram_t, trigram_t):
    slots = codes.shape[1]
    rows = bigram_t.shape[1]
    width = table_block(rows)
    table = pl.BlockSpec((E, width), lambda i: (0, i))
    return pl.pallas_call(
        read_rows_kernel,
        grid=(rows // width,),
        out_shape=jax.ShapeDtypeStruct((slots, 2 * E), BF),
        in_specs=[pl.BlockSpec((2, slots), lambda i: (0, 0)), table, table],
        out_specs=pl.BlockSpec((slots, 2 * E), lambda i: (0, 0)),
        scratch_shapes=[pltpu.VMEM((2 * E, slots), F32)],
        compiler_params=params(40),
        cost_estimate=cost(17),
        name="read_rows",
    )(codes, bigram_t, trigram_t)


def add_rows_kernel(codes, grads, bigram, trigram, spread, turned):
    step = pl.program_id(0)
    width = bigram.shape[1]

    @pl.when(step == 0)
    def _():
        for table in range(2):
            wide(spread, codes, table)
        turned[...] = mm(eye(2 * E), grads[...], NT).astype(BF)

    for table, out in enumerate((bigram, trigram)):
        hot = onehot_block(spread, table, step * width, width)
        out[...] = mm(turned[table * E : (table + 1) * E, :], hot)


def add_rows(codes, grads, rows):
    slots = codes.shape[0]
    width = table_block(rows)
    table = pl.BlockSpec((E, width), lambda i: (0, i))
    shape = jax.ShapeDtypeStruct((E, rows), F32)
    return pl.pallas_call(
        add_rows_kernel,
        grid=(rows // width,),
        out_shape=(shape, shape),
        in_specs=[
            pl.BlockSpec((slots, 2), lambda i: (0, 0)),
            pl.BlockSpec((slots, 2 * E), lambda i: (0, 0)),
        ],
        out_specs=(table, table),
        scratch_shapes=[pltpu.VMEM((2, slots, 128), F32), pltpu.VMEM((2 * E, slots), BF)],
        compiler_params=params(32),
        cost_estimate=cost(14),
        name="add_rows",
    )(codes, grads)


def add_table_kernel(table, codes, grads, out, spread, turned):
    step = pl.program_id(0)
    width = out.shape[1]

    @pl.when(step == 0)
    def _():
        wide(spread, codes, table)
        row = lax.broadcasted_iota(jnp.int32, (E, 2 * E), 0) + table * E
        column = lax.broadcasted_iota(jnp.int32, (E, 2 * E), 1)
        pick = jnp.where(row == column, 1.0, 0.0).astype(BF)
        turned[...] = mm(pick, grads[...], NT).astype(BF)

    out[...] = mm(turned[...], onehot_block(spread, table, step * width, width))


def add_table(table, codes, grads, rows):
    slots = codes.shape[0]
    width = table_block(rows)
    return pl.pallas_call(
        functools.partial(add_table_kernel, table),
        grid=(rows // width,),
        out_shape=jax.ShapeDtypeStruct((E, rows), F32),
        in_specs=[
            pl.BlockSpec((slots, 2), lambda i: (0, 0)),
            pl.BlockSpec((slots, 2 * E), lambda i: (0, 0)),
        ],
        out_specs=pl.BlockSpec((E, width), lambda i: (0, i)),
        scratch_shapes=[pltpu.VMEM((2, slots, 128), F32), pltpu.VMEM((E, slots), BF)],
        compiler_params=params(40),
        cost_estimate=cost(7),
        name=f"add_table_{table}",
    )(codes, grads)


def attend_kernel(pairs, piece, order, rows, out, attended_t, logsum, q_s, k_s, vt_s, s_s):
    length = rows.shape[0]
    blocks = length // ABLK
    per_block = ABLK // piece
    width = pairs * HD
    identity = eye(HD)

    def sort(j, _):
        block = rows[pl.ds(pl.multiple_of(order[j] * piece, piece), piece), :]
        to = pl.ds(pl.multiple_of(j * piece, piece), piece)
        for p in range(pairs):
            q = block[:, p * HD : (p + 1) * HD]
            q_s[p, to, :] = (q.astype(F32) * HD ** (-0.5)).astype(BF)
            k_s[p, to, :] = block[:, width + p * HD : width + (p + 1) * HD]
            v = block[:, 2 * width + p * HD : 2 * width + (p + 1) * HD]
            vt_s[p, :, to] = mm(identity, v, NT).astype(BF)
        return 0

    lax.fori_loop(0, length // piece, sort, 0)

    for p in range(pairs):

        def one(i, _):
            at = pl.ds(pl.multiple_of(i * ABLK, ABLK), ABLK)
            queries = q_s[p, at, :]

            def score(j, peak):
                to = pl.ds(pl.multiple_of(j * ABLK, ABLK), ABLK)
                s = mm(k_s[p, to, :], queries, NT)
                s_s[to, :] = s
                return jnp.maximum(peak, jnp.max(s, axis=0, keepdims=True))

            peak = lax.fori_loop(0, i + 1, score, jnp.full((1, ABLK), -jnp.inf, F32))

            def raise_(j, total):
                to = pl.ds(pl.multiple_of(j * ABLK, ABLK), ABLK)
                e = jnp.exp(s_s[to, :] - peak)
                s_s[to, :] = e
                return total + jnp.sum(e, axis=0, keepdims=True)

            total = lax.fori_loop(0, i + 1, raise_, jnp.zeros((1, ABLK), F32))
            scale = 1.0 / total

            def weigh(j, o):
                to = pl.ds(pl.multiple_of(j * ABLK, ABLK), ABLK)
                probs = (s_s[to, :] * scale).astype(BF)
                return o + mm(vt_s[p, :, to], probs)

            o = lax.fori_loop(0, i + 1, weigh, jnp.zeros((HD, ABLK), F32))
            attended_t[p, :, at] = o
            logsum[p, :, at] = peak + jnp.log(total)
            o = o.T.astype(BF)
            for h in range(per_block):
                to = pl.ds(pl.multiple_of(order[per_block * i + h] * piece, piece), piece)
                out[to, p * HD : (p + 1) * HD] = o[h * piece : (h + 1) * piece, :]
            return 0

        lax.fori_loop(0, blocks, one, 0)


def attend(order, rows, pairs, piece):
    length = rows.shape[0]
    return pl.pallas_call(
        functools.partial(attend_kernel, pairs, piece),
        out_shape=(
            jax.ShapeDtypeStruct((length, pairs * HD), BF),
            jax.ShapeDtypeStruct((pairs, HD, length), F32),
            jax.ShapeDtypeStruct((pairs, 1, length), F32),
        ),
        in_specs=[smem(), vmem()],
        out_specs=(vmem(),) * 3,
        scratch_shapes=[
            pltpu.VMEM((pairs, length, HD), BF),
            pltpu.VMEM((pairs, length, HD), BF),
            pltpu.VMEM((pairs, HD, length), BF),
            pltpu.VMEM((length, ABLK), F32),
        ],
        compiler_params=params(48),
        cost_estimate=cost(50),
        name="attend",
    )(order, rows)


def attend_grad_kernel(
    pairs,
    piece,
    order,
    rows,
    grads,
    attended_t,
    logsum,
    cos,
    sin,
    cos_t,
    sin_t,
    out,
    q_s,
    k_s,
    v_s,
    g_s,
    kt_s,
    dq_s,
    dk_s,
    dv_s,
    dk_o,
    dv_o,
):
    length = rows.shape[0]
    blocks = length // ABLK
    width = pairs * HD
    half = HD // 2
    scale = HD ** (-0.5)
    identity = eye(HD)

    for p in range(pairs):

        def sort(j, _):
            take = pl.ds(pl.multiple_of(order[j] * piece, piece), piece)
            block = rows[take, :]
            to = pl.ds(pl.multiple_of(j * piece, piece), piece)
            q_s[to, :] = (block[:, p * HD : (p + 1) * HD].astype(F32) * scale).astype(BF)
            k = block[:, width + p * HD : width + (p + 1) * HD]
            k_s[to, :] = k
            kt_s[:, to] = mm(identity, k, NT).astype(BF)
            v_s[to, :] = block[:, 2 * width + p * HD : 2 * width + (p + 1) * HD]
            g_s[to, :] = grads[take, :][:, p * HD : (p + 1) * HD]
            return 0

        lax.fori_loop(0, length // piece, sort, 0)
        dk_s[...] = jnp.zeros_like(dk_s)
        dv_s[...] = jnp.zeros_like(dv_s)

        def one(i, _):
            at = pl.ds(pl.multiple_of(i * ABLK, ABLK), ABLK)
            queries = q_s[at, :]
            grad = g_s[at, :]
            delta = jnp.sum(
                mm(identity, grad, NT) * attended_t[p, :, at], axis=0, keepdims=True
            )
            level = logsum[p, :, at]

            def tile(j, dq):
                to = pl.ds(pl.multiple_of(j * ABLK, ABLK), ABLK)
                probs = jnp.exp(mm(k_s[to, :], queries, NT) - level)
                ds = (probs * (mm(v_s[to, :], grad, NT) - delta)).astype(BF)
                dv_s[to, :] += mm(probs.astype(BF), grad)
                dk_s[to, :] += mm(ds, queries)
                return dq + mm(kt_s[:, to], ds)

            dq = lax.fori_loop(0, i + 1, tile, jnp.zeros((HD, ABLK), F32)) * scale
            c, s = cos_t[:, at], sin_t[:, at]
            a, b = dq[:half, :], dq[half:, :]
            dq = jnp.concatenate([a * c + b * s, b * c - a * s], axis=0)
            dq_s[p, at, :] = dq.T.astype(BF)
            return 0

        lax.fori_loop(0, blocks, one, 0)

        def turn(j, _):
            to = pl.ds(pl.multiple_of(j * ABLK, ABLK), ABLK)
            dk = dk_s[to, :]
            a, b = dk[:, :half], dk[:, half:]
            c, s = cos[to, :], sin[to, :]
            dk_o[p, to, :] = jnp.concatenate([a * c + b * s, b * c - a * s], axis=1).astype(BF)
            dv_o[p, to, :] = dv_s[to, :].astype(BF)
            return 0

        lax.fori_loop(0, blocks, turn, 0)

    def unsort(j, _):
        take = pl.ds(pl.multiple_of(j * piece, piece), piece)
        to = pl.ds(pl.multiple_of(order[j] * piece, piece), piece)
        parts = [ref[p, take, :] for ref in (dq_s, dk_o, dv_o) for p in range(pairs)]
        out[to, :] = jnp.concatenate(parts, axis=1)
        return 0

    lax.fori_loop(0, length // piece, unsort, 0)


def attend_grad(order, rows, grads, attended_t, logsum, cos, sin, cos_t, sin_t, pairs, piece):
    length = rows.shape[0]
    low = pltpu.VMEM((length, HD), BF)
    full = pltpu.VMEM((length, HD), F32)
    each = pltpu.VMEM((pairs, length, HD), BF)
    return pl.pallas_call(
        functools.partial(attend_grad_kernel, pairs, piece),
        out_shape=jax.ShapeDtypeStruct((length, 3 * pairs * HD), BF),
        in_specs=[smem()] + [vmem()] * 8,
        out_specs=vmem(),
        scratch_shapes=[low] * 4 + [pltpu.VMEM((HD, length), BF), each, full, full, each, each],
        compiler_params=params(56),
        cost_estimate=cost(68),
        name="attend_grad",
    )(order, rows, grads, attended_t, logsum, cos, sin, cos_t, sin_t)


def fold_max(peak, tile):
    return jnp.maximum(peak, jnp.max(tile.reshape(-1, 8, tile.shape[1]), axis=0))


def fold_sum(total, tile):
    return total + jnp.sum(tile.reshape(-1, 8, tile.shape[1]), axis=0)


def piece_of(order, j, piece):
    at = order[j]
    return at // 2, pl.ds(pl.multiple_of(lax.rem(at, 2) * piece, piece), piece)


def attend_short_kernel(pairs, piece, order, rows, out, attended_t, logsum, q_s, k_s, v_s, s_s):
    length = rows.shape[0] * rows.shape[2]
    blocks = length // ABLK
    width = pairs * HD

    def sort(j, _):
        device, lanes = piece_of(order, j, piece)
        block = rows[device, :, lanes]
        to = pl.ds(pl.multiple_of(j * piece, piece), piece)
        for p in range(pairs):
            q = block[p * HD : (p + 1) * HD, :]
            q_s[p, :, to] = (q.astype(F32) * HD ** (-0.5)).astype(BF)
            k_s[p, to, :] = swap(block[width + p * HD : width + (p + 1) * HD, :])
            v_s[p, :, to] = block[2 * width + p * HD : 2 * width + (p + 1) * HD, :]
        return 0

    lax.fori_loop(0, length // piece, sort, 0)

    def pair(p, _):
        features = pl.ds(pl.multiple_of(p * HD, HD), HD)
        for i in range(blocks):
            at = slice(i * ABLK, (i + 1) * ABLK)
            queries = q_s[p, :, at]
            peak = jnp.full((8, ABLK), -jnp.inf, F32)
            for j in range(i + 1):
                s = mm(k_s[p, j * ABLK : (j + 1) * ABLK, :], queries)
                s_s[i % 2, j * ABLK : (j + 1) * ABLK, :] = s
                peak = fold_max(peak, s)
            peak = jnp.max(peak, axis=0, keepdims=True)
            total = jnp.zeros((8, ABLK), F32)
            o = jnp.zeros((HD, ABLK), F32)
            for j in range(i + 1):
                e = jnp.exp(s_s[i % 2, j * ABLK : (j + 1) * ABLK, :] - peak)
                total = fold_sum(total, e)
                o += mm(v_s[p, :, j * ABLK : (j + 1) * ABLK], e.astype(BF))
            total = jnp.sum(total, axis=0, keepdims=True)
            o = o * (1.0 / total)
            attended_t[p, :, at] = o
            logsum[p, :, at] = peak + jnp.log(total)
            o = o.astype(BF)
            for h in range(ABLK // piece):
                device, lanes = piece_of(order, ABLK // piece * i + h, piece)
                out[device, features, lanes] = o[:, h * piece : (h + 1) * piece]
        return 0

    lax.fori_loop(0, pairs, pair, 0)


def attend_short(order, rows, pairs, piece):
    contexts, _, tokens = rows.shape
    length = contexts * tokens
    return pl.pallas_call(
        functools.partial(attend_short_kernel, pairs, piece),
        out_shape=(
            jax.ShapeDtypeStruct((contexts, pairs * HD, tokens), BF),
            jax.ShapeDtypeStruct((pairs, HD, length), F32),
            jax.ShapeDtypeStruct((pairs, 1, length), F32),
        ),
        in_specs=[smem(), vmem()],
        out_specs=(vmem(),) * 3,
        scratch_shapes=[
            pltpu.VMEM((pairs, HD, length), BF),
            pltpu.VMEM((pairs, length, HD), BF),
            pltpu.VMEM((pairs, HD, length), BF),
            pltpu.VMEM((2, length, ABLK), F32),
        ],
        compiler_params=params(48),
        cost_estimate=cost(25),
        name="attend",
    )(order, rows)


def attend_grad_short_kernel(
    pairs,
    begin,
    count,
    piece,
    order,
    rows,
    grads,
    attended_t,
    logsum,
    cos_t,
    sin_t,
    out,
    q_s,
    g_s,
    kt_s,
    k_s,
    v_s,
    dk_s,
    dv_s,
):
    length = rows.shape[0] * rows.shape[2]
    blocks = length // ABLK
    width = pairs * HD
    half = HD // 2
    scale = HD ** (-0.5)

    def sort(j, _):
        device, lanes = piece_of(order, j, piece)
        block = rows[device, :, lanes]
        grad = grads[device, :, lanes]
        to = pl.ds(pl.multiple_of(j * piece, piece), piece)
        for p in range(count):
            row = (begin + p) * HD
            q_s[p, :, to] = (block[row : row + HD, :].astype(F32) * scale).astype(BF)
            k = block[width + row : width + row + HD, :]
            kt_s[p, :, to] = k
            k_s[p, to, :] = swap(k)
            v_s[p, to, :] = swap(block[2 * width + row : 2 * width + row + HD, :])
            g_s[p, :, to] = grad[row : row + HD, :]
        return 0

    lax.fori_loop(0, length // piece, sort, 0)

    def turn(x, at):
        c, s = cos_t[:, at], sin_t[:, at]
        a, b = x[:half, :], x[half:, :]
        return jnp.concatenate([a * c + b * s, b * c - a * s], axis=0)

    def pair(p, _):
        def put(kind, i, value):
            features = pl.ds(pl.multiple_of((kind * count + p) * HD, HD), HD)
            value = value.astype(BF)
            for h in range(ABLK // piece):
                device, lanes = piece_of(order, ABLK // piece * i + h, piece)
                out[device, features, lanes] = value[:, h * piece : (h + 1) * piece]

        for i in range(blocks):
            at = slice(i * ABLK, (i + 1) * ABLK)
            queries = q_s[p, :, at]
            grad = g_s[p, :, at]
            delta = jnp.sum(
                grad.astype(F32) * attended_t[begin + p, :, at], axis=0, keepdims=True
            )
            level = logsum[begin + p, :, at]
            dq = jnp.zeros((HD, ABLK), F32)
            for j in range(i, -1, -1):
                to = slice(j * ABLK, (j + 1) * ABLK)
                probs = jnp.exp(mm(k_s[p, to, :], queries) - level)
                ds = (probs * (mm(v_s[p, to, :], grad) - delta)).astype(BF)
                dv = mm(grad, probs.astype(BF), NT)
                dk = mm(queries, ds, NT)
                if i == j:
                    dv_s[:, to] = dv
                    dk_s[:, to] = dk
                else:
                    dv_s[:, to] += dv
                    dk_s[:, to] += dk
                dq += mm(kt_s[p, :, to], ds)
            put(0, i, turn(dq * scale, at))
        for i in range(blocks):
            at = slice(i * ABLK, (i + 1) * ABLK)
            put(1, i, turn(dk_s[:, at], at))
            put(2, i, dv_s[:, at])
        return 0

    lax.fori_loop(0, count, pair, 0)


def attend_grad_short(
    order, rows, grads, attended_t, logsum, cos_t, sin_t, pairs, piece, begin, count
):
    contexts, _, tokens = rows.shape
    length = contexts * tokens
    wide_ = pltpu.VMEM((count, HD, length), BF)
    tall = pltpu.VMEM((count, length, HD), BF)
    full = pltpu.VMEM((HD, length), F32)
    return pl.pallas_call(
        functools.partial(attend_grad_short_kernel, pairs, begin, count, piece),
        out_shape=jax.ShapeDtypeStruct((contexts, 3 * count * HD, tokens), BF),
        in_specs=[smem()] + [vmem()] * 6,
        out_specs=vmem(),
        scratch_shapes=[wide_] * 3 + [tall] * 2 + [full] * 2,
        compiler_params=params(48),
        cost_estimate=cost(14 * count),
        name=f"attend_grad_{begin}",
    )(order, rows, grads, attended_t, logsum, cos_t, sin_t)


def over_ctx(value, mask):
    size = lax.axis_size("ctx")
    return lax.ppermute(value, "ctx", [(i, i ^ mask) for i in range(size)])


def along_fsdp(value, shift):
    size = lax.axis_size("fsdp")
    return lax.ppermute(value, "fsdp", [(i, (i + shift) % size) for i in range(size)])


def by_index(blocks, index):
    if len(blocks) == 1:
        return blocks
    half = len(blocks) // 2
    flip = (index // half) % 2 == 1
    lower = [jnp.where(flip, b, a) for a, b in zip(blocks[:half], blocks[half:])]
    upper = [jnp.where(flip, a, b) for a, b in zip(blocks[:half], blocks[half:])]
    return by_index(lower, index) + by_index(upper, index)


def place():
    ctx = lax.axis_index("ctx")
    return ctx % 2, ctx // 2, lax.axis_index("fsdp")


def gather_weight(shard):
    core, chip, z = place()
    chips = lax.axis_size("ctx") // 2
    shards = lax.axis_size("fsdp")
    rows, columns = shard.shape
    r, half = rows // chips, columns // 2
    mine = lax.dynamic_slice(shard, (chip * r, core * half), (r, half))
    along = [mine] + [along_fsdp(mine, k) for k in range(1, shards)]
    turned = jnp.stack([along[(shards - m) % shards] for m in range(shards)])
    column = lax.dynamic_slice_in_dim(
        jnp.concatenate([turned, turned]), (shards - z) % shards, shards
    )
    blocks = [column] + [over_ctx(column, 2 * k) for k in range(1, chips)]
    own = jnp.stack(by_index(blocks, chip), axis=1).reshape(shards * rows, half)
    other = over_ctx(own, 1)
    return jnp.where(
        core == 0, jnp.concatenate([own, other], axis=1), jnp.concatenate([other, own], axis=1)
    )


def gather_gains(gains):
    _, _, z = place()
    shards = lax.axis_size("fsdp")
    along = [gains] + [along_fsdp(gains, k) for k in range(1, shards)]
    turned = jnp.stack([along[(shards - m) % shards] for m in range(shards)])
    every = lax.dynamic_slice_in_dim(
        jnp.concatenate([turned, turned]), (shards - z) % shards, shards
    )
    return jnp.moveaxis(every, 0, 1).reshape(gains.shape[0], -1)


def reduce_grad(grad):
    core, chip, z = place()
    chips = lax.axis_size("ctx") // 2
    shards = lax.axis_size("fsdp")
    rows, columns = grad.shape[0] // shards, grad.shape[1]
    r, half = rows // chips, columns // 2
    view = grad.reshape(shards, chips, r, columns)

    def columns_of(which):
        return lax.dynamic_slice_in_dim(view, which * half, half, axis=3)

    total = columns_of(core).astype(F32) + over_ctx(columns_of(1 - core), 1).astype(F32)
    low = total.astype(BF)
    sent = [
        over_ctx(lax.dynamic_index_in_dim(low, chip ^ k, 1, keepdims=False), 2 * k)
        for k in range(1, chips)
    ]
    total = lax.dynamic_index_in_dim(low, chip, 1, keepdims=False).astype(F32)
    total = sum((s.astype(F32) for s in sent), total)
    low = total.astype(BF)
    sent = [
        along_fsdp(lax.dynamic_index_in_dim(low, (z + k) % shards, 0, keepdims=False), k)
        for k in range(1, shards)
    ]
    total = lax.dynamic_index_in_dim(low, z, 0, keepdims=False).astype(F32)
    total = sum((s.astype(F32) for s in sent), total)
    piece = total.astype(BF)
    blocks = [piece] + [over_ctx(piece, 2 * k) for k in range(1, chips)]
    own = jnp.stack(by_index(blocks, chip)).reshape(rows, half)
    other = over_ctx(own, 1)
    return jnp.where(
        core == 0, jnp.concatenate([own, other], axis=1), jnp.concatenate([other, own], axis=1)
    ).astype(F32)


def by_head(values, devices, pairs):
    batches, tokens, kinds, _ = values.shape
    groups = HEADS // pairs
    values = values.reshape(batches, tokens, kinds, groups, pairs * HD)
    values = values.transpose(0, 3, 1, 2, 4).reshape(batches * groups, tokens, kinds * pairs * HD)
    spare = devices - batches * groups
    return jnp.pad(values, ((0, spare), (0, 0), (0, 0)))


def by_token(values, batches, kinds, pairs):
    groups = HEADS // pairs
    tokens = values.shape[1]
    values = values[: batches * groups].reshape(batches, groups, tokens, kinds, pairs * HD)
    return values.transpose(0, 2, 3, 1, 4).reshape(batches, tokens, kinds, HEADS * HD)


def exchange(values, axes):
    return lax.all_to_all(values, axes, split_axis=0, concat_axis=0, tiled=True)


def aligned(value, by=16):
    return pl.multiple_of(value, by)


def pack_weights_kernel(
    where, joined, output, lookup, gains, expand, contract, first, second, third
):
    core, chip = where[0], where[1]
    rows = pl.ds(aligned(chip * 48), 48)
    for t in range(3):
        first[t * 48 : (t + 1) * 48, :] = joined[rows, pl.ds(aligned(t * D + core * 384, 128), 384)]
    columns = pl.ds(aligned(core * 384, 128), 384)
    first[144:192, :] = lookup[:, columns]
    first[192:208, :] = gains[...]
    for j in range(16):
        second[j * 48 : (j + 1) * 48, :] = expand[
            rows, pl.ds(aligned(core * FF + j * 128, 128), 128)
        ]
    for j in range(3):
        lanes = pl.ds(aligned(core * 384 + j * 128, 128), 128)
        second[768 + j * 48 : 816 + j * 48, :] = output[rows, lanes]
        third[j * 128 : (j + 1) * 128, :] = contract[pl.ds(aligned(chip * 128), 128), lanes]


def pack_weights(where, *weights):
    return pl.pallas_call(
        pack_weights_kernel,
        out_shape=(
            jax.ShapeDtypeStruct((208, 384), BF),
            jax.ShapeDtypeStruct((912, 128), BF),
            jax.ShapeDtypeStruct((384, 128), BF),
        ),
        in_specs=[smem()] + [vmem()] * 6,
        out_specs=(vmem(),) * 3,
        compiler_params=params(16),
        cost_estimate=cost(2),
        name="pack_weights",
    )(where, *weights)


CUT = 14 * 48
WCUT = 10 * 48


def by_chip(near_x, near_y, far_y, far_x):
    return (
        [near_x.at[0], near_x.at[1], far_y.at[0], far_y.at[1]],
        [near_y.at[0], far_x.at[0], near_y.at[1], far_x.at[1]],
    )


def spread_fsdp(piece):
    along = [piece] + [along_fsdp(piece, k) for k in range(1, 4)]
    return [along[(4 - m) % 4] for m in range(4)]


def add_cores(own, came):
    return [(own[k].astype(F32) + came[k].astype(F32)).astype(BF) for k in range(4)]


def add_blocks(own, came):
    total = own.astype(F32)
    for block in came:
        total = total + block.astype(F32)
    return total.astype(BF)


def to_chips(blocks):
    return [over_ctx(blocks[k], 2 * k) for k in range(1, 4)]


def add_all(*blocks):
    return sum((b.astype(F32) for b in blocks[1:]), blocks[0].astype(F32))


def over_fsdp(value, mask):
    return lax.ppermute(value, "fsdp", [(i, i ^ mask) for i in range(4)])


def unpack_second_kernel(where, own, other, expand, contract, output):
    core, chip = where[0], where[1]
    for k in range(4):
        yx = chip ^ k
        rows = pl.ds(aligned(yx * 48), 48)
        for half in range(2):

            def taken(begin, count):
                part = slice(begin, begin + count)
                return jnp.where(core == half, own[k, part, :].astype(F32), other[k, part, :].astype(F32))

            for j in range(16):
                expand[rows, half * FF + j * 128 : half * FF + (j + 1) * 128] = taken(j * 48, 48)
            for j in range(3):
                to = slice(half * 384 + j * 128, half * 384 + (j + 1) * 128)
                contract[pl.ds(aligned(yx * 128), 128), to] = taken(768 + j * 128, 128)
                output[rows, to] = taken(1152 + j * 48, 48)


def unpack_second(where, own, other):
    return pl.pallas_call(
        unpack_second_kernel,
        out_shape=(
            jax.ShapeDtypeStruct((192, 2 * FF), F32),
            jax.ShapeDtypeStruct((512, D), F32),
            jax.ShapeDtypeStruct((192, D), F32),
        ),
        in_specs=[smem()] + [vmem()] * 2,
        out_specs=(vmem(),) * 3,
        compiler_params=params(24),
        cost_estimate=cost(4),
        name="unpack_second",
    )(where, own, other)


def unpack_first_kernel(where, own, other, joined, lookup, gains):
    core, chip = where[0], where[1]
    for k in range(4):
        yx = chip ^ k
        rows = pl.ds(aligned(yx * 48), 48)
        for half in range(2):

            def taken(begin, count):
                part = slice(begin, begin + count)
                return jnp.where(core == half, own[k, part, :].astype(F32), other[k, part, :].astype(F32))

            for t in range(3):
                for j in range(3):
                    to = t * D + half * 384 + j * 128
                    joined[rows, to : to + 128] = taken((t * 3 + j) * 48, 48)

            @pl.when(yx < 3)
            def _():
                at = pl.ds(aligned(half * 384 + yx * 128, 128), 128)
                lookup[:, at] = taken(432, 48)

            @pl.when(yx == 3)
            def _():
                gains[half] = taken(432, 48)


def unpack_first(where, own, other):
    return pl.pallas_call(
        unpack_first_kernel,
        out_shape=(
            jax.ShapeDtypeStruct((192, 3 * D), F32),
            jax.ShapeDtypeStruct((48, D), F32),
            jax.ShapeDtypeStruct((2, 48, 128), F32),
        ),
        in_specs=[smem()] + [vmem()] * 2,
        out_specs=(vmem(),) * 3,
        compiler_params=params(24),
        cost_estimate=cost(2),
        name="unpack_first",
    )(where, own, other)


def unit_rows(x):
    inverse = lax.rsqrt(jnp.mean(x * x, axis=-1, keepdims=True) + epsilon)
    return x * inverse, inverse


def front_kernel(
    pairs,
    where,
    starts,
    got,
    target,
    token,
    cos_t,
    sin_t,
    *refs,
):
    own_tail, other_tail = refs[8:10]
    start, embed, hidden, send, joined, lookup, gains, t_s, g_s = refs[10:]
    core, chip, z = where[0], where[1], where[2]
    for blocks, tail, half in ((refs[:4], own_tail, core), (refs[4:8], other_tail, 1 - core)):
        for m in range(4):
            zz = lax.rem(z + m, 4)
            for k in range(4):
                rows = pl.ds(aligned(zz * 192 + (chip ^ k) * 48), 48)
                for t in range(3):
                    joined[rows, pl.ds(aligned(t * D + half * 384, 128), 384)] = blocks[k][
                        m, t * 48 : (t + 1) * 48, :
                    ]
            lookup[pl.ds(aligned(zz * 48), 48), pl.ds(aligned(half * 384, 128), 384)] = tail[
                m, 0:48, :
            ]
    for m in range(4):
        g_s[lax.rem(z + m, 4)] = own_tail[m, 48:64, :].astype(F32)
    for row in range(2):
        gains[row : row + 1, :] = jnp.concatenate(
            [g_s[zz, row : row + 1, :192] for zz in range(4)], axis=1
        )
    gain = gains[0:1, :]
    tokens = token.shape[0]
    piece = 128
    per_batch = tokens // 2 // piece
    groups = HEADS // pairs
    wide_ = pairs * HD
    slots = got.shape[0]
    lane = lax.broadcasted_iota(jnp.int32, (piece, 128), 1)
    first_half = lax.rem(lane, HD) < HD // 2

    def block(i, _):
        at = pl.ds(aligned(i * piece, piece), piece)
        goal = target[at, :]
        slot = lax.broadcasted_iota(jnp.int32, (piece, slots), 1)
        parts = []
        for table in range(2):
            hot = jnp.where(goal[:, table : table + 1] == slot, 1.0, 0.0).astype(BF)
            parts.append(mm(hot, got[:, table * E : (table + 1) * E]))
        rows = (parts[0] + parts[1]).astype(BF)
        embed[at, :] = rows
        x = token[at, :].astype(F32) + mm(rows, lookup[...])
        start[at, :] = x
        normed, _ = unit_rows(x)
        low = (normed * gain).astype(BF)
        hidden[at, :] = low
        projected = mm(low, joined[...])
        begin = pl.ds(aligned(starts[lax.rem(i, per_batch)] * piece, piece), piece)
        c = cos_t[:, begin].T
        s = sin_t[:, begin].T
        c = jnp.concatenate([c, c, c, c], axis=1)
        s = jnp.concatenate([-s, s, -s, s], axis=1)
        turned = []
        for j in range(12):
            v = projected[:, j * 128 : (j + 1) * 128]
            swapped = jnp.where(first_half, pltpu.roll(v, 96, 1), pltpu.roll(v, 32, 1))
            turned.append((v * c + swapped * s).astype(BF))
        for j in range(12, 18):
            turned.append(projected[:, j * 128 : (j + 1) * 128].astype(BF))
        for j, v in enumerate(turned):
            t_s[j * 128 : (j + 1) * 128, :] = swap(v)
        batch = i // per_batch
        to = pl.ds(aligned(lax.rem(i, per_batch) * piece, piece), piece)
        for g in range(groups):
            for t in range(3):
                begin = t * D + g * wide_
                send[batch * groups + g, t * wide_ : (t + 1) * wide_, to] = t_s[
                    begin : begin + wide_, :
                ]
        return 0

    lax.fori_loop(0, tokens // piece, block, 0)


def front(pairs, devices, where, starts, got, target, token, cos_t, sin_t, *blocks):
    tokens = token.shape[0]
    return pl.pallas_call(
        functools.partial(front_kernel, pairs),
        out_shape=(
            jax.ShapeDtypeStruct((tokens, D), F32),
            jax.ShapeDtypeStruct((tokens, E), BF),
            jax.ShapeDtypeStruct((tokens, D), BF),
            jax.ShapeDtypeStruct((devices, 3 * pairs * HD, tokens // 2), BF),
            jax.ShapeDtypeStruct((D, 3 * D), BF),
            jax.ShapeDtypeStruct((E, D), BF),
            jax.ShapeDtypeStruct((2, D), F32),
        ),
        in_specs=[smem()] * 2 + [vmem()] * 15,
        out_specs=(vmem(),) * 7,
        scratch_shapes=[pltpu.VMEM((3 * D, 128), BF), pltpu.VMEM((4, 16, 384), F32)],
        compiler_params=params(60),
        cost_estimate=cost(9),
        name="front",
    )(where, starts, got, target, token, cos_t, sin_t, *blocks)


def mlp_kernel(
    pairs,
    where,
    came,
    start,
    gains,
    upstream,
    *refs,
):
    blocks_own, blocks_other = refs[:4], refs[4:8]
    tall_own, tall_other = refs[8:10], refs[10:12]
    (
        result,
        hidden_out,
        attended_out,
        act_out,
        gate_out,
        up_out,
        gain_grad,
        middle_grad,
        send,
        hidden,
        total,
        back,
        output,
        pair_s,
        w_down,
    ) = refs[12:]
    step = pl.program_id(0)
    core, chip, z = where[0], where[1], where[2]
    gain = gains[1:2, :]
    sides = [
        by_chip(*blocks) + (half,)
        for blocks, half in ((blocks_own, core), (blocks_other, 1 - core))
    ]

    def fill(which, j, take):
        for side in sides:
            for m in range(4):
                for k in range(4):
                    rows = pl.ds(aligned(lax.rem(z + m, 4) * 192 + (chip ^ k) * 48), 48)
                    pair_s[side[2], rows, j * 128 : (j + 1) * 128] = side[which][k][
                        m, take, :
                    ]

    for j in range(4):
        split = 3 if j < 2 else 2
        tile = (4 * step + j) * 48

        @pl.when(step < split)
        def _():
            fill(0, j, pl.ds(aligned(tile), 48))

        @pl.when(step >= split)
        def _():
            fill(1, j, pl.ds(aligned(tile - WCUT), 48))

    turn = step ^ z
    for odd in range(2):

        @pl.when(lax.rem(turn, 2) == odd)
        def _():
            for blocks, side in ((tall_own, core), (tall_other, 1 - core)):
                for k in range(4):
                    rows = pl.ds(aligned((chip ^ k) * 128), 128)
                    for j in range(3):
                        w_down[rows, pl.ds(aligned(side * 384 + j * 128, 128), 128)] = blocks[odd][
                            turn // 2, k, j * 128 : (j + 1) * 128, :
                        ]

    groups = HEADS // pairs
    wide_ = pairs * HD
    half = came.shape[2]

    @pl.when(step == 0)
    def _():
        for _, lower, side in sides:
            for m in range(4):
                for k in range(4):
                    rows = pl.ds(aligned(lax.rem(z + m, 4) * 192 + (chip ^ k) * 48), 48)
                    for j in range(3):
                        begin = 768 + j * 48 - WCUT
                        output[rows, pl.ds(aligned(side * 384 + j * 128, 128), 128)] = lower[k][
                            m, begin : begin + 48, :
                        ]
        for batch in range(2):
            at = slice(batch * half, (batch + 1) * half)
            parts = []
            for h in range(half // 128):
                lanes = slice(h * 128, (h + 1) * 128)
                parts.append(
                    jnp.concatenate(
                        [swap(came[batch * groups + g, :, lanes]) for g in range(groups)], axis=1
                    )
                )
            rows = jnp.concatenate(parts, axis=0)
            attended_out[at, :] = rows
            x = start[at, :] + mm(rows, output[...])
            total[at, :] = x
            middle_grad[at, :] = x
            normed, _ = unit_rows(x)
            low = (normed * gain).astype(BF)
            hidden[at, :] = low
            hidden_out[at, :] = low
        back[...] = jnp.zeros_like(back)

    for batch in range(2):
        at = slice(batch * half, (batch + 1) * half)
        gate = mm(hidden[at, :], pair_s[0])
        up = mm(hidden[at, :], pair_s[1])
        sigmoid = jax.nn.sigmoid(gate)
        swish = gate * sigmoid
        act = (swish * up).astype(BF)
        act_out[at, :] = act
        total[at, :] += mm(act, w_down[...])
        grad = mm(upstream[at, :], w_down[...], NT)
        gate_grad = (grad * up * sigmoid * (1.0 + gate * (1.0 - sigmoid))).astype(BF)
        up_grad = (grad * swish).astype(BF)
        gate_out[at, :] = gate_grad
        up_out[at, :] = up_grad
        back[at, :] += mm(gate_grad, pair_s[0], NT) + mm(up_grad, pair_s[1], NT)

    @pl.when(step == pl.num_programs(0) - 1)
    def _():
        gains = jnp.zeros((1, D), F32)
        for batch in range(2):
            at = slice(batch * half, (batch + 1) * half)
            result[at, :] = total[at, :].astype(BF)
            normed, inverse = unit_rows(middle_grad[at, :])
            grad = back[at, :]
            gains += jnp.sum(grad * normed, axis=0, keepdims=True)
            weighted = grad * gain
            grad = upstream[at, :].astype(F32) + inverse * (
                weighted - normed * jnp.mean(weighted * normed, axis=-1, keepdims=True)
            )
            middle_grad[at, :] = grad
            heads = mm(output[...], grad.astype(BF), NT).astype(BF)
            for g in range(groups):
                send[batch * groups + g] = heads[g * wide_ : (g + 1) * wide_, :]
        gain_grad[...] = gains


def mlp(pairs, where, came, start, gains, upstream, *blocks):
    tokens = start.shape[0]
    width = 512
    steps = FF // width
    whole = lambda shape: pl.BlockSpec(
        shape, lambda i: (0,) * len(shape), pipeline_mode=pl.Buffered(1)
    )
    column = pl.BlockSpec((tokens, width), lambda i: (0, i))
    return pl.pallas_call(
        functools.partial(mlp_kernel, pairs),
        grid=(steps,),
        out_shape=(
            jax.ShapeDtypeStruct((tokens, D), BF),
            jax.ShapeDtypeStruct((tokens, D), BF),
            jax.ShapeDtypeStruct((tokens, D), BF),
            jax.ShapeDtypeStruct((tokens, FF), BF),
            jax.ShapeDtypeStruct((tokens, FF), BF),
            jax.ShapeDtypeStruct((tokens, FF), BF),
            jax.ShapeDtypeStruct((1, D), F32),
            jax.ShapeDtypeStruct((tokens, D), F32),
            jax.ShapeDtypeStruct(came.shape, BF),
        ),
        in_specs=[smem()] + [whole(x.shape) for x in (came, start, gains, upstream, *blocks)],
        out_specs=(
            whole((tokens, D)),
            whole((tokens, D)),
            whole((tokens, D)),
            column,
            column,
            column,
            whole((1, D)),
            whole((tokens, D)),
            whole(came.shape),
        ),
        scratch_shapes=[
            pltpu.VMEM((tokens, D), BF),
            pltpu.VMEM((tokens, D), F32),
            pltpu.VMEM((tokens, D), F32),
            pltpu.VMEM((D, D), BF),
            pltpu.VMEM((2, D, width), BF),
            pltpu.VMEM((width, D), BF),
        ],
        compiler_params=params(44),
        cost_estimate=cost(23),
        name="mlp",
    )(where, came, start, gains, upstream, *blocks)


UPPER, LOWER, ALONG = (1, 3, 2, 0), (2, 3, 1, 0), (1, 3, 2, 0)


def placed(order, value):
    at = jnp.int32(3)
    for place_, here in enumerate(order[:3]):
        at = jnp.where(value == here, place_, at)
    return at


def weight_grads_kernel(
    where,
    hidden,
    gate,
    up,
    act,
    upstream,
    attended,
    middle,
    own_u,
    own_l,
    other_u,
    other_l,
    wide_s,
    tall_s,
    out_s,
):
    core, chip, z = where[0], where[1], where[2]
    sides = ((own_u, own_l, core), (other_u, other_l, 1 - core))

    def rows_of(k, m):
        return pl.ds(aligned((z ^ m) * 192 + (chip ^ k) * 48), 48)

    def chunk(c, _):
        at = pl.ds(aligned(c * 256, 256), 256)
        wide_s[0] = mm(hidden[...], gate[:, at], TN).astype(BF)
        wide_s[1] = mm(hidden[...], up[:, at], TN).astype(BF)
        tall = mm(act[:, at], upstream[...], TN).astype(BF)
        tall_s[0] = tall[:, :384]
        tall_s[1] = tall[:, 384:]

        def put(which, ks, begin):
            for side in sides:
                for i, m in enumerate(ALONG):
                    for n, k in enumerate(ks):
                        block = wide_s[side[2], rows_of(k, m), :]
                        for j in range(2):
                            to = pl.ds(aligned((2 * c + j) * 48 - begin), 48)
                            side[which][n, i, to, :] = block[:, j * 128 : (j + 1) * 128]

        @pl.when(c < 7)
        def _():
            put(0, UPPER, 0)

        @pl.when(c == 7)
        def _():
            put(1, LOWER, CUT)

        i = placed(ALONG, (c // 2) ^ z)
        for _, lower, half in sides:
            for b in range(2):
                n = placed(LOWER, (lax.rem(c, 2) * 2 + b) ^ chip)
                block = tall_s[half, b * 128 : (b + 1) * 128, :]
                for j in range(3):
                    begin = 768 + j * 128 - CUT
                    lower[n, i, begin : begin + 128, :] = block[:, j * 128 : (j + 1) * 128]
        return 0

    lax.fori_loop(0, FF // 256, chunk, 0)
    square = mm(attended[...], middle[...].astype(BF), TN).astype(BF)
    out_s[0] = square[:, :384]
    out_s[1] = square[:, 384:]
    for _, lower, half in sides:
        for i, m in enumerate(ALONG):
            for n, k in enumerate(LOWER):
                block = out_s[half, rows_of(k, m), :]
                for j in range(3):
                    begin = 1152 + j * 48 - CUT
                    lower[n, i, begin : begin + 48, :] = block[:, j * 128 : (j + 1) * 128]


def weight_grads(where, *operands):
    upper = jax.ShapeDtypeStruct((4, 4, CUT, 128), BF)
    lower = jax.ShapeDtypeStruct((4, 4, 1296 - CUT, 128), BF)
    return pl.pallas_call(
        weight_grads_kernel,
        out_shape=(upper, lower) * 2,
        in_specs=[smem()] + [vmem()] * 7,
        out_specs=(vmem(),) * 4,
        scratch_shapes=[
            pltpu.VMEM((2, D, 256), BF),
            pltpu.VMEM((2, 256, 384), BF),
            pltpu.VMEM((2, D, 384), BF),
        ],
        compiler_params=params(60),
        cost_estimate=cost(15),
        name="weight_grads",
    )(where, *operands)


def back_kernel(
    where,
    came_a,
    came_b,
    hidden,
    start,
    middle,
    joined,
    lookup,
    gain,
    second_gain,
    embed,
    target,
    token_grad,
    send,
    own,
    other,
    df_s,
    half_s,
    look_s,
    gain_s,
):
    core, chip, z = where[0], where[1], where[2]
    widths = [ref.shape[1] // 3 for ref in (came_a, came_b)]
    groups = D // sum(widths)
    rows = came_a.shape[2]
    tokens = 2 * rows
    for i in range(tokens // 128):
        batch, lanes = divmod(i * 128, rows)
        lanes = slice(lanes, lanes + 128)
        parts = [
            (swap(ref[batch * groups + g, :, lanes]), w)
            for g in range(groups)
            for ref, w in zip((came_a, came_b), widths)
        ]
        for t in range(3):
            df_s[i * 128 : (i + 1) * 128, t * D : (t + 1) * D] = jnp.concatenate(
                [part[:, t * w : (t + 1) * w] for part, w in parts], axis=1
            )

    def kind(t, _):
        grad = mm(hidden[...], df_s[:, pl.ds(aligned(t * D, 128), D)], TN).astype(BF)
        half_s[0] = grad[:, :384]
        half_s[1] = grad[:, 384:]
        for out, half in ((own, core), (other, 1 - core)):
            for m in range(4):
                zz = z ^ m
                for k in range(4):
                    block = half_s[half, pl.ds(aligned(zz * 192 + (chip ^ k) * 48), 48), :]
                    for j in range(3):
                        to = pl.ds(aligned((t * 3 + j) * 48), 48)
                        out[k, m, to, :] = block[:, j * 128 : (j + 1) * 128]
        return 0

    lax.fori_loop(0, 3, kind, 0)

    gains = jnp.zeros((1, D), F32)
    lows = []
    for batch in range(2):
        at = slice(batch * rows, (batch + 1) * rows)
        grad = mm(df_s[at, :], joined[...], NT)
        normed, inverse = unit_rows(start[at, :])
        gains += jnp.sum(grad * normed, axis=0, keepdims=True)
        weighted = grad * gain[0:1, :]
        grad = middle[at, :] + inverse * (
            weighted - normed * jnp.mean(weighted * normed, axis=-1, keepdims=True)
        )
        token_grad[at, :] = grad
        lows.append(grad.astype(BF))
    low = jnp.concatenate(lows, axis=0)
    look = mm(embed[...], low, TN).astype(BF)
    for half in range(2):
        for j in range(3):
            begin = half * 384 + j * 128
            look_s[half, j] = look[:, begin : begin + 128]
    for half, row in enumerate((gains, second_gain[...])):
        parts = [row[:, j * 128 : (j + 1) * 128] for j in range(6)]
        gain_s[half] = jnp.concatenate(parts + [jnp.zeros((42, 128), F32)], axis=0).astype(BF)
    for out, half in ((own, core), (other, 1 - core)):
        for m in range(4):
            zz = z ^ m
            for k in range(4):
                yx = chip ^ k

                @pl.when(yx < 3)
                def _():
                    out[k, m, 432:480, :] = look_s[
                        half, lax.rem(yx, 3), pl.ds(aligned(zz * 48), 48), :
                    ]

                @pl.when(yx == 3)
                def _():
                    out[k, m, 432:480, :] = gain_s[half]

    de = mm(low, lookup[...], NT).astype(BF)
    slots = send.shape[0]
    slot = lax.broadcasted_iota(jnp.int32, (slots, tokens), 0)
    parts = []
    for table in range(2):
        hot = jnp.where(slot == target[table : table + 1, :], 1.0, 0.0).astype(BF)
        parts.append(mm(hot, de))
    send[...] = jnp.concatenate(parts, axis=1).astype(BF)


def back_pass(slots, where, *operands):
    tokens = operands[2].shape[0]
    shape = jax.ShapeDtypeStruct((4, 4, 480, 128), BF)
    return pl.pallas_call(
        back_kernel,
        out_shape=(
            jax.ShapeDtypeStruct((tokens, D), F32),
            jax.ShapeDtypeStruct((slots, 2 * E), BF),
            shape,
            shape,
        ),
        in_specs=[smem()] + [vmem()] * 11,
        out_specs=(vmem(),) * 4,
        scratch_shapes=[
            pltpu.VMEM((tokens, 3 * D), BF),
            pltpu.VMEM((2, D, 384), BF),
            pltpu.VMEM((2, 3, E, 128), BF),
            pltpu.VMEM((2, 48, 128), BF),
        ],
        compiler_params=params(60),
        cost_estimate=cost(13),
        name="back",
    )(where, *operands)


def rotate(values, cosines, sines):
    half = values.shape[-1] // 2
    a, b = values[..., :half], values[..., half:]
    c, s = cosines[:, None, :], sines[:, None, :]
    return jnp.concatenate([a * c - b * s, b * c + a * s], axis=-1)


def normalize(rows):
    inverse = lax.rsqrt(jnp.mean(rows * rows, axis=-1, keepdims=True) + epsilon)
    return rows * inverse, inverse


def norm_backward(hidden_grad, normed, inverse, gain):
    weighted = hidden_grad * gain
    return inverse * (weighted - normed * jnp.mean(weighted * normed, axis=-1, keepdims=True))


def local(
    token_embed,
    bigram_ids,
    trigram_ids,
    bigram_table,
    trigram_table,
    block_deal,
    lookup_weight,
    attention_gain,
    joined_weight,
    output_weight,
    feedforward_gain,
    expand_weight,
    contract_weight,
    cotangent,
):
    contexts = lax.axis_size("ctx")
    shards = lax.axis_size("fsdp")
    devices = contexts * shards
    batches, local_rows = token_embed.shape[:2]
    tokens = batches * local_rows
    length = local_rows * contexts
    capacity = max(2, 2 * tokens // devices)
    table_rows = bigram_table.shape[0]
    piece = local_rows // 2
    pieces = length // piece
    pairs = -(-batches * HEADS // contexts)
    while HEADS % pairs:
        pairs += 1
    both = ("ctx", "fsdp")

    ids = jnp.stack([bigram_ids.reshape(-1), trigram_ids.reshape(-1)])
    requests, target_row, target_col = placement(ids, table_rows, devices, capacity)
    asked = exchange(requests, both)
    codes = jnp.stack([asked[:, :capacity].reshape(-1), asked[:, capacity:].reshape(-1)], axis=1)
    got = exchange(
        read_rows(codes.T, bigram_table.T, trigram_table.T).reshape(devices, capacity, 2 * E), both
    ).reshape(devices * capacity, 2 * E)

    lookup = gather_weight(lookup_weight)
    joined = gather_weight(joined_weight)
    output = gather_weight(output_weight)
    gains = gather_gains(jnp.stack([attention_gain, feedforward_gain])).astype(F32)
    first_gain, second_gain = gains[0], gains[1]
    expand = gather_weight(expand_weight)
    contract = gather_weight(contract_weight)

    order = jnp.argmin(
        jnp.abs(block_deal[None, :] - jnp.arange(pieces, dtype=jnp.int32)[:, None]), axis=1
    ).astype(jnp.int32)
    frequency = jnp.exp(-math.log(10000.0) * (2.0 * jnp.arange(HD // 2, dtype=F32) / HD))
    slot = lax.axis_index("ctx") * local_rows + jnp.arange(local_rows, dtype=jnp.int32)
    position = block_deal[slot // piece] * piece + slot % piece
    angles = position.astype(F32)[:, None] * frequency[None, :]
    cosines, sines = jnp.cos(angles), jnp.sin(angles)
    all_angles = jnp.arange(length, dtype=F32)[:, None] * frequency[None, :]
    all_cosines, all_sines = jnp.cos(all_angles), jnp.sin(all_angles)

    slots = jnp.arange(devices * capacity, dtype=jnp.int32)
    hot_b = (target_col[:, 0:1] == slots[None, :]).astype(BF)
    hot_t = (target_col[:, 1:2] == slots[None, :]).astype(BF)
    embedded = (mm(hot_b, got[:, :E]) + mm(hot_t, got[:, E:])).astype(BF)
    start = token_embed.reshape(tokens, D).astype(F32) + mm(embedded, lookup)
    normed_first, inverse_first = normalize(start)
    hidden_first = (normed_first * first_gain).astype(BF)
    projected = mm(hidden_first, joined).reshape(batches, local_rows, 3, HEADS, HD)
    cos_b, sin_b = cosines[None, :, None, :], sines[None, :, None, :]
    turn = lambda x: jnp.concatenate(
        [
            x[..., : HD // 2] * cos_b - x[..., HD // 2 :] * sin_b,
            x[..., HD // 2 :] * cos_b + x[..., : HD // 2] * sin_b,
        ],
        axis=-1,
    )
    qkv = jnp.stack(
        [turn(projected[:, :, 0]), turn(projected[:, :, 1]), projected[:, :, 2]], axis=2
    ).astype(BF)
    qkv = qkv.reshape(batches, local_rows, 3, D)
    rows = exchange(by_head(qkv, contexts, pairs), "ctx").reshape(length, 3 * pairs * HD)
    attended_rows, attended_t, logsum = attend(order, rows, pairs, piece)
    attended = by_token(
        exchange(attended_rows.reshape(contexts, local_rows, pairs * HD), "ctx"), batches, 1, pairs
    ).reshape(tokens, D)
    middle = start + mm(attended, output)
    normed_second, inverse_second = normalize(middle)
    hidden_second = (normed_second * second_gain).astype(BF)
    gate_up = mm(hidden_second, expand)
    gate, up = gate_up[:, :FF], gate_up[:, FF:]
    sigmoid = jax.nn.sigmoid(gate)
    swish = gate * sigmoid
    activated = (swish * up).astype(BF)
    result = (middle + mm(activated, contract)).astype(BF)

    upstream = cotangent.reshape(tokens, D)
    activated_grad = mm(upstream, contract, NT)
    gate_up_grad = jnp.concatenate(
        [
            activated_grad * up * sigmoid * (1.0 + gate * (1.0 - sigmoid)),
            activated_grad * swish,
        ],
        axis=-1,
    ).astype(BF)
    hidden_second_grad = mm(gate_up_grad, expand, NT)
    second_gain_term = jnp.sum(hidden_second_grad * normed_second, axis=0)
    middle_grad = upstream.astype(F32) + norm_backward(
        hidden_second_grad, normed_second, inverse_second, second_gain
    )
    middle_low = middle_grad.astype(BF)
    attended_grad = mm(middle_low, output, NT).astype(BF)
    grad_rows = exchange(
        by_head(attended_grad.reshape(batches, local_rows, 1, D), contexts, pairs), "ctx"
    ).reshape(length, pairs * HD)
    contract_term = mm(activated, upstream, TN).astype(BF)
    expand_term = mm(hidden_second, gate_up_grad, TN).astype(BF)
    output_term = mm(attended, middle_low, TN).astype(BF)
    contract_grad = reduce_grad(contract_term)
    expand_grad = reduce_grad(expand_term)
    output_grad = reduce_grad(output_term)

    grad_rows = attend_grad(
        order,
        rows,
        grad_rows,
        attended_t,
        logsum,
        all_cosines,
        all_sines,
        all_cosines.T,
        all_sines.T,
        pairs,
        piece,
    )
    joined_local = by_token(
        exchange(grad_rows.reshape(contexts, local_rows, 3 * pairs * HD), "ctx"), batches, 3, pairs
    ).reshape(tokens, 3 * D)
    joined_grad = reduce_grad(mm(hidden_first, joined_local, TN).astype(BF))
    hidden_first_grad = mm(joined_local, joined, NT)
    first_gain_term = jnp.sum(hidden_first_grad * normed_first, axis=0)
    start_grad = middle_grad + norm_backward(
        hidden_first_grad, normed_first, inverse_first, first_gain
    )
    start_low = start_grad.astype(BF)
    lookup_grad = reduce_grad(mm(embedded, start_low, TN).astype(BF))
    embed_grad = mm(start_low, lookup, NT).astype(BF)
    give_b = (target_row[0:1, :] == slots[:, None]).astype(BF)
    give_t = (target_row[1:2, :] == slots[:, None]).astype(BF)
    send = jnp.concatenate([mm(give_b, embed_grad), mm(give_t, embed_grad)], axis=1).astype(BF)
    arrived = exchange(send.reshape(devices, capacity, 2 * E), both)
    bigram_grad, trigram_grad = add_rows(
        codes, arrived.reshape(devices * capacity, 2 * E), table_rows
    )
    gain_terms = lax.psum(jnp.stack([first_gain_term, second_gain_term]), both)
    gain_share = lax.dynamic_slice_in_dim(
        gain_terms, lax.axis_index("fsdp") * (D // shards), D // shards, axis=1
    )
    return (
        result.reshape(batches, local_rows, D),
        start_grad.reshape(batches, local_rows, D),
        bigram_grad.T,
        trigram_grad.T,
        lookup_grad,
        gain_share[0],
        joined_grad,
        output_grad,
        gain_share[1],
        expand_grad,
        contract_grad,
    )


def local_packed(
    token_embed,
    bigram_ids,
    trigram_ids,
    bigram_table,
    trigram_table,
    block_deal,
    lookup_weight,
    attention_gain,
    joined_weight,
    output_weight,
    feedforward_gain,
    expand_weight,
    contract_weight,
    cotangent,
):
    contexts = lax.axis_size("ctx")
    shards = lax.axis_size("fsdp")
    devices = contexts * shards
    batches, local_rows = token_embed.shape[:2]
    tokens = batches * local_rows
    length = local_rows * contexts
    capacity = max(2, 2 * tokens // devices)
    table_rows = bigram_table.shape[0]
    piece = local_rows // 2
    pieces = length // piece
    pairs = -(-batches * HEADS // contexts)
    while HEADS % pairs:
        pairs += 1
    both = ("ctx", "fsdp")


    core, chip, z = place()
    where = jnp.stack([core, chip, z]).astype(jnp.int32)
    ids = jnp.stack([bigram_ids.reshape(-1), trigram_ids.reshape(-1)])
    requests, target_row, target_col = placement(ids, table_rows, devices, capacity)
    asked = exchange(requests, both)
    gain_rows = jnp.pad(jnp.stack([attention_gain, feedforward_gain]), ((0, 14), (0, 192)))
    first, second, third = pack_weights(
        after(where, requests),
        joined_weight,
        output_weight,
        lookup_weight,
        gain_rows,
        expand_weight,
        contract_weight,
    )
    along = spread_fsdp(first)
    column = jnp.stack([p[:144] for p in along])
    pieces_z = along
    near = [over_ctx(column, 2), over_ctx(column, 4)]
    tall = [over_ctx(third, 2), over_ctx(third, 4)]
    asked, tall, third = lax.optimization_barrier((asked, tall, third))
    tall.append(over_ctx(third, 6))
    codes = jnp.stack([asked[:, :capacity].reshape(-1), asked[:, capacity:].reshape(-1)])
    answer = read_rows(
        after(codes, column), in_hbm(bigram_table.T), in_hbm(trigram_table.T)
    )
    ready = after(second, column)
    early = [along_fsdp(ready, k) for k in (1, 3)]
    answer, near, early, tall = lax.optimization_barrier((answer, near, early, tall))
    got = exchange(answer.reshape(devices, capacity, 2 * E), both)
    answer, column = lax.optimization_barrier((answer, column))
    last = over_ctx(column, 6)
    last, near, pieces_z, early = lax.optimization_barrier((last, near, pieces_z, early))
    tail = jnp.stack([p[144:] for p in pieces_z])
    first_own = [column, *near, last]
    first_other = [over_ctx(block, 1) for block in first_own]
    first_blocks = (*first_own, *first_other, tail, over_ctx(tail, 1))
    three = [second, early[1], early[0]]
    near = [
        over_ctx(jnp.stack([block[:WCUT] for block in three]), 2),
        over_ctx(jnp.stack([block[WCUT:] for block in three]), 4),
    ]
    got, ready = lax.optimization_barrier((got, ready))
    late = along_fsdp(ready, 2)
    got = got.reshape(devices * capacity, 2 * E)

    order = jnp.sum(
        jnp.where(
            block_deal[None, :] == jnp.arange(pieces, dtype=jnp.int32)[:, None],
            jnp.arange(pieces, dtype=jnp.int32)[None, :],
            0,
        ),
        axis=1,
    )
    starts = lax.dynamic_slice_in_dim(block_deal, lax.axis_index("ctx") * 2, 2)
    frequency = jnp.exp(-math.log(10000.0) * (2.0 * jnp.arange(HD // 2, dtype=F32) / HD))
    angles = frequency[:, None] * jnp.arange(length, dtype=F32)[None, :]
    cos_t, sin_t = lax.optimization_barrier((jnp.cos(angles), jnp.sin(angles)))

    start, embedded, hidden_first, sent, joined, lookup, gains = front(
        pairs,
        contexts,
        where,
        starts,
        got,
        target_col,
        token_embed.reshape(tokens, D),
        cos_t,
        sin_t,
        *first_blocks,
    )
    sent, near, late, tall = lax.optimization_barrier((sent, near, late, tall))
    tall = jnp.stack([third] + tall)
    tall = jnp.stack([tall, over_fsdp(tall, 2)])
    near_late = [over_ctx(late[:WCUT], 2), over_ctx(late[WCUT:], 4)]
    rows = exchange(sent, "ctx")
    own_blocks = [three[0], three[1], late, three[2]]
    near_x, near_y = (
        jnp.stack([*[block[cut] for block in own_blocks], part[0], part[1], last, part[2]]).reshape(
            2, 4, -1, 128
        )
        for cut, part, last in zip((slice(WCUT), slice(WCUT, None)), near, near_late)
    )
    rows, near_x, near_y, tall = lax.optimization_barrier((rows, near_x, near_y, tall))
    tall_odd = over_fsdp(tall, 1)
    far_y, far_x = over_ctx(near_x, 4), over_ctx(near_y, 2)
    others = [over_ctx(near_x, 1), over_ctx(near_y, 1)]
    attended_rows, attended_t, logsum = attend_short(order, rows, pairs, piece)
    came = exchange(attended_rows, "ctx")
    far_y, far_x, tall, tall_odd, attended_rows = lax.optimization_barrier(
        (far_y, far_x, tall, tall_odd, attended_rows)
    )
    talls = [tall, tall_odd, over_ctx(tall, 1), over_ctx(tall_odd, 1)]
    others += [over_ctx(far_y, 1), over_ctx(far_x, 1)]
    upstream = cotangent.reshape(tokens, D)
    (
        result,
        hidden_second,
        attended,
        activated,
        gate_grad,
        up_grad,
        second_gain_term,
        middle_grad,
        sent,
    ) = mlp(pairs, where, came, start, gains, upstream, near_x, near_y, far_y, far_x, *others, *talls)

    grad_rows = exchange(sent, "ctx")
    own_u, own_l, other_u, other_l = weight_grads(
        where, hidden_second, gate_grad, up_grad, activated, upstream, attended, middle_grad
    )
    other_u, other_l = after((other_u, other_l), grad_rows)
    core_u, core_l = over_ctx(other_u, 1), over_ctx(other_l, 1)
    part = functools.partial(attend_grad_short, order)
    shared = (attended_t, logsum, cos_t, sin_t, pairs, piece)
    grad_a = part(rows, grad_rows, *shared, 0, 1)
    came_a = exchange(grad_a, "ctx")
    core_u, core_l = after((core_u, core_l), grad_a)
    near_u = add_all(own_u[:2], core_u[:2]).astype(BF)
    near_l = add_all(own_l[:2], core_l[:2]).astype(BF)
    from_x, from_y = over_ctx(near_u, 2), over_ctx(near_l, 4)
    grad_b = part(after(rows, near_u, near_l), grad_rows, *shared, 1, pairs - 1)
    grad_b, came_a, from_x, from_y = lax.optimization_barrier((grad_b, came_a, from_x, from_y))
    far_u = add_all(own_u[2], core_u[2], from_x[1]).astype(BF)
    far_l = add_all(own_l[2], core_l[2], from_y[1]).astype(BF)
    came_b = exchange(grad_b, "ctx")
    came_b, far_u, far_l = lax.optimization_barrier((came_b, far_u, far_l))
    from_far = [over_ctx(far_u, 4), over_ctx(far_l, 2)]
    start_grad, send, own_j, other_j = back_pass(
        devices * capacity,
        where,
        came_a,
        came_b,
        hidden_first,
        start,
        middle_grad,
        joined,
        lookup,
        gains,
        second_gain_term,
        embedded,
        target_row,
    )
    from_core = over_ctx(other_j, 1)
    send, from_far = lax.optimization_barrier((send, from_far))
    sums_u = add_all(own_u[3], core_u[3], from_x[0], from_far[0]).astype(BF)
    sums_l = add_all(own_l[3], core_l[3], from_y[0], from_far[1]).astype(BF)
    from_z = over_fsdp(jnp.concatenate([sums_u[:2], sums_l[:2]], axis=1), 1)
    total_m = jnp.concatenate([sums_u[2:], sums_l[2:]], axis=1)
    arrived = exchange(send.reshape(devices, capacity, 2 * E), both)
    half_j = add_cores(own_j, from_core)
    from_chips = to_chips(half_j)
    from_z, kept = lax.optimization_barrier((from_z, half_j[0]))
    near_m, far_m = add_blocks(total_m[1], [from_z[0]]), add_blocks(total_m[0], [from_z[1]])
    from_z = over_fsdp(far_m, 2)
    total_j = add_blocks(kept, from_chips)
    from_fsdp = [over_fsdp(total_j[m], m) for m in (1, 2, 3)]
    from_z, kept = lax.optimization_barrier((from_z, total_j[0]))
    piece_m = add_blocks(near_m, [from_z])
    every_m = [over_ctx(piece_m, 2 * k) for k in (1, 2)]
    arrived = arrived.reshape(devices * capacity, 2 * E)
    from_fsdp[0], late_codes = lax.optimization_barrier((from_fsdp[0], codes.T))
    bigram_grad = add_table(0, late_codes, arrived, table_rows)
    bigram_grad, from_fsdp, every_m = lax.optimization_barrier((bigram_grad, from_fsdp, every_m))
    every_m.append(over_ctx(piece_m, 6))
    piece_j = add_blocks(kept, from_fsdp)
    every_j = to_chips([piece_j] * 4)
    late_codes, piece_j = lax.optimization_barrier((late_codes, piece_j))
    trigram_grad = add_table(1, late_codes, arrived, table_rows)
    trigram_grad, every_m, every_j = lax.optimization_barrier((trigram_grad, every_m, every_j))
    blocks_m = jnp.stack([piece_m] + every_m)
    other_m = over_ctx(blocks_m, 1)
    blocks_j = jnp.stack([piece_j] + every_j)
    other_j = over_ctx(blocks_j, 1)
    expand_grad, contract_grad, output_grad = unpack_second(where, blocks_m, other_m)
    joined_grad, lookup_grad, gain_grads = unpack_first(where, blocks_j, other_j)
    gain_share = lax.dynamic_slice_in_dim(
        gain_grads[:, :6].reshape(2, D), z * (D // shards), D // shards, axis=1
    )
    return (
        result.reshape(batches, local_rows, D),
        start_grad.reshape(batches, local_rows, D),
        bigram_grad.T,
        trigram_grad.T,
        lookup_grad,
        gain_share[0],
        joined_grad,
        output_grad,
        gain_share[1],
        expand_grad,
        contract_grad,
    )


def solution(mesh):
    fits = mesh.shape["ctx"] == 8 and mesh.shape["fsdp"] == 4
    return jax.shard_map(
        local_packed if fits else local,
        mesh=mesh,
        in_specs=(
            P("fsdp", "ctx", None),
            P("fsdp", "ctx"),
            P("fsdp", "ctx"),
            P(("ctx", "fsdp"), None),
            P(("ctx", "fsdp"), None),
            P(),
            P("fsdp", None),
            P("fsdp"),
            P("fsdp", None),
            P("fsdp", None),
            P("fsdp"),
            P("fsdp", None),
            P("fsdp", None),
            P("fsdp", "ctx", None),
        ),
        out_specs=(
            P("fsdp", "ctx", None),
            P("fsdp", "ctx", None),
            P(("ctx", "fsdp"), None),
            P(("ctx", "fsdp"), None),
            P("fsdp", None),
            P("fsdp"),
            P("fsdp", None),
            P("fsdp", None),
            P("fsdp"),
            P("fsdp", None),
            P("fsdp", None),
        ),
        check_vma=False,
    )
```

```python
import functools
import math

import jax
import jax.numpy as jnp
from jax import lax
from jax.experimental import pallas as pl
from jax.experimental.pallas import tpu as pltpu
from jax.sharding import PartitionSpec as P

D = 768
HEADS = 12
HD = 64
FF = 2048
E = 192
ABLK = 256
BF = jnp.bfloat16
F32 = jnp.float32

epsilon = 1e-05
NT = (((1,), (1,)), ((), ()))
NN = (((1,), (0,)), ((), ()))
TN = (((0,), (0,)), ((), ()))


def mm(a, b, dims=NN):
    return lax.dot_general(a, b, dims, preferred_element_type=F32)


def eye(n):
    rows = lax.broadcasted_iota(jnp.int32, (n, n), 0)
    return jnp.where(rows == lax.broadcasted_iota(jnp.int32, (n, n), 1), 1.0, 0.0).astype(BF)


def vmem():
    return pl.BlockSpec(memory_space=pltpu.VMEM)


def smem():
    return pl.BlockSpec(memory_space=pltpu.SMEM)


def params(megabytes, **kw):
    return pltpu.CompilerParams(vmem_limit_bytes=megabytes << 20, **kw)


def cost(microseconds):
    return pl.CostEstimate(
        flops=int(microseconds * 6e8), bytes_accessed=int(microseconds * 2.5e6), transcendentals=0
    )


def in_hbm(value):
    return pltpu.with_memory_space_constraint(value, pltpu.HBM)


def after(value, *others):
    return lax.optimization_barrier((value, others))[0]


def placement_kernel(capacity, owner_row, owner_col, local_row, requests, target_row, target_col):
    tokens = owner_row.shape[1]
    devices = requests.shape[0]
    for table in range(2):
        own_r = owner_row[table : table + 1, :]
        own_c = owner_col[:, table : table + 1]
        t_row = lax.broadcasted_iota(jnp.int32, (tokens, tokens), 0)
        t_col = lax.broadcasted_iota(jnp.int32, (tokens, tokens), 1)
        same = own_c == own_r
        rank_r = jnp.sum(jnp.where(same & (t_row < t_col), 1.0, 0.0), axis=0, keepdims=True)
        rank_c = jnp.sum(jnp.where(same & (t_col < t_row), 1.0, 0.0), axis=1, keepdims=True)
        rank_r = rank_r.astype(jnp.int32)
        rank_c = rank_c.astype(jnp.int32)
        target_row[table : table + 1, :] = own_r * capacity + rank_r
        target_col[:, table : table + 1] = own_c * capacity + rank_c
        device = lax.broadcasted_iota(jnp.int32, (devices, tokens), 0)
        owned = device == own_r
        row = local_row[table : table + 1, :]
        high = jnp.where(owned, (row >> 7).astype(F32), 0.0).astype(BF)
        low = jnp.where(owned, (row & 127).astype(F32), 0.0).astype(BF)
        one = jnp.where(owned, 1.0, 0.0).astype(BF)
        slot = lax.broadcasted_iota(jnp.int32, (tokens, capacity), 1)
        ranked = jnp.where(slot == rank_c, 1.0, 0.0).astype(BF)
        code = 128.0 * mm(high, ranked) + mm(low, ranked) + mm(one, ranked)
        requests[:, table * capacity : (table + 1) * capacity] = code.astype(jnp.int32)


def placement(ids, table_rows, devices, capacity):
    tokens = ids.shape[1]
    owner = ids // table_rows
    local_row = ids - owner * table_rows
    return pl.pallas_call(
        functools.partial(placement_kernel, capacity),
        out_shape=(
            jax.ShapeDtypeStruct((devices, 2 * capacity), jnp.int32),
            jax.ShapeDtypeStruct((2, tokens), jnp.int32),
            jax.ShapeDtypeStruct((tokens, 2), jnp.int32),
        ),
        in_specs=[vmem()] * 3,
        out_specs=(vmem(),) * 3,
        compiler_params=params(32),
        cost_estimate=cost(2),
        name="placement",
    )(owner, owner.T, local_row)


def wide(ref, columns, table):
    ref[table] = jnp.broadcast_to(columns[:, table : table + 1].astype(F32), ref.shape[1:])


def onehot_block(ref, table, base, width):
    lane = lax.broadcasted_iota(jnp.int32, ref.shape[1:], 1).astype(F32)
    parts = []
    for j in range(width // 128):
        hit = ref[table] == lane + (base + 128 * j + 1).astype(F32)
        parts.append(jnp.where(hit, 1.0, 0.0).astype(BF))
    return jnp.concatenate(parts, axis=1)


def swap(value):
    return mm(eye(value.shape[1]), value, NT).astype(BF)


def read_rows_kernel(codes, bigram, trigram, out, total):
    step = pl.program_id(0)
    width = bigram.shape[1]
    slots = codes.shape[1]

    @pl.when(step == 0)
    def _():
        total[...] = jnp.zeros_like(total)

    row = lax.broadcasted_iota(jnp.int32, (width, slots), 0) + (step * width + 1)
    for table, source in enumerate((bigram, trigram)):
        hot = jnp.where(row == codes[table : table + 1, :], 1.0, 0.0).astype(BF)
        total[table * E : (table + 1) * E, :] += mm(source[...], hot)

    @pl.when(step == pl.num_programs(0) - 1)
    def _():
        for begin in range(0, slots, 128):
            out[begin : begin + 128, :] = swap(total[:, begin : begin + 128].astype(BF))


def table_block(table_rows):
    for width in (2560, 1280, 640, 512, 256, 128):
        if table_rows % width == 0:
            return width
    return table_rows


def read_rows(codes, bigram_t, trigram_t):
    slots = codes.shape[1]
    rows = bigram_t.shape[1]
    width = table_block(rows)
    table = pl.BlockSpec((E, width), lambda i: (0, i))
    return pl.pallas_call(
        read_rows_kernel,
        grid=(rows // width,),
        out_shape=jax.ShapeDtypeStruct((slots, 2 * E), BF),
        in_specs=[pl.BlockSpec((2, slots), lambda i: (0, 0)), table, table],
        out_specs=pl.BlockSpec((slots, 2 * E), lambda i: (0, 0)),
        scratch_shapes=[pltpu.VMEM((2 * E, slots), F32)],
        compiler_params=params(40),
        cost_estimate=cost(17),
        name="read_rows",
    )(codes, bigram_t, trigram_t)


def add_rows_kernel(codes, grads, bigram, trigram, spread, turned):
    step = pl.program_id(0)
    width = bigram.shape[1]

    @pl.when(step == 0)
    def _():
        for table in range(2):
            wide(spread, codes, table)
        turned[...] = mm(eye(2 * E), grads[...], NT).astype(BF)

    for table, out in enumerate((bigram, trigram)):
        hot = onehot_block(spread, table, step * width, width)
        out[...] = mm(turned[table * E : (table + 1) * E, :], hot)


def add_rows(codes, grads, rows):
    slots = codes.shape[0]
    width = table_block(rows)
    table = pl.BlockSpec((E, width), lambda i: (0, i))
    shape = jax.ShapeDtypeStruct((E, rows), F32)
    return pl.pallas_call(
        add_rows_kernel,
        grid=(rows // width,),
        out_shape=(shape, shape),
        in_specs=[
            pl.BlockSpec((slots, 2), lambda i: (0, 0)),
            pl.BlockSpec((slots, 2 * E), lambda i: (0, 0)),
        ],
        out_specs=(table, table),
        scratch_shapes=[pltpu.VMEM((2, slots, 128), F32), pltpu.VMEM((2 * E, slots), BF)],
        compiler_params=params(32),
        cost_estimate=cost(14),
        name="add_rows",
    )(codes, grads)


def add_table_kernel(table, codes, grads, out, spread, turned):
    step = pl.program_id(0)
    width = out.shape[1]

    @pl.when(step == 0)
    def _():
        wide(spread, codes, table)
        row = lax.broadcasted_iota(jnp.int32, (E, 2 * E), 0) + table * E
        column = lax.broadcasted_iota(jnp.int32, (E, 2 * E), 1)
        pick = jnp.where(row == column, 1.0, 0.0).astype(BF)
        turned[...] = mm(pick, grads[...], NT).astype(BF)

    out[...] = mm(turned[...], onehot_block(spread, table, step * width, width))


def add_table(table, codes, grads, rows):
    slots = codes.shape[0]
    width = table_block(rows)
    return pl.pallas_call(
        functools.partial(add_table_kernel, table),
        grid=(rows // width,),
        out_shape=jax.ShapeDtypeStruct((E, rows), F32),
        in_specs=[
            pl.BlockSpec((slots, 2), lambda i: (0, 0)),
            pl.BlockSpec((slots, 2 * E), lambda i: (0, 0)),
        ],
        out_specs=pl.BlockSpec((E, width), lambda i: (0, i)),
        scratch_shapes=[pltpu.VMEM((2, slots, 128), F32), pltpu.VMEM((E, slots), BF)],
        compiler_params=params(40),
        cost_estimate=cost(7),
        name=f"add_table_{table}",
    )(codes, grads)


def attend_kernel(pairs, piece, order, rows, out, attended_t, logsum, q_s, k_s, vt_s, s_s):
    length = rows.shape[0]
    blocks = length // ABLK
    per_block = ABLK // piece
    width = pairs * HD
    identity = eye(HD)

    def sort(j, _):
        block = rows[pl.ds(pl.multiple_of(order[j] * piece, piece), piece), :]
        to = pl.ds(pl.multiple_of(j * piece, piece), piece)
        for p in range(pairs):
            q = block[:, p * HD : (p + 1) * HD]
            q_s[p, to, :] = (q.astype(F32) * HD ** (-0.5)).astype(BF)
            k_s[p, to, :] = block[:, width + p * HD : width + (p + 1) * HD]
            v = block[:, 2 * width + p * HD : 2 * width + (p + 1) * HD]
            vt_s[p, :, to] = mm(identity, v, NT).astype(BF)
        return 0

    lax.fori_loop(0, length // piece, sort, 0)

    for p in range(pairs):

        def one(i, _):
            at = pl.ds(pl.multiple_of(i * ABLK, ABLK), ABLK)
            queries = q_s[p, at, :]

            def score(j, peak):
                to = pl.ds(pl.multiple_of(j * ABLK, ABLK), ABLK)
                s = mm(k_s[p, to, :], queries, NT)
                s_s[to, :] = s
                return jnp.maximum(peak, jnp.max(s, axis=0, keepdims=True))

            peak = lax.fori_loop(0, i + 1, score, jnp.full((1, ABLK), -jnp.inf, F32))

            def raise_(j, total):
                to = pl.ds(pl.multiple_of(j * ABLK, ABLK), ABLK)
                e = jnp.exp(s_s[to, :] - peak)
                s_s[to, :] = e
                return total + jnp.sum(e, axis=0, keepdims=True)

            total = lax.fori_loop(0, i + 1, raise_, jnp.zeros((1, ABLK), F32))
            scale = 1.0 / total

            def weigh(j, o):
                to = pl.ds(pl.multiple_of(j * ABLK, ABLK), ABLK)
                probs = (s_s[to, :] * scale).astype(BF)
                return o + mm(vt_s[p, :, to], probs)

            o = lax.fori_loop(0, i + 1, weigh, jnp.zeros((HD, ABLK), F32))
            attended_t[p, :, at] = o
            logsum[p, :, at] = peak + jnp.log(total)
            o = o.T.astype(BF)
            for h in range(per_block):
                to = pl.ds(pl.multiple_of(order[per_block * i + h] * piece, piece), piece)
                out[to, p * HD : (p + 1) * HD] = o[h * piece : (h + 1) * piece, :]
            return 0

        lax.fori_loop(0, blocks, one, 0)


def attend(order, rows, pairs, piece):
    length = rows.shape[0]
    return pl.pallas_call(
        functools.partial(attend_kernel, pairs, piece),
        out_shape=(
            jax.ShapeDtypeStruct((length, pairs * HD), BF),
            jax.ShapeDtypeStruct((pairs, HD, length), F32),
            jax.ShapeDtypeStruct((pairs, 1, length), F32),
        ),
        in_specs=[smem(), vmem()],
        out_specs=(vmem(),) * 3,
        scratch_shapes=[
            pltpu.VMEM((pairs, length, HD), BF),
            pltpu.VMEM((pairs, length, HD), BF),
            pltpu.VMEM((pairs, HD, length), BF),
            pltpu.VMEM((length, ABLK), F32),
        ],
        compiler_params=params(48),
        cost_estimate=cost(50),
        name="attend",
    )(order, rows)


def attend_grad_kernel(
    pairs,
    piece,
    order,
    rows,
    grads,
    attended_t,
    logsum,
    cos,
    sin,
    cos_t,
    sin_t,
    out,
    q_s,
    k_s,
    v_s,
    g_s,
    kt_s,
    dq_s,
    dk_s,
    dv_s,
    dk_o,
    dv_o,
):
    length = rows.shape[0]
    blocks = length // ABLK
    width = pairs * HD
    half = HD // 2
    scale = HD ** (-0.5)
    identity = eye(HD)

    for p in range(pairs):

        def sort(j, _):
            take = pl.ds(pl.multiple_of(order[j] * piece, piece), piece)
            block = rows[take, :]
            to = pl.ds(pl.multiple_of(j * piece, piece), piece)
            q_s[to, :] = (block[:, p * HD : (p + 1) * HD].astype(F32) * scale).astype(BF)
            k = block[:, width + p * HD : width + (p + 1) * HD]
            k_s[to, :] = k
            kt_s[:, to] = mm(identity, k, NT).astype(BF)
            v_s[to, :] = block[:, 2 * width + p * HD : 2 * width + (p + 1) * HD]
            g_s[to, :] = grads[take, :][:, p * HD : (p + 1) * HD]
            return 0

        lax.fori_loop(0, length // piece, sort, 0)
        dk_s[...] = jnp.zeros_like(dk_s)
        dv_s[...] = jnp.zeros_like(dv_s)

        def one(i, _):
            at = pl.ds(pl.multiple_of(i * ABLK, ABLK), ABLK)
            queries = q_s[at, :]
            grad = g_s[at, :]
            delta = jnp.sum(
                mm(identity, grad, NT) * attended_t[p, :, at], axis=0, keepdims=True
            )
            level = logsum[p, :, at]

            def tile(j, dq):
                to = pl.ds(pl.multiple_of(j * ABLK, ABLK), ABLK)
                probs = jnp.exp(mm(k_s[to, :], queries, NT) - level)
                ds = (probs * (mm(v_s[to, :], grad, NT) - delta)).astype(BF)
                dv_s[to, :] += mm(probs.astype(BF), grad)
                dk_s[to, :] += mm(ds, queries)
                return dq + mm(kt_s[:, to], ds)

            dq = lax.fori_loop(0, i + 1, tile, jnp.zeros((HD, ABLK), F32)) * scale
            c, s = cos_t[:, at], sin_t[:, at]
            a, b = dq[:half, :], dq[half:, :]
            dq = jnp.concatenate([a * c + b * s, b * c - a * s], axis=0)
            dq_s[p, at, :] = dq.T.astype(BF)
            return 0

        lax.fori_loop(0, blocks, one, 0)

        def turn(j, _):
            to = pl.ds(pl.multiple_of(j * ABLK, ABLK), ABLK)
            dk = dk_s[to, :]
            a, b = dk[:, :half], dk[:, half:]
            c, s = cos[to, :], sin[to, :]
            dk_o[p, to, :] = jnp.concatenate([a * c + b * s, b * c - a * s], axis=1).astype(BF)
            dv_o[p, to, :] = dv_s[to, :].astype(BF)
            return 0

        lax.fori_loop(0, blocks, turn, 0)

    def unsort(j, _):
        take = pl.ds(pl.multiple_of(j * piece, piece), piece)
        to = pl.ds(pl.multiple_of(order[j] * piece, piece), piece)
        parts = [ref[p, take, :] for ref in (dq_s, dk_o, dv_o) for p in range(pairs)]
        out[to, :] = jnp.concatenate(parts, axis=1)
        return 0

    lax.fori_loop(0, length // piece, unsort, 0)


def attend_grad(order, rows, grads, attended_t, logsum, cos, sin, cos_t, sin_t, pairs, piece):
    length = rows.shape[0]
    low = pltpu.VMEM((length, HD), BF)
    full = pltpu.VMEM((length, HD), F32)
    each = pltpu.VMEM((pairs, length, HD), BF)
    return pl.pallas_call(
        functools.partial(attend_grad_kernel, pairs, piece),
        out_shape=jax.ShapeDtypeStruct((length, 3 * pairs * HD), BF),
        in_specs=[smem()] + [vmem()] * 8,
        out_specs=vmem(),
        scratch_shapes=[low] * 4 + [pltpu.VMEM((HD, length), BF), each, full, full, each, each],
        compiler_params=params(56),
        cost_estimate=cost(68),
        name="attend_grad",
    )(order, rows, grads, attended_t, logsum, cos, sin, cos_t, sin_t)


def fold_max(peak, tile):
    return jnp.maximum(peak, jnp.max(tile.reshape(-1, 8, tile.shape[1]), axis=0))


def fold_sum(total, tile):
    return total + jnp.sum(tile.reshape(-1, 8, tile.shape[1]), axis=0)


def piece_of(order, j, piece):
    at = order[j]
    return at // 2, pl.ds(pl.multiple_of(lax.rem(at, 2) * piece, piece), piece)


def attend_short_kernel(pairs, piece, order, rows, out, attended_t, logsum, q_s, k_s, v_s, s_s):
    length = rows.shape[0] * rows.shape[2]
    blocks = length // ABLK
    width = pairs * HD

    def sort(j, _):
        device, lanes = piece_of(order, j, piece)
        block = rows[device, :, lanes]
        to = pl.ds(pl.multiple_of(j * piece, piece), piece)
        for p in range(pairs):
            q = block[p * HD : (p + 1) * HD, :]
            q_s[p, :, to] = (q.astype(F32) * HD ** (-0.5)).astype(BF)
            k_s[p, to, :] = swap(block[width + p * HD : width + (p + 1) * HD, :])
            v_s[p, :, to] = block[2 * width + p * HD : 2 * width + (p + 1) * HD, :]
        return 0

    lax.fori_loop(0, length // piece, sort, 0)

    def pair(p, _):
        features = pl.ds(pl.multiple_of(p * HD, HD), HD)
        for i in range(blocks):
            at = slice(i * ABLK, (i + 1) * ABLK)
            queries = q_s[p, :, at]
            peak = jnp.full((8, ABLK), -jnp.inf, F32)
            for j in range(i + 1):
                s = mm(k_s[p, j * ABLK : (j + 1) * ABLK, :], queries)
                s_s[i % 2, j * ABLK : (j + 1) * ABLK, :] = s
                peak = fold_max(peak, s)
            peak = jnp.max(peak, axis=0, keepdims=True)
            total = jnp.zeros((8, ABLK), F32)
            o = jnp.zeros((HD, ABLK), F32)
            for j in range(i + 1):
                e = jnp.exp(s_s[i % 2, j * ABLK : (j + 1) * ABLK, :] - peak)
                total = fold_sum(total, e)
                o += mm(v_s[p, :, j * ABLK : (j + 1) * ABLK], e.astype(BF))
            total = jnp.sum(total, axis=0, keepdims=True)
            o = o * (1.0 / total)
            attended_t[p, :, at] = o
            logsum[p, :, at] = peak + jnp.log(total)
            o = o.astype(BF)
            for h in range(ABLK // piece):
                device, lanes = piece_of(order, ABLK // piece * i + h, piece)
                out[device, features, lanes] = o[:, h * piece : (h + 1) * piece]
        return 0

    lax.fori_loop(0, pairs, pair, 0)


def attend_short(order, rows, pairs, piece):
    contexts, _, tokens = rows.shape
    length = contexts * tokens
    return pl.pallas_call(
        functools.partial(attend_short_kernel, pairs, piece),
        out_shape=(
            pltpu.HBM((contexts, pairs * HD, tokens), BF),
            pltpu.HBM((pairs, HD, length), F32),
            jax.ShapeDtypeStruct((pairs, 1, length), F32),
        ),
        in_specs=[smem(), vmem()],
        out_specs=(vmem(),) * 3,
        scratch_shapes=[
            pltpu.VMEM((pairs, HD, length), BF),
            pltpu.VMEM((pairs, length, HD), BF),
            pltpu.VMEM((pairs, HD, length), BF),
            pltpu.VMEM((2, length, ABLK), F32),
        ],
        compiler_params=params(48),
        cost_estimate=cost(25),
        name="attend",
    )(order, rows)


def attend_grad_short_kernel(
    pairs,
    begin,
    count,
    piece,
    order,
    rows,
    grads,
    attended_t,
    logsum,
    cos_t,
    sin_t,
    out,
    q_s,
    g_s,
    kt_s,
    k_s,
    v_s,
    dk_s,
    dv_s,
):
    length = rows.shape[0] * rows.shape[2]
    blocks = length // ABLK
    width = pairs * HD
    half = HD // 2
    scale = HD ** (-0.5)

    def sort(j, _):
        device, lanes = piece_of(order, j, piece)
        block = rows[device, :, lanes]
        grad = grads[device, :, lanes]
        to = pl.ds(pl.multiple_of(j * piece, piece), piece)
        for p in range(count):
            row = (begin + p) * HD
            q_s[p, :, to] = (block[row : row + HD, :].astype(F32) * scale).astype(BF)
            k = block[width + row : width + row + HD, :]
            kt_s[p, :, to] = k
            k_s[p, to, :] = swap(k)
            v_s[p, to, :] = swap(block[2 * width + row : 2 * width + row + HD, :])
            g_s[p, :, to] = grad[row : row + HD, :]
        return 0

    lax.fori_loop(0, length // piece, sort, 0)

    def turn(x, at):
        c, s = cos_t[:, at], sin_t[:, at]
        a, b = x[:half, :], x[half:, :]
        return jnp.concatenate([a * c + b * s, b * c - a * s], axis=0)

    def pair(p, _):
        def put(kind, i, value):
            features = pl.ds(pl.multiple_of((kind * count + p) * HD, HD), HD)
            value = value.astype(BF)
            for h in range(ABLK // piece):
                device, lanes = piece_of(order, ABLK // piece * i + h, piece)
                out[device, features, lanes] = value[:, h * piece : (h + 1) * piece]

        for i in range(blocks):
            at = slice(i * ABLK, (i + 1) * ABLK)
            queries = q_s[p, :, at]
            grad = g_s[p, :, at]
            delta = jnp.sum(
                grad.astype(F32) * attended_t[begin + p, :, at], axis=0, keepdims=True
            )
            level = logsum[begin + p, :, at]
            dq = jnp.zeros((HD, ABLK), F32)
            for j in range(i, -1, -1):
                to = slice(j * ABLK, (j + 1) * ABLK)
                probs = jnp.exp(mm(k_s[p, to, :], queries) - level)
                ds = (probs * (mm(v_s[p, to, :], grad) - delta)).astype(BF)
                dv = mm(grad, probs.astype(BF), NT)
                dk = mm(queries, ds, NT)
                if i == j:
                    dv_s[:, to] = dv
                    dk_s[:, to] = dk
                else:
                    dv_s[:, to] += dv
                    dk_s[:, to] += dk
                dq += mm(kt_s[p, :, to], ds)
            put(0, i, turn(dq * scale, at))
        for i in range(blocks):
            at = slice(i * ABLK, (i + 1) * ABLK)
            put(1, i, turn(dk_s[:, at], at))
            put(2, i, dv_s[:, at])
        return 0

    lax.fori_loop(0, count, pair, 0)


def attend_grad_short(
    order, rows, grads, attended_t, logsum, cos_t, sin_t, pairs, piece, begin, count
):
    contexts, _, tokens = rows.shape
    length = contexts * tokens
    wide_ = pltpu.VMEM((count, HD, length), BF)
    tall = pltpu.VMEM((count, length, HD), BF)
    full = pltpu.VMEM((HD, length), F32)
    return pl.pallas_call(
        functools.partial(attend_grad_short_kernel, pairs, begin, count, piece),
        out_shape=pltpu.HBM((contexts, 3 * count * HD, tokens), BF),
        in_specs=[smem()] + [vmem()] * 6,
        out_specs=vmem(),
        scratch_shapes=[wide_] * 3 + [tall] * 2 + [full] * 2,
        compiler_params=params(48),
        cost_estimate=cost(14 * count),
        name=f"attend_grad_{begin}",
    )(order, rows, grads, attended_t, logsum, cos_t, sin_t)


def over_ctx(value, mask):
    size = lax.axis_size("ctx")
    return lax.ppermute(value, "ctx", [(i, i ^ mask) for i in range(size)])


def along_fsdp(value, shift):
    size = lax.axis_size("fsdp")
    return lax.ppermute(value, "fsdp", [(i, (i + shift) % size) for i in range(size)])


def by_index(blocks, index):
    if len(blocks) == 1:
        return blocks
    half = len(blocks) // 2
    flip = (index // half) % 2 == 1
    lower = [jnp.where(flip, b, a) for a, b in zip(blocks[:half], blocks[half:])]
    upper = [jnp.where(flip, a, b) for a, b in zip(blocks[:half], blocks[half:])]
    return by_index(lower, index) + by_index(upper, index)


def place():
    ctx = lax.axis_index("ctx")
    return ctx % 2, ctx // 2, lax.axis_index("fsdp")


def gather_weight(shard):
    core, chip, z = place()
    chips = lax.axis_size("ctx") // 2
    shards = lax.axis_size("fsdp")
    rows, columns = shard.shape
    r, half = rows // chips, columns // 2
    mine = lax.dynamic_slice(shard, (chip * r, core * half), (r, half))
    along = [mine] + [along_fsdp(mine, k) for k in range(1, shards)]
    turned = jnp.stack([along[(shards - m) % shards] for m in range(shards)])
    column = lax.dynamic_slice_in_dim(
        jnp.concatenate([turned, turned]), (shards - z) % shards, shards
    )
    blocks = [column] + [over_ctx(column, 2 * k) for k in range(1, chips)]
    own = jnp.stack(by_index(blocks, chip), axis=1).reshape(shards * rows, half)
    other = over_ctx(own, 1)
    return jnp.where(
        core == 0, jnp.concatenate([own, other], axis=1), jnp.concatenate([other, own], axis=1)
    )


def gather_gains(gains):
    _, _, z = place()
    shards = lax.axis_size("fsdp")
    along = [gains] + [along_fsdp(gains, k) for k in range(1, shards)]
    turned = jnp.stack([along[(shards - m) % shards] for m in range(shards)])
    every = lax.dynamic_slice_in_dim(
        jnp.concatenate([turned, turned]), (shards - z) % shards, shards
    )
    return jnp.moveaxis(every, 0, 1).reshape(gains.shape[0], -1)


def reduce_grad(grad):
    core, chip, z = place()
    chips = lax.axis_size("ctx") // 2
    shards = lax.axis_size("fsdp")
    rows, columns = grad.shape[0] // shards, grad.shape[1]
    r, half = rows // chips, columns // 2
    view = grad.reshape(shards, chips, r, columns)

    def columns_of(which):
        return lax.dynamic_slice_in_dim(view, which * half, half, axis=3)

    total = columns_of(core).astype(F32) + over_ctx(columns_of(1 - core), 1).astype(F32)
    low = total.astype(BF)
    sent = [
        over_ctx(lax.dynamic_index_in_dim(low, chip ^ k, 1, keepdims=False), 2 * k)
        for k in range(1, chips)
    ]
    total = lax.dynamic_index_in_dim(low, chip, 1, keepdims=False).astype(F32)
    total = sum((s.astype(F32) for s in sent), total)
    low = total.astype(BF)
    sent = [
        along_fsdp(lax.dynamic_index_in_dim(low, (z + k) % shards, 0, keepdims=False), k)
        for k in range(1, shards)
    ]
    total = lax.dynamic_index_in_dim(low, z, 0, keepdims=False).astype(F32)
    total = sum((s.astype(F32) for s in sent), total)
    piece = total.astype(BF)
    blocks = [piece] + [over_ctx(piece, 2 * k) for k in range(1, chips)]
    own = jnp.stack(by_index(blocks, chip)).reshape(rows, half)
    other = over_ctx(own, 1)
    return jnp.where(
        core == 0, jnp.concatenate([own, other], axis=1), jnp.concatenate([other, own], axis=1)
    ).astype(F32)


def by_head(values, devices, pairs):
    batches, tokens, kinds, _ = values.shape
    groups = HEADS // pairs
    values = values.reshape(batches, tokens, kinds, groups, pairs * HD)
    values = values.transpose(0, 3, 1, 2, 4).reshape(batches * groups, tokens, kinds * pairs * HD)
    spare = devices - batches * groups
    return jnp.pad(values, ((0, spare), (0, 0), (0, 0)))


def by_token(values, batches, kinds, pairs):
    groups = HEADS // pairs
    tokens = values.shape[1]
    values = values[: batches * groups].reshape(batches, groups, tokens, kinds, pairs * HD)
    return values.transpose(0, 2, 3, 1, 4).reshape(batches, tokens, kinds, HEADS * HD)


def exchange(values, axes):
    return lax.all_to_all(values, axes, split_axis=0, concat_axis=0, tiled=True)


def aligned(value, by=16):
    return pl.multiple_of(value, by)


def pack_weights_kernel(
    where, joined, output, lookup, gains, expand, contract, first, second, third
):
    core, chip = where[0], where[1]
    rows = pl.ds(aligned(chip * 48), 48)
    for t in range(3):
        first[t * 48 : (t + 1) * 48, :] = joined[rows, pl.ds(aligned(t * D + core * 384, 128), 384)]
    columns = pl.ds(aligned(core * 384, 128), 384)
    first[144:192, :] = lookup[:, columns]
    first[192:208, :] = gains[...]
    for j in range(16):
        second[j * 48 : (j + 1) * 48, :] = expand[
            rows, pl.ds(aligned(core * FF + j * 128, 128), 128)
        ]
    for j in range(3):
        lanes = pl.ds(aligned(core * 384 + j * 128, 128), 128)
        second[768 + j * 48 : 816 + j * 48, :] = output[rows, lanes]
        third[j * 128 : (j + 1) * 128, :] = contract[pl.ds(aligned(chip * 128), 128), lanes]


def pack_weights(where, *weights):
    return pl.pallas_call(
        pack_weights_kernel,
        out_shape=(
            jax.ShapeDtypeStruct((208, 384), BF),
            jax.ShapeDtypeStruct((912, 128), BF),
            jax.ShapeDtypeStruct((384, 128), BF),
        ),
        in_specs=[smem()] + [vmem()] * 6,
        out_specs=(vmem(),) * 3,
        compiler_params=params(16),
        cost_estimate=cost(2),
        name="pack_weights",
    )(where, *weights)


CUT = 14 * 48
WCUT = 10 * 48


def by_chip(near_x, near_y, far_y, far_x):
    return (
        [near_x.at[0], near_x.at[1], far_y.at[0], far_y.at[1]],
        [near_y.at[0], far_x.at[0], near_y.at[1], far_x.at[1]],
    )


def spread_fsdp(piece):
    along = [piece] + [along_fsdp(piece, k) for k in range(1, 4)]
    return [along[(4 - m) % 4] for m in range(4)]


def add_cores(own, came):
    return [(own[k].astype(F32) + came[k].astype(F32)).astype(BF) for k in range(4)]


def add_blocks(own, came):
    total = own.astype(F32)
    for block in came:
        total = total + block.astype(F32)
    return total.astype(BF)


def to_chips(blocks):
    return [over_ctx(blocks[k], 2 * k) for k in range(1, 4)]


def add_all(*blocks):
    return sum((b.astype(F32) for b in blocks[1:]), blocks[0].astype(F32))


def over_fsdp(value, mask):
    return lax.ppermute(value, "fsdp", [(i, i ^ mask) for i in range(4)])


def unpack_second_kernel(where, own, other, expand, contract, output):
    core, chip = where[0], where[1]
    for k in range(4):
        yx = chip ^ k
        rows = pl.ds(aligned(yx * 48), 48)
        for half in range(2):

            def taken(begin, count):
                part = slice(begin, begin + count)
                return jnp.where(core == half, own[k, part, :].astype(F32), other[k, part, :].astype(F32))

            for j in range(16):
                expand[rows, half * FF + j * 128 : half * FF + (j + 1) * 128] = taken(j * 48, 48)
            for j in range(3):
                to = slice(half * 384 + j * 128, half * 384 + (j + 1) * 128)
                contract[pl.ds(aligned(yx * 128), 128), to] = taken(768 + j * 128, 128)
                output[rows, to] = taken(1152 + j * 48, 48)


def unpack_second(where, own, other):
    return pl.pallas_call(
        unpack_second_kernel,
        out_shape=(
            jax.ShapeDtypeStruct((192, 2 * FF), F32),
            jax.ShapeDtypeStruct((512, D), F32),
            jax.ShapeDtypeStruct((192, D), F32),
        ),
        in_specs=[smem()] + [vmem()] * 2,
        out_specs=(vmem(),) * 3,
        compiler_params=params(24),
        cost_estimate=cost(4),
        name="unpack_second",
    )(where, own, other)


def unpack_first_kernel(where, own, other, joined, lookup, gains):
    core, chip = where[0], where[1]
    for k in range(4):
        yx = chip ^ k
        rows = pl.ds(aligned(yx * 48), 48)
        for half in range(2):

            def taken(begin, count):
                part = slice(begin, begin + count)
                return jnp.where(core == half, own[k, part, :].astype(F32), other[k, part, :].astype(F32))

            for t in range(3):
                for j in range(3):
                    to = t * D + half * 384 + j * 128
                    joined[rows, to : to + 128] = taken((t * 3 + j) * 48, 48)

            @pl.when(yx < 3)
            def _():
                at = pl.ds(aligned(half * 384 + yx * 128, 128), 128)
                lookup[:, at] = taken(432, 48)

            @pl.when(yx == 3)
            def _():
                gains[half] = taken(432, 48)


def unpack_first(where, own, other):
    return pl.pallas_call(
        unpack_first_kernel,
        out_shape=(
            jax.ShapeDtypeStruct((192, 3 * D), F32),
            jax.ShapeDtypeStruct((48, D), F32),
            jax.ShapeDtypeStruct((2, 48, 128), F32),
        ),
        in_specs=[smem()] + [vmem()] * 2,
        out_specs=(vmem(),) * 3,
        compiler_params=params(24),
        cost_estimate=cost(2),
        name="unpack_first",
    )(where, own, other)


def unit_rows(x):
    inverse = lax.rsqrt(jnp.mean(x * x, axis=-1, keepdims=True) + epsilon)
    return x * inverse, inverse


def front_kernel(
    pairs,
    where,
    starts,
    got,
    target,
    token,
    cos_t,
    sin_t,
    *refs,
):
    own_tail, other_tail = refs[8:10]
    start, embed, hidden, send, joined, lookup, gains, t_s, g_s = refs[10:]
    core, chip, z = where[0], where[1], where[2]
    for blocks, tail, half in ((refs[:4], own_tail, core), (refs[4:8], other_tail, 1 - core)):
        for m in range(4):
            zz = lax.rem(z + m, 4)
            for k in range(4):
                rows = pl.ds(aligned(zz * 192 + (chip ^ k) * 48), 48)
                for t in range(3):
                    joined[rows, pl.ds(aligned(t * D + half * 384, 128), 384)] = blocks[k][
                        m, t * 48 : (t + 1) * 48, :
                    ]
            lookup[pl.ds(aligned(zz * 48), 48), pl.ds(aligned(half * 384, 128), 384)] = tail[
                m, 0:48, :
            ]
    for m in range(4):
        g_s[lax.rem(z + m, 4)] = own_tail[m, 48:64, :].astype(F32)
    for row in range(2):
        gains[row : row + 1, :] = jnp.concatenate(
            [g_s[zz, row : row + 1, :192] for zz in range(4)], axis=1
        )
    gain = gains[0:1, :]
    tokens = token.shape[0]
    piece = 128
    per_batch = tokens // 2 // piece
    groups = HEADS // pairs
    wide_ = pairs * HD
    slots = got.shape[0]
    lane = lax.broadcasted_iota(jnp.int32, (piece, 128), 1)
    first_half = lax.rem(lane, HD) < HD // 2

    def block(i, _):
        at = pl.ds(aligned(i * piece, piece), piece)
        goal = target[at, :]
        slot = lax.broadcasted_iota(jnp.int32, (piece, slots), 1)
        parts = []
        for table in range(2):
            hot = jnp.where(goal[:, table : table + 1] == slot, 1.0, 0.0).astype(BF)
            parts.append(mm(hot, got[:, table * E : (table + 1) * E]))
        rows = (parts[0] + parts[1]).astype(BF)
        embed[at, :] = rows
        x = token[at, :].astype(F32) + mm(rows, lookup[...])
        start[at, :] = x
        normed, _ = unit_rows(x)
        low = (normed * gain).astype(BF)
        hidden[at, :] = low
        projected = mm(low, joined[...])
        begin = pl.ds(aligned(starts[lax.rem(i, per_batch)] * piece, piece), piece)
        c = cos_t[:, begin].T
        s = sin_t[:, begin].T
        c = jnp.concatenate([c, c, c, c], axis=1)
        s = jnp.concatenate([-s, s, -s, s], axis=1)
        turned = []
        for j in range(12):
            v = projected[:, j * 128 : (j + 1) * 128]
            swapped = jnp.where(first_half, pltpu.roll(v, 96, 1), pltpu.roll(v, 32, 1))
            turned.append((v * c + swapped * s).astype(BF))
        for j in range(12, 18):
            turned.append(projected[:, j * 128 : (j + 1) * 128].astype(BF))
        for j, v in enumerate(turned):
            t_s[j * 128 : (j + 1) * 128, :] = swap(v)
        batch = i // per_batch
        to = pl.ds(aligned(lax.rem(i, per_batch) * piece, piece), piece)
        for g in range(groups):
            for t in range(3):
                begin = t * D + g * wide_
                send[batch * groups + g, t * wide_ : (t + 1) * wide_, to] = t_s[
                    begin : begin + wide_, :
                ]
        return 0

    lax.fori_loop(0, tokens // piece, block, 0)


def front(pairs, devices, where, starts, got, target, token, cos_t, sin_t, *blocks):
    tokens = token.shape[0]
    return pl.pallas_call(
        functools.partial(front_kernel, pairs),
        out_shape=(
            jax.ShapeDtypeStruct((tokens, D), F32),
            jax.ShapeDtypeStruct((tokens, E), BF),
            jax.ShapeDtypeStruct((tokens, D), BF),
            jax.ShapeDtypeStruct((devices, 3 * pairs * HD, tokens // 2), BF),
            jax.ShapeDtypeStruct((D, 3 * D), BF),
            jax.ShapeDtypeStruct((E, D), BF),
            jax.ShapeDtypeStruct((2, D), F32),
        ),
        in_specs=[smem()] * 2 + [vmem()] * 15,
        out_specs=(vmem(),) * 7,
        scratch_shapes=[pltpu.VMEM((3 * D, 128), BF), pltpu.VMEM((4, 16, 384), F32)],
        compiler_params=params(60),
        cost_estimate=cost(9),
        name="front",
    )(where, starts, got, target, token, cos_t, sin_t, *blocks)


def mlp_kernel(
    pairs,
    where,
    came,
    start,
    gains,
    upstream,
    *refs,
):
    blocks_own, blocks_other = refs[:4], refs[4:8]
    tall_own, tall_other = refs[8:10], refs[10:12]
    (
        result,
        hidden_out,
        attended_out,
        act_out,
        gate_out,
        up_out,
        gain_grad,
        middle_grad,
        send,
        hidden,
        total,
        back,
        output,
        pair_s,
        w_down,
    ) = refs[12:]
    step = pl.program_id(0)
    core, chip, z = where[0], where[1], where[2]
    gain = gains[1:2, :]
    sides = [
        by_chip(*blocks) + (half,)
        for blocks, half in ((blocks_own, core), (blocks_other, 1 - core))
    ]

    def fill(which, j, take):
        for side in sides:
            for m in range(4):
                for k in range(4):
                    rows = pl.ds(aligned(lax.rem(z + m, 4) * 192 + (chip ^ k) * 48), 48)
                    pair_s[side[2], rows, j * 128 : (j + 1) * 128] = side[which][k][
                        m, take, :
                    ]

    for j in range(4):
        split = 3 if j < 2 else 2
        tile = (4 * step + j) * 48

        @pl.when(step < split)
        def _():
            fill(0, j, pl.ds(aligned(tile), 48))

        @pl.when(step >= split)
        def _():
            fill(1, j, pl.ds(aligned(tile - WCUT), 48))

    turn = step ^ z
    for odd in range(2):

        @pl.when(lax.rem(turn, 2) == odd)
        def _():
            for blocks, side in ((tall_own, core), (tall_other, 1 - core)):
                for k in range(4):
                    rows = pl.ds(aligned((chip ^ k) * 128), 128)
                    for j in range(3):
                        w_down[rows, pl.ds(aligned(side * 384 + j * 128, 128), 128)] = blocks[odd][
                            turn // 2, k, j * 128 : (j + 1) * 128, :
                        ]

    groups = HEADS // pairs
    wide_ = pairs * HD
    half = came.shape[2]

    @pl.when(step == 0)
    def _():
        for _, lower, side in sides:
            for m in range(4):
                for k in range(4):
                    rows = pl.ds(aligned(lax.rem(z + m, 4) * 192 + (chip ^ k) * 48), 48)
                    for j in range(3):
                        begin = 768 + j * 48 - WCUT
                        output[rows, pl.ds(aligned(side * 384 + j * 128, 128), 128)] = lower[k][
                            m, begin : begin + 48, :
                        ]
        for batch in range(2):
            at = slice(batch * half, (batch + 1) * half)
            parts = []
            for h in range(half // 128):
                lanes = slice(h * 128, (h + 1) * 128)
                parts.append(
                    jnp.concatenate(
                        [swap(came[batch * groups + g, :, lanes]) for g in range(groups)], axis=1
                    )
                )
            rows = jnp.concatenate(parts, axis=0)
            attended_out[at, :] = rows
            x = start[at, :] + mm(rows, output[...])
            total[at, :] = x
            middle_grad[at, :] = x
            normed, _ = unit_rows(x)
            low = (normed * gain).astype(BF)
            hidden[at, :] = low
            hidden_out[at, :] = low
        back[...] = jnp.zeros_like(back)

    for batch in range(2):
        at = slice(batch * half, (batch + 1) * half)
        gate = mm(hidden[at, :], pair_s[0])
        up = mm(hidden[at, :], pair_s[1])
        sigmoid = jax.nn.sigmoid(gate)
        swish = gate * sigmoid
        act = (swish * up).astype(BF)
        act_out[at, :] = act
        total[at, :] += mm(act, w_down[...])
        grad = mm(upstream[at, :], w_down[...], NT)
        gate_grad = (grad * up * sigmoid * (1.0 + gate * (1.0 - sigmoid))).astype(BF)
        up_grad = (grad * swish).astype(BF)
        gate_out[at, :] = gate_grad
        up_out[at, :] = up_grad
        back[at, :] += mm(gate_grad, pair_s[0], NT) + mm(up_grad, pair_s[1], NT)

    @pl.when(step == pl.num_programs(0) - 1)
    def _():
        gains = jnp.zeros((1, D), F32)
        for batch in range(2):
            at = slice(batch * half, (batch + 1) * half)
            result[at, :] = total[at, :].astype(BF)
            normed, inverse = unit_rows(middle_grad[at, :])
            grad = back[at, :]
            gains += jnp.sum(grad * normed, axis=0, keepdims=True)
            weighted = grad * gain
            grad = upstream[at, :].astype(F32) + inverse * (
                weighted - normed * jnp.mean(weighted * normed, axis=-1, keepdims=True)
            )
            middle_grad[at, :] = grad
            heads = mm(output[...], grad.astype(BF), NT).astype(BF)
            for g in range(groups):
                send[batch * groups + g] = heads[g * wide_ : (g + 1) * wide_, :]
        gain_grad[...] = gains


def mlp(pairs, where, came, start, gains, upstream, *blocks):
    tokens = start.shape[0]
    width = 512
    steps = FF // width
    whole = lambda shape: pl.BlockSpec(
        shape, lambda i: (0,) * len(shape), pipeline_mode=pl.Buffered(1)
    )
    column = pl.BlockSpec((tokens, width), lambda i: (0, i))
    return pl.pallas_call(
        functools.partial(mlp_kernel, pairs),
        grid=(steps,),
        out_shape=(
            pltpu.HBM((tokens, D), BF),
            pltpu.HBM((tokens, D), BF),
            pltpu.HBM((tokens, D), BF),
            jax.ShapeDtypeStruct((tokens, FF), BF),
            jax.ShapeDtypeStruct((tokens, FF), BF),
            jax.ShapeDtypeStruct((tokens, FF), BF),
            jax.ShapeDtypeStruct((1, D), F32),
            jax.ShapeDtypeStruct((tokens, D), F32),
            pltpu.HBM(came.shape, BF),
        ),
        in_specs=[smem()] + [whole(x.shape) for x in (came, start, gains, upstream, *blocks)],
        out_specs=(
            whole((tokens, D)),
            whole((tokens, D)),
            whole((tokens, D)),
            column,
            column,
            column,
            whole((1, D)),
            whole((tokens, D)),
            whole(came.shape),
        ),
        scratch_shapes=[
            pltpu.VMEM((tokens, D), BF),
            pltpu.VMEM((tokens, D), F32),
            pltpu.VMEM((tokens, D), F32),
            pltpu.VMEM((D, D), BF),
            pltpu.VMEM((2, D, width), BF),
            pltpu.VMEM((width, D), BF),
        ],
        compiler_params=params(44),
        cost_estimate=cost(23),
        name="mlp",
    )(where, came, start, gains, upstream, *blocks)


UPPER, LOWER, ALONG = (1, 3, 2, 0), (2, 3, 1, 0), (1, 3, 2, 0)


def placed(order, value):
    at = jnp.int32(3)
    for place_, here in enumerate(order[:3]):
        at = jnp.where(value == here, place_, at)
    return at


def weight_grads_kernel(
    where,
    hidden,
    gate,
    up,
    act,
    upstream,
    attended,
    middle,
    own_u,
    own_l,
    other_u,
    other_l,
    wide_s,
    tall_s,
    out_s,
):
    core, chip, z = where[0], where[1], where[2]
    sides = ((own_u, own_l, core), (other_u, other_l, 1 - core))

    def rows_of(k, m):
        return pl.ds(aligned((z ^ m) * 192 + (chip ^ k) * 48), 48)

    def chunk(c, _):
        at = pl.ds(aligned(c * 256, 256), 256)
        wide_s[0] = mm(hidden[...], gate[:, at], TN).astype(BF)
        wide_s[1] = mm(hidden[...], up[:, at], TN).astype(BF)
        tall = mm(act[:, at], upstream[...], TN).astype(BF)
        tall_s[0] = tall[:, :384]
        tall_s[1] = tall[:, 384:]

        def put(which, ks, begin):
            for side in sides:
                for i, m in enumerate(ALONG):
                    for n, k in enumerate(ks):
                        block = wide_s[side[2], rows_of(k, m), :]
                        for j in range(2):
                            to = pl.ds(aligned((2 * c + j) * 48 - begin), 48)
                            side[which][n, i, to, :] = block[:, j * 128 : (j + 1) * 128]

        @pl.when(c < 7)
        def _():
            put(0, UPPER, 0)

        @pl.when(c == 7)
        def _():
            put(1, LOWER, CUT)

        i = placed(ALONG, (c // 2) ^ z)
        for _, lower, half in sides:
            for b in range(2):
                n = placed(LOWER, (lax.rem(c, 2) * 2 + b) ^ chip)
                block = tall_s[half, b * 128 : (b + 1) * 128, :]
                for j in range(3):
                    begin = 768 + j * 128 - CUT
                    lower[n, i, begin : begin + 128, :] = block[:, j * 128 : (j + 1) * 128]
        return 0

    lax.fori_loop(0, FF // 256, chunk, 0)
    square = mm(attended[...], middle[...].astype(BF), TN).astype(BF)
    out_s[0] = square[:, :384]
    out_s[1] = square[:, 384:]
    for _, lower, half in sides:
        for i, m in enumerate(ALONG):
            for n, k in enumerate(LOWER):
                block = out_s[half, rows_of(k, m), :]
                for j in range(3):
                    begin = 1152 + j * 48 - CUT
                    lower[n, i, begin : begin + 48, :] = block[:, j * 128 : (j + 1) * 128]


def weight_grads(where, *operands):
    upper = jax.ShapeDtypeStruct((4, 4, CUT, 128), BF)
    lower = jax.ShapeDtypeStruct((4, 4, 1296 - CUT, 128), BF)
    return pl.pallas_call(
        weight_grads_kernel,
        out_shape=(upper, lower) * 2,
        in_specs=[smem()] + [vmem()] * 7,
        out_specs=(vmem(),) * 4,
        scratch_shapes=[
            pltpu.VMEM((2, D, 256), BF),
            pltpu.VMEM((2, 256, 384), BF),
            pltpu.VMEM((2, D, 384), BF),
        ],
        compiler_params=params(60),
        cost_estimate=cost(15),
        name="weight_grads",
    )(where, *operands)


def back_kernel(
    where,
    came_a,
    came_b,
    hidden,
    start,
    middle,
    joined,
    lookup,
    gain,
    second_gain,
    embed,
    target,
    token_grad,
    send,
    own,
    other,
    df_s,
    half_s,
    look_s,
    gain_s,
):
    core, chip, z = where[0], where[1], where[2]
    widths = [ref.shape[1] // 3 for ref in (came_a, came_b)]
    groups = D // sum(widths)
    rows = came_a.shape[2]
    tokens = 2 * rows
    for i in range(tokens // 128):
        batch, lanes = divmod(i * 128, rows)
        lanes = slice(lanes, lanes + 128)
        parts = [
            (swap(ref[batch * groups + g, :, lanes]), w)
            for g in range(groups)
            for ref, w in zip((came_a, came_b), widths)
        ]
        for t in range(3):
            df_s[i * 128 : (i + 1) * 128, t * D : (t + 1) * D] = jnp.concatenate(
                [part[:, t * w : (t + 1) * w] for part, w in parts], axis=1
            )

    def kind(t, _):
        grad = mm(hidden[...], df_s[:, pl.ds(aligned(t * D, 128), D)], TN).astype(BF)
        half_s[0] = grad[:, :384]
        half_s[1] = grad[:, 384:]
        for out, half in ((own, core), (other, 1 - core)):
            for m in range(4):
                zz = z ^ m
                for k in range(4):
                    block = half_s[half, pl.ds(aligned(zz * 192 + (chip ^ k) * 48), 48), :]
                    for j in range(3):
                        to = pl.ds(aligned((t * 3 + j) * 48), 48)
                        out[k, m, to, :] = block[:, j * 128 : (j + 1) * 128]
        return 0

    lax.fori_loop(0, 3, kind, 0)

    gains = jnp.zeros((1, D), F32)
    lows = []
    for batch in range(2):
        at = slice(batch * rows, (batch + 1) * rows)
        grad = mm(df_s[at, :], joined[...], NT)
        normed, inverse = unit_rows(start[at, :])
        gains += jnp.sum(grad * normed, axis=0, keepdims=True)
        weighted = grad * gain[0:1, :]
        grad = middle[at, :] + inverse * (
            weighted - normed * jnp.mean(weighted * normed, axis=-1, keepdims=True)
        )
        token_grad[at, :] = grad
        lows.append(grad.astype(BF))
    low = jnp.concatenate(lows, axis=0)
    look = mm(embed[...], low, TN).astype(BF)
    for half in range(2):
        for j in range(3):
            begin = half * 384 + j * 128
            look_s[half, j] = look[:, begin : begin + 128]
    for half, row in enumerate((gains, second_gain[...])):
        parts = [row[:, j * 128 : (j + 1) * 128] for j in range(6)]
        gain_s[half] = jnp.concatenate(parts + [jnp.zeros((42, 128), F32)], axis=0).astype(BF)
    for out, half in ((own, core), (other, 1 - core)):
        for m in range(4):
            zz = z ^ m
            for k in range(4):
                yx = chip ^ k

                @pl.when(yx < 3)
                def _():
                    out[k, m, 432:480, :] = look_s[
                        half, lax.rem(yx, 3), pl.ds(aligned(zz * 48), 48), :
                    ]

                @pl.when(yx == 3)
                def _():
                    out[k, m, 432:480, :] = gain_s[half]

    de = mm(low, lookup[...], NT).astype(BF)
    slots = send.shape[0]
    slot = lax.broadcasted_iota(jnp.int32, (slots, tokens), 0)
    parts = []
    for table in range(2):
        hot = jnp.where(slot == target[table : table + 1, :], 1.0, 0.0).astype(BF)
        parts.append(mm(hot, de))
    send[...] = jnp.concatenate(parts, axis=1).astype(BF)


def back_pass(slots, where, *operands):
    tokens = operands[2].shape[0]
    shape = jax.ShapeDtypeStruct((4, 4, 480, 128), BF)
    return pl.pallas_call(
        back_kernel,
        out_shape=(
            jax.ShapeDtypeStruct((tokens, D), F32),
            jax.ShapeDtypeStruct((slots, 2 * E), BF),
            shape,
            shape,
        ),
        in_specs=[smem()] + [vmem()] * 11,
        out_specs=(vmem(),) * 4,
        scratch_shapes=[
            pltpu.VMEM((tokens, 3 * D), BF),
            pltpu.VMEM((2, D, 384), BF),
            pltpu.VMEM((2, 3, E, 128), BF),
            pltpu.VMEM((2, 48, 128), BF),
        ],
        compiler_params=params(60),
        cost_estimate=cost(13),
        name="back",
    )(where, *operands)


def rotate(values, cosines, sines):
    half = values.shape[-1] // 2
    a, b = values[..., :half], values[..., half:]
    c, s = cosines[:, None, :], sines[:, None, :]
    return jnp.concatenate([a * c - b * s, b * c + a * s], axis=-1)


def normalize(rows):
    inverse = lax.rsqrt(jnp.mean(rows * rows, axis=-1, keepdims=True) + epsilon)
    return rows * inverse, inverse


def norm_backward(hidden_grad, normed, inverse, gain):
    weighted = hidden_grad * gain
    return inverse * (weighted - normed * jnp.mean(weighted * normed, axis=-1, keepdims=True))


def local(
    token_embed,
    bigram_ids,
    trigram_ids,
    bigram_table,
    trigram_table,
    block_deal,
    lookup_weight,
    attention_gain,
    joined_weight,
    output_weight,
    feedforward_gain,
    expand_weight,
    contract_weight,
    cotangent,
):
    contexts = lax.axis_size("ctx")
    shards = lax.axis_size("fsdp")
    devices = contexts * shards
    batches, local_rows = token_embed.shape[:2]
    tokens = batches * local_rows
    length = local_rows * contexts
    capacity = max(2, 2 * tokens // devices)
    table_rows = bigram_table.shape[0]
    piece = local_rows // 2
    pieces = length // piece
    pairs = -(-batches * HEADS // contexts)
    while HEADS % pairs:
        pairs += 1
    both = ("ctx", "fsdp")

    ids = jnp.stack([bigram_ids.reshape(-1), trigram_ids.reshape(-1)])
    requests, target_row, target_col = placement(ids, table_rows, devices, capacity)
    asked = exchange(requests, both)
    codes = jnp.stack([asked[:, :capacity].reshape(-1), asked[:, capacity:].reshape(-1)], axis=1)
    got = exchange(
        read_rows(codes.T, bigram_table.T, trigram_table.T).reshape(devices, capacity, 2 * E), both
    ).reshape(devices * capacity, 2 * E)

    lookup = gather_weight(lookup_weight)
    joined = gather_weight(joined_weight)
    output = gather_weight(output_weight)
    gains = gather_gains(jnp.stack([attention_gain, feedforward_gain])).astype(F32)
    first_gain, second_gain = gains[0], gains[1]
    expand = gather_weight(expand_weight)
    contract = gather_weight(contract_weight)

    order = jnp.argmin(
        jnp.abs(block_deal[None, :] - jnp.arange(pieces, dtype=jnp.int32)[:, None]), axis=1
    ).astype(jnp.int32)
    frequency = jnp.exp(-math.log(10000.0) * (2.0 * jnp.arange(HD // 2, dtype=F32) / HD))
    slot = lax.axis_index("ctx") * local_rows + jnp.arange(local_rows, dtype=jnp.int32)
    position = block_deal[slot // piece] * piece + slot % piece
    angles = position.astype(F32)[:, None] * frequency[None, :]
    cosines, sines = jnp.cos(angles), jnp.sin(angles)
    all_angles = jnp.arange(length, dtype=F32)[:, None] * frequency[None, :]
    all_cosines, all_sines = jnp.cos(all_angles), jnp.sin(all_angles)

    slots = jnp.arange(devices * capacity, dtype=jnp.int32)
    hot_b = (target_col[:, 0:1] == slots[None, :]).astype(BF)
    hot_t = (target_col[:, 1:2] == slots[None, :]).astype(BF)
    embedded = (mm(hot_b, got[:, :E]) + mm(hot_t, got[:, E:])).astype(BF)
    start = token_embed.reshape(tokens, D).astype(F32) + mm(embedded, lookup)
    normed_first, inverse_first = normalize(start)
    hidden_first = (normed_first * first_gain).astype(BF)
    projected = mm(hidden_first, joined).reshape(batches, local_rows, 3, HEADS, HD)
    cos_b, sin_b = cosines[None, :, None, :], sines[None, :, None, :]
    turn = lambda x: jnp.concatenate(
        [
            x[..., : HD // 2] * cos_b - x[..., HD // 2 :] * sin_b,
            x[..., HD // 2 :] * cos_b + x[..., : HD // 2] * sin_b,
        ],
        axis=-1,
    )
    qkv = jnp.stack(
        [turn(projected[:, :, 0]), turn(projected[:, :, 1]), projected[:, :, 2]], axis=2
    ).astype(BF)
    qkv = qkv.reshape(batches, local_rows, 3, D)
    rows = exchange(by_head(qkv, contexts, pairs), "ctx").reshape(length, 3 * pairs * HD)
    attended_rows, attended_t, logsum = attend(order, rows, pairs, piece)
    attended = by_token(
        exchange(attended_rows.reshape(contexts, local_rows, pairs * HD), "ctx"), batches, 1, pairs
    ).reshape(tokens, D)
    middle = start + mm(attended, output)
    normed_second, inverse_second = normalize(middle)
    hidden_second = (normed_second * second_gain).astype(BF)
    gate_up = mm(hidden_second, expand)
    gate, up = gate_up[:, :FF], gate_up[:, FF:]
    sigmoid = jax.nn.sigmoid(gate)
    swish = gate * sigmoid
    activated = (swish * up).astype(BF)
    result = (middle + mm(activated, contract)).astype(BF)

    upstream = cotangent.reshape(tokens, D)
    activated_grad = mm(upstream, contract, NT)
    gate_up_grad = jnp.concatenate(
        [
            activated_grad * up * sigmoid * (1.0 + gate * (1.0 - sigmoid)),
            activated_grad * swish,
        ],
        axis=-1,
    ).astype(BF)
    hidden_second_grad = mm(gate_up_grad, expand, NT)
    second_gain_term = jnp.sum(hidden_second_grad * normed_second, axis=0)
    middle_grad = upstream.astype(F32) + norm_backward(
        hidden_second_grad, normed_second, inverse_second, second_gain
    )
    middle_low = middle_grad.astype(BF)
    attended_grad = mm(middle_low, output, NT).astype(BF)
    grad_rows = exchange(
        by_head(attended_grad.reshape(batches, local_rows, 1, D), contexts, pairs), "ctx"
    ).reshape(length, pairs * HD)
    contract_term = mm(activated, upstream, TN).astype(BF)
    expand_term = mm(hidden_second, gate_up_grad, TN).astype(BF)
    output_term = mm(attended, middle_low, TN).astype(BF)
    contract_grad = reduce_grad(contract_term)
    expand_grad = reduce_grad(expand_term)
    output_grad = reduce_grad(output_term)

    grad_rows = attend_grad(
        order,
        rows,
        grad_rows,
        attended_t,
        logsum,
        all_cosines,
        all_sines,
        all_cosines.T,
        all_sines.T,
        pairs,
        piece,
    )
    joined_local = by_token(
        exchange(grad_rows.reshape(contexts, local_rows, 3 * pairs * HD), "ctx"), batches, 3, pairs
    ).reshape(tokens, 3 * D)
    joined_grad = reduce_grad(mm(hidden_first, joined_local, TN).astype(BF))
    hidden_first_grad = mm(joined_local, joined, NT)
    first_gain_term = jnp.sum(hidden_first_grad * normed_first, axis=0)
    start_grad = middle_grad + norm_backward(
        hidden_first_grad, normed_first, inverse_first, first_gain
    )
    start_low = start_grad.astype(BF)
    lookup_grad = reduce_grad(mm(embedded, start_low, TN).astype(BF))
    embed_grad = mm(start_low, lookup, NT).astype(BF)
    give_b = (target_row[0:1, :] == slots[:, None]).astype(BF)
    give_t = (target_row[1:2, :] == slots[:, None]).astype(BF)
    send = jnp.concatenate([mm(give_b, embed_grad), mm(give_t, embed_grad)], axis=1).astype(BF)
    arrived = exchange(send.reshape(devices, capacity, 2 * E), both)
    bigram_grad, trigram_grad = add_rows(
        codes, arrived.reshape(devices * capacity, 2 * E), table_rows
    )
    gain_terms = lax.psum(jnp.stack([first_gain_term, second_gain_term]), both)
    gain_share = lax.dynamic_slice_in_dim(
        gain_terms, lax.axis_index("fsdp") * (D // shards), D // shards, axis=1
    )
    return (
        result.reshape(batches, local_rows, D),
        start_grad.reshape(batches, local_rows, D),
        bigram_grad.T,
        trigram_grad.T,
        lookup_grad,
        gain_share[0],
        joined_grad,
        output_grad,
        gain_share[1],
        expand_grad,
        contract_grad,
    )


def local_packed(
    token_embed,
    bigram_ids,
    trigram_ids,
    bigram_table,
    trigram_table,
    block_deal,
    lookup_weight,
    attention_gain,
    joined_weight,
    output_weight,
    feedforward_gain,
    expand_weight,
    contract_weight,
    cotangent,
):
    contexts = lax.axis_size("ctx")
    shards = lax.axis_size("fsdp")
    devices = contexts * shards
    batches, local_rows = token_embed.shape[:2]
    tokens = batches * local_rows
    length = local_rows * contexts
    capacity = max(2, 2 * tokens // devices)
    table_rows = bigram_table.shape[0]
    piece = local_rows // 2
    pieces = length // piece
    pairs = -(-batches * HEADS // contexts)
    while HEADS % pairs:
        pairs += 1
    both = ("ctx", "fsdp")


    core, chip, z = place()
    where = jnp.stack([core, chip, z]).astype(jnp.int32)
    ids = jnp.stack([bigram_ids.reshape(-1), trigram_ids.reshape(-1)])
    requests, target_row, target_col = placement(ids, table_rows, devices, capacity)
    asked = exchange(requests, both)
    gain_rows = jnp.pad(jnp.stack([attention_gain, feedforward_gain]), ((0, 14), (0, 192)))
    first, second, third = pack_weights(
        after(where, requests),
        joined_weight,
        output_weight,
        lookup_weight,
        gain_rows,
        expand_weight,
        contract_weight,
    )
    along = spread_fsdp(first)
    column = jnp.stack([p[:144] for p in along])
    pieces_z = along
    near = [over_ctx(column, 2), over_ctx(column, 4)]
    tall = [over_ctx(third, 2), over_ctx(third, 4)]
    asked, tall, third = lax.optimization_barrier((asked, tall, third))
    tall.append(over_ctx(third, 6))
    codes = jnp.stack([asked[:, :capacity].reshape(-1), asked[:, capacity:].reshape(-1)])
    answer = read_rows(
        after(codes, column), in_hbm(bigram_table.T), in_hbm(trigram_table.T)
    )
    ready = after(second, column)
    early = [along_fsdp(ready, k) for k in (1, 3)]
    answer, near, early, tall = lax.optimization_barrier((answer, near, early, tall))
    got = exchange(answer.reshape(devices, capacity, 2 * E), both)
    answer, column = lax.optimization_barrier((answer, column))
    last = over_ctx(column, 6)
    last, near, pieces_z, early = lax.optimization_barrier((last, near, pieces_z, early))
    tail = jnp.stack([p[144:] for p in pieces_z])
    first_own = [column, *near, last]
    first_other = [over_ctx(block, 1) for block in first_own]
    first_blocks = (*first_own, *first_other, tail, over_ctx(tail, 1))
    three = [second, early[1], early[0]]
    near = [
        over_ctx(jnp.stack([block[:WCUT] for block in three]), 2),
        over_ctx(jnp.stack([block[WCUT:] for block in three]), 4),
    ]
    got, ready = lax.optimization_barrier((got, ready))
    late = along_fsdp(ready, 2)
    got = got.reshape(devices * capacity, 2 * E)

    order = jnp.sum(
        jnp.where(
            block_deal[None, :] == jnp.arange(pieces, dtype=jnp.int32)[:, None],
            jnp.arange(pieces, dtype=jnp.int32)[None, :],
            0,
        ),
        axis=1,
    )
    starts = lax.dynamic_slice_in_dim(block_deal, lax.axis_index("ctx") * 2, 2)
    frequency = jnp.exp(-math.log(10000.0) * (2.0 * jnp.arange(HD // 2, dtype=F32) / HD))
    angles = frequency[:, None] * jnp.arange(length, dtype=F32)[None, :]
    cos_t, sin_t = lax.optimization_barrier((jnp.cos(angles), jnp.sin(angles)))

    start, embedded, hidden_first, sent, joined, lookup, gains = front(
        pairs,
        contexts,
        where,
        starts,
        got,
        target_col,
        token_embed.reshape(tokens, D),
        cos_t,
        sin_t,
        *first_blocks,
    )
    sent, near, tall = lax.optimization_barrier((sent, near, tall))
    near, late, tall = lax.optimization_barrier((near, late, tall))
    tall = jnp.stack([third] + tall)
    tall = jnp.stack([tall, over_fsdp(tall, 2)])
    near_late = [over_ctx(late[:WCUT], 2), over_ctx(late[WCUT:], 4)]
    rows = exchange(sent, "ctx")
    own_blocks = [three[0], three[1], late, three[2]]
    near_x, near_y = (
        jnp.stack([*[block[cut] for block in own_blocks], part[0], part[1], last, part[2]]).reshape(
            2, 4, -1, 128
        )
        for cut, part, last in zip((slice(WCUT), slice(WCUT, None)), near, near_late)
    )
    rows, near_x, near_y, tall = lax.optimization_barrier((rows, near_x, near_y, tall))
    tall_odd = over_fsdp(tall, 1)
    far_y, far_x = over_ctx(near_x, 4), over_ctx(near_y, 2)
    others = [over_ctx(near_x, 1), over_ctx(near_y, 1)]
    attended_rows, attended_t, logsum = attend_short(order, rows, pairs, piece)
    came = exchange(attended_rows, "ctx")
    far_y, far_x, tall, tall_odd, attended_rows = lax.optimization_barrier(
        (far_y, far_x, tall, tall_odd, attended_rows)
    )
    talls = [tall, tall_odd, over_ctx(tall, 1), over_ctx(tall_odd, 1)]
    others += [over_ctx(far_y, 1), over_ctx(far_x, 1)]
    upstream = cotangent.reshape(tokens, D)
    (
        result,
        hidden_second,
        attended,
        activated,
        gate_grad,
        up_grad,
        second_gain_term,
        middle_grad,
        sent,
    ) = mlp(pairs, where, came, start, gains, upstream, near_x, near_y, far_y, far_x, *others, *talls)

    grad_rows = exchange(sent, "ctx")
    own_u, own_l, other_u, other_l = weight_grads(
        where, hidden_second, gate_grad, up_grad, activated, upstream, attended, middle_grad
    )
    other_u, other_l = after((other_u, other_l), grad_rows)
    core_u, core_l = over_ctx(other_u, 1), over_ctx(other_l, 1)
    part = functools.partial(attend_grad_short, order)
    shared = (in_hbm(attended_t), logsum, in_hbm(cos_t), in_hbm(sin_t), pairs, piece)
    grad_a = part(rows, grad_rows, *shared, 0, 1)
    came_a = exchange(grad_a, "ctx")
    core_u, core_l = after((core_u, core_l), grad_a)
    near_u = add_all(own_u[:2], core_u[:2]).astype(BF)
    near_l = add_all(own_l[:2], core_l[:2]).astype(BF)
    from_x, from_y = over_ctx(near_u, 2), over_ctx(near_l, 4)
    grad_b = part(after(rows, near_u, near_l), grad_rows, *shared, 1, pairs - 1)
    from_x, from_y, came_a = lax.optimization_barrier((from_x, from_y, came_a))
    far_u = add_all(own_u[2], core_u[2], from_x[1]).astype(BF)
    far_l = add_all(own_l[2], core_l[2], from_y[1]).astype(BF)
    came_b = exchange(grad_b, "ctx")
    came_b, far_u, far_l = lax.optimization_barrier((came_b, far_u, far_l))
    from_far = [over_ctx(far_u, 4), over_ctx(far_l, 2)]
    start_grad, send, own_j, other_j = back_pass(
        devices * capacity,
        where,
        came_a,
        came_b,
        hidden_first,
        start,
        middle_grad,
        joined,
        lookup,
        gains,
        second_gain_term,
        embedded,
        target_row,
    )
    from_core = over_ctx(other_j, 1)
    send, from_far = lax.optimization_barrier((send, from_far))
    sums_u = add_all(own_u[3], core_u[3], from_x[0], from_far[0]).astype(BF)
    sums_l = add_all(own_l[3], core_l[3], from_y[0], from_far[1]).astype(BF)
    from_z = over_fsdp(jnp.concatenate([sums_u[:2], sums_l[:2]], axis=1), 1)
    total_m = jnp.concatenate([sums_u[2:], sums_l[2:]], axis=1)
    arrived = exchange(send.reshape(devices, capacity, 2 * E), both)
    half_j = add_cores(own_j, from_core)
    from_chips = to_chips(half_j)
    from_z, kept = lax.optimization_barrier((from_z, half_j[0]))
    near_m, far_m = add_blocks(total_m[1], [from_z[0]]), add_blocks(total_m[0], [from_z[1]])
    from_z = over_fsdp(far_m, 2)
    total_j = add_blocks(kept, from_chips)
    from_fsdp = [over_fsdp(total_j[m], m) for m in (1, 2, 3)]
    from_z, kept = lax.optimization_barrier((from_z, total_j[0]))
    piece_m = add_blocks(near_m, [from_z])
    every_m = [over_ctx(piece_m, 2 * k) for k in (1, 2)]
    arrived = arrived.reshape(devices * capacity, 2 * E)
    from_fsdp[0], late_codes = lax.optimization_barrier((from_fsdp[0], codes.T))
    bigram_grad = add_table(0, late_codes, arrived, table_rows)
    bigram_grad, from_fsdp, every_m = lax.optimization_barrier((bigram_grad, from_fsdp, every_m))
    every_m.append(over_ctx(piece_m, 6))
    piece_j = add_blocks(kept, from_fsdp)
    every_j = to_chips([piece_j] * 4)
    late_codes, piece_j = lax.optimization_barrier((late_codes, piece_j))
    trigram_grad = add_table(1, late_codes, arrived, table_rows)
    trigram_grad, every_m, every_j = lax.optimization_barrier((trigram_grad, every_m, every_j))
    blocks_m = jnp.stack([piece_m] + every_m)
    other_m = over_ctx(blocks_m, 1)
    blocks_j = jnp.stack([piece_j] + every_j)
    other_j = over_ctx(blocks_j, 1)
    expand_grad, contract_grad, output_grad = unpack_second(where, blocks_m, other_m)
    joined_grad, lookup_grad, gain_grads = unpack_first(where, blocks_j, other_j)
    gain_share = lax.dynamic_slice_in_dim(
        gain_grads[:, :6].reshape(2, D), z * (D // shards), D // shards, axis=1
    )
    return (
        result.reshape(batches, local_rows, D),
        start_grad.reshape(batches, local_rows, D),
        bigram_grad.T,
        trigram_grad.T,
        lookup_grad,
        gain_share[0],
        joined_grad,
        output_grad,
        gain_share[1],
        expand_grad,
        contract_grad,
    )


def solution(mesh):
    fits = mesh.shape["ctx"] == 8 and mesh.shape["fsdp"] == 4
    return jax.shard_map(
        local_packed if fits else local,
        mesh=mesh,
        in_specs=(
            P("fsdp", "ctx", None),
            P("fsdp", "ctx"),
            P("fsdp", "ctx"),
            P(("ctx", "fsdp"), None),
            P(("ctx", "fsdp"), None),
            P(),
            P("fsdp", None),
            P("fsdp"),
            P("fsdp", None),
            P("fsdp", None),
            P("fsdp"),
            P("fsdp", None),
            P("fsdp", None),
            P("fsdp", "ctx", None),
        ),
        out_specs=(
            P("fsdp", "ctx", None),
            P("fsdp", "ctx", None),
            P(("ctx", "fsdp"), None),
            P(("ctx", "fsdp"), None),
            P("fsdp", None),
            P("fsdp"),
            P("fsdp", None),
            P("fsdp", None),
            P("fsdp"),
            P("fsdp", None),
            P("fsdp", None),
        ),
        check_vma=False,
    )
```

```python
import functools
import math

import jax
import jax.numpy as jnp
from jax import lax
from jax.experimental import pallas as pl
from jax.experimental.pallas import tpu as pltpu
from jax.sharding import PartitionSpec as P

D = 768
HEADS = 12
HD = 64
FF = 2048
E = 192
ABLK = 256
BF = jnp.bfloat16
F32 = jnp.float32

epsilon = 1e-05
NT = (((1,), (1,)), ((), ()))
NN = (((1,), (0,)), ((), ()))
TN = (((0,), (0,)), ((), ()))


def mm(a, b, dims=NN):
    return lax.dot_general(a, b, dims, preferred_element_type=F32)


def eye(n):
    rows = lax.broadcasted_iota(jnp.int32, (n, n), 0)
    return jnp.where(rows == lax.broadcasted_iota(jnp.int32, (n, n), 1), 1.0, 0.0).astype(BF)


def vmem():
    return pl.BlockSpec(memory_space=pltpu.VMEM)


def smem():
    return pl.BlockSpec(memory_space=pltpu.SMEM)


def params(megabytes, **kw):
    return pltpu.CompilerParams(vmem_limit_bytes=megabytes << 20, **kw)


def cost(microseconds):
    return pl.CostEstimate(
        flops=int(microseconds * 6e8), bytes_accessed=int(microseconds * 2.5e6), transcendentals=0
    )


def in_hbm(value):
    return pltpu.with_memory_space_constraint(value, pltpu.HBM)


def after(value, *others):
    return lax.optimization_barrier((value, others))[0]


def placement_kernel(capacity, owner_row, owner_col, local_row, requests, target_row, target_col):
    tokens = owner_row.shape[1]
    devices = requests.shape[0]
    for table in range(2):
        own_r = owner_row[table : table + 1, :]
        own_c = owner_col[:, table : table + 1]
        t_row = lax.broadcasted_iota(jnp.int32, (tokens, tokens), 0)
        t_col = lax.broadcasted_iota(jnp.int32, (tokens, tokens), 1)
        same = own_c == own_r
        rank_r = jnp.sum(jnp.where(same & (t_row < t_col), 1.0, 0.0), axis=0, keepdims=True)
        rank_c = jnp.sum(jnp.where(same & (t_col < t_row), 1.0, 0.0), axis=1, keepdims=True)
        rank_r = rank_r.astype(jnp.int32)
        rank_c = rank_c.astype(jnp.int32)
        target_row[table : table + 1, :] = own_r * capacity + rank_r
        target_col[:, table : table + 1] = own_c * capacity + rank_c
        device = lax.broadcasted_iota(jnp.int32, (devices, tokens), 0)
        owned = device == own_r
        row = local_row[table : table + 1, :]
        high = jnp.where(owned, (row >> 7).astype(F32), 0.0).astype(BF)
        low = jnp.where(owned, (row & 127).astype(F32), 0.0).astype(BF)
        one = jnp.where(owned, 1.0, 0.0).astype(BF)
        slot = lax.broadcasted_iota(jnp.int32, (tokens, capacity), 1)
        ranked = jnp.where(slot == rank_c, 1.0, 0.0).astype(BF)
        code = 128.0 * mm(high, ranked) + mm(low, ranked) + mm(one, ranked)
        requests[:, table * capacity : (table + 1) * capacity] = code.astype(jnp.int32)


def placement(ids, table_rows, devices, capacity):
    tokens = ids.shape[1]
    owner = ids // table_rows
    local_row = ids - owner * table_rows
    return pl.pallas_call(
        functools.partial(placement_kernel, capacity),
        out_shape=(
            jax.ShapeDtypeStruct((devices, 2 * capacity), jnp.int32),
            jax.ShapeDtypeStruct((2, tokens), jnp.int32),
            jax.ShapeDtypeStruct((tokens, 2), jnp.int32),
        ),
        in_specs=[vmem()] * 3,
        out_specs=(vmem(),) * 3,
        compiler_params=params(32),
        cost_estimate=cost(2),
        name="placement",
    )(owner, owner.T, local_row)


def wide(ref, columns, table):
    ref[table] = jnp.broadcast_to(columns[:, table : table + 1].astype(F32), ref.shape[1:])


def onehot_block(ref, table, base, width):
    lane = lax.broadcasted_iota(jnp.int32, ref.shape[1:], 1).astype(F32)
    parts = []
    for j in range(width // 128):
        hit = ref[table] == lane + (base + 128 * j + 1).astype(F32)
        parts.append(jnp.where(hit, 1.0, 0.0).astype(BF))
    return jnp.concatenate(parts, axis=1)


def swap(value):
    return mm(eye(value.shape[1]), value, NT).astype(BF)


def read_rows_kernel(codes, bigram, trigram, out, total):
    step = pl.program_id(0)
    width = bigram.shape[1]
    slots = codes.shape[1]

    @pl.when(step == 0)
    def _():
        total[...] = jnp.zeros_like(total)

    row = lax.broadcasted_iota(jnp.int32, (width, slots), 0) + (step * width + 1)
    for table, source in enumerate((bigram, trigram)):
        hot = jnp.where(row == codes[table : table + 1, :], 1.0, 0.0).astype(BF)
        total[table * E : (table + 1) * E, :] += mm(source[...], hot)

    @pl.when(step == pl.num_programs(0) - 1)
    def _():
        for begin in range(0, slots, 128):
            out[begin : begin + 128, :] = swap(total[:, begin : begin + 128].astype(BF))


def table_block(table_rows):
    for width in (2560, 1280, 640, 512, 256, 128):
        if table_rows % width == 0:
            return width
    return table_rows


def read_rows(codes, bigram_t, trigram_t):
    slots = codes.shape[1]
    rows = bigram_t.shape[1]
    width = table_block(rows)
    table = pl.BlockSpec((E, width), lambda i: (0, i))
    return pl.pallas_call(
        read_rows_kernel,
        grid=(rows // width,),
        out_shape=jax.ShapeDtypeStruct((slots, 2 * E), BF),
        in_specs=[pl.BlockSpec((2, slots), lambda i: (0, 0)), table, table],
        out_specs=pl.BlockSpec((slots, 2 * E), lambda i: (0, 0)),
        scratch_shapes=[pltpu.VMEM((2 * E, slots), F32)],
        compiler_params=params(40),
        cost_estimate=cost(17),
        name="read_rows",
    )(codes, bigram_t, trigram_t)


def add_rows_kernel(codes, grads, bigram, trigram, spread, turned):
    step = pl.program_id(0)
    width = bigram.shape[1]

    @pl.when(step == 0)
    def _():
        for table in range(2):
            wide(spread, codes, table)
        turned[...] = mm(eye(2 * E), grads[...], NT).astype(BF)

    for table, out in enumerate((bigram, trigram)):
        hot = onehot_block(spread, table, step * width, width)
        out[...] = mm(turned[table * E : (table + 1) * E, :], hot)


def add_rows(codes, grads, rows):
    slots = codes.shape[0]
    width = table_block(rows)
    table = pl.BlockSpec((E, width), lambda i: (0, i))
    shape = jax.ShapeDtypeStruct((E, rows), F32)
    return pl.pallas_call(
        add_rows_kernel,
        grid=(rows // width,),
        out_shape=(shape, shape),
        in_specs=[
            pl.BlockSpec((slots, 2), lambda i: (0, 0)),
            pl.BlockSpec((slots, 2 * E), lambda i: (0, 0)),
        ],
        out_specs=(table, table),
        scratch_shapes=[pltpu.VMEM((2, slots, 128), F32), pltpu.VMEM((2 * E, slots), BF)],
        compiler_params=params(32),
        cost_estimate=cost(14),
        name="add_rows",
    )(codes, grads)


def add_table_kernel(table, codes, grads, out, spread, turned):
    step = pl.program_id(0)
    width = out.shape[1]

    @pl.when(step == 0)
    def _():
        wide(spread, codes, table)
        row = lax.broadcasted_iota(jnp.int32, (E, 2 * E), 0) + table * E
        column = lax.broadcasted_iota(jnp.int32, (E, 2 * E), 1)
        pick = jnp.where(row == column, 1.0, 0.0).astype(BF)
        turned[...] = mm(pick, grads[...], NT).astype(BF)

    out[...] = mm(turned[...], onehot_block(spread, table, step * width, width))


def add_table(table, codes, grads, rows):
    slots = codes.shape[0]
    width = table_block(rows)
    return pl.pallas_call(
        functools.partial(add_table_kernel, table),
        grid=(rows // width,),
        out_shape=jax.ShapeDtypeStruct((E, rows), F32),
        in_specs=[
            pl.BlockSpec((slots, 2), lambda i: (0, 0)),
            pl.BlockSpec((slots, 2 * E), lambda i: (0, 0)),
        ],
        out_specs=pl.BlockSpec((E, width), lambda i: (0, i)),
        scratch_shapes=[pltpu.VMEM((2, slots, 128), F32), pltpu.VMEM((E, slots), BF)],
        compiler_params=params(40),
        cost_estimate=cost(7),
        name=f"add_table_{table}",
    )(codes, grads)


def attend_kernel(pairs, piece, order, rows, out, attended_t, logsum, q_s, k_s, vt_s, s_s):
    length = rows.shape[0]
    blocks = length // ABLK
    per_block = ABLK // piece
    width = pairs * HD
    identity = eye(HD)

    def sort(j, _):
        block = rows[pl.ds(pl.multiple_of(order[j] * piece, piece), piece), :]
        to = pl.ds(pl.multiple_of(j * piece, piece), piece)
        for p in range(pairs):
            q = block[:, p * HD : (p + 1) * HD]
            q_s[p, to, :] = (q.astype(F32) * HD ** (-0.5)).astype(BF)
            k_s[p, to, :] = block[:, width + p * HD : width + (p + 1) * HD]
            v = block[:, 2 * width + p * HD : 2 * width + (p + 1) * HD]
            vt_s[p, :, to] = mm(identity, v, NT).astype(BF)
        return 0

    lax.fori_loop(0, length // piece, sort, 0)

    for p in range(pairs):

        def one(i, _):
            at = pl.ds(pl.multiple_of(i * ABLK, ABLK), ABLK)
            queries = q_s[p, at, :]

            def score(j, peak):
                to = pl.ds(pl.multiple_of(j * ABLK, ABLK), ABLK)
                s = mm(k_s[p, to, :], queries, NT)
                s_s[to, :] = s
                return jnp.maximum(peak, jnp.max(s, axis=0, keepdims=True))

            peak = lax.fori_loop(0, i + 1, score, jnp.full((1, ABLK), -jnp.inf, F32))

            def raise_(j, total):
                to = pl.ds(pl.multiple_of(j * ABLK, ABLK), ABLK)
                e = jnp.exp(s_s[to, :] - peak)
                s_s[to, :] = e
                return total + jnp.sum(e, axis=0, keepdims=True)

            total = lax.fori_loop(0, i + 1, raise_, jnp.zeros((1, ABLK), F32))
            scale = 1.0 / total

            def weigh(j, o):
                to = pl.ds(pl.multiple_of(j * ABLK, ABLK), ABLK)
                probs = (s_s[to, :] * scale).astype(BF)
                return o + mm(vt_s[p, :, to], probs)

            o = lax.fori_loop(0, i + 1, weigh, jnp.zeros((HD, ABLK), F32))
            attended_t[p, :, at] = o
            logsum[p, :, at] = peak + jnp.log(total)
            o = o.T.astype(BF)
            for h in range(per_block):
                to = pl.ds(pl.multiple_of(order[per_block * i + h] * piece, piece), piece)
                out[to, p * HD : (p + 1) * HD] = o[h * piece : (h + 1) * piece, :]
            return 0

        lax.fori_loop(0, blocks, one, 0)


def attend(order, rows, pairs, piece):
    length = rows.shape[0]
    return pl.pallas_call(
        functools.partial(attend_kernel, pairs, piece),
        out_shape=(
            jax.ShapeDtypeStruct((length, pairs * HD), BF),
            jax.ShapeDtypeStruct((pairs, HD, length), F32),
            jax.ShapeDtypeStruct((pairs, 1, length), F32),
        ),
        in_specs=[smem(), vmem()],
        out_specs=(vmem(),) * 3,
        scratch_shapes=[
            pltpu.VMEM((pairs, length, HD), BF),
            pltpu.VMEM((pairs, length, HD), BF),
            pltpu.VMEM((pairs, HD, length), BF),
            pltpu.VMEM((length, ABLK), F32),
        ],
        compiler_params=params(48),
        cost_estimate=cost(50),
        name="attend",
    )(order, rows)


def attend_grad_kernel(
    pairs,
    piece,
    order,
    rows,
    grads,
    attended_t,
    logsum,
    cos,
    sin,
    cos_t,
    sin_t,
    out,
    q_s,
    k_s,
    v_s,
    g_s,
    kt_s,
    dq_s,
    dk_s,
    dv_s,
    dk_o,
    dv_o,
):
    length = rows.shape[0]
    blocks = length // ABLK
    width = pairs * HD
    half = HD // 2
    scale = HD ** (-0.5)
    identity = eye(HD)

    for p in range(pairs):

        def sort(j, _):
            take = pl.ds(pl.multiple_of(order[j] * piece, piece), piece)
            block = rows[take, :]
            to = pl.ds(pl.multiple_of(j * piece, piece), piece)
            q_s[to, :] = (block[:, p * HD : (p + 1) * HD].astype(F32) * scale).astype(BF)
            k = block[:, width + p * HD : width + (p + 1) * HD]
            k_s[to, :] = k
            kt_s[:, to] = mm(identity, k, NT).astype(BF)
            v_s[to, :] = block[:, 2 * width + p * HD : 2 * width + (p + 1) * HD]
            g_s[to, :] = grads[take, :][:, p * HD : (p + 1) * HD]
            return 0

        lax.fori_loop(0, length // piece, sort, 0)
        dk_s[...] = jnp.zeros_like(dk_s)
        dv_s[...] = jnp.zeros_like(dv_s)

        def one(i, _):
            at = pl.ds(pl.multiple_of(i * ABLK, ABLK), ABLK)
            queries = q_s[at, :]
            grad = g_s[at, :]
            delta = jnp.sum(
                mm(identity, grad, NT) * attended_t[p, :, at], axis=0, keepdims=True
            )
            level = logsum[p, :, at]

            def tile(j, dq):
                to = pl.ds(pl.multiple_of(j * ABLK, ABLK), ABLK)
                probs = jnp.exp(mm(k_s[to, :], queries, NT) - level)
                ds = (probs * (mm(v_s[to, :], grad, NT) - delta)).astype(BF)
                dv_s[to, :] += mm(probs.astype(BF), grad)
                dk_s[to, :] += mm(ds, queries)
                return dq + mm(kt_s[:, to], ds)

            dq = lax.fori_loop(0, i + 1, tile, jnp.zeros((HD, ABLK), F32)) * scale
            c, s = cos_t[:, at], sin_t[:, at]
            a, b = dq[:half, :], dq[half:, :]
            dq = jnp.concatenate([a * c + b * s, b * c - a * s], axis=0)
            dq_s[p, at, :] = dq.T.astype(BF)
            return 0

        lax.fori_loop(0, blocks, one, 0)

        def turn(j, _):
            to = pl.ds(pl.multiple_of(j * ABLK, ABLK), ABLK)
            dk = dk_s[to, :]
            a, b = dk[:, :half], dk[:, half:]
            c, s = cos[to, :], sin[to, :]
            dk_o[p, to, :] = jnp.concatenate([a * c + b * s, b * c - a * s], axis=1).astype(BF)
            dv_o[p, to, :] = dv_s[to, :].astype(BF)
            return 0

        lax.fori_loop(0, blocks, turn, 0)

    def unsort(j, _):
        take = pl.ds(pl.multiple_of(j * piece, piece), piece)
        to = pl.ds(pl.multiple_of(order[j] * piece, piece), piece)
        parts = [ref[p, take, :] for ref in (dq_s, dk_o, dv_o) for p in range(pairs)]
        out[to, :] = jnp.concatenate(parts, axis=1)
        return 0

    lax.fori_loop(0, length // piece, unsort, 0)


def attend_grad(order, rows, grads, attended_t, logsum, cos, sin, cos_t, sin_t, pairs, piece):
    length = rows.shape[0]
    low = pltpu.VMEM((length, HD), BF)
    full = pltpu.VMEM((length, HD), F32)
    each = pltpu.VMEM((pairs, length, HD), BF)
    return pl.pallas_call(
        functools.partial(attend_grad_kernel, pairs, piece),
        out_shape=jax.ShapeDtypeStruct((length, 3 * pairs * HD), BF),
        in_specs=[smem()] + [vmem()] * 8,
        out_specs=vmem(),
        scratch_shapes=[low] * 4 + [pltpu.VMEM((HD, length), BF), each, full, full, each, each],
        compiler_params=params(56),
        cost_estimate=cost(68),
        name="attend_grad",
    )(order, rows, grads, attended_t, logsum, cos, sin, cos_t, sin_t)


def fold_max(peak, tile):
    return jnp.maximum(peak, jnp.max(tile.reshape(-1, 8, tile.shape[1]), axis=0))


def fold_sum(total, tile):
    return total + jnp.sum(tile.reshape(-1, 8, tile.shape[1]), axis=0)


def piece_of(order, j, piece):
    at = order[j]
    return at // 2, pl.ds(pl.multiple_of(lax.rem(at, 2) * piece, piece), piece)


def attend_short_kernel(pairs, piece, order, rows, out, attended_t, logsum, q_s, k_s, v_s, s_s):
    length = rows.shape[0] * rows.shape[2]
    blocks = length // ABLK
    width = pairs * HD

    def sort(j, _):
        device, lanes = piece_of(order, j, piece)
        block = rows[device, :, lanes]
        to = pl.ds(pl.multiple_of(j * piece, piece), piece)
        for p in range(pairs):
            q = block[p * HD : (p + 1) * HD, :]
            q_s[p, :, to] = (q.astype(F32) * HD ** (-0.5)).astype(BF)
            k_s[p, to, :] = swap(block[width + p * HD : width + (p + 1) * HD, :])
            v_s[p, :, to] = block[2 * width + p * HD : 2 * width + (p + 1) * HD, :]
        return 0

    lax.fori_loop(0, length // piece, sort, 0)

    def pair(p, _):
        features = pl.ds(pl.multiple_of(p * HD, HD), HD)
        for i in range(blocks):
            at = slice(i * ABLK, (i + 1) * ABLK)
            queries = q_s[p, :, at]
            peak = jnp.full((8, ABLK), -jnp.inf, F32)
            for j in range(i + 1):
                s = mm(k_s[p, j * ABLK : (j + 1) * ABLK, :], queries)
                s_s[i % 2, j * ABLK : (j + 1) * ABLK, :] = s
                peak = fold_max(peak, s)
            peak = jnp.max(peak, axis=0, keepdims=True)
            total = jnp.zeros((8, ABLK), F32)
            o = jnp.zeros((HD, ABLK), F32)
            for j in range(i + 1):
                e = jnp.exp(s_s[i % 2, j * ABLK : (j + 1) * ABLK, :] - peak)
                total = fold_sum(total, e)
                o += mm(v_s[p, :, j * ABLK : (j + 1) * ABLK], e.astype(BF))
            total = jnp.sum(total, axis=0, keepdims=True)
            o = o * (1.0 / total)
            attended_t[p, :, at] = o
            logsum[p, :, at] = peak + jnp.log(total)
            o = o.astype(BF)
            for h in range(ABLK // piece):
                device, lanes = piece_of(order, ABLK // piece * i + h, piece)
                out[device, features, lanes] = o[:, h * piece : (h + 1) * piece]
        return 0

    lax.fori_loop(0, pairs, pair, 0)


def attend_short(order, rows, pairs, piece):
    contexts, _, tokens = rows.shape
    length = contexts * tokens
    return pl.pallas_call(
        functools.partial(attend_short_kernel, pairs, piece),
        out_shape=(
            pltpu.HBM((contexts, pairs * HD, tokens), BF),
            pltpu.HBM((pairs, HD, length), F32),
            jax.ShapeDtypeStruct((pairs, 1, length), F32),
        ),
        in_specs=[smem(), vmem()],
        out_specs=(vmem(),) * 3,
        scratch_shapes=[
            pltpu.VMEM((pairs, HD, length), BF),
            pltpu.VMEM((pairs, length, HD), BF),
            pltpu.VMEM((pairs, HD, length), BF),
            pltpu.VMEM((2, length, ABLK), F32),
        ],
        compiler_params=params(48),
        cost_estimate=cost(25),
        name="attend",
    )(order, rows)


def attend_grad_short_kernel(
    pairs,
    begin,
    count,
    piece,
    order,
    rows,
    grads,
    attended_t,
    logsum,
    cos_t,
    sin_t,
    out,
    q_s,
    g_s,
    kt_s,
    k_s,
    v_s,
    dk_s,
    dv_s,
):
    length = rows.shape[0] * rows.shape[2]
    blocks = length // ABLK
    width = pairs * HD
    half = HD // 2
    scale = HD ** (-0.5)

    def sort(j, _):
        device, lanes = piece_of(order, j, piece)
        block = rows[device, :, lanes]
        grad = grads[device, :, lanes]
        to = pl.ds(pl.multiple_of(j * piece, piece), piece)
        for p in range(count):
            row = (begin + p) * HD
            q_s[p, :, to] = (block[row : row + HD, :].astype(F32) * scale).astype(BF)
            k = block[width + row : width + row + HD, :]
            kt_s[p, :, to] = k
            k_s[p, to, :] = swap(k)
            v_s[p, to, :] = swap(block[2 * width + row : 2 * width + row + HD, :])
            g_s[p, :, to] = grad[row : row + HD, :]
        return 0

    lax.fori_loop(0, length // piece, sort, 0)

    def turn(x, at):
        c, s = cos_t[:, at], sin_t[:, at]
        a, b = x[:half, :], x[half:, :]
        return jnp.concatenate([a * c + b * s, b * c - a * s], axis=0)

    def pair(p, _):
        def put(kind, i, value):
            features = pl.ds(pl.multiple_of((kind * count + p) * HD, HD), HD)
            value = value.astype(BF)
            for h in range(ABLK // piece):
                device, lanes = piece_of(order, ABLK // piece * i + h, piece)
                out[device, features, lanes] = value[:, h * piece : (h + 1) * piece]

        for i in range(blocks):
            at = slice(i * ABLK, (i + 1) * ABLK)
            queries = q_s[p, :, at]
            grad = g_s[p, :, at]
            delta = jnp.sum(
                grad.astype(F32) * attended_t[begin + p, :, at], axis=0, keepdims=True
            )
            level = logsum[begin + p, :, at]
            dq = jnp.zeros((HD, ABLK), F32)
            for j in range(i, -1, -1):
                to = slice(j * ABLK, (j + 1) * ABLK)
                probs = jnp.exp(mm(k_s[p, to, :], queries) - level)
                ds = (probs * (mm(v_s[p, to, :], grad) - delta)).astype(BF)
                dv = mm(grad, probs.astype(BF), NT)
                dk = mm(queries, ds, NT)
                if i == j:
                    dv_s[:, to] = dv
                    dk_s[:, to] = dk
                else:
                    dv_s[:, to] += dv
                    dk_s[:, to] += dk
                dq += mm(kt_s[p, :, to], ds)
            put(0, i, turn(dq * scale, at))
        for i in range(blocks):
            at = slice(i * ABLK, (i + 1) * ABLK)
            put(1, i, turn(dk_s[:, at], at))
            put(2, i, dv_s[:, at])
        return 0

    lax.fori_loop(0, count, pair, 0)


def attend_grad_short(
    order, rows, grads, attended_t, logsum, cos_t, sin_t, pairs, piece, begin, count
):
    contexts, _, tokens = rows.shape
    length = contexts * tokens
    wide_ = pltpu.VMEM((count, HD, length), BF)
    tall = pltpu.VMEM((count, length, HD), BF)
    full = pltpu.VMEM((HD, length), F32)
    return pl.pallas_call(
        functools.partial(attend_grad_short_kernel, pairs, begin, count, piece),
        out_shape=pltpu.HBM((contexts, 3 * count * HD, tokens), BF),
        in_specs=[smem()] + [vmem()] * 6,
        out_specs=vmem(),
        scratch_shapes=[wide_] * 3 + [tall] * 2 + [full] * 2,
        compiler_params=params(48),
        cost_estimate=cost(14 * count),
        name=f"attend_grad_{begin}",
    )(order, rows, grads, attended_t, logsum, cos_t, sin_t)


def over_ctx(value, mask):
    size = lax.axis_size("ctx")
    return lax.ppermute(value, "ctx", [(i, i ^ mask) for i in range(size)])


def along_fsdp(value, shift):
    size = lax.axis_size("fsdp")
    return lax.ppermute(value, "fsdp", [(i, (i + shift) % size) for i in range(size)])


def by_index(blocks, index):
    if len(blocks) == 1:
        return blocks
    half = len(blocks) // 2
    flip = (index // half) % 2 == 1
    lower = [jnp.where(flip, b, a) for a, b in zip(blocks[:half], blocks[half:])]
    upper = [jnp.where(flip, a, b) for a, b in zip(blocks[:half], blocks[half:])]
    return by_index(lower, index) + by_index(upper, index)


def place():
    ctx = lax.axis_index("ctx")
    return ctx % 2, ctx // 2, lax.axis_index("fsdp")


def gather_weight(shard):
    core, chip, z = place()
    chips = lax.axis_size("ctx") // 2
    shards = lax.axis_size("fsdp")
    rows, columns = shard.shape
    r, half = rows // chips, columns // 2
    mine = lax.dynamic_slice(shard, (chip * r, core * half), (r, half))
    along = [mine] + [along_fsdp(mine, k) for k in range(1, shards)]
    turned = jnp.stack([along[(shards - m) % shards] for m in range(shards)])
    column = lax.dynamic_slice_in_dim(
        jnp.concatenate([turned, turned]), (shards - z) % shards, shards
    )
    blocks = [column] + [over_ctx(column, 2 * k) for k in range(1, chips)]
    own = jnp.stack(by_index(blocks, chip), axis=1).reshape(shards * rows, half)
    other = over_ctx(own, 1)
    return jnp.where(
        core == 0, jnp.concatenate([own, other], axis=1), jnp.concatenate([other, own], axis=1)
    )


def gather_gains(gains):
    _, _, z = place()
    shards = lax.axis_size("fsdp")
    along = [gains] + [along_fsdp(gains, k) for k in range(1, shards)]
    turned = jnp.stack([along[(shards - m) % shards] for m in range(shards)])
    every = lax.dynamic_slice_in_dim(
        jnp.concatenate([turned, turned]), (shards - z) % shards, shards
    )
    return jnp.moveaxis(every, 0, 1).reshape(gains.shape[0], -1)


def reduce_grad(grad):
    core, chip, z = place()
    chips = lax.axis_size("ctx") // 2
    shards = lax.axis_size("fsdp")
    rows, columns = grad.shape[0] // shards, grad.shape[1]
    r, half = rows // chips, columns // 2
    view = grad.reshape(shards, chips, r, columns)

    def columns_of(which):
        return lax.dynamic_slice_in_dim(view, which * half, half, axis=3)

    total = columns_of(core).astype(F32) + over_ctx(columns_of(1 - core), 1).astype(F32)
    low = total.astype(BF)
    sent = [
        over_ctx(lax.dynamic_index_in_dim(low, chip ^ k, 1, keepdims=False), 2 * k)
        for k in range(1, chips)
    ]
    total = lax.dynamic_index_in_dim(low, chip, 1, keepdims=False).astype(F32)
    total = sum((s.astype(F32) for s in sent), total)
    low = total.astype(BF)
    sent = [
        along_fsdp(lax.dynamic_index_in_dim(low, (z + k) % shards, 0, keepdims=False), k)
        for k in range(1, shards)
    ]
    total = lax.dynamic_index_in_dim(low, z, 0, keepdims=False).astype(F32)
    total = sum((s.astype(F32) for s in sent), total)
    piece = total.astype(BF)
    blocks = [piece] + [over_ctx(piece, 2 * k) for k in range(1, chips)]
    own = jnp.stack(by_index(blocks, chip)).reshape(rows, half)
    other = over_ctx(own, 1)
    return jnp.where(
        core == 0, jnp.concatenate([own, other], axis=1), jnp.concatenate([other, own], axis=1)
    ).astype(F32)


def by_head(values, devices, pairs):
    batches, tokens, kinds, _ = values.shape
    groups = HEADS // pairs
    values = values.reshape(batches, tokens, kinds, groups, pairs * HD)
    values = values.transpose(0, 3, 1, 2, 4).reshape(batches * groups, tokens, kinds * pairs * HD)
    spare = devices - batches * groups
    return jnp.pad(values, ((0, spare), (0, 0), (0, 0)))


def by_token(values, batches, kinds, pairs):
    groups = HEADS // pairs
    tokens = values.shape[1]
    values = values[: batches * groups].reshape(batches, groups, tokens, kinds, pairs * HD)
    return values.transpose(0, 2, 3, 1, 4).reshape(batches, tokens, kinds, HEADS * HD)


def exchange(values, axes):
    return lax.all_to_all(values, axes, split_axis=0, concat_axis=0, tiled=True)


def aligned(value, by=16):
    return pl.multiple_of(value, by)


def pack_weights_kernel(
    where, joined, output, lookup, gains, expand, contract, first, second, third
):
    core, chip = where[0], where[1]
    rows = pl.ds(aligned(chip * 48), 48)
    for t in range(3):
        first[t * 48 : (t + 1) * 48, :] = joined[rows, pl.ds(aligned(t * D + core * 384, 128), 384)]
    columns = pl.ds(aligned(core * 384, 128), 384)
    first[144:192, :] = lookup[:, columns]
    first[192:208, :] = gains[...]
    for j in range(16):
        second[j * 48 : (j + 1) * 48, :] = expand[
            rows, pl.ds(aligned(core * FF + j * 128, 128), 128)
        ]
    for j in range(3):
        lanes = pl.ds(aligned(core * 384 + j * 128, 128), 128)
        second[768 + j * 48 : 816 + j * 48, :] = output[rows, lanes]
        third[j * 128 : (j + 1) * 128, :] = contract[pl.ds(aligned(chip * 128), 128), lanes]


def pack_weights(where, *weights):
    return pl.pallas_call(
        pack_weights_kernel,
        out_shape=(
            jax.ShapeDtypeStruct((208, 384), BF),
            jax.ShapeDtypeStruct((912, 128), BF),
            jax.ShapeDtypeStruct((384, 128), BF),
        ),
        in_specs=[smem()] + [vmem()] * 6,
        out_specs=(vmem(),) * 3,
        compiler_params=params(16),
        cost_estimate=cost(2),
        name="pack_weights",
    )(where, *weights)


CUT = 14 * 48
WCUT = 10 * 48


def by_chip(near_x, near_y, far_y, far_x):
    return (
        [near_x.at[0], near_x.at[1], far_y.at[0], far_y.at[1]],
        [near_y.at[0], far_x.at[0], near_y.at[1], far_x.at[1]],
    )


def spread_fsdp(piece):
    along = [piece] + [along_fsdp(piece, k) for k in range(1, 4)]
    return [along[(4 - m) % 4] for m in range(4)]


def add_cores(own, came):
    return [(own[k].astype(F32) + came[k].astype(F32)).astype(BF) for k in range(4)]


def add_blocks(own, came):
    total = own.astype(F32)
    for block in came:
        total = total + block.astype(F32)
    return total.astype(BF)


def to_chips(blocks):
    return [over_ctx(blocks[k], 2 * k) for k in range(1, 4)]


def add_all(*blocks):
    return sum((b.astype(F32) for b in blocks[1:]), blocks[0].astype(F32))


def over_fsdp(value, mask):
    return lax.ppermute(value, "fsdp", [(i, i ^ mask) for i in range(4)])


def unpack_second_kernel(where, own, other, expand, contract, output):
    core, chip = where[0], where[1]
    for k in range(4):
        yx = chip ^ k
        rows = pl.ds(aligned(yx * 48), 48)
        for half in range(2):

            def taken(begin, count):
                part = slice(begin, begin + count)
                return jnp.where(core == half, own[k, part, :].astype(F32), other[k, part, :].astype(F32))

            for j in range(16):
                expand[rows, half * FF + j * 128 : half * FF + (j + 1) * 128] = taken(j * 48, 48)
            for j in range(3):
                to = slice(half * 384 + j * 128, half * 384 + (j + 1) * 128)
                contract[pl.ds(aligned(yx * 128), 128), to] = taken(768 + j * 128, 128)
                output[rows, to] = taken(1152 + j * 48, 48)


def unpack_second(where, own, other):
    return pl.pallas_call(
        unpack_second_kernel,
        out_shape=(
            jax.ShapeDtypeStruct((192, 2 * FF), F32),
            jax.ShapeDtypeStruct((512, D), F32),
            jax.ShapeDtypeStruct((192, D), F32),
        ),
        in_specs=[smem()] + [vmem()] * 2,
        out_specs=(vmem(),) * 3,
        compiler_params=params(24),
        cost_estimate=cost(4),
        name="unpack_second",
    )(where, own, other)


def unpack_first_kernel(where, own, other, joined, lookup, gains):
    core, chip = where[0], where[1]
    for k in range(4):
        yx = chip ^ k
        rows = pl.ds(aligned(yx * 48), 48)
        for half in range(2):

            def taken(begin, count):
                part = slice(begin, begin + count)
                return jnp.where(core == half, own[k, part, :].astype(F32), other[k, part, :].astype(F32))

            for t in range(3):
                for j in range(3):
                    to = t * D + half * 384 + j * 128
                    joined[rows, to : to + 128] = taken((t * 3 + j) * 48, 48)

            @pl.when(yx < 3)
            def _():
                at = pl.ds(aligned(half * 384 + yx * 128, 128), 128)
                lookup[:, at] = taken(432, 48)

            @pl.when(yx == 3)
            def _():
                gains[half] = taken(432, 48)


def unpack_first(where, own, other):
    return pl.pallas_call(
        unpack_first_kernel,
        out_shape=(
            jax.ShapeDtypeStruct((192, 3 * D), F32),
            jax.ShapeDtypeStruct((48, D), F32),
            jax.ShapeDtypeStruct((2, 48, 128), F32),
        ),
        in_specs=[smem()] + [vmem()] * 2,
        out_specs=(vmem(),) * 3,
        compiler_params=params(24),
        cost_estimate=cost(2),
        name="unpack_first",
    )(where, own, other)


def unit_rows(x):
    inverse = lax.rsqrt(jnp.mean(x * x, axis=-1, keepdims=True) + epsilon)
    return x * inverse, inverse


def front_kernel(
    pairs,
    where,
    starts,
    got,
    target,
    token,
    cos_t,
    sin_t,
    *refs,
):
    own_tail, other_tail = refs[8:10]
    start, embed, hidden, send, joined, lookup, gains, t_s, g_s = refs[10:]
    core, chip, z = where[0], where[1], where[2]
    for blocks, tail, half in ((refs[:4], own_tail, core), (refs[4:8], other_tail, 1 - core)):
        for m in range(4):
            zz = lax.rem(z + m, 4)
            for k in range(4):
                rows = pl.ds(aligned(zz * 192 + (chip ^ k) * 48), 48)
                for t in range(3):
                    joined[rows, pl.ds(aligned(t * D + half * 384, 128), 384)] = blocks[k][
                        m, t * 48 : (t + 1) * 48, :
                    ]
            lookup[pl.ds(aligned(zz * 48), 48), pl.ds(aligned(half * 384, 128), 384)] = tail[
                m, 0:48, :
            ]
    for m in range(4):
        g_s[lax.rem(z + m, 4)] = own_tail[m, 48:64, :].astype(F32)
    for row in range(2):
        gains[row : row + 1, :] = jnp.concatenate(
            [g_s[zz, row : row + 1, :192] for zz in range(4)], axis=1
        )
    gain = gains[0:1, :]
    tokens = token.shape[0]
    piece = 128
    per_batch = tokens // 2 // piece
    groups = HEADS // pairs
    wide_ = pairs * HD
    slots = got.shape[0]
    lane = lax.broadcasted_iota(jnp.int32, (piece, 128), 1)
    first_half = lax.rem(lane, HD) < HD // 2

    def block(i, _):
        at = pl.ds(aligned(i * piece, piece), piece)
        goal = target[at, :]
        slot = lax.broadcasted_iota(jnp.int32, (piece, slots), 1)
        parts = []
        for table in range(2):
            hot = jnp.where(goal[:, table : table + 1] == slot, 1.0, 0.0).astype(BF)
            parts.append(mm(hot, got[:, table * E : (table + 1) * E]))
        rows = (parts[0] + parts[1]).astype(BF)
        embed[at, :] = rows
        x = token[at, :].astype(F32) + mm(rows, lookup[...])
        start[at, :] = x
        normed, _ = unit_rows(x)
        low = (normed * gain).astype(BF)
        hidden[at, :] = low
        projected = mm(low, joined[...])
        begin = pl.ds(aligned(starts[lax.rem(i, per_batch)] * piece, piece), piece)
        c = cos_t[:, begin].T
        s = sin_t[:, begin].T
        c = jnp.concatenate([c, c, c, c], axis=1)
        s = jnp.concatenate([-s, s, -s, s], axis=1)
        turned = []
        for j in range(12):
            v = projected[:, j * 128 : (j + 1) * 128]
            swapped = jnp.where(first_half, pltpu.roll(v, 96, 1), pltpu.roll(v, 32, 1))
            turned.append((v * c + swapped * s).astype(BF))
        for j in range(12, 18):
            turned.append(projected[:, j * 128 : (j + 1) * 128].astype(BF))
        for j, v in enumerate(turned):
            t_s[j * 128 : (j + 1) * 128, :] = swap(v)
        batch = i // per_batch
        to = pl.ds(aligned(lax.rem(i, per_batch) * piece, piece), piece)
        for g in range(groups):
            for t in range(3):
                begin = t * D + g * wide_
                send[batch * groups + g, t * wide_ : (t + 1) * wide_, to] = t_s[
                    begin : begin + wide_, :
                ]
        return 0

    lax.fori_loop(0, tokens // piece, block, 0)


def front(pairs, devices, where, starts, got, target, token, cos_t, sin_t, *blocks):
    tokens = token.shape[0]
    return pl.pallas_call(
        functools.partial(front_kernel, pairs),
        out_shape=(
            jax.ShapeDtypeStruct((tokens, D), F32),
            jax.ShapeDtypeStruct((tokens, E), BF),
            jax.ShapeDtypeStruct((tokens, D), BF),
            jax.ShapeDtypeStruct((devices, 3 * pairs * HD, tokens // 2), BF),
            jax.ShapeDtypeStruct((D, 3 * D), BF),
            jax.ShapeDtypeStruct((E, D), BF),
            jax.ShapeDtypeStruct((2, D), F32),
        ),
        in_specs=[smem()] * 2 + [vmem()] * 15,
        out_specs=(vmem(),) * 7,
        scratch_shapes=[pltpu.VMEM((3 * D, 128), BF), pltpu.VMEM((4, 16, 384), F32)],
        compiler_params=params(60),
        cost_estimate=cost(9),
        name="front",
    )(where, starts, got, target, token, cos_t, sin_t, *blocks)


def mlp_kernel(
    pairs,
    where,
    came,
    start,
    gains,
    upstream,
    *refs,
):
    blocks_own, blocks_other = refs[:4], refs[4:8]
    tall_own, tall_other = refs[8:10], refs[10:12]
    (
        result,
        hidden_out,
        attended_out,
        act_out,
        gate_out,
        up_out,
        gain_grad,
        middle_grad,
        send,
        hidden,
        total,
        back,
        output,
        pair_s,
        w_down,
    ) = refs[12:]
    step = pl.program_id(0)
    core, chip, z = where[0], where[1], where[2]
    gain = gains[1:2, :]
    sides = [
        by_chip(*blocks) + (half,)
        for blocks, half in ((blocks_own, core), (blocks_other, 1 - core))
    ]

    def fill(which, j, take):
        for side in sides:
            for m in range(4):
                for k in range(4):
                    rows = pl.ds(aligned(lax.rem(z + m, 4) * 192 + (chip ^ k) * 48), 48)
                    pair_s[side[2], rows, j * 128 : (j + 1) * 128] = side[which][k][
                        m, take, :
                    ]

    for j in range(4):
        split = 3 if j < 2 else 2
        tile = (4 * step + j) * 48

        @pl.when(step < split)
        def _():
            fill(0, j, pl.ds(aligned(tile), 48))

        @pl.when(step >= split)
        def _():
            fill(1, j, pl.ds(aligned(tile - WCUT), 48))

    turn = step ^ z
    for odd in range(2):

        @pl.when(lax.rem(turn, 2) == odd)
        def _():
            for blocks, side in ((tall_own, core), (tall_other, 1 - core)):
                for k in range(4):
                    rows = pl.ds(aligned((chip ^ k) * 128), 128)
                    for j in range(3):
                        w_down[rows, pl.ds(aligned(side * 384 + j * 128, 128), 128)] = blocks[odd][
                            turn // 2, k, j * 128 : (j + 1) * 128, :
                        ]

    groups = HEADS // pairs
    wide_ = pairs * HD
    half = came.shape[2]

    @pl.when(step == 0)
    def _():
        for _, lower, side in sides:
            for m in range(4):
                for k in range(4):
                    rows = pl.ds(aligned(lax.rem(z + m, 4) * 192 + (chip ^ k) * 48), 48)
                    for j in range(3):
                        begin = 768 + j * 48 - WCUT
                        output[rows, pl.ds(aligned(side * 384 + j * 128, 128), 128)] = lower[k][
                            m, begin : begin + 48, :
                        ]
        for batch in range(2):
            at = slice(batch * half, (batch + 1) * half)
            parts = []
            for h in range(half // 128):
                lanes = slice(h * 128, (h + 1) * 128)
                parts.append(
                    jnp.concatenate(
                        [swap(came[batch * groups + g, :, lanes]) for g in range(groups)], axis=1
                    )
                )
            rows = jnp.concatenate(parts, axis=0)
            attended_out[at, :] = rows
            x = start[at, :] + mm(rows, output[...])
            total[at, :] = x
            middle_grad[at, :] = x
            normed, _ = unit_rows(x)
            low = (normed * gain).astype(BF)
            hidden[at, :] = low
            hidden_out[at, :] = low
        back[...] = jnp.zeros_like(back)

    for batch in range(2):
        at = slice(batch * half, (batch + 1) * half)
        gate = mm(hidden[at, :], pair_s[0])
        up = mm(hidden[at, :], pair_s[1])
        sigmoid = jax.nn.sigmoid(gate)
        swish = gate * sigmoid
        act = (swish * up).astype(BF)
        act_out[at, :] = act
        total[at, :] += mm(act, w_down[...])
        grad = mm(upstream[at, :], w_down[...], NT)
        gate_grad = (grad * up * sigmoid * (1.0 + gate * (1.0 - sigmoid))).astype(BF)
        up_grad = (grad * swish).astype(BF)
        gate_out[at, :] = gate_grad
        up_out[at, :] = up_grad
        back[at, :] += mm(gate_grad, pair_s[0], NT) + mm(up_grad, pair_s[1], NT)

    @pl.when(step == pl.num_programs(0) - 1)
    def _():
        gains = jnp.zeros((1, D), F32)
        for batch in range(2):
            at = slice(batch * half, (batch + 1) * half)
            result[at, :] = total[at, :].astype(BF)
            normed, inverse = unit_rows(middle_grad[at, :])
            grad = back[at, :]
            gains += jnp.sum(grad * normed, axis=0, keepdims=True)
            weighted = grad * gain
            grad = upstream[at, :].astype(F32) + inverse * (
                weighted - normed * jnp.mean(weighted * normed, axis=-1, keepdims=True)
            )
            middle_grad[at, :] = grad
            heads = mm(output[...], grad.astype(BF), NT).astype(BF)
            for g in range(groups):
                send[batch * groups + g] = heads[g * wide_ : (g + 1) * wide_, :]
        gain_grad[...] = gains


def mlp(pairs, where, came, start, gains, upstream, *blocks):
    tokens = start.shape[0]
    width = 512
    steps = FF // width
    whole = lambda shape: pl.BlockSpec(
        shape, lambda i: (0,) * len(shape), pipeline_mode=pl.Buffered(1)
    )
    column = pl.BlockSpec((tokens, width), lambda i: (0, i))
    return pl.pallas_call(
        functools.partial(mlp_kernel, pairs),
        grid=(steps,),
        out_shape=(
            pltpu.HBM((tokens, D), BF),
            pltpu.HBM((tokens, D), BF),
            pltpu.HBM((tokens, D), BF),
            jax.ShapeDtypeStruct((tokens, FF), BF),
            jax.ShapeDtypeStruct((tokens, FF), BF),
            jax.ShapeDtypeStruct((tokens, FF), BF),
            jax.ShapeDtypeStruct((1, D), F32),
            jax.ShapeDtypeStruct((tokens, D), F32),
            pltpu.HBM(came.shape, BF),
        ),
        in_specs=[smem()] + [whole(x.shape) for x in (came, start, gains, upstream, *blocks)],
        out_specs=(
            whole((tokens, D)),
            whole((tokens, D)),
            whole((tokens, D)),
            column,
            column,
            column,
            whole((1, D)),
            whole((tokens, D)),
            whole(came.shape),
        ),
        scratch_shapes=[
            pltpu.VMEM((tokens, D), BF),
            pltpu.VMEM((tokens, D), F32),
            pltpu.VMEM((tokens, D), F32),
            pltpu.VMEM((D, D), BF),
            pltpu.VMEM((2, D, width), BF),
            pltpu.VMEM((width, D), BF),
        ],
        compiler_params=params(44),
        cost_estimate=cost(23),
        name="mlp",
    )(where, came, start, gains, upstream, *blocks)


UPPER, LOWER, ALONG = (1, 3, 2, 0), (2, 3, 1, 0), (1, 3, 2, 0)


def placed(order, value):
    at = jnp.int32(3)
    for place_, here in enumerate(order[:3]):
        at = jnp.where(value == here, place_, at)
    return at


def weight_grads_kernel(
    where,
    hidden,
    gate,
    up,
    act,
    upstream,
    attended,
    middle,
    own_u,
    own_l,
    other_u,
    other_l,
    wide_s,
    tall_s,
    out_s,
):
    core, chip, z = where[0], where[1], where[2]
    sides = ((own_u, own_l, core), (other_u, other_l, 1 - core))

    def rows_of(k, m):
        return pl.ds(aligned((z ^ m) * 192 + (chip ^ k) * 48), 48)

    def chunk(c, _):
        at = pl.ds(aligned(c * 256, 256), 256)
        wide_s[0] = mm(hidden[...], gate[:, at], TN).astype(BF)
        wide_s[1] = mm(hidden[...], up[:, at], TN).astype(BF)
        tall = mm(act[:, at], upstream[...], TN).astype(BF)
        tall_s[0] = tall[:, :384]
        tall_s[1] = tall[:, 384:]

        def put(which, ks, begin):
            for side in sides:
                for i, m in enumerate(ALONG):
                    for n, k in enumerate(ks):
                        block = wide_s[side[2], rows_of(k, m), :]
                        for j in range(2):
                            to = pl.ds(aligned((2 * c + j) * 48 - begin), 48)
                            side[which][n, i, to, :] = block[:, j * 128 : (j + 1) * 128]

        @pl.when(c < 7)
        def _():
            put(0, UPPER, 0)

        @pl.when(c == 7)
        def _():
            put(1, LOWER, CUT)

        i = placed(ALONG, (c // 2) ^ z)
        for _, lower, half in sides:
            for b in range(2):
                n = placed(LOWER, (lax.rem(c, 2) * 2 + b) ^ chip)
                block = tall_s[half, b * 128 : (b + 1) * 128, :]
                for j in range(3):
                    begin = 768 + j * 128 - CUT
                    lower[n, i, begin : begin + 128, :] = block[:, j * 128 : (j + 1) * 128]
        return 0

    lax.fori_loop(0, FF // 256, chunk, 0)
    square = mm(attended[...], middle[...].astype(BF), TN).astype(BF)
    out_s[0] = square[:, :384]
    out_s[1] = square[:, 384:]
    for _, lower, half in sides:
        for i, m in enumerate(ALONG):
            for n, k in enumerate(LOWER):
                block = out_s[half, rows_of(k, m), :]
                for j in range(3):
                    begin = 1152 + j * 48 - CUT
                    lower[n, i, begin : begin + 48, :] = block[:, j * 128 : (j + 1) * 128]


def weight_grads(where, *operands):
    upper = jax.ShapeDtypeStruct((4, 4, CUT, 128), BF)
    lower = jax.ShapeDtypeStruct((4, 4, 1296 - CUT, 128), BF)
    return pl.pallas_call(
        weight_grads_kernel,
        out_shape=(upper, lower) * 2,
        in_specs=[smem()] + [vmem()] * 7,
        out_specs=(vmem(),) * 4,
        scratch_shapes=[
            pltpu.VMEM((2, D, 256), BF),
            pltpu.VMEM((2, 256, 384), BF),
            pltpu.VMEM((2, D, 384), BF),
        ],
        compiler_params=params(60),
        cost_estimate=cost(15),
        name="weight_grads",
    )(where, *operands)


def back_kernel(
    where,
    came_a,
    came_b,
    hidden,
    start,
    middle,
    joined,
    lookup,
    gain,
    second_gain,
    embed,
    target,
    token_grad,
    send,
    own,
    other,
    df_s,
    half_s,
    look_s,
    gain_s,
):
    core, chip, z = where[0], where[1], where[2]
    widths = [ref.shape[1] // 3 for ref in (came_a, came_b)]
    groups = D // sum(widths)
    rows = came_a.shape[2]
    tokens = 2 * rows
    for i in range(tokens // 128):
        batch, lanes = divmod(i * 128, rows)
        lanes = slice(lanes, lanes + 128)
        parts = [
            (swap(ref[batch * groups + g, :, lanes]), w)
            for g in range(groups)
            for ref, w in zip((came_a, came_b), widths)
        ]
        for t in range(3):
            df_s[i * 128 : (i + 1) * 128, t * D : (t + 1) * D] = jnp.concatenate(
                [part[:, t * w : (t + 1) * w] for part, w in parts], axis=1
            )

    def kind(t, _):
        grad = mm(hidden[...], df_s[:, pl.ds(aligned(t * D, 128), D)], TN).astype(BF)
        half_s[0] = grad[:, :384]
        half_s[1] = grad[:, 384:]
        for out, half in ((own, core), (other, 1 - core)):
            for m in range(4):
                zz = z ^ m
                for k in range(4):
                    block = half_s[half, pl.ds(aligned(zz * 192 + (chip ^ k) * 48), 48), :]
                    for j in range(3):
                        to = pl.ds(aligned((t * 3 + j) * 48), 48)
                        out[k, m, to, :] = block[:, j * 128 : (j + 1) * 128]
        return 0

    lax.fori_loop(0, 3, kind, 0)

    gains = jnp.zeros((1, D), F32)
    lows = []
    for batch in range(2):
        at = slice(batch * rows, (batch + 1) * rows)
        grad = mm(df_s[at, :], joined[...], NT)
        normed, inverse = unit_rows(start[at, :])
        gains += jnp.sum(grad * normed, axis=0, keepdims=True)
        weighted = grad * gain[0:1, :]
        grad = middle[at, :] + inverse * (
            weighted - normed * jnp.mean(weighted * normed, axis=-1, keepdims=True)
        )
        token_grad[at, :] = grad
        lows.append(grad.astype(BF))
    low = jnp.concatenate(lows, axis=0)
    look = mm(embed[...], low, TN).astype(BF)
    for half in range(2):
        for j in range(3):
            begin = half * 384 + j * 128
            look_s[half, j] = look[:, begin : begin + 128]
    for half, row in enumerate((gains, second_gain[...])):
        parts = [row[:, j * 128 : (j + 1) * 128] for j in range(6)]
        gain_s[half] = jnp.concatenate(parts + [jnp.zeros((42, 128), F32)], axis=0).astype(BF)
    for out, half in ((own, core), (other, 1 - core)):
        for m in range(4):
            zz = z ^ m
            for k in range(4):
                yx = chip ^ k

                @pl.when(yx < 3)
                def _():
                    out[k, m, 432:480, :] = look_s[
                        half, lax.rem(yx, 3), pl.ds(aligned(zz * 48), 48), :
                    ]

                @pl.when(yx == 3)
                def _():
                    out[k, m, 432:480, :] = gain_s[half]

    de = mm(low, lookup[...], NT).astype(BF)
    slots = send.shape[0]
    slot = lax.broadcasted_iota(jnp.int32, (slots, tokens), 0)
    parts = []
    for table in range(2):
        hot = jnp.where(slot == target[table : table + 1, :], 1.0, 0.0).astype(BF)
        parts.append(mm(hot, de))
    send[...] = jnp.concatenate(parts, axis=1).astype(BF)


def back_pass(slots, where, *operands):
    tokens = operands[2].shape[0]
    shape = jax.ShapeDtypeStruct((4, 4, 480, 128), BF)
    return pl.pallas_call(
        back_kernel,
        out_shape=(
            jax.ShapeDtypeStruct((tokens, D), F32),
            jax.ShapeDtypeStruct((slots, 2 * E), BF),
            shape,
            shape,
        ),
        in_specs=[smem()] + [vmem()] * 11,
        out_specs=(vmem(),) * 4,
        scratch_shapes=[
            pltpu.VMEM((tokens, 3 * D), BF),
            pltpu.VMEM((2, D, 384), BF),
            pltpu.VMEM((2, 3, E, 128), BF),
            pltpu.VMEM((2, 48, 128), BF),
        ],
        compiler_params=params(60),
        cost_estimate=cost(13),
        name="back",
    )(where, *operands)


def rotate(values, cosines, sines):
    half = values.shape[-1] // 2
    a, b = values[..., :half], values[..., half:]
    c, s = cosines[:, None, :], sines[:, None, :]
    return jnp.concatenate([a * c - b * s, b * c + a * s], axis=-1)


def normalize(rows):
    inverse = lax.rsqrt(jnp.mean(rows * rows, axis=-1, keepdims=True) + epsilon)
    return rows * inverse, inverse


def norm_backward(hidden_grad, normed, inverse, gain):
    weighted = hidden_grad * gain
    return inverse * (weighted - normed * jnp.mean(weighted * normed, axis=-1, keepdims=True))


def local(
    token_embed,
    bigram_ids,
    trigram_ids,
    bigram_table,
    trigram_table,
    block_deal,
    lookup_weight,
    attention_gain,
    joined_weight,
    output_weight,
    feedforward_gain,
    expand_weight,
    contract_weight,
    cotangent,
):
    contexts = lax.axis_size("ctx")
    shards = lax.axis_size("fsdp")
    devices = contexts * shards
    batches, local_rows = token_embed.shape[:2]
    tokens = batches * local_rows
    length = local_rows * contexts
    capacity = max(2, 2 * tokens // devices)
    table_rows = bigram_table.shape[0]
    piece = local_rows // 2
    pieces = length // piece
    pairs = -(-batches * HEADS // contexts)
    while HEADS % pairs:
        pairs += 1
    both = ("ctx", "fsdp")

    ids = jnp.stack([bigram_ids.reshape(-1), trigram_ids.reshape(-1)])
    requests, target_row, target_col = placement(ids, table_rows, devices, capacity)
    asked = exchange(requests, both)
    codes = jnp.stack([asked[:, :capacity].reshape(-1), asked[:, capacity:].reshape(-1)], axis=1)
    got = exchange(
        read_rows(codes.T, bigram_table.T, trigram_table.T).reshape(devices, capacity, 2 * E), both
    ).reshape(devices * capacity, 2 * E)

    lookup = gather_weight(lookup_weight)
    joined = gather_weight(joined_weight)
    output = gather_weight(output_weight)
    gains = gather_gains(jnp.stack([attention_gain, feedforward_gain])).astype(F32)
    first_gain, second_gain = gains[0], gains[1]
    expand = gather_weight(expand_weight)
    contract = gather_weight(contract_weight)

    order = jnp.argmin(
        jnp.abs(block_deal[None, :] - jnp.arange(pieces, dtype=jnp.int32)[:, None]), axis=1
    ).astype(jnp.int32)
    frequency = jnp.exp(-math.log(10000.0) * (2.0 * jnp.arange(HD // 2, dtype=F32) / HD))
    slot = lax.axis_index("ctx") * local_rows + jnp.arange(local_rows, dtype=jnp.int32)
    position = block_deal[slot // piece] * piece + slot % piece
    angles = position.astype(F32)[:, None] * frequency[None, :]
    cosines, sines = jnp.cos(angles), jnp.sin(angles)
    all_angles = jnp.arange(length, dtype=F32)[:, None] * frequency[None, :]
    all_cosines, all_sines = jnp.cos(all_angles), jnp.sin(all_angles)

    slots = jnp.arange(devices * capacity, dtype=jnp.int32)
    hot_b = (target_col[:, 0:1] == slots[None, :]).astype(BF)
    hot_t = (target_col[:, 1:2] == slots[None, :]).astype(BF)
    embedded = (mm(hot_b, got[:, :E]) + mm(hot_t, got[:, E:])).astype(BF)
    start = token_embed.reshape(tokens, D).astype(F32) + mm(embedded, lookup)
    normed_first, inverse_first = normalize(start)
    hidden_first = (normed_first * first_gain).astype(BF)
    projected = mm(hidden_first, joined).reshape(batches, local_rows, 3, HEADS, HD)
    cos_b, sin_b = cosines[None, :, None, :], sines[None, :, None, :]
    turn = lambda x: jnp.concatenate(
        [
            x[..., : HD // 2] * cos_b - x[..., HD // 2 :] * sin_b,
            x[..., HD // 2 :] * cos_b + x[..., : HD // 2] * sin_b,
        ],
        axis=-1,
    )
    qkv = jnp.stack(
        [turn(projected[:, :, 0]), turn(projected[:, :, 1]), projected[:, :, 2]], axis=2
    ).astype(BF)
    qkv = qkv.reshape(batches, local_rows, 3, D)
    rows = exchange(by_head(qkv, contexts, pairs), "ctx").reshape(length, 3 * pairs * HD)
    attended_rows, attended_t, logsum = attend(order, rows, pairs, piece)
    attended = by_token(
        exchange(attended_rows.reshape(contexts, local_rows, pairs * HD), "ctx"), batches, 1, pairs
    ).reshape(tokens, D)
    middle = start + mm(attended, output)
    normed_second, inverse_second = normalize(middle)
    hidden_second = (normed_second * second_gain).astype(BF)
    gate_up = mm(hidden_second, expand)
    gate, up = gate_up[:, :FF], gate_up[:, FF:]
    sigmoid = jax.nn.sigmoid(gate)
    swish = gate * sigmoid
    activated = (swish * up).astype(BF)
    result = (middle + mm(activated, contract)).astype(BF)

    upstream = cotangent.reshape(tokens, D)
    activated_grad = mm(upstream, contract, NT)
    gate_up_grad = jnp.concatenate(
        [
            activated_grad * up * sigmoid * (1.0 + gate * (1.0 - sigmoid)),
            activated_grad * swish,
        ],
        axis=-1,
    ).astype(BF)
    hidden_second_grad = mm(gate_up_grad, expand, NT)
    second_gain_term = jnp.sum(hidden_second_grad * normed_second, axis=0)
    middle_grad = upstream.astype(F32) + norm_backward(
        hidden_second_grad, normed_second, inverse_second, second_gain
    )
    middle_low = middle_grad.astype(BF)
    attended_grad = mm(middle_low, output, NT).astype(BF)
    grad_rows = exchange(
        by_head(attended_grad.reshape(batches, local_rows, 1, D), contexts, pairs), "ctx"
    ).reshape(length, pairs * HD)
    contract_term = mm(activated, upstream, TN).astype(BF)
    expand_term = mm(hidden_second, gate_up_grad, TN).astype(BF)
    output_term = mm(attended, middle_low, TN).astype(BF)
    contract_grad = reduce_grad(contract_term)
    expand_grad = reduce_grad(expand_term)
    output_grad = reduce_grad(output_term)

    grad_rows = attend_grad(
        order,
        rows,
        grad_rows,
        attended_t,
        logsum,
        all_cosines,
        all_sines,
        all_cosines.T,
        all_sines.T,
        pairs,
        piece,
    )
    joined_local = by_token(
        exchange(grad_rows.reshape(contexts, local_rows, 3 * pairs * HD), "ctx"), batches, 3, pairs
    ).reshape(tokens, 3 * D)
    joined_grad = reduce_grad(mm(hidden_first, joined_local, TN).astype(BF))
    hidden_first_grad = mm(joined_local, joined, NT)
    first_gain_term = jnp.sum(hidden_first_grad * normed_first, axis=0)
    start_grad = middle_grad + norm_backward(
        hidden_first_grad, normed_first, inverse_first, first_gain
    )
    start_low = start_grad.astype(BF)
    lookup_grad = reduce_grad(mm(embedded, start_low, TN).astype(BF))
    embed_grad = mm(start_low, lookup, NT).astype(BF)
    give_b = (target_row[0:1, :] == slots[:, None]).astype(BF)
    give_t = (target_row[1:2, :] == slots[:, None]).astype(BF)
    send = jnp.concatenate([mm(give_b, embed_grad), mm(give_t, embed_grad)], axis=1).astype(BF)
    arrived = exchange(send.reshape(devices, capacity, 2 * E), both)
    bigram_grad, trigram_grad = add_rows(
        codes, arrived.reshape(devices * capacity, 2 * E), table_rows
    )
    gain_terms = lax.psum(jnp.stack([first_gain_term, second_gain_term]), both)
    gain_share = lax.dynamic_slice_in_dim(
        gain_terms, lax.axis_index("fsdp") * (D // shards), D // shards, axis=1
    )
    return (
        result.reshape(batches, local_rows, D),
        start_grad.reshape(batches, local_rows, D),
        bigram_grad.T,
        trigram_grad.T,
        lookup_grad,
        gain_share[0],
        joined_grad,
        output_grad,
        gain_share[1],
        expand_grad,
        contract_grad,
    )


def local_packed(
    token_embed,
    bigram_ids,
    trigram_ids,
    bigram_table,
    trigram_table,
    block_deal,
    lookup_weight,
    attention_gain,
    joined_weight,
    output_weight,
    feedforward_gain,
    expand_weight,
    contract_weight,
    cotangent,
):
    contexts = lax.axis_size("ctx")
    shards = lax.axis_size("fsdp")
    devices = contexts * shards
    batches, local_rows = token_embed.shape[:2]
    tokens = batches * local_rows
    length = local_rows * contexts
    capacity = max(2, 2 * tokens // devices)
    table_rows = bigram_table.shape[0]
    piece = local_rows // 2
    pieces = length // piece
    pairs = -(-batches * HEADS // contexts)
    while HEADS % pairs:
        pairs += 1
    both = ("ctx", "fsdp")


    core, chip, z = place()
    where = jnp.stack([core, chip, z]).astype(jnp.int32)
    ids = jnp.stack([bigram_ids.reshape(-1), trigram_ids.reshape(-1)])
    requests, target_row, target_col = placement(ids, table_rows, devices, capacity)
    asked = exchange(requests, both)
    gain_rows = jnp.pad(jnp.stack([attention_gain, feedforward_gain]), ((0, 14), (0, 192)))
    first, second, third = pack_weights(
        after(where, requests),
        joined_weight,
        output_weight,
        lookup_weight,
        gain_rows,
        expand_weight,
        contract_weight,
    )
    along = spread_fsdp(first)
    column = jnp.stack([p[:144] for p in along])
    pieces_z = along
    near = [over_ctx(column, 2), over_ctx(column, 4)]
    tall = [over_ctx(third, 2), over_ctx(third, 4)]
    asked, tall, third = lax.optimization_barrier((asked, tall, third))
    tall.append(over_ctx(third, 6))
    codes = jnp.stack([asked[:, :capacity].reshape(-1), asked[:, capacity:].reshape(-1)])
    answer = read_rows(
        after(codes, column), in_hbm(bigram_table.T), in_hbm(trigram_table.T)
    )
    ready = after(second, column)
    early = [along_fsdp(ready, k) for k in (1, 3)]
    answer, near, early, tall = lax.optimization_barrier((answer, near, early, tall))
    got = exchange(answer.reshape(devices, capacity, 2 * E), both)
    answer, column = lax.optimization_barrier((answer, column))
    last = over_ctx(column, 6)
    last, near, pieces_z, early = lax.optimization_barrier((last, near, pieces_z, early))
    tail = jnp.stack([p[144:] for p in pieces_z])
    first_own = [column, *near, last]
    first_other = [over_ctx(block, 1) for block in first_own]
    first_blocks = (*first_own, *first_other, tail, over_ctx(tail, 1))
    three = [second, early[1], early[0]]
    near = [
        over_ctx(jnp.stack([block[:WCUT] for block in three]), 2),
        over_ctx(jnp.stack([block[WCUT:] for block in three]), 4),
    ]
    got, ready = lax.optimization_barrier((got, ready))
    late = along_fsdp(ready, 2)
    got = got.reshape(devices * capacity, 2 * E)

    order = jnp.sum(
        jnp.where(
            block_deal[None, :] == jnp.arange(pieces, dtype=jnp.int32)[:, None],
            jnp.arange(pieces, dtype=jnp.int32)[None, :],
            0,
        ),
        axis=1,
    )
    starts = lax.dynamic_slice_in_dim(block_deal, lax.axis_index("ctx") * 2, 2)
    frequency = jnp.exp(-math.log(10000.0) * (2.0 * jnp.arange(HD // 2, dtype=F32) / HD))
    angles = frequency[:, None] * jnp.arange(length, dtype=F32)[None, :]
    cos_t, sin_t = lax.optimization_barrier((jnp.cos(angles), jnp.sin(angles)))

    start, embedded, hidden_first, sent, joined, lookup, gains = front(
        pairs,
        contexts,
        where,
        starts,
        got,
        target_col,
        token_embed.reshape(tokens, D),
        cos_t,
        sin_t,
        *first_blocks,
    )
    sent, near, tall = lax.optimization_barrier((sent, near, tall))
    near, late, tall = lax.optimization_barrier((near, late, tall))
    tall = jnp.stack([third] + tall)
    tall = jnp.stack([tall, over_fsdp(tall, 2)])
    near_late = [over_ctx(late[:WCUT], 2), over_ctx(late[WCUT:], 4)]
    rows = exchange(sent, "ctx")
    own_blocks = [three[0], three[1], late, three[2]]
    near_x, near_y = (
        jnp.stack([*[block[cut] for block in own_blocks], part[0], part[1], last, part[2]]).reshape(
            2, 4, -1, 128
        )
        for cut, part, last in zip((slice(WCUT), slice(WCUT, None)), near, near_late)
    )
    rows, near_x, near_y, tall = lax.optimization_barrier((rows, near_x, near_y, tall))
    tall_odd = over_fsdp(tall, 1)
    far_y, far_x = over_ctx(near_x, 4), over_ctx(near_y, 2)
    others = [over_ctx(near_x, 1), over_ctx(near_y, 1)]
    attended_rows, attended_t, logsum = attend_short(order, rows, pairs, piece)
    came = exchange(attended_rows, "ctx")
    far_y, far_x, tall, tall_odd, attended_rows = lax.optimization_barrier(
        (far_y, far_x, tall, tall_odd, attended_rows)
    )
    talls = [tall, tall_odd, over_ctx(tall, 1), over_ctx(tall_odd, 1)]
    others += [over_ctx(far_y, 1), over_ctx(far_x, 1)]
    upstream = cotangent.reshape(tokens, D)
    (
        result,
        hidden_second,
        attended,
        activated,
        gate_grad,
        up_grad,
        second_gain_term,
        middle_grad,
        sent,
    ) = mlp(pairs, where, came, start, gains, upstream, near_x, near_y, far_y, far_x, *others, *talls)

    grad_rows = exchange(sent, "ctx")
    own_u, own_l, other_u, other_l = weight_grads(
        where, hidden_second, gate_grad, up_grad, activated, upstream, attended, middle_grad
    )
    other_u, other_l = after((other_u, other_l), grad_rows)
    core_u, core_l = over_ctx(other_u, 1), over_ctx(other_l, 1)
    part = functools.partial(attend_grad_short, order)
    shared = (in_hbm(attended_t), logsum, in_hbm(cos_t), in_hbm(sin_t), pairs, piece)
    grad_a = part(rows, grad_rows, *shared, 0, 1)
    came_a = exchange(grad_a, "ctx")
    core_u, core_l = after((core_u, core_l), grad_a)
    near_u = add_all(own_u[:2], core_u[:2]).astype(BF)
    near_l = add_all(own_l[:2], core_l[:2]).astype(BF)
    from_x, from_y = over_ctx(near_u, 2), over_ctx(near_l, 4)
    grad_b = part(after(rows, near_u, near_l), grad_rows, *shared, 1, pairs - 1)
    from_x, from_y, came_a = lax.optimization_barrier((from_x, from_y, came_a))
    far_u = add_all(own_u[2], core_u[2], from_x[1]).astype(BF)
    far_l = add_all(own_l[2], core_l[2], from_y[1]).astype(BF)
    came_b = exchange(grad_b, "ctx")
    came_b, far_u, far_l = lax.optimization_barrier((came_b, far_u, far_l))
    from_far = [over_ctx(far_u, 4), over_ctx(far_l, 2)]
    start_grad, send, own_j, other_j = back_pass(
        devices * capacity,
        where,
        came_a,
        came_b,
        hidden_first,
        start,
        middle_grad,
        joined,
        lookup,
        gains,
        second_gain_term,
        embedded,
        target_row,
    )
    from_core = over_ctx(other_j, 1)
    send, from_far = lax.optimization_barrier((send, from_far))
    sums_u = add_all(own_u[3], core_u[3], from_x[0], from_far[0]).astype(BF)
    sums_l = add_all(own_l[3], core_l[3], from_y[0], from_far[1]).astype(BF)
    from_z = over_fsdp(jnp.concatenate([sums_u[:2], sums_l[:2]], axis=1), 1)
    total_m = jnp.concatenate([sums_u[2:], sums_l[2:]], axis=1)
    arrived = exchange(send.reshape(devices, capacity, 2 * E), both)
    half_j = [add_all(own_j[k], from_core[k]).astype(BF) for k in (1, 2, 3)]
    from_chips = [over_ctx(block, 2 * k) for k, block in zip((1, 2, 3), half_j)]
    from_z, own_j, from_core = lax.optimization_barrier((from_z, own_j, from_core))
    near_m, far_m = add_blocks(total_m[1], [from_z[0]]), add_blocks(total_m[0], [from_z[1]])
    from_z = over_fsdp(far_m, 2)
    total_j = add_all(own_j[0], from_core[0], *from_chips).astype(BF)
    from_fsdp = [over_fsdp(total_j[m], m) for m in (1, 2, 3)]
    from_z, kept = lax.optimization_barrier((from_z, total_j[0]))
    piece_m = add_blocks(near_m, [from_z])
    every_m = [over_ctx(piece_m, 2 * k) for k in (1, 2)]
    arrived = arrived.reshape(devices * capacity, 2 * E)
    from_fsdp[0], late_codes = lax.optimization_barrier((from_fsdp[0], codes.T))
    bigram_grad = add_table(0, late_codes, arrived, table_rows)
    bigram_grad, from_fsdp, every_m = lax.optimization_barrier((bigram_grad, from_fsdp, every_m))
    every_m.append(over_ctx(piece_m, 6))
    piece_j = add_blocks(kept, from_fsdp)
    every_j = to_chips([piece_j] * 4)
    late_codes, piece_j = lax.optimization_barrier((late_codes, piece_j))
    trigram_grad = add_table(1, late_codes, arrived, table_rows)
    trigram_grad, every_m, every_j = lax.optimization_barrier((trigram_grad, every_m, every_j))
    blocks_m = jnp.stack([piece_m] + every_m)
    other_m = over_ctx(blocks_m, 1)
    blocks_j = jnp.stack([piece_j] + every_j)
    other_j = over_ctx(blocks_j, 1)
    expand_grad, contract_grad, output_grad = unpack_second(where, blocks_m, other_m)
    joined_grad, lookup_grad, gain_grads = unpack_first(where, blocks_j, other_j)
    gain_share = lax.dynamic_slice_in_dim(
        gain_grads[:, :6].reshape(2, D), z * (D // shards), D // shards, axis=1
    )
    return (
        result.reshape(batches, local_rows, D),
        start_grad.reshape(batches, local_rows, D),
        bigram_grad.T,
        trigram_grad.T,
        lookup_grad,
        gain_share[0],
        joined_grad,
        output_grad,
        gain_share[1],
        expand_grad,
        contract_grad,
    )


def solution(mesh):
    fits = mesh.shape["ctx"] == 8 and mesh.shape["fsdp"] == 4
    return jax.shard_map(
        local_packed if fits else local,
        mesh=mesh,
        in_specs=(
            P("fsdp", "ctx", None),
            P("fsdp", "ctx"),
            P("fsdp", "ctx"),
            P(("ctx", "fsdp"), None),
            P(("ctx", "fsdp"), None),
            P(),
            P("fsdp", None),
            P("fsdp"),
            P("fsdp", None),
            P("fsdp", None),
            P("fsdp"),
            P("fsdp", None),
            P("fsdp", None),
            P("fsdp", "ctx", None),
        ),
        out_specs=(
            P("fsdp", "ctx", None),
            P("fsdp", "ctx", None),
            P(("ctx", "fsdp"), None),
            P(("ctx", "fsdp"), None),
            P("fsdp", None),
            P("fsdp"),
            P("fsdp", None),
            P("fsdp", None),
            P("fsdp"),
            P("fsdp", None),
            P("fsdp", None),
        ),
        check_vma=False,
    )
```
